32 devices in a mesh: gx: 8 (over z, y), gz: 4 (over x, core).
Axes of the slice: x: 2, y: 2, z: 4, core: 2. Of those that a mesh axis runs over, the one named last changes fastest.
Arguments:
- flow_state: float32 [4, 128, 128, 128], P(None, 'gx', 'gz'), may hold values from -6 to 6
- slot_ids: int32 [256], P(('gx', 'gz')), may hold values from -1 to 127, as said below
- corners: int32 [3, 256], P(None, ('gx', 'gz')), may hold values from 0 to 127, as said below
- marker_cells: int32 [3, 256, 512], P(None, ('gx', 'gz')), may hold values from 1 to 21
- marker_frac: float32 [3, 256, 512], P(None, ('gx', 'gz')), may hold values from 0 to 1
- particle_velocity: float32 [3, 128], replicated, may hold values from -4 to 4
- particle_spin: float32 [3, 128], replicated, may hold values from -0.6 to 0.6
Outputs:
- velocity: float32 [3, 128, 128, 128], P(None, 'gx', 'gz')
- source: float32 [2, 128, 128, 128], P(None, 'gz', 'gx')
The draws below stay inside these ranges and needn't reach their ends.
Inputs may be any that keep to these rules, and one draw needn't show every extreme that they name: `slot_ids`: the ids of the particles that a tile's device owns stand in its 8 slots and -1 in each empty slot; every id 0 to 127 stands in exactly one slot; some device has all of its slots full. corners[:, s] is the first cell of the box of slot s; the box's x and z ranges wrap around the grid; the cells (corners[0, s] + 12) mod 128 and (corners[2, s] + 12) mod 128 lie in the x and z ranges of the tile whose device holds slot s, and corners[1, s] <= 104.
All inputs are finite; a program needn't handle non-finite values.
Results may differ from the reference program's by a relative error of at most 0.0003.
Values sent between devices are 32-bit elements; how exact they have to be, the bound alone decides.
No kernel may reach another device: no remote copies, remote signals or barrier semaphores. Data moves between devices by JAX's collectives and lax.ppermute only.
A program may use at most 64 MiB of HBM per device.

```python
import math
import jax
import jax.numpy as jnp
from jax import lax

CX = 16
CZ = 32
CY = 128
BOX = 24
NM = 512
MAXB = 8
HALF = 12
NX = 128
NZ = 128
SLOTS = 256
NP = 128


def draw_slot_ids(key, part):
    devices = SLOTS // MAXB
    half_load = MAXB // 2
    order_key, count_key, ident_key = jax.random.split(jax.random.fold_in(key, 11), 3)
    pairing = jax.random.permutation(order_key, devices)
    surplus = jax.random.randint(count_key, (devices // 2,), 0, half_load + 1, dtype=jnp.int32)
    surplus = surplus.at[0].set(half_load)
    counts = jnp.zeros((devices,), jnp.int32)
    counts = counts.at[pairing[0::2]].set(half_load + surplus)
    counts = counts.at[pairing[1::2]].set(half_load - surplus)
    occupied = jnp.arange(MAXB, dtype=jnp.int32)[None, :] < counts[:, None]
    flat_live = occupied.reshape(-1).astype(jnp.int32)
    rank_index = jnp.clip(jnp.cumsum(flat_live) - 1, 0, NP - 1)
    particle_ids = jax.random.permutation(ident_key, NP).astype(jnp.int32)
    return jnp.where(flat_live > 0, particle_ids[rank_index], -1).astype(jnp.int32)


def draw_corners(key, part):
    tiles_z = NZ // CZ
    owner_index = jnp.arange(SLOTS, dtype=jnp.int32) // MAXB
    tile_x = owner_index // tiles_z
    tile_z = owner_index % tiles_z
    draw_keys = jax.random.split(jax.random.fold_in(key, 23), 3)
    centre_x = tile_x * CX + jax.random.randint(draw_keys[0], (SLOTS,), 0, CX, dtype=jnp.int32)
    centre_z = tile_z * CZ + jax.random.randint(draw_keys[2], (SLOTS,), 0, CZ, dtype=jnp.int32)
    first_y = jax.random.randint(draw_keys[1], (SLOTS,), 0, CY - BOX + 1, dtype=jnp.int32)
    first_x = (centre_x - BOX // 2) % NX
    first_z = (centre_z - BOX // 2) % NZ
    return jnp.stack([first_x, first_y, first_z]).astype(jnp.int32)


def with_ends(entries, stream_key, least, top_value):
    index_at = [jax.random.randint(jax.random.fold_in(stream_key, axis), (), 0, length) for axis, length in enumerate(entries.shape)]
    widest = entries.shape.index(max(entries.shape))
    neighbour = index_at[:widest] + [(index_at[widest] + 1) % entries.shape[widest]] + index_at[widest + 1:]
    return entries.at[tuple(index_at)].set(least).at[tuple(neighbour)].set(top_value)


def steps_of(rng, extent, cuts, least, high):
    gain, own = 1.0, jax.random.fold_in(rng, 6)
    for dim, blocks in cuts:
        heights = jnp.exp(jax.random.uniform(jax.random.fold_in(own, dim), (blocks,), jnp.float32, least / len(cuts), high / len(cuts)))
        gain = gain * jnp.repeat(heights, extent[dim] // blocks).reshape([-1 if axis == dim else 1 for axis in range(len(extent))])
    return gain


def gaussian(key, dims, scale, most, pieces=(), kind=jnp.bfloat16):
    result = scale * jax.random.normal(key, dims, jnp.float32)
    if pieces:
        result = result * steps_of(key, dims, pieces, -0.22, 0.18)
    return jnp.clip(result, -most, most).astype(kind)


def setup_inputs(seed: int = 0) -> dict:
    splits = jax.random.split(jax.random.key(seed), 8)
    flow_state = gaussian(splits[0], (4, NX, NZ, CY), 1.0, 6.0, ((1, 8), (2, 4)), jnp.float32)
    slot_ids = draw_slot_ids(jax.random.fold_in(splits[7], 71), 0)
    corners = draw_corners(jax.random.fold_in(splits[7], 71), 0)
    marker_cells = with_ends(jax.random.randint(splits[3], (3, SLOTS, NM), 1, BOX - 2), jax.random.fold_in(splits[3], 1), 1, (BOX - 2) - 1).astype(jnp.int32)
    marker_frac = jnp.clip(1.0 * jax.random.uniform(splits[4], (3, SLOTS, NM), jnp.float32) ** steps_of(splits[4], (3, SLOTS, NM), ((1, 32),), -0.2, 0.2), 0.0, 1.0)
    particle_velocity = gaussian(splits[5], (3, NP), 1.0, 4.0, (), jnp.float32)
    particle_spin = gaussian(splits[6], (3, NP), 0.15, 0.6, (), jnp.float32)
    return dict(flow_state=flow_state, slot_ids=slot_ids, corners=corners, marker_cells=marker_cells, marker_frac=marker_frac, particle_velocity=particle_velocity, particle_spin=particle_spin)


time_step = 0.1
viscosity = 0.2
drive_force = 1.0

def predict(padded):
    velocity = padded[:3]
    pressure = padded[3]
    wall_zeros = jnp.zeros(velocity.shape[:3] + (1,), jnp.float32)
    fields = jnp.concatenate([wall_zeros, velocity, wall_zeros], axis=3)
    pressure_y = jnp.concatenate([pressure[:, :, :1], pressure, pressure[:, :, -1:]], axis=2)
    centre = fields[:, 1:-1, 1:-1, 1:-1]
    x_plus = fields[:, 2:, 1:-1, 1:-1]
    x_minus = fields[:, :-2, 1:-1, 1:-1]
    z_plus = fields[:, 1:-1, 2:, 1:-1]
    z_minus = fields[:, 1:-1, :-2, 1:-1]
    y_plus = fields[:, 1:-1, 1:-1, 2:]
    y_minus = fields[:, 1:-1, 1:-1, :-2]
    laplace = x_plus + x_minus + z_plus + z_minus + y_plus + y_minus - 6.0 * centre
    advect = (centre[0:1] * (x_plus - x_minus) + centre[1:2] * (y_plus - y_minus) + centre[2:3] * (z_plus - z_minus)) * 0.5
    gradient_x = (pressure_y[2:, 1:-1, 1:-1] - pressure_y[:-2, 1:-1, 1:-1]) * 0.5
    gradient_y = (pressure_y[1:-1, 1:-1, 2:] - pressure_y[1:-1, 1:-1, :-2]) * 0.5
    gradient_z = (pressure_y[1:-1, 2:, 1:-1] - pressure_y[1:-1, :-2, 1:-1]) * 0.5
    gradient = jnp.stack([gradient_x - drive_force, gradient_y, gradient_z])
    return centre + time_step * (viscosity * laplace - advect - gradient)

def diverge(padded):
    along_x = (padded[0, 2:, 1:-1] - padded[0, :-2, 1:-1]) * 0.5
    along_z = (padded[2, 1:-1, 2:] - padded[2, 1:-1, :-2]) * 0.5
    normal = padded[1, 1:-1, 1:-1]
    wall_zeros = jnp.zeros(normal.shape[:2] + (1,), jnp.float32)
    normal = jnp.concatenate([wall_zeros, normal, wall_zeros], axis=2)
    along_y = (normal[:, :, 2:] - normal[:, :, :-2]) * 0.5
    return along_x + along_y + along_z

def rigid_target(velocity, angular, position):
    lever_arm = position - HALF
    rotation = jnp.stack([angular[1] * lever_arm[2] - angular[2] * lever_arm[1], angular[2] * lever_arm[0] - angular[0] * lever_arm[2], angular[0] * lever_arm[1] - angular[1] * lever_arm[0]])
    return velocity[:, None] + rotation

def reference(flow_state, slot_ids, corners, marker_cells, marker_frac, particle_velocity, particle_spin):
    wrapped = jnp.pad(flow_state, ((0, 0), (1, 1), (1, 1), (0, 0)), mode='wrap')
    predicted = predict(wrapped)
    tap_offsets = jnp.arange(4, dtype=jnp.int32) - 1
    tap_values = tap_offsets.astype(jnp.float32)

    def one_slot(spread, inputs):
        particle, corner, cell_offsets, fraction = inputs
        occupied = (particle >= 0).astype(jnp.float32)
        column = jnp.maximum(particle, 0).astype(jnp.int32)
        velocity = lax.dynamic_index_in_dim(particle_velocity, column, 1, keepdims=False)
        angular = lax.dynamic_index_in_dim(particle_spin, column, 1, keepdims=False)
        cell_index = corner[:, None, None] + cell_offsets[:, :, None] + tap_offsets[None, None, :]
        along_x = cell_index[0] % NX
        along_y = cell_index[1]
        along_z = cell_index[2] % NZ
        weight = 0.25 * (1.0 + jnp.cos(0.5 * math.pi * (tap_values[None, None, :] - fraction[:, :, None])))
        triple = weight[0][:, :, None, None] * weight[2][:, None, :, None] * weight[1][:, None, None, :]
        pick_x = along_x[:, :, None, None]
        pick_z = along_z[:, None, :, None]
        pick_y = along_y[:, None, None, :]
        values = predicted[:, pick_x, pick_z, pick_y]
        sampled = lax.optimization_barrier(jnp.sum(values * triple[None], axis=(2, 3, 4)))
        target = rigid_target(velocity, angular, cell_offsets.astype(jnp.float32) + fraction)
        pushing = occupied * (target - sampled)
        spread = spread.at[:, pick_x, pick_z, pick_y].add(pushing[:, :, None, None, None] * triple[None])
        return (spread, None)
    scanned = (slot_ids, jnp.transpose(corners), jnp.transpose(marker_cells, (1, 0, 2)), jnp.transpose(marker_frac, (1, 0, 2)))
    forcing = lax.scan(one_slot, jnp.zeros_like(predicted), scanned)[0]
    velocity = predicted + forcing
    divergence = diverge(jnp.pad(velocity, ((0, 0), (1, 1), (1, 1), (0, 0)), mode='wrap'))
    spectrum = jnp.fft.fft2(divergence, axes=(0, 1))
    spectrum = jnp.transpose(spectrum, (2, 1, 0)) / math.sqrt(NX * NZ)
    source = jnp.stack([jnp.real(spectrum), jnp.imag(spectrum)]).astype(jnp.float32)
    return (velocity, source)
```

```python
import functools
import math

import jax
import jax.numpy as jnp
import numpy as np
from jax import lax
from jax.experimental import pallas as pl
from jax.experimental.pallas import tpu as pltpu
from jax.sharding import PartitionSpec as P

BOX = 24
HALF = 12
WINDOW = 32
LANES = 128

time_step = 0.1
viscosity = 0.2
drive_force = 1.0


IN_VMEM = pl.BlockSpec(memory_space=pltpu.VMEM)
IN_SMEM = pl.BlockSpec(memory_space=pltpu.SMEM)
TRANSPOSED = (((1,), (1,)), ((), ()))


def float32(*shape):
    return jax.ShapeDtypeStruct(shape, jnp.float32)


def call(kernel, out_shape, scalars, arrays, scratch, name, flops, moved):
    outputs = len(out_shape) if isinstance(out_shape, (list, tuple)) else 0
    return pl.pallas_call(
        kernel,
        out_shape=out_shape,
        in_specs=[IN_SMEM] * len(scalars) + [IN_VMEM] * len(arrays),
        out_specs=[IN_VMEM] * outputs if outputs else IN_VMEM,
        scratch_shapes=scratch,
        name=name,
        cost_estimate=pl.CostEstimate(flops=flops, bytes_accessed=moved, transcendentals=0),
    )(*scalars, *arrays)


def shift(array, axis, step):
    devices = lax.axis_size(axis)
    return lax.ppermute(array, axis, [(i, (i + step) % devices) for i in range(devices)])


def cosine_coefficients():
    samples = 2.0 + 2.0 * np.cos(np.pi * (np.arange(64) + 0.5) / 64)
    values = np.cos(np.pi / 4 * np.sqrt(samples))
    fit = np.polynomial.chebyshev.Chebyshev.fit(samples, values, 6, domain=[0, 4])
    return [float(v) for v in fit.convert(kind=np.polynomial.Polynomial).coef]


COSINE = cosine_coefficients()


def weight(offset):
    square = jnp.minimum(offset * offset, 4.0)
    value = jnp.full_like(square, COSINE[-1])
    for coefficient in COSINE[-2::-1]:
        value = value * square + coefficient
    return 0.5 * value * value


def split(value):
    high = value.astype(jnp.bfloat16)
    low = (value - high.astype(jnp.float32)).astype(jnp.bfloat16)
    return high, low


def row_weights(count, start, position):
    cells = lax.broadcasted_iota(jnp.int32, (count, position.shape[1]), 0) - start
    return weight(cells.astype(jnp.float32) - position)


def plane_weights(weight_x, weight_z, high, low):
    size_z = weight_z.shape[0]
    for x in range(weight_x.shape[0]):
        rows = slice(x * size_z, (x + 1) * size_z)
        high[rows], low[rows] = split(weight_x[x : x + 1] * weight_z)


def window_start(first_y, size_y):
    return pl.multiple_of(jnp.minimum((first_y // 8) * 8, size_y - WINDOW), 8)


def slot_weights(sizes, info, marks, block, row, slot, high, low):
    size_x, size_z, size_y = sizes
    first = window_start(info[slot, 2], size_y)
    weight_x = row_weights(size_x, info[slot, 0], marks[block, pl.ds(row, 1), :])
    weight_z = row_weights(size_z, info[slot, 1], marks[block, pl.ds(row + 8, 1), :])
    plane_weights(weight_x, weight_z, high, low)
    weight_y = row_weights(WINDOW, info[slot, 2] - first, marks[block, pl.ds(row + 16, 1), :])
    return first, weight_y


def sample_kernel(sizes, info, marks, field, out, high, low):
    def visit(slot, carry):
        block, row = slot // 8, slot % 8
        active = info[slot, 3] != 0

        @pl.when(jnp.logical_not(active))
        def _():
            for c in range(3):
                out[c, pl.ds(slot, 1), :] = jnp.zeros((1, out.shape[2]), jnp.float32)

        @pl.when(active)
        def _():
            first, weight_y = slot_weights(sizes, info, marks, block, row, slot, high, low)
            window = jnp.concatenate(
                [field[c, pl.ds(first, WINDOW), :] for c in range(3)], axis=0
            )
            window_high, window_low = split(window)
            both = jnp.concatenate([window_high, window_low], axis=0)
            value = jnp.dot(both, high[...], preferred_element_type=jnp.float32)
            rest = jnp.dot(window_high, low[...], preferred_element_type=jnp.float32)
            value = value[: 3 * WINDOW] + value[3 * WINDOW :] + rest
            for c in range(3):
                part = value[c * WINDOW : (c + 1) * WINDOW] * weight_y
                out[c, pl.ds(slot, 1), :] = jnp.sum(part, axis=0, keepdims=True)

        return carry

    lax.fori_loop(0, out.shape[1], visit, 0)


def sample(sizes, info, marks, field, name):
    slots, markers = info.shape[0], marks.shape[2]
    plane = sizes[0] * sizes[1]
    return call(
        functools.partial(sample_kernel, sizes),
        float32(3, slots, markers),
        [info],
        [marks, field],
        [pltpu.VMEM((plane, markers), jnp.bfloat16)] * 2,
        name,
        slots * 3 * 6 * WINDOW * plane * markers,
        4 * (field.size + marks.size),
    )


def spread_slots(sizes, info, marks, push, total, high, low):
    def visit(slot, carry):
        block, row = slot // 8, slot % 8

        @pl.when(info[slot, 3] != 0)
        def _():
            first, weight_y = slot_weights(sizes, info, marks, block, row, slot, high, low)
            value = jnp.concatenate(
                [weight_y * push[c, pl.ds(slot, 1), :] for c in range(3)], axis=0
            )
            value_high, value_low = split(value)
            both = jnp.concatenate([value_high, value_low], axis=0)
            added = lax.dot_general(
                both, high[...], TRANSPOSED, preferred_element_type=jnp.float32
            )
            rest = lax.dot_general(
                value_high, low[...], TRANSPOSED, preferred_element_type=jnp.float32
            )
            added = added[: 3 * WINDOW] + added[3 * WINDOW :] + rest
            for c in range(3):
                total[c, pl.ds(first, WINDOW), :] += added[c * WINDOW : (c + 1) * WINDOW]

        return carry

    lax.fori_loop(0, info.shape[0], visit, 0)


def spread_first_kernel(sizes, info, marks, push, total, high, low):
    total[...] = jnp.zeros(total.shape, jnp.float32)
    spread_slots(sizes, info, marks, push, total, high, low)


def spread_next_kernel(sizes, info, marks, push, before, total, high, low):
    total[...] = before[...]
    spread_slots(sizes, info, marks, push, total, high, low)


def spread(sizes, info, marks, push, before, name):
    slots, markers = info.shape[0], marks.shape[2]
    size_x, size_z, size_y = sizes
    plane = size_x * size_z
    kernel = spread_first_kernel if before is None else spread_next_kernel
    return call(
        functools.partial(kernel, sizes),
        float32(3, size_y, plane),
        [info],
        [marks, push] + ([] if before is None else [before]),
        [pltpu.VMEM((plane, markers), jnp.bfloat16)] * 2,
        name,
        slots * 3 * 6 * WINDOW * plane * markers,
        4 * (6 * size_y * plane + marks.size),
    )


def finish_kernel(sizes, forcing, predicted, velocity, u_first, u_last, w_first, w_last):
    size_x, size_z, size_y = sizes
    group = LANES // size_z
    for c in range(3):
        for q in range(size_x // group):
            part = jnp.transpose(forcing[c, :, q * LANES : (q + 1) * LANES])
            part = part.reshape(group, size_z, size_y)
            rows = slice(q * group, (q + 1) * group)
            velocity[c, rows] = predicted[c, rows] + part
    u_first[...] = velocity[0, 0]
    u_last[...] = velocity[0, size_x - 1]
    for x in range(size_x):
        w_first[x : x + 1] = velocity[2, x, 0:1]
        w_last[x : x + 1] = velocity[2, x, size_z - 1 : size_z]


def finish(sizes, forcing, predicted):
    size_x, size_z, size_y = sizes
    return call(
        functools.partial(finish_kernel, sizes),
        [float32(3, *sizes)] + [float32(size_z, size_y)] * 2 + [float32(size_x, size_y)] * 2,
        [],
        [forcing, predicted],
        [],
        "finish",
        forcing.size,
        12 * forcing.size,
    )


def y_neighbours(value, lane, below, above):
    size_y = value.shape[-1]
    minus = jnp.where(lane == 0, below, pltpu.roll(value, 1, 1))
    plus = jnp.where(lane == size_y - 1, above, pltpu.roll(value, size_y - 1, 1))
    return minus, plus


def z_neighbours(value, row, below, above):
    size_z = value.shape[0]
    minus = jnp.where(row == 0, below, pltpu.roll(value, 1, 0))
    plus = jnp.where(row == size_z - 1, above, pltpu.roll(value, size_z - 1, 0))
    return minus, plus


def predict_kernel(sizes, flow, x_below, x_above, z_below, z_above, predicted, field):
    size_x, size_z, size_y = sizes
    row = lax.broadcasted_iota(jnp.int32, (size_z, size_y), 0)
    lane = lax.broadcasted_iota(jnp.int32, (size_z, size_y), 1)
    group = LANES // size_z

    def around(c, x):
        value = flow[c, x]
        x_minus = flow[c, x - 1] if x > 0 else x_below[c]
        x_plus = flow[c, x + 1] if x < size_x - 1 else x_above[c]
        z_minus, z_plus = z_neighbours(value, row, z_below[c, x : x + 1], z_above[c, x : x + 1])
        edges = (0.0, 0.0) if c < 3 else (value, value)
        y_minus, y_plus = y_neighbours(value, lane, *edges)
        return value, x_minus, x_plus, z_minus, z_plus, y_minus, y_plus

    for x in range(size_x):
        _, x_minus, x_plus, z_minus, z_plus, y_minus, y_plus = around(3, x)
        gradient = (
            (x_plus - x_minus) * 0.5 - drive_force,
            (y_plus - y_minus) * 0.5,
            (z_plus - z_minus) * 0.5,
        )
        carried = (flow[0, x], flow[1, x], flow[2, x])
        for c in range(3):
            value, x_minus, x_plus, z_minus, z_plus, y_minus, y_plus = around(c, x)
            laplace = x_plus + x_minus + z_plus + z_minus + y_plus + y_minus - 6.0 * value
            advect = (
                carried[0] * (x_plus - x_minus)
                + carried[1] * (y_plus - y_minus)
                + carried[2] * (z_plus - z_minus)
            ) * 0.5
            predicted[c, x] = value + time_step * (viscosity * laplace - advect - gradient[c])
    for c in range(3):
        for q in range(size_x // group):
            part = predicted[c, q * group : (q + 1) * group].reshape(LANES, size_y)
            field[c, :, q * LANES : (q + 1) * LANES] = jnp.transpose(part)


def predict(sizes, flow, x_below, x_above, z_below, z_above):
    size_x, size_z, size_y = sizes
    return call(
        functools.partial(predict_kernel, sizes),
        [float32(3, *sizes), float32(3, size_y, size_x * size_z)],
        [],
        [flow, x_below, x_above, z_below, z_above],
        [],
        "predict",
        40 * flow.size,
        12 * flow.size,
    )


def divergence_kernel(sizes, parts, place, velocity, u_below, u_above, w_below, w_above, *rest):
    outs, whole = rest[:parts], rest[parts]
    size_x, size_z, size_y = sizes
    row = lax.broadcasted_iota(jnp.int32, (size_z, size_y), 0)
    lane = lax.broadcasted_iota(jnp.int32, (size_z, size_y), 1)
    group = LANES // size_z
    for q in range(size_x // group):
        pieces = []
        for x in range(q * group, (q + 1) * group):
            x_minus = velocity[0, x - 1] if x > 0 else u_below[...]
            x_plus = velocity[0, x + 1] if x < size_x - 1 else u_above[...]
            y_minus, y_plus = y_neighbours(velocity[1, x], lane, 0.0, 0.0)
            z_minus, z_plus = z_neighbours(
                velocity[2, x], row, w_below[x : x + 1], w_above[x : x + 1]
            )
            along_x = (x_plus - x_minus) * 0.5
            along_z = (z_plus - z_minus) * 0.5
            pieces.append(along_x + (y_plus - y_minus) * 0.5 + along_z)
        part = jnp.concatenate(pieces, axis=0)
        whole[:, q * LANES : (q + 1) * LANES] = jnp.transpose(part)
    height = size_y // parts
    for step in range(parts):
        first = pl.multiple_of(((place[0] + step) % parts) * height, 8)
        outs[step][...] = whole[pl.ds(first, height), :]


def divergence(sizes, parts, place, velocity, ghosts):
    size_x, size_z, size_y = sizes
    plane = size_x * size_z
    return call(
        functools.partial(divergence_kernel, sizes, parts),
        [float32(size_y // parts, plane)] * parts,
        [place],
        [velocity, *ghosts],
        [pltpu.VMEM((size_y, plane), jnp.float32)],
        "divergence",
        10 * velocity.size,
        6 * velocity.size,
    )


def swap_groups(values, width):
    count = LANES // width
    lane = lax.broadcasted_iota(jnp.int32, values[0].shape, 1)
    values = list(values)
    step = count // 2
    while step:
        reach = step * width
        keep = lane % (2 * reach) < reach
        for i in range(count):
            if i & step == 0:
                a, b = values[i], values[i + step]
                values[i] = jnp.where(keep, a, pltpu.roll(b, reach, 1))
                values[i + step] = jnp.where(keep, pltpu.roll(a, LANES - reach, 1), b)
        step //= 2
    return values


def transform_z_kernel(sizes, counts, place, table_high, table_low, *refs):
    size_x, size_z, size_y = sizes
    parts_x, parts_z = counts
    pieces, refs = refs[:parts_z], refs[parts_z:]
    outs, (gathered, turned, whole) = refs[:parts_x], refs[parts_x:]
    height = size_y // parts_z
    group = LANES // size_z
    for step in range(parts_z):
        gathered[(place[1] + parts_z - step) % parts_z] = pieces[step][...]
    for block in range(parts_z // group):
        for q in range(size_x // group):
            lanes = slice(q * LANES, (q + 1) * LANES)
            values = [gathered[block * group + i, :, lanes] for i in range(group)]
            for j, value in enumerate(swap_groups(values, size_z)):
                turned[block, pl.ds(q * group + j, height, stride=size_x), :] = value
    lines = jnp.concatenate([turned[b] for b in range(turned.shape[0])], axis=1)
    high, low = split(lines)
    result = lax.dot_general(
        table_high[...], high, TRANSPOSED, preferred_element_type=jnp.float32
    )
    result += lax.dot_general(
        table_low[...], high, TRANSPOSED, preferred_element_type=jnp.float32
    )
    result += lax.dot_general(
        table_high[...], low, TRANSPOSED, preferred_element_type=jnp.float32
    )
    whole[...] = result
    rows = whole.shape[0] // parts_x
    for step in range(parts_x):
        first = pl.multiple_of(((place[0] + step) % parts_x) * rows, 8)
        outs[step][...] = whole[pl.ds(first, rows), :]


def transform_z(sizes, counts, place, table, pieces):
    size_x, size_z, size_y = sizes
    parts_x, parts_z = counts
    length_z = size_z * parts_z
    height = size_y // parts_z
    columns = height * size_x
    return call(
        functools.partial(transform_z_kernel, sizes, counts),
        [float32(2 * length_z // parts_x, columns)] * parts_x,
        [place],
        [*table, *pieces],
        [
            pltpu.VMEM((parts_z, height, size_x * size_z), jnp.float32),
            pltpu.VMEM((length_z // LANES, columns, LANES), jnp.float32),
            pltpu.VMEM((2 * length_z, columns), jnp.float32),
        ],
        "transform_z",
        12 * length_z * length_z * columns,
        12 * length_z * columns,
    )


def transform_x_kernel(sizes, counts, place, table_high, table_low, *refs):
    size_x, size_z, size_y = sizes
    parts_x, parts_z = counts
    pieces, (source, gathered, turned) = refs[:parts_x], refs[parts_x:]
    length_x = size_x * parts_x
    modes = size_z * parts_z // parts_x
    height = size_y // parts_z
    group = LANES // size_x
    for step in range(parts_x):
        gathered[(place[0] + parts_x - step) % parts_x] = pieces[step][...]
    for block in range(parts_x // group):
        for q in range(height // group):
            lanes = slice(q * LANES, (q + 1) * LANES)
            values = [gathered[block * group + i, :, lanes] for i in range(group)]
            for j, value in enumerate(swap_groups(values, size_x)):
                first = (q * group + j) * modes
                for c in range(2):
                    column = c * length_x + block * LANES
                    turned[first : first + modes, column : column + LANES] = value[
                        c * modes : (c + 1) * modes
                    ]
    high, low = split(turned[...])
    result = jnp.dot(high, table_high[...], preferred_element_type=jnp.float32)
    result += jnp.dot(low, table_high[...], preferred_element_type=jnp.float32)
    result += jnp.dot(high, table_low[...], preferred_element_type=jnp.float32)
    source[0] = result[:, :length_x].reshape(height, modes, length_x)
    source[1] = result[:, length_x:].reshape(height, modes, length_x)


def transform_x(sizes, counts, place, table, pieces):
    size_x, size_z, size_y = sizes
    parts_x, parts_z = counts
    length_x = size_x * parts_x
    modes = size_z * parts_z // parts_x
    height = size_y // parts_z
    return call(
        functools.partial(transform_x_kernel, sizes, counts),
        float32(2, height, modes, length_x),
        [place],
        [*table, *pieces],
        [
            pltpu.VMEM((parts_x, *pieces[0].shape), jnp.float32),
            pltpu.VMEM((height * modes, 2 * length_x), jnp.float32),
        ],
        "transform_x",
        24 * length_x * length_x * height * modes,
        24 * length_x * height * modes,
    )


def split_table(table):
    high = table.astype(np.float32).astype(jnp.bfloat16)
    low = (table - high.astype(np.float64)).astype(np.float32).astype(jnp.bfloat16)
    return jnp.asarray(high), jnp.asarray(low)


def angles(length):
    counter = np.arange(length)
    turn = (counter[:, None] * counter[None, :] % length) * (2.0 * np.pi / length)
    return np.cos(turn), np.sin(turn)


def table_z(length, blocks):
    cosine, sine = angles(length)
    modes = length // blocks
    table = np.stack([cosine, -sine]).reshape(2, blocks, modes, length)
    return split_table(table.transpose(1, 0, 2, 3).reshape(2 * length, length))


def table_x(length, scale):
    cosine, sine = angles(length)
    return split_table(np.block([[cosine, -sine], [sine, cosine]]) * scale)


def exchange(pieces, axis):
    return [pieces[0]] + [shift(pieces[d], axis, d) for d in range(1, len(pieces))]


def on_device(
    flow_state, slot_ids, corners, marker_cells, marker_frac, particle_velocity, particle_spin
):
    sizes = flow_state.shape[1:]
    size_x, size_z, size_y = sizes
    counts = (lax.axis_size("gx"), lax.axis_size("gz"))
    length_x, length_z = (size_x * counts[0], size_z * counts[1])
    slots, markers = marker_cells.shape[1:]
    place_x, place_z = (lax.axis_index("gx"), lax.axis_index("gz"))
    place = jnp.stack([place_x, place_z]).astype(jnp.int32)

    x_below = shift(flow_state[:, size_x - 1], "gx", 1)
    x_above = shift(flow_state[:, 0], "gx", -1)
    z_below = shift(flow_state[:, :, size_z - 1], "gz", 1)
    z_above = shift(flow_state[:, :, 0], "gz", -1)

    positions = marker_cells.astype(jnp.float32) + marker_frac
    start_x = (corners[0] + HALF - place_x * size_x) % length_x - HALF
    start_z = (corners[2] + HALF - place_z * size_z) % length_z - HALF
    occupied = (slot_ids >= 0).astype(jnp.int32)
    facts = jnp.stack([start_x, start_z, corners[1], occupied], axis=1).astype(jnp.float32)
    facts_rows = jnp.pad(facts, ((0, 0), (0, markers - 4)))
    own_marks = jnp.concatenate([positions[0], positions[2], positions[1], facts_rows], axis=0)
    left_marks = shift(own_marks, "gx", 1)
    right_marks = shift(own_marks, "gx", -1)
    row_marks = jnp.stack([left_marks, own_marks, right_marks])
    lower_marks = shift(row_marks, "gz", 1)
    upper_marks = shift(row_marks, "gz", -1)
    side_marks = jnp.stack([left_marks, right_marks])

    def slot_info(marks, steps_x, step_z):
        fact = marks[:, 3 * slots :, :4].astype(jnp.int32)
        moved = jnp.asarray(np.array(steps_x, np.int32) * size_x)[:, None]
        first_x = fact[:, :, 0] + moved
        first_z = fact[:, :, 1] + step_z * size_z
        meets = (first_x > -BOX) & (first_x < size_x) & (first_z > -BOX) & (first_z < size_z)
        active = fact[:, :, 3] * meets.astype(jnp.int32)
        info = jnp.stack([first_x, first_z, fact[:, :, 2], active], axis=2)
        return info.reshape(-1, 4)

    lower_info = slot_info(lower_marks, (-1, 0, 1), -1)
    upper_info = slot_info(upper_marks, (-1, 0, 1), 1)
    side_info = slot_info(side_marks, (-1, 1), 0)
    own_info = slot_info(own_marks[None], (0,), 0)

    chosen = slot_ids[:, None] == jnp.arange(particle_velocity.shape[1], dtype=jnp.int32)[None, :]
    moving = jnp.sum(jnp.where(chosen[None], particle_velocity[:, None, :], 0.0), axis=2)
    turning = jnp.sum(jnp.where(chosen[None], particle_spin[:, None, :], 0.0), axis=2)
    lever = positions - HALF
    moving, turning = (moving[:, :, None], turning[:, :, None])
    target = moving + jnp.stack(
        [
            turning[1] * lever[2] - turning[2] * lever[1],
            turning[2] * lever[0] - turning[0] * lever[2],
            turning[0] * lever[1] - turning[1] * lever[0],
        ]
    )
    living = occupied.astype(jnp.float32)[None, :, None]

    predicted, field = predict(sizes, flow_state, x_below, x_above, z_below, z_above)

    lower_part = sample(sizes, lower_info, lower_marks, field, "sample_lower")
    to_lower = shift(lower_part, "gz", -1)
    upper_part = sample(sizes, upper_info, upper_marks, field, "sample_upper")
    to_upper = shift(upper_part, "gz", 1)
    side_part = sample(sizes, side_info, side_marks, field, "sample_side")
    from_z = to_lower + to_upper
    to_left = shift(side_part[:, :slots] + from_z[:, :slots], "gx", -1)
    to_right = shift(side_part[:, slots:] + from_z[:, 2 * slots :], "gx", 1)
    own_part = sample(sizes, own_info, own_marks[None], field, "sample_own")
    sampled = own_part + from_z[:, slots : 2 * slots] + to_left + to_right
    push = living * (target - sampled)

    left_push = shift(push, "gx", 1)
    right_push = shift(push, "gx", -1)
    row_push = jnp.concatenate([left_push, push, right_push], axis=1)
    lower_push = shift(row_push, "gz", 1)
    upper_push = shift(row_push, "gz", -1)
    side_push = jnp.concatenate([left_push, right_push], axis=1)
    forcing = spread(sizes, own_info, own_marks[None], push, None, "spread_own")
    forcing = spread(sizes, side_info, side_marks, side_push, forcing, "spread_side")
    forcing = spread(sizes, lower_info, lower_marks, lower_push, forcing, "spread_lower")
    forcing = spread(sizes, upper_info, upper_marks, upper_push, forcing, "spread_upper")
    velocity, u_first, u_last, w_first, w_last = finish(sizes, forcing, predicted)

    ghosts = (
        shift(u_last, "gx", 1),
        shift(u_first, "gx", -1),
        shift(w_last, "gz", 1),
        shift(w_first, "gz", -1),
    )
    pieces = divergence(sizes, counts[1], place[1:], velocity, ghosts)
    pieces = exchange(pieces, "gz")
    pieces = transform_z(sizes, counts, place, table_z(length_z, counts[0]), pieces)
    pieces = exchange(pieces, "gx")
    scale = 1.0 / math.sqrt(length_x * length_z)
    source = transform_x(sizes, counts, place, table_x(length_x, scale), pieces)
    return velocity, source


def solution(mesh):
    return jax.shard_map(
        on_device,
        mesh=mesh,
        in_specs=(
            P(None, "gx", "gz", None),
            P(("gx", "gz")),
            P(None, ("gx", "gz")),
            P(None, ("gx", "gz"), None),
            P(None, ("gx", "gz"), None),
            P(),
            P(),
        ),
        out_specs=(P(None, "gx", "gz", None), P(None, "gz", "gx", None)),
        check_vma=False,
    )
```

```python
import functools
import math

import jax
import jax.numpy as jnp
import numpy as np
from jax import lax
from jax.experimental import pallas as pl
from jax.experimental.pallas import tpu as pltpu
from jax.sharding import PartitionSpec as P

BOX = 24
HALF = 12
WINDOW = 32
LANES = 128

time_step = 0.1
viscosity = 0.2
drive_force = 1.0


IN_VMEM = pl.BlockSpec(memory_space=pltpu.VMEM)
IN_SMEM = pl.BlockSpec(memory_space=pltpu.SMEM)
TRANSPOSED = (((1,), (1,)), ((), ()))


def float32(*shape):
    return jax.ShapeDtypeStruct(shape, jnp.float32)


def call(kernel, out_shape, scalars, arrays, scratch, name, flops, moved):
    outputs = len(out_shape) if isinstance(out_shape, (list, tuple)) else 0
    return pl.pallas_call(
        kernel,
        out_shape=out_shape,
        in_specs=[IN_SMEM] * len(scalars) + [IN_VMEM] * len(arrays),
        out_specs=[IN_VMEM] * outputs if outputs else IN_VMEM,
        scratch_shapes=scratch,
        name=name,
        cost_estimate=pl.CostEstimate(flops=flops, bytes_accessed=moved, transcendentals=0),
    )(*scalars, *arrays)


def shift(array, axis, step):
    devices = lax.axis_size(axis)
    return lax.ppermute(array, axis, [(i, (i + step) % devices) for i in range(devices)])


def cosine_coefficients():
    samples = 2.0 + 2.0 * np.cos(np.pi * (np.arange(64) + 0.5) / 64)
    values = np.cos(np.pi / 4 * np.sqrt(samples)) * np.sqrt(0.5)
    fit = np.polynomial.chebyshev.Chebyshev.fit(samples, values, 4, domain=[0, 4])
    return [float(v) for v in fit.convert(kind=np.polynomial.Polynomial).coef]


COSINE = cosine_coefficients()


def weight(offset):
    square = jnp.minimum(offset * offset, 4.0)
    value = COSINE[-1] * square + COSINE[-2]
    for coefficient in COSINE[-3::-1]:
        value = value * square + coefficient
    return value * value


def split(value):
    high = value.astype(jnp.bfloat16)
    low = (value - high.astype(jnp.float32)).astype(jnp.bfloat16)
    return high, low


def row_weights(count, position):
    cells = lax.broadcasted_iota(jnp.int32, (count, position.shape[1]), 0)
    return weight(cells.astype(jnp.float32) - position)


def plane_weights(weight_x, weight_z, high, low):
    size_z = weight_z.shape[0]
    for x in range(weight_x.shape[0]):
        rows = slice(x * size_z, (x + 1) * size_z)
        high[rows], low[rows] = split(weight_x[x : x + 1] * weight_z)


def window_start(first_y, size_y):
    return pl.multiple_of(jnp.minimum((first_y // 8) * 8, size_y - WINDOW), 8)


class Layout:
    def __init__(self, sizes, slots, markers):
        self.sizes, self.slots, self.markers = sizes, slots, markers
        self.tiles = markers // LANES
        self.fact_row = 3 * self.tiles * slots
        self.rows = self.fact_row + slots
        self.ghost_x = 4 * sizes[1]
        self.ghost_z = 4 * sizes[0]
        self.plane = sizes[0] * sizes[1]


def marker_row(layout, marks, base, direction, slot):
    first = base + direction * layout.tiles * layout.slots + slot
    rows = [marks[pl.ds(first + t * layout.slots, 1), :] for t in range(layout.tiles)]
    return jnp.concatenate(rows, axis=1)


def slot_visits(layout, facts, marks, blocks, step_z, high, low, visit, skip):
    size_x, size_z, size_y = layout.sizes
    slots = layout.slots

    def body(index, carry):
        block, slot = index // slots, index % slots
        block = blocks[0] + block * (blocks[1] - blocks[0] if len(blocks) > 1 else 0)
        fact = (step_z + 1) * 3 * slots + block * slots + slot
        first_x = facts[fact, 0] + (block - 1) * size_x
        first_z = facts[fact, 1] + step_z * size_z
        first_y = facts[fact, 2]
        meets_x = (first_x > -BOX) & (first_x < size_x)
        meets_z = (first_z > -BOX) & (first_z < size_z)
        active = (facts[fact, 3] != 0) & meets_x & meets_z

        @pl.when(active)
        def _():
            base = layout.ghost_z + block * layout.rows
            first = window_start(first_y, size_y)
            position = marker_row(layout, marks, base, 0, slot) + first_x.astype(jnp.float32)
            weight_x = row_weights(size_x, position)
            position = marker_row(layout, marks, base, 1, slot) + first_z.astype(jnp.float32)
            weight_z = row_weights(size_z, position)
            plane_weights(weight_x, weight_z, high, low)
            ahead = (first_y - first).astype(jnp.float32)
            position = marker_row(layout, marks, base, 2, slot) + ahead
            visit(index, block * slots + slot, first, row_weights(WINDOW, position))

        if skip is not None:

            @pl.when(jnp.logical_not(active))
            def _():
                skip(index)

        return carry

    lax.fori_loop(0, len(blocks) * slots, body, 0)


def sample_kernel(layout, blocks, step_z, facts, marks, field, out, high, low):
    def visit(index, _, first, weight_y):
        window = jnp.concatenate([field[c, pl.ds(first, WINDOW), :] for c in range(3)], axis=0)
        window_high, window_low = split(window)
        both = jnp.concatenate([window_high, window_low], axis=0)
        value = jnp.dot(both, high[...], preferred_element_type=jnp.float32)
        rest = jnp.dot(window_high, low[...], preferred_element_type=jnp.float32)
        value = value[: 3 * WINDOW] + value[3 * WINDOW :] + rest
        for c in range(3):
            part = value[c * WINDOW : (c + 1) * WINDOW] * weight_y
            out[c, pl.ds(index, 1), :] = jnp.sum(part, axis=0, keepdims=True)

    def skip(index):
        for c in range(3):
            out[c, pl.ds(index, 1), :] = jnp.zeros((1, layout.markers), jnp.float32)

    slot_visits(layout, facts, marks, blocks, step_z, high, low, visit, skip)


def visit_cost(layout, blocks):
    return len(blocks) * layout.slots * 18 * WINDOW * layout.plane * layout.markers


def weight_scratch(layout):
    return [pltpu.VMEM((layout.plane, layout.markers), jnp.bfloat16)] * 2


def sample(layout, blocks, step_z, facts, marks, field, name):
    return call(
        functools.partial(sample_kernel, layout, blocks, step_z),
        float32(3, len(blocks) * layout.slots, layout.markers),
        [facts],
        [marks, field],
        weight_scratch(layout),
        name,
        visit_cost(layout, blocks),
        4 * (field.size + marks.size),
    )


def spread_slots(layout, blocks, step_z, facts, marks, push, own_rows, total, high, low):
    def visit(index, row, first, weight_y):
        slot = index if own_rows else row
        value = jnp.concatenate(
            [weight_y * push[c, pl.ds(slot, 1), :] for c in range(3)], axis=0
        )
        value_high, value_low = split(value)
        both = jnp.concatenate([value_high, value_low], axis=0)
        added = lax.dot_general(both, high[...], TRANSPOSED, preferred_element_type=jnp.float32)
        rest = lax.dot_general(
            value_high, low[...], TRANSPOSED, preferred_element_type=jnp.float32
        )
        added = added[: 3 * WINDOW] + added[3 * WINDOW :] + rest
        for c in range(3):
            total[c, pl.ds(first, WINDOW), :] += added[c * WINDOW : (c + 1) * WINDOW]

    slot_visits(layout, facts, marks, blocks, step_z, high, low, visit, None)


def spread_own_kernel(layout, facts, marks, push, total, high, low):
    total[...] = jnp.zeros(total.shape, jnp.float32)
    spread_slots(layout, (1,), 0, facts, marks, push, True, total, high, low)


def spread_own(layout, facts, marks, push):
    return call(
        functools.partial(spread_own_kernel, layout),
        float32(3, layout.sizes[2], layout.plane),
        [facts],
        [marks, push],
        weight_scratch(layout),
        "spread_own",
        visit_cost(layout, (1,)),
        12 * layout.sizes[2] * layout.plane,
    )


def spread_side_kernel(layout, facts, marks, push, before, total, high, low):
    total[...] = before[...]
    spread_slots(layout, (0, 2), 0, facts, marks, push, False, total, high, low)


def spread_side(layout, facts, marks, push, before):
    return call(
        functools.partial(spread_side_kernel, layout),
        float32(*before.shape),
        [facts],
        [marks, push, before],
        weight_scratch(layout),
        "spread_side",
        visit_cost(layout, (0, 2)),
        8 * before.size,
    )


def spread_rest_kernel(
    layout,
    facts,
    lower_marks,
    upper_marks,
    lower_push,
    upper_push,
    before,
    predicted,
    velocity,
    u_first,
    u_last,
    w_first,
    w_last,
    total,
    high,
    low,
):
    size_x, size_z, size_y = layout.sizes
    total[...] = before[...]
    row = (0, 1, 2)
    spread_slots(layout, row, -1, facts, lower_marks, lower_push, False, total, high, low)
    spread_slots(layout, row, 1, facts, upper_marks, upper_push, False, total, high, low)
    group = LANES // size_z
    for c in range(3):
        for q in range(size_x // group):
            part = jnp.transpose(total[c, :, q * LANES : (q + 1) * LANES])
            part = part.reshape(group, size_z, size_y)
            rows = slice(q * group, (q + 1) * group)
            velocity[c, rows] = predicted[c, rows] + part
    u_first[...] = velocity[0, 0]
    u_last[...] = velocity[0, size_x - 1]
    for x in range(size_x):
        w_first[x : x + 1] = velocity[2, x, 0:1]
        w_last[x : x + 1] = velocity[2, x, size_z - 1 : size_z]


def spread_rest(layout, facts, marks, pushes, before, predicted):
    size_x, size_z, size_y = layout.sizes
    return call(
        functools.partial(spread_rest_kernel, layout),
        [float32(3, size_x, size_z, size_y)]
        + [float32(size_z, size_y)] * 2
        + [float32(size_x, size_y)] * 2,
        [facts],
        [*marks, *pushes, before, predicted],
        [pltpu.VMEM(before.shape, jnp.float32)] + weight_scratch(layout),
        "spread_rest",
        2 * visit_cost(layout, (0, 1, 2)),
        12 * before.size,
    )


def pack_x_kernel(layout, slot_ids, corners, flow, cells, fraction, own, to_right, to_left):
    size_x, size_z, size_y = layout.sizes
    slots = layout.slots
    length_x = size_x * lax.axis_size("gx")
    length_z = size_z * lax.axis_size("gz")
    offset_x = length_x + HALF - lax.axis_index("gx") * size_x
    offset_z = length_z + HALF - lax.axis_index("gz") * size_z
    for a, direction in enumerate((0, 2, 1)):
        for t in range(layout.tiles):
            lanes = slice(t * LANES, (t + 1) * LANES)
            place = cells[direction, :, lanes].astype(jnp.float32) + fraction[direction, :, lanes]
            first = (a * layout.tiles + t) * slots
            own[first : first + slots] = place
    lane = lax.broadcasted_iota(jnp.int32, (1, LANES), 1)
    for slot in range(slots):
        first_x = lax.rem(corners[0, slot] + offset_x, length_x) - HALF
        first_z = lax.rem(corners[2, slot] + offset_z, length_z) - HALF
        held = (slot_ids[slot] >= 0).astype(jnp.int32)
        fact = jnp.where(lane == 0, first_x, held)
        fact = jnp.where(lane == 1, first_z, fact)
        fact = jnp.where(lane == 2, corners[1, slot], fact)
        row = layout.fact_row + slot
        own[row : row + 1] = fact.astype(jnp.float32)
    for c in range(4):
        rows = slice(c * size_z, (c + 1) * size_z)
        to_right[rows] = flow[c, size_x - 1]
        to_left[rows] = flow[c, 0]
    to_right[layout.ghost_x :] = own[...]
    to_left[layout.ghost_x :] = own[...]


def pack_x(layout, slot_ids, corners, flow, cells, fraction):
    rows = layout.ghost_x + layout.rows
    return call(
        functools.partial(pack_x_kernel, layout),
        [float32(layout.rows, LANES)] + [float32(rows, LANES)] * 2,
        [slot_ids, corners],
        [flow, cells, fraction],
        [],
        "pack_x",
        flow.size,
        8 * rows * LANES,
    )


def pack_z_kernel(layout, flow, own, left, right, to_upper, to_lower):
    size_x, size_z, size_y = layout.sizes
    for c in range(4):
        for x in range(size_x):
            row = c * size_x + x
            to_upper[row : row + 1] = flow[c, x, size_z - 1 : size_z]
            to_lower[row : row + 1] = flow[c, x, 0:1]
    tiles = (left[layout.ghost_x :], own[...], right[layout.ghost_x :])
    for block, tile in enumerate(tiles):
        first = layout.ghost_z + block * layout.rows
        to_upper[first : first + layout.rows] = tile
        to_lower[first : first + layout.rows] = tile


def pack_z(layout, flow, own, left, right):
    rows = layout.ghost_z + 3 * layout.rows
    return call(
        functools.partial(pack_z_kernel, layout),
        [float32(rows, LANES)] * 2,
        [],
        [flow, own, left, right],
        [],
        "pack_z",
        flow.size,
        8 * rows * LANES,
    )


def y_neighbours(value, lane, below, above):
    size_y = value.shape[-1]
    minus = jnp.where(lane == 0, below, pltpu.roll(value, 1, 1))
    plus = jnp.where(lane == size_y - 1, above, pltpu.roll(value, size_y - 1, 1))
    return minus, plus


def z_neighbours(value, row, below, above):
    size_z = value.shape[0]
    minus = jnp.where(row == 0, below, pltpu.roll(value, 1, 0))
    plus = jnp.where(row == size_z - 1, above, pltpu.roll(value, size_z - 1, 0))
    return minus, plus


def predict_inner_kernel(sizes, flow, left, right, predicted):
    size_x, size_z, size_y = sizes
    row = lax.broadcasted_iota(jnp.int32, (size_z, size_y), 0)
    lane = lax.broadcasted_iota(jnp.int32, (size_z, size_y), 1)

    def around(c, x):
        value = flow[c, x]
        ghost = slice(c * size_z, (c + 1) * size_z)
        x_minus = flow[c, x - 1] if x > 0 else left[ghost]
        x_plus = flow[c, x + 1] if x < size_x - 1 else right[ghost]
        z_minus, z_plus = z_neighbours(value, row, 0.0, 0.0)
        edges = (0.0, 0.0) if c < 3 else (value, value)
        y_minus, y_plus = y_neighbours(value, lane, *edges)
        return value, x_minus, x_plus, z_minus, z_plus, y_minus, y_plus

    for x in range(size_x):
        _, x_minus, x_plus, z_minus, z_plus, y_minus, y_plus = around(3, x)
        gradient = (
            (x_plus - x_minus) * 0.5 - drive_force,
            (y_plus - y_minus) * 0.5,
            (z_plus - z_minus) * 0.5,
        )
        carried = (flow[0, x], flow[1, x], flow[2, x])
        for c in range(3):
            value, x_minus, x_plus, z_minus, z_plus, y_minus, y_plus = around(c, x)
            laplace = x_plus + x_minus + z_plus + z_minus + y_plus + y_minus - 6.0 * value
            advect = (
                carried[0] * (x_plus - x_minus)
                + carried[1] * (y_plus - y_minus)
                + carried[2] * (z_plus - z_minus)
            ) * 0.5
            predicted[c, x] = value + time_step * (viscosity * laplace - advect - gradient[c])


def predict_inner(sizes, flow, left, right):
    return call(
        functools.partial(predict_inner_kernel, sizes),
        float32(3, *sizes),
        [],
        [flow, left, right],
        [],
        "predict_inner",
        200 * flow.size,
        8 * flow.size,
    )


def predict_outer_kernel(layout, flow, inner, lower, own, upper, predicted, field, facts):
    size_x, size_z, size_y = layout.sizes
    row = lax.broadcasted_iota(jnp.int32, (8, size_y), 0)
    group = LANES // size_z
    for block in range(9):
        payload = (lower, own, upper)[block // 3]
        first = layout.ghost_z + (block % 3) * layout.rows + layout.fact_row
        out = slice(block * layout.slots, (block + 1) * layout.slots)
        facts[out] = payload[first : first + layout.slots].astype(jnp.int32)
    for q in range(size_x // group):
        for x in range(q * group, (q + 1) * group):
            carried_low = flow[2, x, 0:1]
            carried_high = flow[2, x, size_z - 1 : size_z]
            for c in range(3):
                ghost = c * size_x + x
                below, above = lower[ghost : ghost + 1], upper[ghost : ghost + 1]
                change_low = (viscosity + 0.5 * carried_low) * below
                change_high = (viscosity - 0.5 * carried_high) * above
                if c == 2:
                    ghost = 3 * size_x + x
                    change_low += 0.5 * lower[ghost : ghost + 1]
                    change_high -= 0.5 * upper[ghost : ghost + 1]
                predicted[c, x] = inner[c, x]
                first = inner[c, x, 0:8]
                predicted[c, x, 0:8] = first + jnp.where(row == 0, time_step * change_low, 0.0)
                last = inner[c, x, size_z - 8 : size_z]
                predicted[c, x, size_z - 8 : size_z] = last + jnp.where(
                    row == 7, time_step * change_high, 0.0
                )
        for c in range(3):
            part = predicted[c, q * group : (q + 1) * group].reshape(LANES, size_y)
            field[c, :, q * LANES : (q + 1) * LANES] = jnp.transpose(part)


def predict_outer(layout, flow, inner, lower, own, upper):
    size_x, size_z, size_y = layout.sizes
    return call(
        functools.partial(predict_outer_kernel, layout),
        [
            float32(3, *layout.sizes),
            float32(3, size_y, layout.plane),
            jax.ShapeDtypeStruct((9 * layout.slots, LANES), jnp.int32),
        ],
        [],
        [flow, inner, lower, own, upper],
        [],
        "predict_outer",
        10 * flow.size,
        12 * flow.size,
    )


def divergence_kernel(sizes, parts, velocity, u_below, u_above, w_below, w_above, *rest):
    outs, whole = rest[:parts], rest[parts]
    size_x, size_z, size_y = sizes
    row = lax.broadcasted_iota(jnp.int32, (size_z, size_y), 0)
    lane = lax.broadcasted_iota(jnp.int32, (size_z, size_y), 1)
    group = LANES // size_z
    for q in range(size_x // group):
        pieces = []
        for x in range(q * group, (q + 1) * group):
            x_minus = velocity[0, x - 1] if x > 0 else u_below[...]
            x_plus = velocity[0, x + 1] if x < size_x - 1 else u_above[...]
            y_minus, y_plus = y_neighbours(velocity[1, x], lane, 0.0, 0.0)
            z_minus, z_plus = z_neighbours(
                velocity[2, x], row, w_below[x : x + 1], w_above[x : x + 1]
            )
            along_x = (x_plus - x_minus) * 0.5
            along_z = (z_plus - z_minus) * 0.5
            pieces.append(along_x + (y_plus - y_minus) * 0.5 + along_z)
        part = jnp.concatenate(pieces, axis=0)
        whole[:, q * LANES : (q + 1) * LANES] = jnp.transpose(part)
    height = size_y // parts
    for step in range(parts):
        first = pl.multiple_of(lax.rem(lax.axis_index("gz") + step, parts) * height, 8)
        outs[step][...] = whole[pl.ds(first, height), :]


def divergence(sizes, parts, velocity, ghosts):
    size_x, size_z, size_y = sizes
    plane = size_x * size_z
    return call(
        functools.partial(divergence_kernel, sizes, parts),
        [float32(size_y // parts, plane)] * parts,
        [],
        [velocity, *ghosts],
        [pltpu.VMEM((size_y, plane), jnp.float32)],
        "divergence",
        10 * velocity.size,
        6 * velocity.size,
    )


def swap_groups(values, width):
    count = LANES // width
    lane = lax.broadcasted_iota(jnp.int32, values[0].shape, 1)
    values = list(values)
    step = count // 2
    while step:
        reach = step * width
        keep = lane % (2 * reach) < reach
        for i in range(count):
            if i & step == 0:
                a, b = values[i], values[i + step]
                values[i] = jnp.where(keep, a, pltpu.roll(b, reach, 1))
                values[i + step] = jnp.where(keep, pltpu.roll(a, LANES - reach, 1), b)
        step //= 2
    return values


def transform_z_kernel(sizes, counts, table_high, table_low, *refs):
    size_x, size_z, size_y = sizes
    parts_x, parts_z = counts
    pieces, refs = refs[:parts_z], refs[parts_z:]
    outs, (gathered, turned, whole) = refs[:parts_x], refs[parts_x:]
    height = size_y // parts_z
    group = LANES // size_z
    for step in range(parts_z):
        gathered[lax.rem(lax.axis_index("gz") + parts_z - step, parts_z)] = pieces[step][...]
    for block in range(parts_z // group):
        for q in range(size_x // group):
            lanes = slice(q * LANES, (q + 1) * LANES)
            values = [gathered[block * group + i, :, lanes] for i in range(group)]
            for j, value in enumerate(swap_groups(values, size_z)):
                turned[block, pl.ds(q * group + j, height, stride=size_x), :] = value
    lines = jnp.concatenate([turned[b] for b in range(turned.shape[0])], axis=1)
    high, low = split(lines)
    result = lax.dot_general(
        table_high[...], high, TRANSPOSED, preferred_element_type=jnp.float32
    )
    result += lax.dot_general(
        table_low[...], high, TRANSPOSED, preferred_element_type=jnp.float32
    )
    result += lax.dot_general(
        table_high[...], low, TRANSPOSED, preferred_element_type=jnp.float32
    )
    whole[...] = result
    rows = whole.shape[0] // parts_x
    for step in range(parts_x):
        first = pl.multiple_of(lax.rem(lax.axis_index("gx") + step, parts_x) * rows, 8)
        outs[step][...] = whole[pl.ds(first, rows), :]


def transform_z(sizes, counts, table, pieces):
    size_x, size_z, size_y = sizes
    parts_x, parts_z = counts
    length_z = size_z * parts_z
    height = size_y // parts_z
    columns = height * size_x
    return call(
        functools.partial(transform_z_kernel, sizes, counts),
        [float32(2 * length_z // parts_x, columns)] * parts_x,
        [],
        [*table, *pieces],
        [
            pltpu.VMEM((parts_z, height, size_x * size_z), jnp.float32),
            pltpu.VMEM((length_z // LANES, columns, LANES), jnp.float32),
            pltpu.VMEM((2 * length_z, columns), jnp.float32),
        ],
        "transform_z",
        12 * length_z * length_z * columns,
        12 * length_z * columns,
    )


def transform_x_kernel(sizes, counts, table_high, table_low, *refs):
    size_x, size_z, size_y = sizes
    parts_x, parts_z = counts
    pieces, (source, gathered, turned) = refs[:parts_x], refs[parts_x:]
    length_x = size_x * parts_x
    modes = size_z * parts_z // parts_x
    height = size_y // parts_z
    group = LANES // size_x
    for step in range(parts_x):
        gathered[lax.rem(lax.axis_index("gx") + parts_x - step, parts_x)] = pieces[step][...]
    for block in range(parts_x // group):
        for q in range(height // group):
            lanes = slice(q * LANES, (q + 1) * LANES)
            values = [gathered[block * group + i, :, lanes] for i in range(group)]
            for j, value in enumerate(swap_groups(values, size_x)):
                first = (q * group + j) * modes
                for c in range(2):
                    column = c * length_x + block * LANES
                    turned[first : first + modes, column : column + LANES] = value[
                        c * modes : (c + 1) * modes
                    ]
    high, low = split(turned[...])
    result = jnp.dot(high, table_high[...], preferred_element_type=jnp.float32)
    result += jnp.dot(low, table_high[...], preferred_element_type=jnp.float32)
    result += jnp.dot(high, table_low[...], preferred_element_type=jnp.float32)
    source[0] = result[:, :length_x].reshape(height, modes, length_x)
    source[1] = result[:, length_x:].reshape(height, modes, length_x)


def transform_x(sizes, counts, table, pieces):
    size_x, size_z, size_y = sizes
    parts_x, parts_z = counts
    length_x = size_x * parts_x
    modes = size_z * parts_z // parts_x
    height = size_y // parts_z
    return call(
        functools.partial(transform_x_kernel, sizes, counts),
        float32(2, height, modes, length_x),
        [],
        [*table, *pieces],
        [
            pltpu.VMEM((parts_x, *pieces[0].shape), jnp.float32),
            pltpu.VMEM((height * modes, 2 * length_x), jnp.float32),
        ],
        "transform_x",
        24 * length_x * length_x * height * modes,
        24 * length_x * height * modes,
    )


def split_table(table):
    high = table.astype(np.float32).astype(jnp.bfloat16)
    low = (table - high.astype(np.float64)).astype(np.float32).astype(jnp.bfloat16)
    return jnp.asarray(high), jnp.asarray(low)


def angles(length):
    counter = np.arange(length)
    turn = (counter[:, None] * counter[None, :] % length) * (2.0 * np.pi / length)
    return np.cos(turn), np.sin(turn)


def table_z(length, blocks):
    cosine, sine = angles(length)
    modes = length // blocks
    table = np.stack([cosine, -sine]).reshape(2, blocks, modes, length)
    return split_table(table.transpose(1, 0, 2, 3).reshape(2 * length, length))


def table_x(length, scale):
    cosine, sine = angles(length)
    return split_table(np.block([[cosine, -sine], [sine, cosine]]) * scale)


def exchange(pieces, axis):
    return [pieces[0]] + [shift(pieces[d], axis, d) for d in range(1, len(pieces))]


def on_device(
    flow_state, slot_ids, corners, marker_cells, marker_frac, particle_velocity, particle_spin
):
    sizes = flow_state.shape[1:]
    size_x, size_z, size_y = sizes
    counts = (lax.axis_size("gx"), lax.axis_size("gz"))
    length_x, length_z = (size_x * counts[0], size_z * counts[1])
    slots, markers = marker_cells.shape[1:]
    layout = Layout(sizes, slots, markers)

    own, to_right, to_left = pack_x(
        layout, slot_ids, corners, flow_state, marker_cells, marker_frac
    )
    left = shift(to_right, "gx", 1)
    right = shift(to_left, "gx", -1)
    row, to_lower = pack_z(layout, flow_state, own, left, right)
    lower = shift(row, "gz", 1)
    upper = shift(to_lower, "gz", -1)
    inner = predict_inner(sizes, flow_state, left, right)
    predicted, field, facts = predict_outer(layout, flow_state, inner, lower, row, upper)

    positions = marker_cells.astype(jnp.float32) + marker_frac
    chosen = slot_ids[:, None] == jnp.arange(particle_velocity.shape[1], dtype=jnp.int32)[None, :]
    moving = jnp.sum(jnp.where(chosen[None], particle_velocity[:, None, :], 0.0), axis=2)
    turning = jnp.sum(jnp.where(chosen[None], particle_spin[:, None, :], 0.0), axis=2)
    lever = positions - HALF
    moving, turning = (moving[:, :, None], turning[:, :, None])
    target = moving + jnp.stack(
        [
            turning[1] * lever[2] - turning[2] * lever[1],
            turning[2] * lever[0] - turning[0] * lever[2],
            turning[0] * lever[1] - turning[1] * lever[0],
        ]
    )
    living = (slot_ids >= 0).astype(jnp.float32)[None, :, None]

    tiles = (0, 1, 2)
    lower_part = sample(layout, tiles, -1, facts, lower, field, "sample_lower")
    from_upper = shift(lower_part, "gz", -1)
    upper_part = sample(layout, tiles, 1, facts, upper, field, "sample_upper")
    from_lower = shift(upper_part, "gz", 1)
    side_part = sample(layout, (0, 2), 0, facts, row, field, "sample_side")
    from_z = from_upper + from_lower
    from_right = shift(side_part[:, :slots] + from_z[:, :slots], "gx", -1)
    from_left = shift(side_part[:, slots:] + from_z[:, 2 * slots :], "gx", 1)
    own_part = sample(layout, (1,), 0, facts, row, field, "sample_own")
    sampled = own_part + from_z[:, slots : 2 * slots] + from_right + from_left
    push = living * (target - sampled)

    left_push = shift(push, "gx", 1)
    right_push = shift(push, "gx", -1)
    row_push = jnp.concatenate([left_push, push, right_push], axis=1)
    lower_push = shift(row_push, "gz", 1)
    upper_push = shift(row_push, "gz", -1)
    forcing = spread_own(layout, facts, row, push)
    forcing = spread_side(layout, facts, row, row_push, forcing)
    velocity, u_first, u_last, w_first, w_last = spread_rest(
        layout, facts, (lower, upper), (lower_push, upper_push), forcing, predicted
    )

    ghosts = (
        shift(u_last, "gx", 1),
        shift(u_first, "gx", -1),
        shift(w_last, "gz", 1),
        shift(w_first, "gz", -1),
    )
    pieces = divergence(sizes, counts[1], velocity, ghosts)
    pieces = exchange(pieces, "gz")
    pieces = transform_z(sizes, counts, table_z(length_z, counts[0]), pieces)
    pieces = exchange(pieces, "gx")
    scale = 1.0 / math.sqrt(length_x * length_z)
    source = transform_x(sizes, counts, table_x(length_x, scale), pieces)
    return velocity, source


def solution(mesh):
    return jax.shard_map(
        on_device,
        mesh=mesh,
        in_specs=(
            P(None, "gx", "gz", None),
            P(("gx", "gz")),
            P(None, ("gx", "gz")),
            P(None, ("gx", "gz"), None),
            P(None, ("gx", "gz"), None),
            P(),
            P(),
        ),
        out_specs=(P(None, "gx", "gz", None), P(None, "gz", "gx", None)),
        check_vma=False,
    )
```

```python
import functools
import math

import jax
import jax.numpy as jnp
import numpy as np
from jax import lax
from jax.experimental import pallas as pl
from jax.experimental.pallas import tpu as pltpu
from jax.sharding import PartitionSpec as P

BOX = 24
HALF = 12
WINDOW = 32
LANES = 128
KERNEL_BYTES = 16 * 1024 * 1024

time_step = 0.1
viscosity = 0.2
drive_force = 1.0


IN_VMEM = pl.BlockSpec(memory_space=pltpu.VMEM)
IN_SMEM = pl.BlockSpec(memory_space=pltpu.SMEM)
TRANSPOSED = (((1,), (1,)), ((), ()))


def float32(*shape):
    return jax.ShapeDtypeStruct(shape, jnp.float32)


def call(kernel, out_shape, scalars, arrays, scratch, name, flops, moved):
    outputs = len(out_shape) if isinstance(out_shape, (list, tuple)) else 0
    return pl.pallas_call(
        kernel,
        out_shape=out_shape,
        in_specs=[IN_SMEM] * len(scalars) + [IN_VMEM] * len(arrays),
        out_specs=[IN_VMEM] * outputs if outputs else IN_VMEM,
        scratch_shapes=scratch,
        name=name,
        compiler_params=pltpu.CompilerParams(vmem_limit_bytes=KERNEL_BYTES),
        cost_estimate=pl.CostEstimate(flops=flops, bytes_accessed=moved, transcendentals=0),
    )(*scalars, *arrays)


def shift(array, axis, step):
    devices = lax.axis_size(axis)
    return lax.ppermute(array, axis, [(i, (i + step) % devices) for i in range(devices)])


def cosine_coefficients():
    samples = 2.0 + 2.0 * np.cos(np.pi * (np.arange(64) + 0.5) / 64)
    values = np.cos(np.pi / 4 * np.sqrt(samples)) * np.sqrt(0.5)
    fit = np.polynomial.chebyshev.Chebyshev.fit(samples, values, 4, domain=[0, 4])
    return [float(v) for v in fit.convert(kind=np.polynomial.Polynomial).coef]


COSINE = cosine_coefficients()


def weight(offset):
    square = jnp.minimum(offset * offset, 4.0)
    value = COSINE[-1] * square + COSINE[-2]
    for coefficient in COSINE[-3::-1]:
        value = value * square + coefficient
    return value * value


def split(value):
    high = value.astype(jnp.bfloat16)
    low = (value - high.astype(jnp.float32)).astype(jnp.bfloat16)
    return high, low


def row_weights(count, position):
    cells = lax.broadcasted_iota(jnp.int32, (count, position.shape[1]), 0)
    return weight(cells.astype(jnp.float32) - position)


def plane_weights(weight_x, weight_z, high, low):
    size_z = weight_z.shape[0]
    for x in range(weight_x.shape[0]):
        rows = slice(x * size_z, (x + 1) * size_z)
        high[rows], low[rows] = split(weight_x[x : x + 1] * weight_z)


def window_start(first_y, size_y):
    return pl.multiple_of(jnp.minimum((first_y // 8) * 8, size_y - WINDOW), 8)


class Layout:
    def __init__(self, sizes, slots, markers):
        self.sizes, self.slots, self.markers = sizes, slots, markers
        self.tiles = markers // LANES
        self.fact_row = 3 * self.tiles * slots
        self.rows = self.fact_row + slots
        self.ghost_x = 4 * sizes[1]
        self.ghost_z = 4 * sizes[0]
        self.plane = sizes[0] * sizes[1]


def marker_row(layout, marks, base, direction, slot):
    first = base + direction * layout.tiles * layout.slots + slot
    rows = [marks[pl.ds(first + t * layout.slots, 1), :] for t in range(layout.tiles)]
    return jnp.concatenate(rows, axis=1)


def slot_visits(layout, facts, marks, blocks, step_z, high, low, visit, skip):
    size_x, size_z, size_y = layout.sizes
    slots = layout.slots

    def body(index, carry):
        block, slot = index // slots, index % slots
        block = blocks[0] + block * (blocks[1] - blocks[0] if len(blocks) > 1 else 0)
        fact = (step_z + 1) * 3 * slots + block * slots + slot
        first_x = facts[fact, 0] + (block - 1) * size_x
        first_z = facts[fact, 1] + step_z * size_z
        first_y = facts[fact, 2]
        meets_x = (first_x > -BOX) & (first_x < size_x)
        meets_z = (first_z > -BOX) & (first_z < size_z)
        active = (facts[fact, 3] != 0) & meets_x & meets_z

        @pl.when(active)
        def _():
            base = layout.ghost_z + block * layout.rows
            first = window_start(first_y, size_y)
            position = marker_row(layout, marks, base, 0, slot) + first_x.astype(jnp.float32)
            weight_x = row_weights(size_x, position)
            position = marker_row(layout, marks, base, 1, slot) + first_z.astype(jnp.float32)
            weight_z = row_weights(size_z, position)
            plane_weights(weight_x, weight_z, high, low)
            ahead = (first_y - first).astype(jnp.float32)
            position = marker_row(layout, marks, base, 2, slot) + ahead
            visit(index, block * slots + slot, first, row_weights(WINDOW, position))

        if skip is not None:

            @pl.when(jnp.logical_not(active))
            def _():
                skip(index)

        return carry

    lax.fori_loop(0, len(blocks) * slots, body, 0)


def sample_kernel(layout, blocks, step_z, facts, marks, field, out, high, low):
    def visit(index, _, first, weight_y):
        window = jnp.concatenate([field[c, pl.ds(first, WINDOW), :] for c in range(3)], axis=0)
        window_high, window_low = split(window)
        both = jnp.concatenate([window_high, window_low], axis=0)
        value = jnp.dot(both, high[...], preferred_element_type=jnp.float32)
        rest = jnp.dot(window_high, low[...], preferred_element_type=jnp.float32)
        value = value[: 3 * WINDOW] + value[3 * WINDOW :] + rest
        for c in range(3):
            part = value[c * WINDOW : (c + 1) * WINDOW] * weight_y
            out[c, pl.ds(index, 1), :] = jnp.sum(part, axis=0, keepdims=True)

    def skip(index):
        for c in range(3):
            out[c, pl.ds(index, 1), :] = jnp.zeros((1, layout.markers), jnp.float32)

    slot_visits(layout, facts, marks, blocks, step_z, high, low, visit, skip)


def visit_cost(layout, blocks):
    return len(blocks) * layout.slots * 18 * WINDOW * layout.plane * layout.markers


def weight_scratch(layout):
    return [pltpu.VMEM((layout.plane, layout.markers), jnp.bfloat16)] * 2


def sample(layout, blocks, step_z, facts, marks, field, name):
    return call(
        functools.partial(sample_kernel, layout, blocks, step_z),
        float32(3, len(blocks) * layout.slots, layout.markers),
        [facts],
        [marks, field],
        weight_scratch(layout),
        name,
        visit_cost(layout, blocks),
        4 * (field.size + marks.size),
    )


def spread_slots(layout, blocks, step_z, facts, marks, push, own_rows, total, high, low):
    def visit(index, row, first, weight_y):
        slot = index if own_rows else row
        value = jnp.concatenate(
            [weight_y * push[c, pl.ds(slot, 1), :] for c in range(3)], axis=0
        )
        value_high, value_low = split(value)
        both = jnp.concatenate([value_high, value_low], axis=0)
        added = lax.dot_general(both, high[...], TRANSPOSED, preferred_element_type=jnp.float32)
        rest = lax.dot_general(
            value_high, low[...], TRANSPOSED, preferred_element_type=jnp.float32
        )
        added = added[: 3 * WINDOW] + added[3 * WINDOW :] + rest
        for c in range(3):
            total[c, pl.ds(first, WINDOW), :] += added[c * WINDOW : (c + 1) * WINDOW]

    slot_visits(layout, facts, marks, blocks, step_z, high, low, visit, None)


def spread_own_kernel(layout, facts, marks, push, total, high, low):
    total[...] = jnp.zeros(total.shape, jnp.float32)
    spread_slots(layout, (1,), 0, facts, marks, push, True, total, high, low)


def spread_own(layout, facts, marks, push):
    return call(
        functools.partial(spread_own_kernel, layout),
        float32(3, layout.sizes[2], layout.plane),
        [facts],
        [marks, push],
        weight_scratch(layout),
        "spread_own",
        visit_cost(layout, (1,)),
        12 * layout.sizes[2] * layout.plane,
    )


def spread_side_kernel(layout, facts, marks, push, before, total, high, low):
    total[...] = before[...]
    spread_slots(layout, (0, 2), 0, facts, marks, push, False, total, high, low)


def spread_side(layout, facts, marks, push, before):
    return call(
        functools.partial(spread_side_kernel, layout),
        float32(*before.shape),
        [facts],
        [marks, push, before],
        weight_scratch(layout),
        "spread_side",
        visit_cost(layout, (0, 2)),
        8 * before.size,
    )


def spread_rest_kernel(
    layout,
    facts,
    lower_marks,
    upper_marks,
    lower_push,
    upper_push,
    before,
    predicted,
    velocity,
    u_first,
    u_last,
    w_first,
    w_last,
    total,
    high,
    low,
):
    size_x, size_z, size_y = layout.sizes
    total[...] = before[...]
    row = (0, 1, 2)
    spread_slots(layout, row, -1, facts, lower_marks, lower_push, False, total, high, low)
    spread_slots(layout, row, 1, facts, upper_marks, upper_push, False, total, high, low)
    group = LANES // size_z
    for c in range(3):
        for q in range(size_x // group):
            part = jnp.transpose(total[c, :, q * LANES : (q + 1) * LANES])
            part = part.reshape(group, size_z, size_y)
            rows = slice(q * group, (q + 1) * group)
            velocity[c, rows] = predicted[c, rows] + part
    u_first[...] = velocity[0, 0]
    u_last[...] = velocity[0, size_x - 1]
    for x in range(size_x):
        w_first[x : x + 1] = velocity[2, x, 0:1]
        w_last[x : x + 1] = velocity[2, x, size_z - 1 : size_z]


def spread_rest(layout, facts, marks, pushes, before, predicted):
    size_x, size_z, size_y = layout.sizes
    return call(
        functools.partial(spread_rest_kernel, layout),
        [float32(3, size_x, size_z, size_y)]
        + [float32(size_z, size_y)] * 2
        + [float32(size_x, size_y)] * 2,
        [facts],
        [*marks, *pushes, before, predicted],
        [pltpu.VMEM(before.shape, jnp.float32)] + weight_scratch(layout),
        "spread_rest",
        2 * visit_cost(layout, (0, 1, 2)),
        12 * before.size,
    )


def pack_x_kernel(layout, slot_ids, corners, flow, cells, fraction, own, to_right, to_left):
    size_x, size_z, size_y = layout.sizes
    slots = layout.slots
    length_x = size_x * lax.axis_size("gx")
    length_z = size_z * lax.axis_size("gz")
    offset_x = length_x + HALF - lax.axis_index("gx") * size_x
    offset_z = length_z + HALF - lax.axis_index("gz") * size_z
    for a, direction in enumerate((0, 2, 1)):
        for t in range(layout.tiles):
            lanes = slice(t * LANES, (t + 1) * LANES)
            place = cells[direction, :, lanes].astype(jnp.float32) + fraction[direction, :, lanes]
            first = (a * layout.tiles + t) * slots
            own[first : first + slots] = place
    lane = lax.broadcasted_iota(jnp.int32, (1, LANES), 1)
    for slot in range(slots):
        first_x = lax.rem(corners[0, slot] + offset_x, length_x) - HALF
        first_z = lax.rem(corners[2, slot] + offset_z, length_z) - HALF
        held = (slot_ids[slot] >= 0).astype(jnp.int32)
        fact = jnp.where(lane == 0, first_x, held)
        fact = jnp.where(lane == 1, first_z, fact)
        fact = jnp.where(lane == 2, corners[1, slot], fact)
        row = layout.fact_row + slot
        own[row : row + 1] = fact.astype(jnp.float32)
    for c in range(4):
        rows = slice(c * size_z, (c + 1) * size_z)
        to_right[rows] = flow[c, size_x - 1]
        to_left[rows] = flow[c, 0]
    to_right[layout.ghost_x :] = own[...]
    to_left[layout.ghost_x :] = own[...]


def pack_x(layout, slot_ids, corners, flow, cells, fraction):
    rows = layout.ghost_x + layout.rows
    return call(
        functools.partial(pack_x_kernel, layout),
        [float32(layout.rows, LANES)] + [float32(rows, LANES)] * 2,
        [slot_ids, corners],
        [flow, cells, fraction],
        [],
        "pack_x",
        flow.size,
        8 * rows * LANES,
    )


def pack_z_kernel(layout, flow, own, left, right, to_upper, to_lower):
    size_x, size_z, size_y = layout.sizes
    for c in range(4):
        for x in range(size_x):
            row = c * size_x + x
            to_upper[row : row + 1] = flow[c, x, size_z - 1 : size_z]
            to_lower[row : row + 1] = flow[c, x, 0:1]
    tiles = (left[layout.ghost_x :], own[...], right[layout.ghost_x :])
    for block, tile in enumerate(tiles):
        first = layout.ghost_z + block * layout.rows
        to_upper[first : first + layout.rows] = tile
        to_lower[first : first + layout.rows] = tile


def pack_z(layout, flow, own, left, right):
    rows = layout.ghost_z + 3 * layout.rows
    return call(
        functools.partial(pack_z_kernel, layout),
        [float32(rows, LANES)] * 2,
        [],
        [flow, own, left, right],
        [],
        "pack_z",
        flow.size,
        8 * rows * LANES,
    )


def y_neighbours(value, lane, below, above):
    size_y = value.shape[-1]
    minus = jnp.where(lane == 0, below, pltpu.roll(value, 1, 1))
    plus = jnp.where(lane == size_y - 1, above, pltpu.roll(value, size_y - 1, 1))
    return minus, plus


def z_neighbours(value, row, below, above):
    size_z = value.shape[0]
    minus = jnp.where(row == 0, below, pltpu.roll(value, 1, 0))
    plus = jnp.where(row == size_z - 1, above, pltpu.roll(value, size_z - 1, 0))
    return minus, plus


def predict_inner_kernel(sizes, flow, left, right, predicted):
    size_x, size_z, size_y = sizes
    row = lax.broadcasted_iota(jnp.int32, (size_z, size_y), 0)
    lane = lax.broadcasted_iota(jnp.int32, (size_z, size_y), 1)

    def around(c, x):
        value = flow[c, x]
        ghost = slice(c * size_z, (c + 1) * size_z)
        x_minus = flow[c, x - 1] if x > 0 else left[ghost]
        x_plus = flow[c, x + 1] if x < size_x - 1 else right[ghost]
        z_minus, z_plus = z_neighbours(value, row, 0.0, 0.0)
        edges = (0.0, 0.0) if c < 3 else (value, value)
        y_minus, y_plus = y_neighbours(value, lane, *edges)
        return value, x_minus, x_plus, z_minus, z_plus, y_minus, y_plus

    for x in range(size_x):
        _, x_minus, x_plus, z_minus, z_plus, y_minus, y_plus = around(3, x)
        gradient = (
            (x_plus - x_minus) * 0.5 - drive_force,
            (y_plus - y_minus) * 0.5,
            (z_plus - z_minus) * 0.5,
        )
        carried = (flow[0, x], flow[1, x], flow[2, x])
        for c in range(3):
            value, x_minus, x_plus, z_minus, z_plus, y_minus, y_plus = around(c, x)
            laplace = x_plus + x_minus + z_plus + z_minus + y_plus + y_minus - 6.0 * value
            advect = (
                carried[0] * (x_plus - x_minus)
                + carried[1] * (y_plus - y_minus)
                + carried[2] * (z_plus - z_minus)
            ) * 0.5
            predicted[c, x] = value + time_step * (viscosity * laplace - advect - gradient[c])


def predict_inner(sizes, flow, left, right):
    return call(
        functools.partial(predict_inner_kernel, sizes),
        float32(3, *sizes),
        [],
        [flow, left, right],
        [],
        "predict_inner",
        200 * flow.size,
        8 * flow.size,
    )


def predict_outer_kernel(layout, flow, inner, lower, own, upper, predicted, field, facts):
    size_x, size_z, size_y = layout.sizes
    row = lax.broadcasted_iota(jnp.int32, (8, size_y), 0)
    group = LANES // size_z
    for block in range(9):
        payload = (lower, own, upper)[block // 3]
        first = layout.ghost_z + (block % 3) * layout.rows + layout.fact_row
        out = slice(block * layout.slots, (block + 1) * layout.slots)
        facts[out] = payload[first : first + layout.slots].astype(jnp.int32)
    for q in range(size_x // group):
        for x in range(q * group, (q + 1) * group):
            carried_low = flow[2, x, 0:1]
            carried_high = flow[2, x, size_z - 1 : size_z]
            for c in range(3):
                ghost = c * size_x + x
                below, above = lower[ghost : ghost + 1], upper[ghost : ghost + 1]
                change_low = (viscosity + 0.5 * carried_low) * below
                change_high = (viscosity - 0.5 * carried_high) * above
                if c == 2:
                    ghost = 3 * size_x + x
                    change_low += 0.5 * lower[ghost : ghost + 1]
                    change_high -= 0.5 * upper[ghost : ghost + 1]
                predicted[c, x] = inner[c, x]
                first = inner[c, x, 0:8]
                predicted[c, x, 0:8] = first + jnp.where(row == 0, time_step * change_low, 0.0)
                last = inner[c, x, size_z - 8 : size_z]
                predicted[c, x, size_z - 8 : size_z] = last + jnp.where(
                    row == 7, time_step * change_high, 0.0
                )
        for c in range(3):
            part = predicted[c, q * group : (q + 1) * group].reshape(LANES, size_y)
            field[c, :, q * LANES : (q + 1) * LANES] = jnp.transpose(part)


def predict_outer(layout, flow, inner, lower, own, upper):
    size_x, size_z, size_y = layout.sizes
    return call(
        functools.partial(predict_outer_kernel, layout),
        [
            float32(3, *layout.sizes),
            float32(3, size_y, layout.plane),
            jax.ShapeDtypeStruct((9 * layout.slots, LANES), jnp.int32),
        ],
        [],
        [flow, inner, lower, own, upper],
        [],
        "predict_outer",
        10 * flow.size,
        12 * flow.size,
    )


def divergence_kernel(sizes, parts, velocity, u_below, u_above, w_below, w_above, *rest):
    outs, whole = rest[:parts], rest[parts]
    size_x, size_z, size_y = sizes
    row = lax.broadcasted_iota(jnp.int32, (size_z, size_y), 0)
    lane = lax.broadcasted_iota(jnp.int32, (size_z, size_y), 1)
    group = LANES // size_z
    for q in range(size_x // group):
        pieces = []
        for x in range(q * group, (q + 1) * group):
            x_minus = velocity[0, x - 1] if x > 0 else u_below[...]
            x_plus = velocity[0, x + 1] if x < size_x - 1 else u_above[...]
            y_minus, y_plus = y_neighbours(velocity[1, x], lane, 0.0, 0.0)
            z_minus, z_plus = z_neighbours(
                velocity[2, x], row, w_below[x : x + 1], w_above[x : x + 1]
            )
            along_x = (x_plus - x_minus) * 0.5
            along_z = (z_plus - z_minus) * 0.5
            pieces.append(along_x + (y_plus - y_minus) * 0.5 + along_z)
        part = jnp.concatenate(pieces, axis=0)
        whole[:, q * LANES : (q + 1) * LANES] = jnp.transpose(part)
    height = size_y // parts
    for step in range(parts):
        first = pl.multiple_of(lax.rem(lax.axis_index("gz") + step, parts) * height, 8)
        outs[step][...] = whole[pl.ds(first, height), :]


def divergence(sizes, parts, velocity, ghosts):
    size_x, size_z, size_y = sizes
    plane = size_x * size_z
    return call(
        functools.partial(divergence_kernel, sizes, parts),
        [float32(size_y // parts, plane)] * parts,
        [],
        [velocity, *ghosts],
        [pltpu.VMEM((size_y, plane), jnp.float32)],
        "divergence",
        10 * velocity.size,
        6 * velocity.size,
    )


def swap_groups(values, width):
    count = LANES // width
    lane = lax.broadcasted_iota(jnp.int32, values[0].shape, 1)
    values = list(values)
    step = count // 2
    while step:
        reach = step * width
        keep = lane % (2 * reach) < reach
        for i in range(count):
            if i & step == 0:
                a, b = values[i], values[i + step]
                values[i] = jnp.where(keep, a, pltpu.roll(b, reach, 1))
                values[i + step] = jnp.where(keep, pltpu.roll(a, LANES - reach, 1), b)
        step //= 2
    return values


def transform_z_kernel(sizes, counts, table_high, table_low, *refs):
    size_x, size_z, size_y = sizes
    parts_x, parts_z = counts
    pieces, refs = refs[:parts_z], refs[parts_z:]
    outs, (gathered, turned, whole) = refs[:parts_x], refs[parts_x:]
    height = size_y // parts_z
    group = LANES // size_z
    for step in range(parts_z):
        gathered[lax.rem(lax.axis_index("gz") + parts_z - step, parts_z)] = pieces[step][...]
    for block in range(parts_z // group):
        for q in range(size_x // group):
            lanes = slice(q * LANES, (q + 1) * LANES)
            values = [gathered[block * group + i, :, lanes] for i in range(group)]
            for j, value in enumerate(swap_groups(values, size_z)):
                turned[block, pl.ds(q * group + j, height, stride=size_x), :] = value
    lines = jnp.concatenate([turned[b] for b in range(turned.shape[0])], axis=1)
    high, low = split(lines)
    result = lax.dot_general(
        table_high[...], high, TRANSPOSED, preferred_element_type=jnp.float32
    )
    result += lax.dot_general(
        table_low[...], high, TRANSPOSED, preferred_element_type=jnp.float32
    )
    result += lax.dot_general(
        table_high[...], low, TRANSPOSED, preferred_element_type=jnp.float32
    )
    whole[...] = result
    rows = whole.shape[0] // parts_x
    for step in range(parts_x):
        first = pl.multiple_of(lax.rem(lax.axis_index("gx") + step, parts_x) * rows, 8)
        outs[step][...] = whole[pl.ds(first, rows), :]


def transform_z(sizes, counts, table, pieces):
    size_x, size_z, size_y = sizes
    parts_x, parts_z = counts
    length_z = size_z * parts_z
    height = size_y // parts_z
    columns = height * size_x
    return call(
        functools.partial(transform_z_kernel, sizes, counts),
        [float32(2 * length_z // parts_x, columns)] * parts_x,
        [],
        [*table, *pieces],
        [
            pltpu.VMEM((parts_z, height, size_x * size_z), jnp.float32),
            pltpu.VMEM((length_z // LANES, columns, LANES), jnp.float32),
            pltpu.VMEM((2 * length_z, columns), jnp.float32),
        ],
        "transform_z",
        12 * length_z * length_z * columns,
        12 * length_z * columns,
    )


def transform_x_kernel(sizes, counts, table_high, table_low, *refs):
    size_x, size_z, size_y = sizes
    parts_x, parts_z = counts
    pieces, (source, gathered, turned) = refs[:parts_x], refs[parts_x:]
    length_x = size_x * parts_x
    modes = size_z * parts_z // parts_x
    height = size_y // parts_z
    group = LANES // size_x
    for step in range(parts_x):
        gathered[lax.rem(lax.axis_index("gx") + parts_x - step, parts_x)] = pieces[step][...]
    for block in range(parts_x // group):
        for q in range(height // group):
            lanes = slice(q * LANES, (q + 1) * LANES)
            values = [gathered[block * group + i, :, lanes] for i in range(group)]
            for j, value in enumerate(swap_groups(values, size_x)):
                first = (q * group + j) * modes
                for c in range(2):
                    column = c * length_x + block * LANES
                    turned[first : first + modes, column : column + LANES] = value[
                        c * modes : (c + 1) * modes
                    ]
    high, low = split(turned[...])
    result = jnp.dot(high, table_high[...], preferred_element_type=jnp.float32)
    result += jnp.dot(low, table_high[...], preferred_element_type=jnp.float32)
    result += jnp.dot(high, table_low[...], preferred_element_type=jnp.float32)
    source[0] = result[:, :length_x].reshape(height, modes, length_x)
    source[1] = result[:, length_x:].reshape(height, modes, length_x)


def transform_x(sizes, counts, table, pieces):
    size_x, size_z, size_y = sizes
    parts_x, parts_z = counts
    length_x = size_x * parts_x
    modes = size_z * parts_z // parts_x
    height = size_y // parts_z
    return call(
        functools.partial(transform_x_kernel, sizes, counts),
        float32(2, height, modes, length_x),
        [],
        [*table, *pieces],
        [
            pltpu.VMEM((parts_x, *pieces[0].shape), jnp.float32),
            pltpu.VMEM((height * modes, 2 * length_x), jnp.float32),
        ],
        "transform_x",
        24 * length_x * length_x * height * modes,
        24 * length_x * height * modes,
    )


def split_table(table):
    high = table.astype(np.float32).astype(jnp.bfloat16)
    low = (table - high.astype(np.float64)).astype(np.float32).astype(jnp.bfloat16)
    return jnp.asarray(high), jnp.asarray(low)


def angles(length):
    counter = np.arange(length)
    turn = (counter[:, None] * counter[None, :] % length) * (2.0 * np.pi / length)
    return np.cos(turn), np.sin(turn)


def table_z(length, blocks):
    cosine, sine = angles(length)
    modes = length // blocks
    table = np.stack([cosine, -sine]).reshape(2, blocks, modes, length)
    return split_table(table.transpose(1, 0, 2, 3).reshape(2 * length, length))


def table_x(length, scale):
    cosine, sine = angles(length)
    return split_table(np.block([[cosine, -sine], [sine, cosine]]) * scale)


def exchange(pieces, axis):
    return [pieces[0]] + [shift(pieces[d], axis, d) for d in range(1, len(pieces))]


def on_device(
    flow_state, slot_ids, corners, marker_cells, marker_frac, particle_velocity, particle_spin
):
    sizes = flow_state.shape[1:]
    size_x, size_z, size_y = sizes
    counts = (lax.axis_size("gx"), lax.axis_size("gz"))
    length_x, length_z = (size_x * counts[0], size_z * counts[1])
    slots, markers = marker_cells.shape[1:]
    layout = Layout(sizes, slots, markers)

    own, to_right, to_left = pack_x(
        layout, slot_ids, corners, flow_state, marker_cells, marker_frac
    )
    left = shift(to_right, "gx", 1)
    right = shift(to_left, "gx", -1)
    row, to_lower = pack_z(layout, flow_state, own, left, right)
    lower = shift(row, "gz", 1)
    upper = shift(to_lower, "gz", -1)
    inner = predict_inner(sizes, flow_state, left, right)
    predicted, field, facts = predict_outer(layout, flow_state, inner, lower, row, upper)

    positions = marker_cells.astype(jnp.float32) + marker_frac
    chosen = slot_ids[:, None] == jnp.arange(particle_velocity.shape[1], dtype=jnp.int32)[None, :]
    moving = jnp.sum(jnp.where(chosen[None], particle_velocity[:, None, :], 0.0), axis=2)
    turning = jnp.sum(jnp.where(chosen[None], particle_spin[:, None, :], 0.0), axis=2)
    lever = positions - HALF
    moving, turning = (moving[:, :, None], turning[:, :, None])
    target = moving + jnp.stack(
        [
            turning[1] * lever[2] - turning[2] * lever[1],
            turning[2] * lever[0] - turning[0] * lever[2],
            turning[0] * lever[1] - turning[1] * lever[0],
        ]
    )
    living = (slot_ids >= 0).astype(jnp.float32)[None, :, None]

    tiles = (0, 1, 2)
    lower_part = sample(layout, tiles, -1, facts, lower, field, "sample_lower")
    from_upper = shift(lower_part, "gz", -1)
    upper_part = sample(layout, tiles, 1, facts, upper, field, "sample_upper")
    from_lower = shift(upper_part, "gz", 1)
    side_part = sample(layout, (0, 2), 0, facts, row, field, "sample_side")
    from_z = from_upper + from_lower
    from_right = shift(side_part[:, :slots] + from_z[:, :slots], "gx", -1)
    from_left = shift(side_part[:, slots:] + from_z[:, 2 * slots :], "gx", 1)
    own_part = sample(layout, (1,), 0, facts, row, field, "sample_own")
    sampled = own_part + from_z[:, slots : 2 * slots] + from_right + from_left
    push = living * (target - sampled)

    left_push = shift(push, "gx", 1)
    right_push = shift(push, "gx", -1)
    row_push = jnp.concatenate([left_push, push, right_push], axis=1)
    lower_push = shift(row_push, "gz", 1)
    upper_push = shift(row_push, "gz", -1)
    forcing = spread_own(layout, facts, row, push)
    forcing = spread_side(layout, facts, row, row_push, forcing)
    velocity, u_first, u_last, w_first, w_last = spread_rest(
        layout, facts, (lower, upper), (lower_push, upper_push), forcing, predicted
    )

    ghosts = (
        shift(u_last, "gx", 1),
        shift(u_first, "gx", -1),
        shift(w_last, "gz", 1),
        shift(w_first, "gz", -1),
    )
    pieces = divergence(sizes, counts[1], velocity, ghosts)
    pieces = exchange(pieces, "gz")
    pieces = transform_z(sizes, counts, table_z(length_z, counts[0]), pieces)
    pieces = exchange(pieces, "gx")
    scale = 1.0 / math.sqrt(length_x * length_z)
    source = transform_x(sizes, counts, table_x(length_x, scale), pieces)
    return velocity, source


def solution(mesh):
    return jax.shard_map(
        on_device,
        mesh=mesh,
        in_specs=(
            P(None, "gx", "gz", None),
            P(("gx", "gz")),
            P(None, ("gx", "gz")),
            P(None, ("gx", "gz"), None),
            P(None, ("gx", "gz"), None),
            P(),
            P(),
        ),
        out_specs=(P(None, "gx", "gz", None), P(None, "gz", "gx", None)),
        check_vma=False,
    )
```

```python
import functools
import math

import jax
import jax.numpy as jnp
import numpy as np
from jax import lax
from jax.experimental import pallas as pl
from jax.experimental.pallas import tpu as pltpu
from jax.sharding import PartitionSpec as P

BOX = 24
HALF = 12
WINDOW = 32
LANES = 128
KERNEL_BYTES = 16 * 1024 * 1024

time_step = 0.1
viscosity = 0.2
drive_force = 1.0


IN_VMEM = pl.BlockSpec(memory_space=pltpu.VMEM)
IN_SMEM = pl.BlockSpec(memory_space=pltpu.SMEM)
TRANSPOSED = (((1,), (1,)), ((), ()))


def float32(*shape):
    return jax.ShapeDtypeStruct(shape, jnp.float32)


def call(kernel, out_shape, scalars, arrays, scratch, name, flops, moved):
    outputs = len(out_shape) if isinstance(out_shape, (list, tuple)) else 0
    return pl.pallas_call(
        kernel,
        out_shape=out_shape,
        in_specs=[IN_SMEM] * len(scalars) + [IN_VMEM] * len(arrays),
        out_specs=[IN_VMEM] * outputs if outputs else IN_VMEM,
        scratch_shapes=scratch,
        name=name,
        compiler_params=pltpu.CompilerParams(vmem_limit_bytes=KERNEL_BYTES),
        cost_estimate=pl.CostEstimate(flops=flops, bytes_accessed=moved, transcendentals=0),
    )(*scalars, *arrays)


def shift(array, axis, step):
    devices = lax.axis_size(axis)
    return lax.ppermute(array, axis, [(i, (i + step) % devices) for i in range(devices)])


def cosine_coefficients():
    samples = 2.0 + 2.0 * np.cos(np.pi * (np.arange(64) + 0.5) / 64)
    values = np.cos(np.pi / 4 * np.sqrt(samples)) * np.sqrt(0.5)
    fit = np.polynomial.chebyshev.Chebyshev.fit(samples, values, 4, domain=[0, 4])
    return [float(v) for v in fit.convert(kind=np.polynomial.Polynomial).coef]


COSINE = cosine_coefficients()


def weight(offset):
    square = jnp.minimum(offset * offset, 4.0)
    value = COSINE[-1] * square + COSINE[-2]
    for coefficient in COSINE[-3::-1]:
        value = value * square + coefficient
    return value * value


def split(value):
    high = value.astype(jnp.bfloat16)
    low = (value - high.astype(jnp.float32)).astype(jnp.bfloat16)
    return high, low


def row_weights(count, position):
    cells = lax.broadcasted_iota(jnp.int32, (count, position.shape[1]), 0)
    return weight(cells.astype(jnp.float32) - position)


def plane_weights(weight_x, weight_z, half_z, high, low):
    count = 0
    for z in range(0, weight_z.shape[0], half_z):
        part = weight_z[z : z + half_z]
        for x in range(weight_x.shape[0]):
            rows = slice(count * half_z, (count + 1) * half_z)
            high[rows], low[rows] = split(weight_x[x : x + 1] * part)
            count += 1


def window_start(first_y, size_y):
    return pl.multiple_of(jnp.minimum((first_y // 8) * 8, size_y - WINDOW), 8)


def quarters(sizes):
    half_x, half_z = sizes[0] // 2, sizes[1] // 2
    for z in range(2):
        for x in range(2):
            yield slice(x * half_x, (x + 1) * half_x), slice(z * half_z, (z + 1) * half_z)


class Layout:
    def __init__(self, sizes, slots, markers):
        self.sizes, self.slots, self.markers = sizes, slots, markers
        self.tiles = markers // LANES
        self.fact_row = 3 * self.tiles * slots
        self.rows = self.fact_row + slots
        self.ghost_x = 4 * sizes[1]
        self.ghost_z = 4 * sizes[0]
        self.plane = sizes[0] * sizes[1]


def marker_row(layout, marks, base, direction, slot):
    first = base + direction * layout.tiles * layout.slots + slot
    rows = [marks[pl.ds(first + t * layout.slots, 1), :] for t in range(layout.tiles)]
    return jnp.concatenate(rows, axis=1)


def slot_visits(layout, facts, marks, blocks, step_z, high, low, visit, skip):
    size_x, size_z, size_y = layout.sizes
    half_x, half_z = size_x // 2, size_z // 2
    slots = layout.slots

    def body(index, carry):
        block, slot = index // slots, index % slots
        block = blocks[0] + block * (blocks[1] - blocks[0] if len(blocks) > 1 else 0)
        fact = (step_z + 1) * 3 * slots + block * slots + slot
        first_x = facts[fact, 0] + (block - 1) * size_x
        first_z = facts[fact, 1] + step_z * size_z
        first_y = facts[fact, 2]
        meets_x = (first_x > -BOX) & (first_x < size_x)
        meets_z = (first_z > -BOX) & (first_z < size_z)
        active = (facts[fact, 3] != 0) & meets_x & meets_z
        whole_x = (first_x > half_x - BOX) & (first_x < half_x)
        whole_z = (first_z > half_z - BOX) & (first_z < half_z)
        upper_x = (first_x >= half_x).astype(jnp.int32)
        upper_z = (first_z >= half_z).astype(jnp.int32)

        def part(all_x, all_z):
            start_x = 0 if all_x else upper_x * half_x
            start_z = 0 if all_z else upper_z * half_z
            lanes = [
                ((0 if all_z else upper_z) + z) * 2 * LANES + (0 if all_x else upper_x) * LANES
                for z in range(2 if all_z else 1)
            ]
            width = (2 if all_x else 1) * LANES
            if all_x and all_z:
                pieces = [(0, 4 * LANES)]
            else:
                pieces = [(pl.multiple_of(lane, LANES), width) for lane in lanes]
            base = layout.ghost_z + block * layout.rows
            first = window_start(first_y, size_y)
            move = (first_x - start_x).astype(jnp.float32)
            position = marker_row(layout, marks, base, 0, slot) + move
            weight_x = row_weights(size_x if all_x else half_x, position)
            move = (first_z - start_z).astype(jnp.float32)
            position = marker_row(layout, marks, base, 1, slot) + move
            weight_z = row_weights(size_z if all_z else half_z, position)
            plane_weights(weight_x, weight_z, half_z, high, low)
            move = (first_y - first).astype(jnp.float32)
            position = marker_row(layout, marks, base, 2, slot) + move
            weight_y = row_weights(WINDOW, position)
            visit(index, block * slots + slot, first, weight_y, pieces)

        for all_x in (True, False):
            for all_z in (True, False):
                one = whole_x if all_x else jnp.logical_not(whole_x)
                two = whole_z if all_z else jnp.logical_not(whole_z)
                pl.when(active & one & two)(functools.partial(part, all_x, all_z))

        if skip is not None:

            @pl.when(jnp.logical_not(active))
            def _():
                skip(index)

        return carry

    lax.fori_loop(0, len(blocks) * slots, body, 0)


def sample_kernel(layout, blocks, step_z, facts, marks, field, out, high, low):
    def visit(index, _, first, weight_y, pieces):
        rows = pl.ds(first, WINDOW)
        parts = [
            jnp.concatenate([field[c, rows, pl.ds(lane, width)] for c in range(3)], axis=0)
            for lane, width in pieces
        ]
        window = jnp.concatenate(parts, axis=1)
        count = window.shape[1]
        window_high, window_low = split(window)
        both = jnp.concatenate([window_high, window_low], axis=0)
        value = jnp.dot(both, high[:count], preferred_element_type=jnp.float32)
        rest = jnp.dot(window_high, low[:count], preferred_element_type=jnp.float32)
        value = value[: 3 * WINDOW] + value[3 * WINDOW :] + rest
        for c in range(3):
            part = value[c * WINDOW : (c + 1) * WINDOW] * weight_y
            out[c, pl.ds(index, 1), :] = jnp.sum(part, axis=0, keepdims=True)

    def skip(index):
        for c in range(3):
            out[c, pl.ds(index, 1), :] = jnp.zeros((1, layout.markers), jnp.float32)

    slot_visits(layout, facts, marks, blocks, step_z, high, low, visit, skip)


def visit_cost(layout, blocks):
    return len(blocks) * layout.slots * 18 * WINDOW * layout.plane * layout.markers


def weight_scratch(layout):
    return [pltpu.VMEM((layout.plane, layout.markers), jnp.bfloat16)] * 2


def sample(layout, blocks, step_z, facts, marks, field, name):
    return call(
        functools.partial(sample_kernel, layout, blocks, step_z),
        float32(3, len(blocks) * layout.slots, layout.markers),
        [facts],
        [marks, field],
        weight_scratch(layout),
        name,
        visit_cost(layout, blocks),
        4 * (field.size + marks.size),
    )


def spread_slots(layout, blocks, step_z, facts, marks, push, own_rows, total, high, low):
    def visit(index, row, first, weight_y, pieces):
        slot = index if own_rows else row
        count = sum(width for _, width in pieces)
        value = jnp.concatenate(
            [weight_y * push[c, pl.ds(slot, 1), :] for c in range(3)], axis=0
        )
        value_high, value_low = split(value)
        both = jnp.concatenate([value_high, value_low], axis=0)
        added = lax.dot_general(
            both, high[:count], TRANSPOSED, preferred_element_type=jnp.float32
        )
        rest = lax.dot_general(
            value_high, low[:count], TRANSPOSED, preferred_element_type=jnp.float32
        )
        added = added[: 3 * WINDOW] + added[3 * WINDOW :] + rest
        column = 0
        for lane, width in pieces:
            for c in range(3):
                part = added[c * WINDOW : (c + 1) * WINDOW, column : column + width]
                total[c, pl.ds(first, WINDOW), pl.ds(lane, width)] += part
            column += width

    slot_visits(layout, facts, marks, blocks, step_z, high, low, visit, None)


def spread_own_kernel(layout, facts, marks, push, total, high, low):
    total[...] = jnp.zeros(total.shape, jnp.float32)
    spread_slots(layout, (1,), 0, facts, marks, push, True, total, high, low)


def spread_own(layout, facts, marks, push):
    return call(
        functools.partial(spread_own_kernel, layout),
        float32(3, layout.sizes[2], layout.plane),
        [facts],
        [marks, push],
        weight_scratch(layout),
        "spread_own",
        visit_cost(layout, (1,)),
        12 * layout.sizes[2] * layout.plane,
    )


def spread_side_kernel(layout, facts, marks, push, before, total, high, low):
    total[...] = before[...]
    spread_slots(layout, (0, 2), 0, facts, marks, push, False, total, high, low)


def spread_side(layout, facts, marks, push, before):
    return call(
        functools.partial(spread_side_kernel, layout),
        float32(*before.shape),
        [facts],
        [marks, push, before],
        weight_scratch(layout),
        "spread_side",
        visit_cost(layout, (0, 2)),
        8 * before.size,
    )


def spread_rest_kernel(
    layout,
    facts,
    lower_marks,
    upper_marks,
    lower_push,
    upper_push,
    before,
    predicted,
    velocity,
    u_first,
    u_last,
    w_first,
    w_last,
    inner,
    total,
    high,
    low,
):
    size_x, size_z, size_y = layout.sizes
    total[...] = before[...]
    row = (0, 1, 2)
    spread_slots(layout, row, -1, facts, lower_marks, lower_push, False, total, high, low)
    spread_slots(layout, row, 1, facts, upper_marks, upper_push, False, total, high, low)
    for c in range(3):
        for q, (xs, zs) in enumerate(quarters(layout.sizes)):
            part = jnp.transpose(total[c, :, q * LANES : (q + 1) * LANES])
            part = part.reshape(size_x // 2, size_z // 2, size_y)
            velocity[c, xs, zs] = predicted[c, xs, zs] + part
    u_first[...] = velocity[0, 0]
    u_last[...] = velocity[0, size_x - 1]
    for x in range(size_x):
        w_first[x : x + 1] = velocity[2, x, 0:1]
        w_last[x : x + 1] = velocity[2, x, size_z - 1 : size_z]
    row = lax.broadcasted_iota(jnp.int32, (size_z, size_y), 0)
    lane = lax.broadcasted_iota(jnp.int32, (size_z, size_y), 1)
    for x in range(size_x):
        y_minus, y_plus = y_neighbours(velocity[1, x], lane, 0.0, 0.0)
        z_minus, z_plus = z_neighbours(velocity[2, x], row, 0.0, 0.0)
        change = y_plus - y_minus + z_plus - z_minus
        if x > 0:
            change -= velocity[0, x - 1]
        if x < size_x - 1:
            change += velocity[0, x + 1]
        inner[x] = change * 0.5


def spread_rest(layout, facts, marks, pushes, before, predicted):
    size_x, size_z, size_y = layout.sizes
    return call(
        functools.partial(spread_rest_kernel, layout),
        [float32(3, size_x, size_z, size_y)]
        + [float32(size_z, size_y)] * 2
        + [float32(size_x, size_y)] * 2
        + [float32(size_x, size_z, size_y)],
        [facts],
        [*marks, *pushes, before, predicted],
        [pltpu.VMEM(before.shape, jnp.float32)] + weight_scratch(layout),
        "spread_rest",
        2 * visit_cost(layout, (0, 1, 2)),
        12 * before.size,
    )


def pack_x_kernel(
    layout,
    slot_ids_hbm,
    corners_hbm,
    flow,
    cells_hbm,
    fraction_hbm,
    own,
    to_right,
    to_left,
    slot_ids,
    corners,
    cells,
    fraction,
    done,
):
    size_x, size_z, size_y = layout.sizes
    slots = layout.slots
    moves = [
        (slot_ids_hbm, slot_ids),
        (corners_hbm, corners),
        (cells_hbm, cells),
        (fraction_hbm, fraction),
    ]
    for c in range(4):
        rows = pl.ds(c * size_z, size_z)
        moves.append((flow.at[c, size_x - 1], to_right.at[rows]))
        moves.append((flow.at[c, 0], to_left.at[rows]))
    copies = [pltpu.make_async_copy(a, b, done.at[i]) for i, (a, b) in enumerate(moves)]
    for copy in copies:
        copy.start()
    for copy in copies[:4]:
        copy.wait()
    length_x = size_x * lax.axis_size("gx")
    length_z = size_z * lax.axis_size("gz")
    offset_x = length_x + HALF - lax.axis_index("gx") * size_x
    offset_z = length_z + HALF - lax.axis_index("gz") * size_z
    targets = ((own, 0), (to_right, layout.ghost_x), (to_left, layout.ghost_x))
    for a, direction in enumerate((0, 2, 1)):
        for t in range(layout.tiles):
            lanes = slice(t * LANES, (t + 1) * LANES)
            place = cells[direction, :, lanes].astype(jnp.float32) + fraction[direction, :, lanes]
            for target, base in targets:
                first = base + (a * layout.tiles + t) * slots
                target[first : first + slots] = place
    lane = lax.broadcasted_iota(jnp.int32, (1, LANES), 1)
    for slot in range(slots):
        first_x = lax.rem(corners[0, slot] + offset_x, length_x) - HALF
        first_z = lax.rem(corners[2, slot] + offset_z, length_z) - HALF
        held = (slot_ids[slot] >= 0).astype(jnp.int32)
        fact = jnp.where(lane == 0, first_x, held)
        fact = jnp.where(lane == 1, first_z, fact)
        fact = jnp.where(lane == 2, corners[1, slot], fact)
        for target, base in targets:
            row = base + layout.fact_row + slot
            target[row : row + 1] = fact.astype(jnp.float32)
    for copy in copies[4:]:
        copy.wait()


def pack_x(layout, slot_ids, corners, flow, cells, fraction):
    rows = layout.ghost_x + layout.rows
    in_hbm = pl.BlockSpec(memory_space=pltpu.HBM)
    return pl.pallas_call(
        functools.partial(pack_x_kernel, layout),
        out_shape=[float32(layout.rows, LANES)] + [float32(rows, LANES)] * 2,
        in_specs=[in_hbm] * 5,
        out_specs=[IN_VMEM] * 3,
        scratch_shapes=[
            pltpu.SMEM(slot_ids.shape, jnp.int32),
            pltpu.SMEM(corners.shape, jnp.int32),
            pltpu.VMEM(cells.shape, jnp.int32),
            pltpu.VMEM(fraction.shape, jnp.float32),
            pltpu.SemaphoreType.DMA((12,)),
        ],
        name="pack_x",
        compiler_params=pltpu.CompilerParams(vmem_limit_bytes=KERNEL_BYTES),
        cost_estimate=pl.CostEstimate(
            flops=flow.size, bytes_accessed=8 * rows * LANES, transcendentals=0
        ),
    )(slot_ids, corners, flow, cells, fraction)


def pack_z_kernel(layout, flow, own, left, right, to_upper, to_lower):
    size_x, size_z, size_y = layout.sizes
    for c in range(4):
        for x in range(size_x):
            row = c * size_x + x
            to_upper[row : row + 1] = flow[c, x, size_z - 1 : size_z]
            to_lower[row : row + 1] = flow[c, x, 0:1]
    tiles = (left[layout.ghost_x :], own[...], right[layout.ghost_x :])
    for block, tile in enumerate(tiles):
        first = layout.ghost_z + block * layout.rows
        to_upper[first : first + layout.rows] = tile
        to_lower[first : first + layout.rows] = tile


def pack_z(layout, flow, own, left, right):
    rows = layout.ghost_z + 3 * layout.rows
    return call(
        functools.partial(pack_z_kernel, layout),
        [float32(rows, LANES)] * 2,
        [],
        [flow, own, left, right],
        [],
        "pack_z",
        flow.size,
        8 * rows * LANES,
    )


def y_neighbours(value, lane, below, above):
    size_y = value.shape[-1]
    minus = jnp.where(lane == 0, below, pltpu.roll(value, 1, 1))
    plus = jnp.where(lane == size_y - 1, above, pltpu.roll(value, size_y - 1, 1))
    return minus, plus


def z_neighbours(value, row, below, above):
    size_z = value.shape[0]
    minus = jnp.where(row == 0, below, pltpu.roll(value, 1, 0))
    plus = jnp.where(row == size_z - 1, above, pltpu.roll(value, size_z - 1, 0))
    return minus, plus


def predict_inner_kernel(sizes, flow, left, right, predicted):
    size_x, size_z, size_y = sizes
    row = lax.broadcasted_iota(jnp.int32, (size_z, size_y), 0)
    lane = lax.broadcasted_iota(jnp.int32, (size_z, size_y), 1)

    def around(c, x):
        value = flow[c, x]
        ghost = slice(c * size_z, (c + 1) * size_z)
        x_minus = flow[c, x - 1] if x > 0 else left[ghost]
        x_plus = flow[c, x + 1] if x < size_x - 1 else right[ghost]
        z_minus, z_plus = z_neighbours(value, row, 0.0, 0.0)
        edges = (0.0, 0.0) if c < 3 else (value, value)
        y_minus, y_plus = y_neighbours(value, lane, *edges)
        return value, x_minus, x_plus, z_minus, z_plus, y_minus, y_plus

    for x in range(size_x):
        _, x_minus, x_plus, z_minus, z_plus, y_minus, y_plus = around(3, x)
        gradient = (
            (x_plus - x_minus) * 0.5 - drive_force,
            (y_plus - y_minus) * 0.5,
            (z_plus - z_minus) * 0.5,
        )
        carried = (flow[0, x], flow[1, x], flow[2, x])
        for c in range(3):
            value, x_minus, x_plus, z_minus, z_plus, y_minus, y_plus = around(c, x)
            laplace = x_plus + x_minus + z_plus + z_minus + y_plus + y_minus - 6.0 * value
            advect = (
                carried[0] * (x_plus - x_minus)
                + carried[1] * (y_plus - y_minus)
                + carried[2] * (z_plus - z_minus)
            ) * 0.5
            predicted[c, x] = value + time_step * (viscosity * laplace - advect - gradient[c])


def predict_inner(sizes, flow, left, right):
    return call(
        functools.partial(predict_inner_kernel, sizes),
        float32(3, *sizes),
        [],
        [flow, left, right],
        [],
        "predict_inner",
        200 * flow.size,
        8 * flow.size,
    )


def predict_outer_kernel(layout, flow, inner, lower, own, upper, predicted, field, facts):
    size_x, size_z, size_y = layout.sizes
    row = lax.broadcasted_iota(jnp.int32, (8, size_y), 0)
    for block in range(9):
        payload = (lower, own, upper)[block // 3]
        first = layout.ghost_z + (block % 3) * layout.rows + layout.fact_row
        out = slice(block * layout.slots, (block + 1) * layout.slots)
        facts[out] = payload[first : first + layout.slots].astype(jnp.int32)
    for x in range(size_x):
        carried_low = flow[2, x, 0:1]
        carried_high = flow[2, x, size_z - 1 : size_z]
        for c in range(3):
            ghost = c * size_x + x
            below, above = lower[ghost : ghost + 1], upper[ghost : ghost + 1]
            change_low = (viscosity + 0.5 * carried_low) * below
            change_high = (viscosity - 0.5 * carried_high) * above
            if c == 2:
                ghost = 3 * size_x + x
                change_low += 0.5 * lower[ghost : ghost + 1]
                change_high -= 0.5 * upper[ghost : ghost + 1]
            predicted[c, x] = inner[c, x]
            first = inner[c, x, 0:8]
            predicted[c, x, 0:8] = first + jnp.where(row == 0, time_step * change_low, 0.0)
            last = inner[c, x, size_z - 8 : size_z]
            predicted[c, x, size_z - 8 : size_z] = last + jnp.where(
                row == 7, time_step * change_high, 0.0
            )
    for c in range(3):
        for q, (xs, zs) in enumerate(quarters(layout.sizes)):
            part = predicted[c, xs, zs].reshape(LANES, size_y)
            field[c, :, q * LANES : (q + 1) * LANES] = jnp.transpose(part)


def predict_outer(layout, flow, inner, lower, own, upper):
    size_x, size_z, size_y = layout.sizes
    return call(
        functools.partial(predict_outer_kernel, layout),
        [
            float32(3, *layout.sizes),
            float32(3, size_y, layout.plane),
            jax.ShapeDtypeStruct((9 * layout.slots, LANES), jnp.int32),
        ],
        [],
        [flow, inner, lower, own, upper],
        [],
        "predict_outer",
        10 * flow.size,
        12 * flow.size,
    )


def divergence_kernel(sizes, parts, inner, u_below, u_above, w_below, w_above, *rest):
    outs, whole = rest[:parts], rest[parts]
    size_x, size_z, size_y = sizes
    row = lax.broadcasted_iota(jnp.int32, (size_z, size_y), 0)
    group = LANES // size_z
    for q in range(size_x // group):
        pieces = []
        for x in range(q * group, (q + 1) * group):
            piece = inner[x]
            if x == 0:
                piece -= 0.5 * u_below[...]
            if x == size_x - 1:
                piece += 0.5 * u_above[...]
            piece -= jnp.where(row == 0, 0.5 * w_below[x : x + 1], 0.0)
            piece += jnp.where(row == size_z - 1, 0.5 * w_above[x : x + 1], 0.0)
            pieces.append(piece)
        part = jnp.concatenate(pieces, axis=0)
        whole[:, q * LANES : (q + 1) * LANES] = jnp.transpose(part)
    height = size_y // parts
    for step in range(parts):
        first = pl.multiple_of(lax.rem(lax.axis_index("gz") + step, parts) * height, 8)
        outs[step][...] = whole[pl.ds(first, height), :]


def divergence(sizes, parts, inner, ghosts):
    size_x, size_z, size_y = sizes
    plane = size_x * size_z
    return call(
        functools.partial(divergence_kernel, sizes, parts),
        [float32(size_y // parts, plane)] * parts,
        [],
        [inner, *ghosts],
        [pltpu.VMEM((size_y, plane), jnp.float32)],
        "divergence",
        10 * inner.size,
        8 * inner.size,
    )


def swap_groups(values, width):
    count = LANES // width
    lane = lax.broadcasted_iota(jnp.int32, values[0].shape, 1)
    values = list(values)
    step = count // 2
    while step:
        reach = step * width
        keep = lane % (2 * reach) < reach
        for i in range(count):
            if i & step == 0:
                a, b = values[i], values[i + step]
                values[i] = jnp.where(keep, a, pltpu.roll(b, reach, 1))
                values[i + step] = jnp.where(keep, pltpu.roll(a, LANES - reach, 1), b)
        step //= 2
    return values


def transform_z_kernel(sizes, counts, table_high, table_low, *refs):
    size_x, size_z, size_y = sizes
    parts_x, parts_z = counts
    pieces, refs = refs[:parts_z], refs[parts_z:]
    outs, (gathered, turned, whole) = refs[:parts_x], refs[parts_x:]
    height = size_y // parts_z
    group = LANES // size_z
    for step in range(parts_z):
        gathered[lax.rem(lax.axis_index("gz") + parts_z - step, parts_z)] = pieces[step][...]
    for block in range(parts_z // group):
        for q in range(size_x // group):
            lanes = slice(q * LANES, (q + 1) * LANES)
            values = [gathered[block * group + i, :, lanes] for i in range(group)]
            for j, value in enumerate(swap_groups(values, size_z)):
                turned[block, pl.ds(q * group + j, height, stride=size_x), :] = value
    lines = jnp.concatenate([turned[b] for b in range(turned.shape[0])], axis=1)
    high, low = split(lines)
    result = lax.dot_general(
        table_high[...], high, TRANSPOSED, preferred_element_type=jnp.float32
    )
    result += lax.dot_general(
        table_low[...], high, TRANSPOSED, preferred_element_type=jnp.float32
    )
    result += lax.dot_general(
        table_high[...], low, TRANSPOSED, preferred_element_type=jnp.float32
    )
    whole[...] = result
    rows = whole.shape[0] // parts_x
    for step in range(parts_x):
        first = pl.multiple_of(lax.rem(lax.axis_index("gx") + step, parts_x) * rows, 8)
        outs[step][...] = whole[pl.ds(first, rows), :]


def transform_z(sizes, counts, table, pieces):
    size_x, size_z, size_y = sizes
    parts_x, parts_z = counts
    length_z = size_z * parts_z
    height = size_y // parts_z
    columns = height * size_x
    return call(
        functools.partial(transform_z_kernel, sizes, counts),
        [float32(2 * length_z // parts_x, columns)] * parts_x,
        [],
        [*table, *pieces],
        [
            pltpu.VMEM((parts_z, height, size_x * size_z), jnp.float32),
            pltpu.VMEM((length_z // LANES, columns, LANES), jnp.float32),
            pltpu.VMEM((2 * length_z, columns), jnp.float32),
        ],
        "transform_z",
        12 * length_z * length_z * columns,
        12 * length_z * columns,
    )


def transform_x_kernel(sizes, counts, table_high, table_low, *refs):
    size_x, size_z, size_y = sizes
    parts_x, parts_z = counts
    pieces, (source, gathered, turned) = refs[:parts_x], refs[parts_x:]
    length_x = size_x * parts_x
    modes = size_z * parts_z // parts_x
    height = size_y // parts_z
    group = LANES // size_x
    for step in range(parts_x):
        gathered[lax.rem(lax.axis_index("gx") + parts_x - step, parts_x)] = pieces[step][...]
    for block in range(parts_x // group):
        for q in range(height // group):
            lanes = slice(q * LANES, (q + 1) * LANES)
            values = [gathered[block * group + i, :, lanes] for i in range(group)]
            for j, value in enumerate(swap_groups(values, size_x)):
                first = (q * group + j) * modes
                for c in range(2):
                    column = c * length_x + block * LANES
                    turned[first : first + modes, column : column + LANES] = value[
                        c * modes : (c + 1) * modes
                    ]
    high, low = split(turned[...])
    result = jnp.dot(high, table_high[...], preferred_element_type=jnp.float32)
    result += jnp.dot(low, table_high[...], preferred_element_type=jnp.float32)
    result += jnp.dot(high, table_low[...], preferred_element_type=jnp.float32)
    source[0] = result[:, :length_x].reshape(height, modes, length_x)
    source[1] = result[:, length_x:].reshape(height, modes, length_x)


def transform_x(sizes, counts, table, pieces):
    size_x, size_z, size_y = sizes
    parts_x, parts_z = counts
    length_x = size_x * parts_x
    modes = size_z * parts_z // parts_x
    height = size_y // parts_z
    return call(
        functools.partial(transform_x_kernel, sizes, counts),
        float32(2, height, modes, length_x),
        [],
        [*table, *pieces],
        [
            pltpu.VMEM((parts_x, *pieces[0].shape), jnp.float32),
            pltpu.VMEM((height * modes, 2 * length_x), jnp.float32),
        ],
        "transform_x",
        24 * length_x * length_x * height * modes,
        24 * length_x * height * modes,
    )


def split_table(table):
    high = table.astype(np.float32).astype(jnp.bfloat16)
    low = (table - high.astype(np.float64)).astype(np.float32).astype(jnp.bfloat16)
    return jnp.asarray(high), jnp.asarray(low)


def angles(length):
    counter = np.arange(length)
    turn = (counter[:, None] * counter[None, :] % length) * (2.0 * np.pi / length)
    return np.cos(turn), np.sin(turn)


def table_z(length, blocks):
    cosine, sine = angles(length)
    modes = length // blocks
    table = np.stack([cosine, -sine]).reshape(2, blocks, modes, length)
    return split_table(table.transpose(1, 0, 2, 3).reshape(2 * length, length))


def table_x(length, scale):
    cosine, sine = angles(length)
    return split_table(np.block([[cosine, -sine], [sine, cosine]]) * scale)


def exchange(pieces, axis):
    return [pieces[0]] + [shift(pieces[d], axis, d) for d in range(1, len(pieces))]


def on_device(
    flow_state, slot_ids, corners, marker_cells, marker_frac, particle_velocity, particle_spin
):
    sizes = flow_state.shape[1:]
    size_x, size_z, size_y = sizes
    counts = (lax.axis_size("gx"), lax.axis_size("gz"))
    length_x, length_z = (size_x * counts[0], size_z * counts[1])
    slots, markers = marker_cells.shape[1:]
    layout = Layout(sizes, slots, markers)

    own, to_right, to_left = pack_x(
        layout, slot_ids, corners, flow_state, marker_cells, marker_frac
    )
    left = shift(to_right, "gx", 1)
    right = shift(to_left, "gx", -1)
    row, to_lower = pack_z(layout, flow_state, own, left, right)
    lower = shift(row, "gz", 1)
    upper = shift(to_lower, "gz", -1)
    inner = predict_inner(sizes, flow_state, left, right)
    predicted, field, facts = predict_outer(layout, flow_state, inner, lower, row, upper)

    positions = marker_cells.astype(jnp.float32) + marker_frac
    chosen = slot_ids[:, None] == jnp.arange(particle_velocity.shape[1], dtype=jnp.int32)[None, :]
    moving = jnp.sum(jnp.where(chosen[None], particle_velocity[:, None, :], 0.0), axis=2)
    turning = jnp.sum(jnp.where(chosen[None], particle_spin[:, None, :], 0.0), axis=2)
    lever = positions - HALF
    moving, turning = (moving[:, :, None], turning[:, :, None])
    target = moving + jnp.stack(
        [
            turning[1] * lever[2] - turning[2] * lever[1],
            turning[2] * lever[0] - turning[0] * lever[2],
            turning[0] * lever[1] - turning[1] * lever[0],
        ]
    )
    living = (slot_ids >= 0).astype(jnp.float32)[None, :, None]

    tiles = (0, 1, 2)
    lower_part = sample(layout, tiles, -1, facts, lower, field, "sample_lower")
    from_upper = shift(lower_part, "gz", -1)
    upper_part = sample(layout, tiles, 1, facts, upper, field, "sample_upper")
    from_lower = shift(upper_part, "gz", 1)
    side_part = sample(layout, (0, 2), 0, facts, row, field, "sample_side")
    from_z = from_upper + from_lower
    from_right = shift(side_part[:, :slots] + from_z[:, :slots], "gx", -1)
    from_left = shift(side_part[:, slots:] + from_z[:, 2 * slots :], "gx", 1)
    own_part = sample(layout, (1,), 0, facts, row, field, "sample_own")
    sampled = own_part + from_z[:, slots : 2 * slots] + from_right + from_left
    push = living * (target - sampled)

    left_push = shift(push, "gx", 1)
    right_push = shift(push, "gx", -1)
    row_push = jnp.concatenate([left_push, push, right_push], axis=1)
    lower_push = shift(row_push, "gz", 1)
    upper_push = shift(row_push, "gz", -1)
    forcing = spread_own(layout, facts, row, push)
    forcing = spread_side(layout, facts, row, row_push, forcing)
    velocity, u_first, u_last, w_first, w_last, change = spread_rest(
        layout, facts, (lower, upper), (lower_push, upper_push), forcing, predicted
    )

    ghosts = (
        shift(u_last, "gx", 1),
        shift(u_first, "gx", -1),
        shift(w_last, "gz", 1),
        shift(w_first, "gz", -1),
    )
    pieces = divergence(sizes, counts[1], change, ghosts)
    pieces = exchange(pieces, "gz")
    pieces = transform_z(sizes, counts, table_z(length_z, counts[0]), pieces)
    pieces = exchange(pieces, "gx")
    scale = 1.0 / math.sqrt(length_x * length_z)
    source = transform_x(sizes, counts, table_x(length_x, scale), pieces)
    return velocity, source


def solution(mesh):
    return jax.shard_map(
        on_device,
        mesh=mesh,
        in_specs=(
            P(None, "gx", "gz", None),
            P(("gx", "gz")),
            P(None, ("gx", "gz")),
            P(None, ("gx", "gz"), None),
            P(None, ("gx", "gz"), None),
            P(),
            P(),
        ),
        out_specs=(P(None, "gx", "gz", None), P(None, "gz", "gx", None)),
        check_vma=False,
    )
```

```python
import functools
import math

import jax
import jax.numpy as jnp
import numpy as np
from jax import lax
from jax.experimental import pallas as pl
from jax.experimental.pallas import tpu as pltpu
from jax.sharding import PartitionSpec as P

BOX = 24
HALF = 12
WINDOW = 32
LANES = 128
KERNEL_BYTES = 16 * 1024 * 1024

time_step = 0.1
viscosity = 0.2
drive_force = 1.0


IN_VMEM = pl.BlockSpec(memory_space=pltpu.VMEM)
IN_SMEM = pl.BlockSpec(memory_space=pltpu.SMEM)
TRANSPOSED = (((1,), (1,)), ((), ()))


def float32(*shape):
    return jax.ShapeDtypeStruct(shape, jnp.float32)


def call(kernel, out_shape, scalars, arrays, scratch, name, flops, moved):
    outputs = len(out_shape) if isinstance(out_shape, (list, tuple)) else 0
    return pl.pallas_call(
        kernel,
        out_shape=out_shape,
        in_specs=[IN_SMEM] * len(scalars) + [IN_VMEM] * len(arrays),
        out_specs=[IN_VMEM] * outputs if outputs else IN_VMEM,
        scratch_shapes=scratch,
        name=name,
        compiler_params=pltpu.CompilerParams(vmem_limit_bytes=KERNEL_BYTES),
        cost_estimate=pl.CostEstimate(flops=flops, bytes_accessed=moved, transcendentals=0),
    )(*scalars, *arrays)


def shift(array, axis, step):
    devices = lax.axis_size(axis)
    return lax.ppermute(array, axis, [(i, (i + step) % devices) for i in range(devices)])


def cosine_coefficients():
    samples = 2.0 + 2.0 * np.cos(np.pi * (np.arange(64) + 0.5) / 64)
    values = np.cos(np.pi / 4 * np.sqrt(samples)) * np.sqrt(0.5)
    fit = np.polynomial.chebyshev.Chebyshev.fit(samples, values, 4, domain=[0, 4])
    return [float(v) for v in fit.convert(kind=np.polynomial.Polynomial).coef]


COSINE = cosine_coefficients()


def weight(offset):
    square = jnp.minimum(offset * offset, 4.0)
    value = COSINE[-1] * square + COSINE[-2]
    for coefficient in COSINE[-3::-1]:
        value = value * square + coefficient
    return value * value


def split(value):
    high = value.astype(jnp.bfloat16)
    low = (value - high.astype(jnp.float32)).astype(jnp.bfloat16)
    return high, low


def row_weights(count, position):
    cells = lax.broadcasted_iota(jnp.int32, (count, position.shape[1]), 0)
    return weight(cells.astype(jnp.float32) - position)


def plane_weights(weight_x, weight_z, half_z, high, low):
    count = 0
    for z in range(0, weight_z.shape[0], half_z):
        part = weight_z[z : z + half_z]
        for x in range(weight_x.shape[0]):
            rows = slice(count * half_z, (count + 1) * half_z)
            high[rows], low[rows] = split(weight_x[x : x + 1] * part)
            count += 1


def window_start(first_y, size_y):
    return pl.multiple_of(jnp.minimum((first_y // 8) * 8, size_y - WINDOW), 8)


def quarters(sizes):
    half_x, half_z = sizes[0] // 2, sizes[1] // 2
    for z in range(2):
        for x in range(2):
            yield slice(x * half_x, (x + 1) * half_x), slice(z * half_z, (z + 1) * half_z)


class Layout:
    def __init__(self, sizes, slots, markers):
        self.sizes, self.slots, self.markers = sizes, slots, markers
        self.tiles = markers // LANES
        self.fact_row = 3 * self.tiles * slots
        self.rows = self.fact_row + slots
        self.ghost_x = 4 * sizes[1]
        self.ghost_z = 4 * sizes[0]
        self.plane = sizes[0] * sizes[1]


def marker_row(layout, marks, base, direction, slot):
    first = base + direction * layout.tiles * layout.slots + slot
    rows = [marks[pl.ds(first + t * layout.slots, 1), :] for t in range(layout.tiles)]
    return jnp.concatenate(rows, axis=1)


def slot_visits(layout, facts, marks, blocks, step_z, high, low, visit, skip):
    size_x, size_z, size_y = layout.sizes
    half_x, half_z = size_x // 2, size_z // 2
    slots = layout.slots

    def body(index, carry):
        block, slot = index // slots, index % slots
        block = blocks[0] + block * (blocks[1] - blocks[0] if len(blocks) > 1 else 0)
        fact = (step_z + 1) * 3 * slots + block * slots + slot
        first_x = facts[0, fact] + (block - 1) * size_x
        first_z = facts[1, fact] + step_z * size_z
        first_y = facts[2, fact]
        meets_x = (first_x > -BOX) & (first_x < size_x)
        meets_z = (first_z > -BOX) & (first_z < size_z)
        active = (facts[3, fact] != 0) & meets_x & meets_z
        whole_x = (first_x > half_x - BOX) & (first_x < half_x)
        whole_z = (first_z > half_z - BOX) & (first_z < half_z)
        upper_x = (first_x >= half_x).astype(jnp.int32)
        upper_z = (first_z >= half_z).astype(jnp.int32)

        def part(all_x, all_z):
            start_x = 0 if all_x else upper_x * half_x
            start_z = 0 if all_z else upper_z * half_z
            lanes = [
                ((0 if all_z else upper_z) + z) * 2 * LANES + (0 if all_x else upper_x) * LANES
                for z in range(2 if all_z else 1)
            ]
            width = (2 if all_x else 1) * LANES
            if all_x and all_z:
                pieces = [(0, 4 * LANES)]
            else:
                pieces = [(pl.multiple_of(lane, LANES), width) for lane in lanes]
            base = layout.ghost_z + block * layout.rows
            first = window_start(first_y, size_y)
            move = (first_x - start_x).astype(jnp.float32)
            position = marker_row(layout, marks, base, 0, slot) + move
            weight_x = row_weights(size_x if all_x else half_x, position)
            move = (first_z - start_z).astype(jnp.float32)
            position = marker_row(layout, marks, base, 1, slot) + move
            weight_z = row_weights(size_z if all_z else half_z, position)
            plane_weights(weight_x, weight_z, half_z, high, low)
            move = (first_y - first).astype(jnp.float32)
            position = marker_row(layout, marks, base, 2, slot) + move
            weight_y = row_weights(WINDOW, position)
            visit(index, block * slots + slot, first, weight_y, pieces)

        for all_x in (True, False):
            for all_z in (True, False):
                one = whole_x if all_x else jnp.logical_not(whole_x)
                two = whole_z if all_z else jnp.logical_not(whole_z)
                pl.when(active & one & two)(functools.partial(part, all_x, all_z))

        if skip is not None:

            @pl.when(jnp.logical_not(active))
            def _():
                skip(index)

        return carry

    lax.fori_loop(0, len(blocks) * slots, body, 0)


def sample_kernel(layout, blocks, step_z, facts, marks, field, out, high, low):
    def visit(index, _, first, weight_y, pieces):
        rows = pl.ds(first, WINDOW)
        parts = [
            jnp.concatenate([field[c, rows, pl.ds(lane, width)] for c in range(3)], axis=0)
            for lane, width in pieces
        ]
        window = jnp.concatenate(parts, axis=1)
        count = window.shape[1]
        window_high, window_low = split(window)
        both = jnp.concatenate([window_high, window_low], axis=0)
        value = jnp.dot(both, high[:count], preferred_element_type=jnp.float32)
        rest = jnp.dot(window_high, low[:count], preferred_element_type=jnp.float32)
        value = value[: 3 * WINDOW] + value[3 * WINDOW :] + rest
        for c in range(3):
            part = value[c * WINDOW : (c + 1) * WINDOW] * weight_y
            out[c, pl.ds(index, 1), :] = jnp.sum(part, axis=0, keepdims=True)

    def skip(index):
        for c in range(3):
            out[c, pl.ds(index, 1), :] = jnp.zeros((1, layout.markers), jnp.float32)

    slot_visits(layout, facts, marks, blocks, step_z, high, low, visit, skip)


def visit_cost(layout, blocks):
    return len(blocks) * layout.slots * 18 * WINDOW * layout.plane * layout.markers


def weight_scratch(layout):
    return [pltpu.VMEM((layout.plane, layout.markers), jnp.bfloat16)] * 2


def sample(layout, blocks, step_z, facts, marks, field, name):
    return call(
        functools.partial(sample_kernel, layout, blocks, step_z),
        float32(3, len(blocks) * layout.slots, layout.markers),
        [facts],
        [marks, field],
        weight_scratch(layout),
        name,
        visit_cost(layout, blocks),
        4 * (field.size + marks.size),
    )


def spread_slots(layout, blocks, step_z, facts, marks, push, own_rows, total, high, low):
    def visit(index, row, first, weight_y, pieces):
        slot = index if own_rows else row
        count = sum(width for _, width in pieces)
        value = jnp.concatenate(
            [weight_y * push[c, pl.ds(slot, 1), :] for c in range(3)], axis=0
        )
        value_high, value_low = split(value)
        both = jnp.concatenate([value_high, value_low], axis=0)
        added = lax.dot_general(
            both, high[:count], TRANSPOSED, preferred_element_type=jnp.float32
        )
        rest = lax.dot_general(
            value_high, low[:count], TRANSPOSED, preferred_element_type=jnp.float32
        )
        added = added[: 3 * WINDOW] + added[3 * WINDOW :] + rest
        column = 0
        for lane, width in pieces:
            for c in range(3):
                part = added[c * WINDOW : (c + 1) * WINDOW, column : column + width]
                total[c, pl.ds(first, WINDOW), pl.ds(lane, width)] += part
            column += width

    slot_visits(layout, facts, marks, blocks, step_z, high, low, visit, None)


def spread_own_kernel(layout, facts, marks, push, total, high, low):
    total[...] = jnp.zeros(total.shape, jnp.float32)
    spread_slots(layout, (1,), 0, facts, marks, push, True, total, high, low)


def spread_own(layout, facts, marks, push):
    return call(
        functools.partial(spread_own_kernel, layout),
        float32(3, layout.sizes[2], layout.plane),
        [facts],
        [marks, push],
        weight_scratch(layout),
        "spread_own",
        visit_cost(layout, (1,)),
        12 * layout.sizes[2] * layout.plane,
    )


def spread_side_kernel(layout, facts, marks, push, before, total, high, low):
    total[...] = before[...]
    spread_slots(layout, (0, 2), 0, facts, marks, push, False, total, high, low)


def spread_side(layout, facts, marks, push, before):
    return call(
        functools.partial(spread_side_kernel, layout),
        float32(*before.shape),
        [facts],
        [marks, push, before],
        weight_scratch(layout),
        "spread_side",
        visit_cost(layout, (0, 2)),
        8 * before.size,
    )


def spread_rest_kernel(
    layout,
    facts,
    lower_marks,
    upper_marks,
    lower_push,
    upper_push,
    before,
    predicted,
    velocity,
    u_first,
    u_last,
    w_first,
    w_last,
    inner,
    total,
    high,
    low,
):
    size_x, size_z, size_y = layout.sizes
    total[...] = before[...]
    row = (0, 1, 2)
    spread_slots(layout, row, -1, facts, lower_marks, lower_push, False, total, high, low)
    spread_slots(layout, row, 1, facts, upper_marks, upper_push, False, total, high, low)
    for c in range(3):
        for q, (xs, zs) in enumerate(quarters(layout.sizes)):
            part = jnp.transpose(total[c, :, q * LANES : (q + 1) * LANES])
            part = part.reshape(size_x // 2, size_z // 2, size_y)
            velocity[c, xs, zs] = predicted[c, xs, zs] + part
    u_first[...] = velocity[0, 0]
    u_last[...] = velocity[0, size_x - 1]
    for x in range(size_x):
        w_first[x : x + 1] = velocity[2, x, 0:1]
        w_last[x : x + 1] = velocity[2, x, size_z - 1 : size_z]
    row = lax.broadcasted_iota(jnp.int32, (size_z, size_y), 0)
    lane = lax.broadcasted_iota(jnp.int32, (size_z, size_y), 1)
    for x in range(size_x):
        y_minus, y_plus = y_neighbours(velocity[1, x], lane, 0.0, 0.0)
        z_minus, z_plus = z_neighbours(velocity[2, x], row, 0.0, 0.0)
        change = y_plus - y_minus + z_plus - z_minus
        if x > 0:
            change -= velocity[0, x - 1]
        if x < size_x - 1:
            change += velocity[0, x + 1]
        inner[x] = change * 0.5


def spread_rest(layout, facts, marks, pushes, before, predicted):
    size_x, size_z, size_y = layout.sizes
    return call(
        functools.partial(spread_rest_kernel, layout),
        [float32(3, size_x, size_z, size_y)]
        + [float32(size_z, size_y)] * 2
        + [float32(size_x, size_y)] * 2
        + [float32(size_x, size_z, size_y)],
        [facts],
        [*marks, *pushes, before, predicted],
        [pltpu.VMEM(before.shape, jnp.float32)] + weight_scratch(layout),
        "spread_rest",
        2 * visit_cost(layout, (0, 1, 2)),
        12 * before.size,
    )


def pack_x_kernel(
    layout,
    slot_ids_hbm,
    corners_hbm,
    flow,
    cells_hbm,
    fraction_hbm,
    own,
    to_right,
    to_left,
    slot_ids,
    corners,
    cells,
    fraction,
    done,
):
    size_x, size_z, size_y = layout.sizes
    slots = layout.slots
    moves = [
        (slot_ids_hbm, slot_ids),
        (corners_hbm, corners),
        (cells_hbm, cells),
        (fraction_hbm, fraction),
    ]
    for c in range(4):
        rows = pl.ds(c * size_z, size_z)
        moves.append((flow.at[c, size_x - 1], to_right.at[rows]))
        moves.append((flow.at[c, 0], to_left.at[rows]))
    copies = [pltpu.make_async_copy(a, b, done.at[i]) for i, (a, b) in enumerate(moves)]
    for copy in copies:
        copy.start()
    for copy in copies[:4]:
        copy.wait()
    length_x = size_x * lax.axis_size("gx")
    length_z = size_z * lax.axis_size("gz")
    offset_x = length_x + HALF - lax.axis_index("gx") * size_x
    offset_z = length_z + HALF - lax.axis_index("gz") * size_z
    targets = ((own, 0), (to_right, layout.ghost_x), (to_left, layout.ghost_x))
    for a, direction in enumerate((0, 2, 1)):
        for t in range(layout.tiles):
            lanes = slice(t * LANES, (t + 1) * LANES)
            place = cells[direction, :, lanes].astype(jnp.float32) + fraction[direction, :, lanes]
            for target, base in targets:
                first = base + (a * layout.tiles + t) * slots
                target[first : first + slots] = place
    lane = lax.broadcasted_iota(jnp.int32, (1, LANES), 1)
    for slot in range(slots):
        first_x = lax.rem(corners[0, slot] + offset_x, length_x) - HALF
        first_z = lax.rem(corners[2, slot] + offset_z, length_z) - HALF
        held = (slot_ids[slot] >= 0).astype(jnp.int32)
        fact = jnp.where(lane == 0, first_x, held)
        fact = jnp.where(lane == 1, first_z, fact)
        fact = jnp.where(lane == 2, corners[1, slot], fact)
        for target, base in targets:
            row = base + layout.fact_row + slot
            target[row : row + 1] = fact.astype(jnp.float32)
    for copy in copies[4:]:
        copy.wait()


def pack_x(layout, slot_ids, corners, flow, cells, fraction):
    rows = layout.ghost_x + layout.rows
    in_hbm = pl.BlockSpec(memory_space=pltpu.HBM)
    return pl.pallas_call(
        functools.partial(pack_x_kernel, layout),
        out_shape=[float32(layout.rows, LANES)] + [float32(rows, LANES)] * 2,
        in_specs=[in_hbm] * 5,
        out_specs=[IN_VMEM] * 3,
        scratch_shapes=[
            pltpu.SMEM(slot_ids.shape, jnp.int32),
            pltpu.SMEM(corners.shape, jnp.int32),
            pltpu.VMEM(cells.shape, jnp.int32),
            pltpu.VMEM(fraction.shape, jnp.float32),
            pltpu.SemaphoreType.DMA((12,)),
        ],
        name="pack_x",
        cost_estimate=pl.CostEstimate(
            flops=flow.size, bytes_accessed=8 * rows * LANES, transcendentals=0
        ),
    )(slot_ids, corners, flow, cells, fraction)


def pack_z_kernel(layout, flow, own, left, right, to_upper, to_lower):
    size_x, size_z, size_y = layout.sizes
    for c in range(4):
        for x in range(size_x):
            row = c * size_x + x
            to_upper[row : row + 1] = flow[c, x, size_z - 1 : size_z]
            to_lower[row : row + 1] = flow[c, x, 0:1]
    tiles = (left[layout.ghost_x :], own[...], right[layout.ghost_x :])
    for block, tile in enumerate(tiles):
        first = layout.ghost_z + block * layout.rows
        to_upper[first : first + layout.rows] = tile
        to_lower[first : first + layout.rows] = tile


def pack_z(layout, flow, own, left, right):
    rows = layout.ghost_z + 3 * layout.rows
    return call(
        functools.partial(pack_z_kernel, layout),
        [float32(rows, LANES)] * 2,
        [],
        [flow, own, left, right],
        [],
        "pack_z",
        flow.size,
        8 * rows * LANES,
    )


def y_neighbours(value, lane, below, above):
    size_y = value.shape[-1]
    minus = jnp.where(lane == 0, below, pltpu.roll(value, 1, 1))
    plus = jnp.where(lane == size_y - 1, above, pltpu.roll(value, size_y - 1, 1))
    return minus, plus


def z_neighbours(value, row, below, above):
    size_z = value.shape[0]
    minus = jnp.where(row == 0, below, pltpu.roll(value, 1, 0))
    plus = jnp.where(row == size_z - 1, above, pltpu.roll(value, size_z - 1, 0))
    return minus, plus


def predict_inner_kernel(sizes, flow, left, right, predicted):
    size_x, size_z, size_y = sizes
    row = lax.broadcasted_iota(jnp.int32, (size_z, size_y), 0)
    lane = lax.broadcasted_iota(jnp.int32, (size_z, size_y), 1)

    def around(c, x):
        value = flow[c, x]
        ghost = slice(c * size_z, (c + 1) * size_z)
        x_minus = flow[c, x - 1] if x > 0 else left[ghost]
        x_plus = flow[c, x + 1] if x < size_x - 1 else right[ghost]
        z_minus, z_plus = z_neighbours(value, row, 0.0, 0.0)
        edges = (0.0, 0.0) if c < 3 else (value, value)
        y_minus, y_plus = y_neighbours(value, lane, *edges)
        return value, x_minus, x_plus, z_minus, z_plus, y_minus, y_plus

    for x in range(size_x):
        _, x_minus, x_plus, z_minus, z_plus, y_minus, y_plus = around(3, x)
        gradient = (
            (x_plus - x_minus) * 0.5 - drive_force,
            (y_plus - y_minus) * 0.5,
            (z_plus - z_minus) * 0.5,
        )
        carried = (flow[0, x], flow[1, x], flow[2, x])
        for c in range(3):
            value, x_minus, x_plus, z_minus, z_plus, y_minus, y_plus = around(c, x)
            laplace = x_plus + x_minus + z_plus + z_minus + y_plus + y_minus - 6.0 * value
            advect = (
                carried[0] * (x_plus - x_minus)
                + carried[1] * (y_plus - y_minus)
                + carried[2] * (z_plus - z_minus)
            ) * 0.5
            predicted[c, x] = value + time_step * (viscosity * laplace - advect - gradient[c])


def predict_inner(sizes, flow, left, right):
    return call(
        functools.partial(predict_inner_kernel, sizes),
        float32(3, *sizes),
        [],
        [flow, left, right],
        [],
        "predict_inner",
        200 * flow.size,
        8 * flow.size,
    )


def predict_outer_kernel(
    layout, flow, inner, lower, own, upper, predicted, field, facts, table
):
    size_x, size_z, size_y = layout.sizes
    row = lax.broadcasted_iota(jnp.int32, (8, size_y), 0)
    for block in range(9):
        payload = (lower, own, upper)[block // 3]
        first = layout.ghost_z + (block % 3) * layout.rows + layout.fact_row
        out = slice(block * layout.slots, (block + 1) * layout.slots)
        table[out] = payload[first : first + layout.slots]
    facts[...] = jnp.transpose(table[...])[:8].astype(jnp.int32)
    for x in range(size_x):
        carried_low = flow[2, x, 0:1]
        carried_high = flow[2, x, size_z - 1 : size_z]
        for c in range(3):
            ghost = c * size_x + x
            below, above = lower[ghost : ghost + 1], upper[ghost : ghost + 1]
            change_low = (viscosity + 0.5 * carried_low) * below
            change_high = (viscosity - 0.5 * carried_high) * above
            if c == 2:
                ghost = 3 * size_x + x
                change_low += 0.5 * lower[ghost : ghost + 1]
                change_high -= 0.5 * upper[ghost : ghost + 1]
            predicted[c, x] = inner[c, x]
            first = inner[c, x, 0:8]
            predicted[c, x, 0:8] = first + jnp.where(row == 0, time_step * change_low, 0.0)
            last = inner[c, x, size_z - 8 : size_z]
            predicted[c, x, size_z - 8 : size_z] = last + jnp.where(
                row == 7, time_step * change_high, 0.0
            )
    for c in range(3):
        for q, (xs, zs) in enumerate(quarters(layout.sizes)):
            part = predicted[c, xs, zs].reshape(LANES, size_y)
            field[c, :, q * LANES : (q + 1) * LANES] = jnp.transpose(part)


def predict_outer(layout, flow, inner, lower, own, upper):
    size_x, size_z, size_y = layout.sizes
    return call(
        functools.partial(predict_outer_kernel, layout),
        [
            float32(3, *layout.sizes),
            float32(3, size_y, layout.plane),
            jax.ShapeDtypeStruct((8, LANES), jnp.int32),
        ],
        [],
        [flow, inner, lower, own, upper],
        [pltpu.VMEM((LANES, LANES), jnp.float32)],
        "predict_outer",
        10 * flow.size,
        12 * flow.size,
    )


def divergence_kernel(sizes, parts, inner, u_below, u_above, w_below, w_above, *rest):
    outs, whole = rest[:parts], rest[parts]
    size_x, size_z, size_y = sizes
    row = lax.broadcasted_iota(jnp.int32, (size_z, size_y), 0)
    group = LANES // size_z
    for q in range(size_x // group):
        pieces = []
        for x in range(q * group, (q + 1) * group):
            piece = inner[x]
            if x == 0:
                piece -= 0.5 * u_below[...]
            if x == size_x - 1:
                piece += 0.5 * u_above[...]
            piece -= jnp.where(row == 0, 0.5 * w_below[x : x + 1], 0.0)
            piece += jnp.where(row == size_z - 1, 0.5 * w_above[x : x + 1], 0.0)
            pieces.append(piece)
        part = jnp.concatenate(pieces, axis=0)
        whole[:, q * LANES : (q + 1) * LANES] = jnp.transpose(part)
    height = size_y // parts
    for step in range(parts):
        first = pl.multiple_of(lax.rem(lax.axis_index("gz") + step, parts) * height, 8)
        outs[step][...] = whole[pl.ds(first, height), :]


def divergence(sizes, parts, inner, ghosts):
    size_x, size_z, size_y = sizes
    plane = size_x * size_z
    return call(
        functools.partial(divergence_kernel, sizes, parts),
        [float32(size_y // parts, plane)] * parts,
        [],
        [inner, *ghosts],
        [pltpu.VMEM((size_y, plane), jnp.float32)],
        "divergence",
        10 * inner.size,
        8 * inner.size,
    )


def swap_groups(values, width):
    count = LANES // width
    lane = lax.broadcasted_iota(jnp.int32, values[0].shape, 1)
    values = list(values)
    step = count // 2
    while step:
        reach = step * width
        keep = lane % (2 * reach) < reach
        for i in range(count):
            if i & step == 0:
                a, b = values[i], values[i + step]
                values[i] = jnp.where(keep, a, pltpu.roll(b, reach, 1))
                values[i + step] = jnp.where(keep, pltpu.roll(a, LANES - reach, 1), b)
        step //= 2
    return values


def transform_z_kernel(sizes, counts, table_high, table_low, *refs):
    size_x, size_z, size_y = sizes
    parts_x, parts_z = counts
    pieces, refs = refs[:parts_z], refs[parts_z:]
    outs, (gathered, turned, whole) = refs[:parts_x], refs[parts_x:]
    height = size_y // parts_z
    group = LANES // size_z
    for step in range(parts_z):
        gathered[lax.rem(lax.axis_index("gz") + parts_z - step, parts_z)] = pieces[step][...]
    for block in range(parts_z // group):
        for q in range(size_x // group):
            lanes = slice(q * LANES, (q + 1) * LANES)
            values = [gathered[block * group + i, :, lanes] for i in range(group)]
            for j, value in enumerate(swap_groups(values, size_z)):
                turned[block, pl.ds(q * group + j, height, stride=size_x), :] = value
    lines = jnp.concatenate([turned[b] for b in range(turned.shape[0])], axis=1)
    high, low = split(lines)
    result = lax.dot_general(
        table_high[...], high, TRANSPOSED, preferred_element_type=jnp.float32
    )
    result += lax.dot_general(
        table_low[...], high, TRANSPOSED, preferred_element_type=jnp.float32
    )
    result += lax.dot_general(
        table_high[...], low, TRANSPOSED, preferred_element_type=jnp.float32
    )
    whole[...] = result
    rows = whole.shape[0] // parts_x
    for step in range(parts_x):
        first = pl.multiple_of(lax.rem(lax.axis_index("gx") + step, parts_x) * rows, 8)
        outs[step][...] = whole[pl.ds(first, rows), :]


def transform_z(sizes, counts, table, pieces):
    size_x, size_z, size_y = sizes
    parts_x, parts_z = counts
    length_z = size_z * parts_z
    height = size_y // parts_z
    columns = height * size_x
    return call(
        functools.partial(transform_z_kernel, sizes, counts),
        [float32(2 * length_z // parts_x, columns)] * parts_x,
        [],
        [*table, *pieces],
        [
            pltpu.VMEM((parts_z, height, size_x * size_z), jnp.float32),
            pltpu.VMEM((length_z // LANES, columns, LANES), jnp.float32),
            pltpu.VMEM((2 * length_z, columns), jnp.float32),
        ],
        "transform_z",
        12 * length_z * length_z * columns,
        12 * length_z * columns,
    )


def transform_x_kernel(sizes, counts, table_high, table_low, *refs):
    size_x, size_z, size_y = sizes
    parts_x, parts_z = counts
    pieces, (source, gathered, turned) = refs[:parts_x], refs[parts_x:]
    length_x = size_x * parts_x
    modes = size_z * parts_z // parts_x
    height = size_y // parts_z
    group = LANES // size_x
    for step in range(parts_x):
        gathered[lax.rem(lax.axis_index("gx") + parts_x - step, parts_x)] = pieces[step][...]
    for block in range(parts_x // group):
        for q in range(height // group):
            lanes = slice(q * LANES, (q + 1) * LANES)
            values = [gathered[block * group + i, :, lanes] for i in range(group)]
            for j, value in enumerate(swap_groups(values, size_x)):
                first = (q * group + j) * modes
                for c in range(2):
                    column = c * length_x + block * LANES
                    turned[first : first + modes, column : column + LANES] = value[
                        c * modes : (c + 1) * modes
                    ]
    high, low = split(turned[...])
    result = jnp.dot(high, table_high[...], preferred_element_type=jnp.float32)
    result += jnp.dot(low, table_high[...], preferred_element_type=jnp.float32)
    result += jnp.dot(high, table_low[...], preferred_element_type=jnp.float32)
    source[0] = result[:, :length_x].reshape(height, modes, length_x)
    source[1] = result[:, length_x:].reshape(height, modes, length_x)


def transform_x(sizes, counts, table, pieces):
    size_x, size_z, size_y = sizes
    parts_x, parts_z = counts
    length_x = size_x * parts_x
    modes = size_z * parts_z // parts_x
    height = size_y // parts_z
    return call(
        functools.partial(transform_x_kernel, sizes, counts),
        float32(2, height, modes, length_x),
        [],
        [*table, *pieces],
        [
            pltpu.VMEM((parts_x, *pieces[0].shape), jnp.float32),
            pltpu.VMEM((height * modes, 2 * length_x), jnp.float32),
        ],
        "transform_x",
        24 * length_x * length_x * height * modes,
        24 * length_x * height * modes,
    )


def split_table(table):
    high = table.astype(np.float32).astype(jnp.bfloat16)
    low = (table - high.astype(np.float64)).astype(np.float32).astype(jnp.bfloat16)
    return jnp.asarray(high), jnp.asarray(low)


def angles(length):
    counter = np.arange(length)
    turn = (counter[:, None] * counter[None, :] % length) * (2.0 * np.pi / length)
    return np.cos(turn), np.sin(turn)


def table_z(length, blocks):
    cosine, sine = angles(length)
    modes = length // blocks
    table = np.stack([cosine, -sine]).reshape(2, blocks, modes, length)
    return split_table(table.transpose(1, 0, 2, 3).reshape(2 * length, length))


def table_x(length, scale):
    cosine, sine = angles(length)
    return split_table(np.block([[cosine, -sine], [sine, cosine]]) * scale)


def exchange(pieces, axis):
    return [pieces[0]] + [shift(pieces[d], axis, d) for d in range(1, len(pieces))]


def on_device(
    flow_state, slot_ids, corners, marker_cells, marker_frac, particle_velocity, particle_spin
):
    sizes = flow_state.shape[1:]
    size_x, size_z, size_y = sizes
    counts = (lax.axis_size("gx"), lax.axis_size("gz"))
    length_x, length_z = (size_x * counts[0], size_z * counts[1])
    slots, markers = marker_cells.shape[1:]
    layout = Layout(sizes, slots, markers)

    own, to_right, to_left = pack_x(
        layout, slot_ids, corners, flow_state, marker_cells, marker_frac
    )
    left = shift(to_right, "gx", 1)
    right = shift(to_left, "gx", -1)
    row, to_lower = pack_z(layout, flow_state, own, left, right)
    lower = shift(row, "gz", 1)
    upper = shift(to_lower, "gz", -1)
    inner = predict_inner(sizes, flow_state, left, right)
    predicted, field, facts = predict_outer(layout, flow_state, inner, lower, row, upper)

    positions = marker_cells.astype(jnp.float32) + marker_frac
    chosen = slot_ids[:, None] == jnp.arange(particle_velocity.shape[1], dtype=jnp.int32)[None, :]
    moving = jnp.sum(jnp.where(chosen[None], particle_velocity[:, None, :], 0.0), axis=2)
    turning = jnp.sum(jnp.where(chosen[None], particle_spin[:, None, :], 0.0), axis=2)
    lever = positions - HALF
    moving, turning = (moving[:, :, None], turning[:, :, None])
    target = moving + jnp.stack(
        [
            turning[1] * lever[2] - turning[2] * lever[1],
            turning[2] * lever[0] - turning[0] * lever[2],
            turning[0] * lever[1] - turning[1] * lever[0],
        ]
    )
    living = (slot_ids >= 0).astype(jnp.float32)[None, :, None]

    tiles = (0, 1, 2)
    lower_part = sample(layout, tiles, -1, facts, lower, field, "sample_lower")
    from_upper = shift(lower_part, "gz", -1)
    upper_part = sample(layout, tiles, 1, facts, upper, field, "sample_upper")
    from_lower = shift(upper_part, "gz", 1)
    side_part = sample(layout, (0, 2), 0, facts, row, field, "sample_side")
    from_z = from_upper + from_lower
    from_right = shift(side_part[:, :slots] + from_z[:, :slots], "gx", -1)
    from_left = shift(side_part[:, slots:] + from_z[:, 2 * slots :], "gx", 1)
    own_part = sample(layout, (1,), 0, facts, row, field, "sample_own")
    sampled = own_part + from_z[:, slots : 2 * slots] + from_right + from_left
    push = living * (target - sampled)

    left_push = shift(push, "gx", 1)
    right_push = shift(push, "gx", -1)
    row_push = jnp.concatenate([left_push, push, right_push], axis=1)
    lower_push = shift(row_push, "gz", 1)
    upper_push = shift(row_push, "gz", -1)
    forcing = spread_own(layout, facts, row, push)
    forcing = spread_side(layout, facts, row, row_push, forcing)
    velocity, u_first, u_last, w_first, w_last, change = spread_rest(
        layout, facts, (lower, upper), (lower_push, upper_push), forcing, predicted
    )

    ghosts = (
        shift(u_last, "gx", 1),
        shift(u_first, "gx", -1),
        shift(w_last, "gz", 1),
        shift(w_first, "gz", -1),
    )
    pieces = divergence(sizes, counts[1], change, ghosts)
    pieces = exchange(pieces, "gz")
    pieces = transform_z(sizes, counts, table_z(length_z, counts[0]), pieces)
    pieces = exchange(pieces, "gx")
    scale = 1.0 / math.sqrt(length_x * length_z)
    source = transform_x(sizes, counts, table_x(length_x, scale), pieces)
    return velocity, source


def solution(mesh):
    return jax.shard_map(
        on_device,
        mesh=mesh,
        in_specs=(
            P(None, "gx", "gz", None),
            P(("gx", "gz")),
            P(None, ("gx", "gz")),
            P(None, ("gx", "gz"), None),
            P(None, ("gx", "gz"), None),
            P(),
            P(),
        ),
        out_specs=(P(None, "gx", "gz", None), P(None, "gz", "gx", None)),
        check_vma=False,
    )
```

```python
import functools
import math

import jax
import jax.numpy as jnp
import numpy as np
from jax import lax
from jax.experimental import pallas as pl
from jax.experimental.pallas import tpu as pltpu
from jax.sharding import PartitionSpec as P

BOX = 24
HALF = 12
WINDOW = 32
LANES = 128
KERNEL_BYTES = 16 * 1024 * 1024

time_step = 0.1
viscosity = 0.2
drive_force = 1.0


IN_VMEM = pl.BlockSpec(memory_space=pltpu.VMEM)
IN_SMEM = pl.BlockSpec(memory_space=pltpu.SMEM)
TRANSPOSED = (((1,), (1,)), ((), ()))


def float32(*shape):
    return jax.ShapeDtypeStruct(shape, jnp.float32)


def call(kernel, out_shape, scalars, arrays, scratch, name, flops, moved):
    outputs = len(out_shape) if isinstance(out_shape, (list, tuple)) else 0
    return pl.pallas_call(
        kernel,
        out_shape=out_shape,
        in_specs=[IN_SMEM] * len(scalars) + [IN_VMEM] * len(arrays),
        out_specs=[IN_VMEM] * outputs if outputs else IN_VMEM,
        scratch_shapes=scratch,
        name=name,
        compiler_params=pltpu.CompilerParams(vmem_limit_bytes=KERNEL_BYTES),
        cost_estimate=pl.CostEstimate(flops=flops, bytes_accessed=moved, transcendentals=0),
    )(*scalars, *arrays)


def shift(array, axis, step):
    devices = lax.axis_size(axis)
    return lax.ppermute(array, axis, [(i, (i + step) % devices) for i in range(devices)])


def cosine_coefficients():
    samples = 2.0 + 2.0 * np.cos(np.pi * (np.arange(64) + 0.5) / 64)
    values = np.cos(np.pi / 4 * np.sqrt(samples)) * np.sqrt(0.5)
    fit = np.polynomial.chebyshev.Chebyshev.fit(samples, values, 4, domain=[0, 4])
    return [float(v) for v in fit.convert(kind=np.polynomial.Polynomial).coef]


COSINE = cosine_coefficients()


def weight(offset):
    square = jnp.minimum(offset * offset, 4.0)
    value = COSINE[-1] * square + COSINE[-2]
    for coefficient in COSINE[-3::-1]:
        value = value * square + coefficient
    return value * value


def split(value):
    high = value.astype(jnp.bfloat16)
    low = (value - high.astype(jnp.float32)).astype(jnp.bfloat16)
    return high, low


def row_weights(count, position):
    cells = lax.broadcasted_iota(jnp.int32, (count, position.shape[1]), 0)
    return weight(cells.astype(jnp.float32) - position)


def plane_weights(weight_x, weight_z, half_z, high, low):
    count = 0
    for z in range(0, weight_z.shape[0], half_z):
        part = weight_z[z : z + half_z]
        for x in range(weight_x.shape[0]):
            rows = slice(count * half_z, (count + 1) * half_z)
            high[rows], low[rows] = split(weight_x[x : x + 1] * part)
            count += 1


def window_start(first_y, size_y):
    return pl.multiple_of(jnp.minimum((first_y // 8) * 8, size_y - WINDOW), 8)


def quarters(sizes):
    half_x, half_z = sizes[0] // 2, sizes[1] // 2
    for z in range(2):
        for x in range(2):
            yield slice(x * half_x, (x + 1) * half_x), slice(z * half_z, (z + 1) * half_z)


class Layout:
    def __init__(self, sizes, slots, markers):
        self.sizes, self.slots, self.markers = sizes, slots, markers
        self.tiles = markers // LANES
        self.fact_row = 3 * self.tiles * slots
        self.rows = self.fact_row + slots
        self.ghost_x = 4 * sizes[1]
        self.ghost_z = 4 * sizes[0]
        self.plane = sizes[0] * sizes[1]


def marker_row(layout, marks, base, direction, slot):
    first = base + direction * layout.tiles * layout.slots + slot
    rows = [marks[pl.ds(first + t * layout.slots, 1), :] for t in range(layout.tiles)]
    return jnp.concatenate(rows, axis=1)


def slot_visits(layout, facts, marks, saved, blocks, step_z, high, low, visit, skip):
    size_x, size_z, size_y = layout.sizes
    half_x, half_z = size_x // 2, size_z // 2
    slots = layout.slots

    def body(index, carry):
        block, slot = index // slots, index % slots
        block = blocks[0] + block * (blocks[1] - blocks[0] if len(blocks) > 1 else 0)
        fact = (step_z + 1) * 3 * slots + block * slots + slot
        first_x = facts[0, fact] + (block - 1) * size_x
        first_z = facts[1, fact] + step_z * size_z
        first_y = facts[2, fact]
        meets_x = (first_x > -BOX) & (first_x < size_x)
        meets_z = (first_z > -BOX) & (first_z < size_z)
        active = (facts[3, fact] != 0) & meets_x & meets_z
        whole_x = (first_x > half_x - BOX) & (first_x < half_x)
        whole_z = (first_z > half_z - BOX) & (first_z < half_z)
        upper_x = (first_x >= half_x).astype(jnp.int32)
        upper_z = (first_z >= half_z).astype(jnp.int32)

        def part(all_x, all_z):
            start_x = 0 if all_x else upper_x * half_x
            start_z = 0 if all_z else upper_z * half_z
            lanes = [
                ((0 if all_z else upper_z) + z) * 2 * LANES + (0 if all_x else upper_x) * LANES
                for z in range(2 if all_z else 1)
            ]
            width = (2 if all_x else 1) * LANES
            if all_x and all_z:
                pieces = [(0, 4 * LANES)]
            else:
                pieces = [(pl.multiple_of(lane, LANES), width) for lane in lanes]
            first = window_start(first_y, size_y)
            rows_x = slice(0, size_x if all_x else half_x)
            rows_z = slice(size_x, size_x + (size_z if all_z else half_z))
            rows_y = slice(size_x + size_z, size_x + size_z + WINDOW)
            if marks is not None:
                base = layout.ghost_z + block * layout.rows
                starts = (first_x - start_x, first_z - start_z, first_y - first)
                for direction, rows in enumerate((rows_x, rows_z, rows_y)):
                    position = marker_row(layout, marks, base, direction, slot)
                    position += starts[direction].astype(jnp.float32)
                    saved[index, rows, :] = row_weights(rows.stop - rows.start, position)
            plane_weights(saved[index, rows_x, :], saved[index, rows_z, :], half_z, high, low)
            weight_y = saved[index, rows_y, :]
            visit(index, block * slots + slot, first, weight_y, pieces)

        for all_x in (True, False):
            for all_z in (True, False):
                one = whole_x if all_x else jnp.logical_not(whole_x)
                two = whole_z if all_z else jnp.logical_not(whole_z)
                pl.when(active & one & two)(functools.partial(part, all_x, all_z))

        if skip is not None:

            @pl.when(jnp.logical_not(active))
            def _():
                skip(index)

        return carry

    lax.fori_loop(0, len(blocks) * slots, body, 0)


def sample_slots(
    layout, facts, marks, field_high, field_low, out, saved, blocks, step_z, high, low
):
    def visit(index, _, first, weight_y, pieces):
        rows = pl.ds(first, WINDOW)

        def window(field):
            parts = [
                jnp.concatenate([field[c, rows, pl.ds(lane, width)] for c in range(3)], axis=0)
                for lane, width in pieces
            ]
            return jnp.concatenate(parts, axis=1).astype(jnp.bfloat16)

        window_high, window_low = window(field_high), window(field_low)
        count = window_high.shape[1]
        both = jnp.concatenate([window_high, window_low], axis=0)
        value = jnp.dot(both, high[:count], preferred_element_type=jnp.float32)
        rest = jnp.dot(window_high, low[:count], preferred_element_type=jnp.float32)
        value = value[: 3 * WINDOW] + value[3 * WINDOW :] + rest
        for c in range(3):
            part = value[c * WINDOW : (c + 1) * WINDOW] * weight_y
            out[c, pl.ds(index, 1), :] = jnp.sum(part, axis=0, keepdims=True)

    def skip(index):
        for c in range(3):
            out[c, pl.ds(index, 1), :] = jnp.zeros((1, layout.markers), jnp.float32)

    slot_visits(layout, facts, marks, saved, blocks, step_z, high, low, visit, skip)


def sample_kernel(layout, groups, facts, *refs):
    count = len(groups)
    marks, refs = refs[:count], refs[count:]
    (field_high, field_low), refs = refs[:2], refs[2:]
    outs, refs = refs[:count], refs[count:]
    saved, (high, low) = refs[:count], refs[count:]
    for i, (blocks, step_z) in enumerate(groups):
        sample_slots(
            layout,
            facts,
            marks[i],
            field_high,
            field_low,
            outs[i],
            saved[i],
            blocks,
            step_z,
            high,
            low,
        )


def visit_cost(layout, blocks):
    return len(blocks) * layout.slots * 18 * WINDOW * layout.plane * layout.markers


def weight_scratch(layout):
    return [pltpu.VMEM((layout.plane, layout.markers), jnp.bfloat16)] * 2


def sample(layout, groups, facts, marks, fields, name):
    markers, weights = layout.markers, layout.sizes[0] + layout.sizes[1] + WINDOW
    counts = [len(blocks) * layout.slots for blocks, _ in groups]
    results = call(
        functools.partial(sample_kernel, layout, groups),
        [float32(3, count, markers) for count in counts]
        + [float32(count, weights, markers) for count in counts],
        [facts],
        [*marks, *fields],
        weight_scratch(layout),
        name,
        sum(visit_cost(layout, blocks) for blocks, _ in groups),
        8 * fields[0].size,
    )
    return results[: len(groups)], results[len(groups) :]


def spread_slots(layout, blocks, step_z, facts, saved, push, own_rows, total, high, low):
    def visit(index, row, first, weight_y, pieces):
        slot = index if own_rows else row
        count = sum(width for _, width in pieces)
        value = jnp.concatenate(
            [weight_y * push[c, pl.ds(slot, 1), :] for c in range(3)], axis=0
        )
        value_high, value_low = split(value)
        both = jnp.concatenate([value_high, value_low], axis=0)
        added = lax.dot_general(
            both, high[:count], TRANSPOSED, preferred_element_type=jnp.float32
        )
        rest = lax.dot_general(
            value_high, low[:count], TRANSPOSED, preferred_element_type=jnp.float32
        )
        added = added[: 3 * WINDOW] + added[3 * WINDOW :] + rest
        column = 0
        for lane, width in pieces:
            for c in range(3):
                part = added[c * WINDOW : (c + 1) * WINDOW, column : column + width]
                total[c, pl.ds(first, WINDOW), pl.ds(lane, width)] += part
            column += width

    slot_visits(layout, facts, None, saved, blocks, step_z, high, low, visit, None)


def spread_own_kernel(layout, facts, saved, push, total, high, low):
    total[...] = jnp.zeros(total.shape, jnp.float32)
    spread_slots(layout, (1,), 0, facts, saved, push, True, total, high, low)


def spread_own(layout, facts, saved, push):
    return call(
        functools.partial(spread_own_kernel, layout),
        float32(3, layout.sizes[2], layout.plane),
        [facts],
        [saved, push],
        weight_scratch(layout),
        "spread_own",
        visit_cost(layout, (1,)),
        12 * layout.sizes[2] * layout.plane,
    )


def spread_side_kernel(layout, facts, saved, push, before, total, high, low):
    total[...] = before[...]
    spread_slots(layout, (0, 2), 0, facts, saved, push, False, total, high, low)


def spread_side(layout, facts, saved, push, before):
    return call(
        functools.partial(spread_side_kernel, layout),
        float32(*before.shape),
        [facts],
        [saved, push, before],
        weight_scratch(layout),
        "spread_side",
        visit_cost(layout, (0, 2)),
        8 * before.size,
    )


def spread_rest_kernel(
    layout,
    facts,
    lower_saved,
    upper_saved,
    lower_push,
    upper_push,
    before,
    predicted,
    velocity,
    u_first,
    u_last,
    w_first,
    w_last,
    inner,
    total,
    high,
    low,
):
    size_x, size_z, size_y = layout.sizes
    total[...] = before[...]
    row = (0, 1, 2)
    spread_slots(layout, row, -1, facts, lower_saved, lower_push, False, total, high, low)
    spread_slots(layout, row, 1, facts, upper_saved, upper_push, False, total, high, low)
    for c in range(3):
        for q, (xs, zs) in enumerate(quarters(layout.sizes)):
            part = jnp.transpose(total[c, :, q * LANES : (q + 1) * LANES])
            part = part.reshape(size_x // 2, size_z // 2, size_y)
            velocity[c, xs, zs] = predicted[c, xs, zs] + part
    u_first[...] = velocity[0, 0]
    u_last[...] = velocity[0, size_x - 1]
    for x in range(size_x):
        w_first[x : x + 1] = velocity[2, x, 0:1]
        w_last[x : x + 1] = velocity[2, x, size_z - 1 : size_z]
    row = lax.broadcasted_iota(jnp.int32, (size_z, size_y), 0)
    lane = lax.broadcasted_iota(jnp.int32, (size_z, size_y), 1)
    for x in range(size_x):
        y_minus, y_plus = y_neighbours(velocity[1, x], lane, 0.0, 0.0)
        z_minus, z_plus = z_neighbours(velocity[2, x], row, 0.0, 0.0)
        change = y_plus - y_minus + z_plus - z_minus
        if x > 0:
            change -= velocity[0, x - 1]
        if x < size_x - 1:
            change += velocity[0, x + 1]
        inner[x] = change * 0.5


def spread_rest(layout, facts, saved, pushes, before, predicted):
    size_x, size_z, size_y = layout.sizes
    return call(
        functools.partial(spread_rest_kernel, layout),
        [float32(3, size_x, size_z, size_y)]
        + [float32(size_z, size_y)] * 2
        + [float32(size_x, size_y)] * 2
        + [float32(size_x, size_z, size_y)],
        [facts],
        [*saved, *pushes, before, predicted],
        [pltpu.VMEM(before.shape, jnp.float32)] + weight_scratch(layout),
        "spread_rest",
        2 * visit_cost(layout, (0, 1, 2)),
        12 * before.size,
    )


def pack_x_kernel(
    layout,
    slot_ids_hbm,
    corners_hbm,
    flow,
    cells_hbm,
    fraction_hbm,
    own,
    last,
    first_layer,
    slot_ids,
    corners,
    cells,
    fraction,
    done,
):
    size_x, size_z, size_y = layout.sizes
    slots = layout.slots
    moves = [
        (slot_ids_hbm, slot_ids),
        (corners_hbm, corners),
        (cells_hbm, cells),
        (fraction_hbm, fraction),
    ]
    for c in range(4):
        rows = pl.ds(c * size_z, size_z)
        moves.append((flow.at[c, size_x - 1], last.at[rows]))
        moves.append((flow.at[c, 0], first_layer.at[rows]))
    copies = [pltpu.make_async_copy(a, b, done.at[i]) for i, (a, b) in enumerate(moves)]
    for copy in copies:
        copy.start()
    for copy in copies[:4]:
        copy.wait()
    length_x = size_x * lax.axis_size("gx")
    length_z = size_z * lax.axis_size("gz")
    offset_x = length_x + HALF - lax.axis_index("gx") * size_x
    offset_z = length_z + HALF - lax.axis_index("gz") * size_z
    for a, direction in enumerate((0, 2, 1)):
        for t in range(layout.tiles):
            lanes = slice(t * LANES, (t + 1) * LANES)
            place = cells[direction, :, lanes].astype(jnp.float32) + fraction[direction, :, lanes]
            first = (a * layout.tiles + t) * slots
            own[first : first + slots] = place
    lane = lax.broadcasted_iota(jnp.int32, (1, LANES), 1)
    for slot in range(slots):
        first_x = lax.rem(corners[0, slot] + offset_x, length_x) - HALF
        first_z = lax.rem(corners[2, slot] + offset_z, length_z) - HALF
        held = (slot_ids[slot] >= 0).astype(jnp.int32)
        fact = jnp.where(lane == 0, first_x, held)
        fact = jnp.where(lane == 1, first_z, fact)
        fact = jnp.where(lane == 2, corners[1, slot], fact)
        row = layout.fact_row + slot
        own[row : row + 1] = fact.astype(jnp.float32)
    for copy in copies[4:]:
        copy.wait()


def pack_x(layout, slot_ids, corners, flow, cells, fraction):
    in_hbm = pl.BlockSpec(memory_space=pltpu.HBM)
    return pl.pallas_call(
        functools.partial(pack_x_kernel, layout),
        out_shape=[float32(layout.rows, LANES)] + [float32(layout.ghost_x, LANES)] * 2,
        in_specs=[in_hbm] * 5,
        out_specs=[IN_VMEM] * 3,
        scratch_shapes=[
            pltpu.SMEM(slot_ids.shape, jnp.int32),
            pltpu.SMEM(corners.shape, jnp.int32),
            pltpu.VMEM(cells.shape, jnp.int32),
            pltpu.VMEM(fraction.shape, jnp.float32),
            pltpu.SemaphoreType.DMA((12,)),
        ],
        name="pack_x",
        cost_estimate=pl.CostEstimate(
            flops=flow.size, bytes_accessed=8 * flow.size // 16, transcendentals=0
        ),
    )(slot_ids, corners, flow, cells, fraction)


def pack_z_kernel(layout, flow, own, left, right, to_upper, to_lower):
    size_x, size_z, size_y = layout.sizes
    for c in range(4):
        for x in range(size_x):
            row = c * size_x + x
            to_upper[row : row + 1] = flow[c, x, size_z - 1 : size_z]
            to_lower[row : row + 1] = flow[c, x, 0:1]
    tiles = (left[...], own[...], right[...])
    for block, tile in enumerate(tiles):
        first = layout.ghost_z + block * layout.rows
        to_upper[first : first + layout.rows] = tile
        to_lower[first : first + layout.rows] = tile


def pack_z(layout, flow, own, left, right):
    rows = layout.ghost_z + 3 * layout.rows
    return call(
        functools.partial(pack_z_kernel, layout),
        [float32(rows, LANES)] * 2,
        [],
        [flow, own, left, right],
        [],
        "pack_z",
        flow.size,
        8 * rows * LANES,
    )


def y_neighbours(value, lane, below, above):
    size_y = value.shape[-1]
    minus = jnp.where(lane == 0, below, pltpu.roll(value, 1, 1))
    plus = jnp.where(lane == size_y - 1, above, pltpu.roll(value, size_y - 1, 1))
    return minus, plus


def z_neighbours(value, row, below, above):
    size_z = value.shape[0]
    minus = jnp.where(row == 0, below, pltpu.roll(value, 1, 0))
    plus = jnp.where(row == size_z - 1, above, pltpu.roll(value, size_z - 1, 0))
    return minus, plus


def predict_inner_kernel(sizes, flow, left, right, predicted):
    size_x, size_z, size_y = sizes
    row = lax.broadcasted_iota(jnp.int32, (size_z, size_y), 0)
    lane = lax.broadcasted_iota(jnp.int32, (size_z, size_y), 1)

    def around(c, x):
        value = flow[c, x]
        ghost = slice(c * size_z, (c + 1) * size_z)
        x_minus = flow[c, x - 1] if x > 0 else left[ghost]
        x_plus = flow[c, x + 1] if x < size_x - 1 else right[ghost]
        z_minus, z_plus = z_neighbours(value, row, 0.0, 0.0)
        edges = (0.0, 0.0) if c < 3 else (value, value)
        y_minus, y_plus = y_neighbours(value, lane, *edges)
        return value, x_minus, x_plus, z_minus, z_plus, y_minus, y_plus

    for x in range(size_x):
        _, x_minus, x_plus, z_minus, z_plus, y_minus, y_plus = around(3, x)
        gradient = (
            (x_plus - x_minus) * 0.5 - drive_force,
            (y_plus - y_minus) * 0.5,
            (z_plus - z_minus) * 0.5,
        )
        carried = (flow[0, x], flow[1, x], flow[2, x])
        for c in range(3):
            value, x_minus, x_plus, z_minus, z_plus, y_minus, y_plus = around(c, x)
            laplace = x_plus + x_minus + z_plus + z_minus + y_plus + y_minus - 6.0 * value
            advect = (
                carried[0] * (x_plus - x_minus)
                + carried[1] * (y_plus - y_minus)
                + carried[2] * (z_plus - z_minus)
            ) * 0.5
            predicted[c, x] = value + time_step * (viscosity * laplace - advect - gradient[c])


def predict_inner(sizes, flow, left, right):
    return call(
        functools.partial(predict_inner_kernel, sizes),
        float32(3, *sizes),
        [],
        [flow, left, right],
        [],
        "predict_inner",
        200 * flow.size,
        8 * flow.size,
    )


def predict_outer_kernel(
    layout, flow, inner, lower, own, upper, predicted, field_high, field_low, facts, table
):
    size_x, size_z, size_y = layout.sizes
    row = lax.broadcasted_iota(jnp.int32, (8, size_y), 0)
    for block in range(9):
        payload = (lower, own, upper)[block // 3]
        first = layout.ghost_z + (block % 3) * layout.rows + layout.fact_row
        out = slice(block * layout.slots, (block + 1) * layout.slots)
        table[out] = payload[first : first + layout.slots]
    facts[...] = jnp.transpose(table[...])[:8].astype(jnp.int32)
    for x in range(size_x):
        carried_low = flow[2, x, 0:1]
        carried_high = flow[2, x, size_z - 1 : size_z]
        for c in range(3):
            ghost = c * size_x + x
            below, above = lower[ghost : ghost + 1], upper[ghost : ghost + 1]
            change_low = (viscosity + 0.5 * carried_low) * below
            change_high = (viscosity - 0.5 * carried_high) * above
            if c == 2:
                ghost = 3 * size_x + x
                change_low += 0.5 * lower[ghost : ghost + 1]
                change_high -= 0.5 * upper[ghost : ghost + 1]
            predicted[c, x] = inner[c, x]
            first = inner[c, x, 0:8]
            predicted[c, x, 0:8] = first + jnp.where(row == 0, time_step * change_low, 0.0)
            last = inner[c, x, size_z - 8 : size_z]
            predicted[c, x, size_z - 8 : size_z] = last + jnp.where(
                row == 7, time_step * change_high, 0.0
            )
    for c in range(3):
        for q, (xs, zs) in enumerate(quarters(layout.sizes)):
            part = predicted[c, xs, zs].reshape(LANES, size_y)
            part = jnp.transpose(part)
            high = part.astype(jnp.bfloat16).astype(jnp.float32)
            field_high[c, :, q * LANES : (q + 1) * LANES] = high
            field_low[c, :, q * LANES : (q + 1) * LANES] = part - high


def predict_outer(layout, flow, inner, lower, own, upper):
    size_x, size_z, size_y = layout.sizes
    return call(
        functools.partial(predict_outer_kernel, layout),
        [
            float32(3, *layout.sizes),
            float32(3, size_y, layout.plane),
            float32(3, size_y, layout.plane),
            jax.ShapeDtypeStruct((8, LANES), jnp.int32),
        ],
        [],
        [flow, inner, lower, own, upper],
        [pltpu.VMEM((LANES, LANES), jnp.float32)],
        "predict_outer",
        10 * flow.size,
        12 * flow.size,
    )


def divergence_kernel(sizes, parts, inner, u_below, u_above, w_below, w_above, *rest):
    outs, whole = rest[:parts], rest[parts]
    size_x, size_z, size_y = sizes
    row = lax.broadcasted_iota(jnp.int32, (size_z, size_y), 0)
    group = LANES // size_z
    for q in range(size_x // group):
        pieces = []
        for x in range(q * group, (q + 1) * group):
            piece = inner[x]
            if x == 0:
                piece -= 0.5 * u_below[...]
            if x == size_x - 1:
                piece += 0.5 * u_above[...]
            piece -= jnp.where(row == 0, 0.5 * w_below[x : x + 1], 0.0)
            piece += jnp.where(row == size_z - 1, 0.5 * w_above[x : x + 1], 0.0)
            pieces.append(piece)
        part = jnp.concatenate(pieces, axis=0)
        whole[:, q * LANES : (q + 1) * LANES] = jnp.transpose(part)
    height = size_y // parts
    for step in range(parts):
        first = pl.multiple_of(lax.rem(lax.axis_index("gz") + step, parts) * height, 8)
        outs[step][...] = whole[pl.ds(first, height), :]


def divergence(sizes, parts, inner, ghosts):
    size_x, size_z, size_y = sizes
    plane = size_x * size_z
    return call(
        functools.partial(divergence_kernel, sizes, parts),
        [float32(size_y // parts, plane)] * parts,
        [],
        [inner, *ghosts],
        [pltpu.VMEM((size_y, plane), jnp.float32)],
        "divergence",
        10 * inner.size,
        8 * inner.size,
    )


def swap_groups(values, width):
    count = LANES // width
    lane = lax.broadcasted_iota(jnp.int32, values[0].shape, 1)
    values = list(values)
    step = count // 2
    while step:
        reach = step * width
        keep = lane % (2 * reach) < reach
        for i in range(count):
            if i & step == 0:
                a, b = values[i], values[i + step]
                values[i] = jnp.where(keep, a, pltpu.roll(b, reach, 1))
                values[i + step] = jnp.where(keep, pltpu.roll(a, LANES - reach, 1), b)
        step //= 2
    return values


def transform_z_kernel(sizes, counts, table_high, table_low, *refs):
    size_x, size_z, size_y = sizes
    parts_x, parts_z = counts
    pieces, refs = refs[:parts_z], refs[parts_z:]
    outs, (gathered, turned, whole) = refs[:parts_x], refs[parts_x:]
    height = size_y // parts_z
    group = LANES // size_z
    for step in range(parts_z):
        gathered[lax.rem(lax.axis_index("gz") + parts_z - step, parts_z)] = pieces[step][...]
    for block in range(parts_z // group):
        for q in range(size_x // group):
            lanes = slice(q * LANES, (q + 1) * LANES)
            values = [gathered[block * group + i, :, lanes] for i in range(group)]
            for j, value in enumerate(swap_groups(values, size_z)):
                turned[block, pl.ds(q * group + j, height, stride=size_x), :] = value
    lines = jnp.concatenate([turned[b] for b in range(turned.shape[0])], axis=1)
    high, low = split(lines)
    result = lax.dot_general(
        table_high[...], high, TRANSPOSED, preferred_element_type=jnp.float32
    )
    result += lax.dot_general(
        table_low[...], high, TRANSPOSED, preferred_element_type=jnp.float32
    )
    result += lax.dot_general(
        table_high[...], low, TRANSPOSED, preferred_element_type=jnp.float32
    )
    whole[...] = result
    rows = whole.shape[0] // parts_x
    for step in range(parts_x):
        first = pl.multiple_of(lax.rem(lax.axis_index("gx") + step, parts_x) * rows, 8)
        outs[step][...] = whole[pl.ds(first, rows), :]


def transform_z(sizes, counts, table, pieces):
    size_x, size_z, size_y = sizes
    parts_x, parts_z = counts
    length_z = size_z * parts_z
    height = size_y // parts_z
    columns = height * size_x
    return call(
        functools.partial(transform_z_kernel, sizes, counts),
        [float32(2 * length_z // parts_x, columns)] * parts_x,
        [],
        [*table, *pieces],
        [
            pltpu.VMEM((parts_z, height, size_x * size_z), jnp.float32),
            pltpu.VMEM((length_z // LANES, columns, LANES), jnp.float32),
            pltpu.VMEM((2 * length_z, columns), jnp.float32),
        ],
        "transform_z",
        12 * length_z * length_z * columns,
        12 * length_z * columns,
    )


def transform_x_kernel(sizes, counts, table_high, table_low, *refs):
    size_x, size_z, size_y = sizes
    parts_x, parts_z = counts
    pieces, (source, gathered, turned) = refs[:parts_x], refs[parts_x:]
    length_x = size_x * parts_x
    modes = size_z * parts_z // parts_x
    height = size_y // parts_z
    group = LANES // size_x
    for step in range(parts_x):
        gathered[lax.rem(lax.axis_index("gx") + parts_x - step, parts_x)] = pieces[step][...]
    for block in range(parts_x // group):
        for q in range(height // group):
            lanes = slice(q * LANES, (q + 1) * LANES)
            values = [gathered[block * group + i, :, lanes] for i in range(group)]
            for j, value in enumerate(swap_groups(values, size_x)):
                first = (q * group + j) * modes
                for c in range(2):
                    column = c * length_x + block * LANES
                    turned[first : first + modes, column : column + LANES] = value[
                        c * modes : (c + 1) * modes
                    ]
    high, low = split(turned[...])
    result = jnp.dot(high, table_high[...], preferred_element_type=jnp.float32)
    result += jnp.dot(low, table_high[...], preferred_element_type=jnp.float32)
    result += jnp.dot(high, table_low[...], preferred_element_type=jnp.float32)
    source[0] = result[:, :length_x].reshape(height, modes, length_x)
    source[1] = result[:, length_x:].reshape(height, modes, length_x)


def transform_x(sizes, counts, table, pieces):
    size_x, size_z, size_y = sizes
    parts_x, parts_z = counts
    length_x = size_x * parts_x
    modes = size_z * parts_z // parts_x
    height = size_y // parts_z
    return call(
        functools.partial(transform_x_kernel, sizes, counts),
        float32(2, height, modes, length_x),
        [],
        [*table, *pieces],
        [
            pltpu.VMEM((parts_x, *pieces[0].shape), jnp.float32),
            pltpu.VMEM((height * modes, 2 * length_x), jnp.float32),
        ],
        "transform_x",
        24 * length_x * length_x * height * modes,
        24 * length_x * height * modes,
    )


def split_table(table):
    high = table.astype(np.float32).astype(jnp.bfloat16)
    low = (table - high.astype(np.float64)).astype(np.float32).astype(jnp.bfloat16)
    return jnp.asarray(high), jnp.asarray(low)


def angles(length):
    counter = np.arange(length)
    turn = (counter[:, None] * counter[None, :] % length) * (2.0 * np.pi / length)
    return np.cos(turn), np.sin(turn)


def table_z(length, blocks):
    cosine, sine = angles(length)
    modes = length // blocks
    table = np.stack([cosine, -sine]).reshape(2, blocks, modes, length)
    return split_table(table.transpose(1, 0, 2, 3).reshape(2 * length, length))


def table_x(length, scale):
    cosine, sine = angles(length)
    return split_table(np.block([[cosine, -sine], [sine, cosine]]) * scale)


def exchange(pieces, axis):
    return [pieces[0]] + [shift(pieces[d], axis, d) for d in range(1, len(pieces))]


def on_device(
    flow_state, slot_ids, corners, marker_cells, marker_frac, particle_velocity, particle_spin
):
    sizes = flow_state.shape[1:]
    size_x, size_z, size_y = sizes
    counts = (lax.axis_size("gx"), lax.axis_size("gz"))
    length_x, length_z = (size_x * counts[0], size_z * counts[1])
    slots, markers = marker_cells.shape[1:]
    layout = Layout(sizes, slots, markers)

    own, last, first = pack_x(layout, slot_ids, corners, flow_state, marker_cells, marker_frac)
    left = shift(own, "gx", 1)
    right = shift(own, "gx", -1)
    ghosts = (shift(last, "gx", 1), shift(first, "gx", -1))
    row, to_lower = pack_z(layout, flow_state, own, left, right)
    lower = shift(row, "gz", 1)
    upper = shift(to_lower, "gz", -1)
    inner = predict_inner(sizes, flow_state, *ghosts)
    predicted, *fields, facts = predict_outer(layout, flow_state, inner, lower, row, upper)

    positions = marker_cells.astype(jnp.float32) + marker_frac
    chosen = slot_ids[:, None] == jnp.arange(particle_velocity.shape[1], dtype=jnp.int32)[None, :]
    moving = jnp.sum(jnp.where(chosen[None], particle_velocity[:, None, :], 0.0), axis=2)
    turning = jnp.sum(jnp.where(chosen[None], particle_spin[:, None, :], 0.0), axis=2)
    lever = positions - HALF
    moving, turning = (moving[:, :, None], turning[:, :, None])
    target = moving + jnp.stack(
        [
            turning[1] * lever[2] - turning[2] * lever[1],
            turning[2] * lever[0] - turning[0] * lever[2],
            turning[0] * lever[1] - turning[1] * lever[0],
        ]
    )
    living = (slot_ids >= 0).astype(jnp.float32)[None, :, None]

    tiles = (0, 1, 2)
    parts, (lower_saved, upper_saved) = sample(
        layout, ((tiles, -1), (tiles, 1)), facts, (lower, upper), fields, "sample_rows"
    )
    from_upper = shift(parts[0], "gz", -1)
    from_lower = shift(parts[1], "gz", 1)
    (side_part,), (side_saved,) = sample(
        layout, (((0, 2), 0),), facts, (row,), fields, "sample_side"
    )
    from_z = from_upper + from_lower
    from_right = shift(side_part[:, :slots] + from_z[:, :slots], "gx", -1)
    from_left = shift(side_part[:, slots:] + from_z[:, 2 * slots :], "gx", 1)
    (own_part,), (own_saved,) = sample(
        layout, (((1,), 0),), facts, (row,), fields, "sample_own"
    )
    sampled = own_part + from_z[:, slots : 2 * slots] + from_right + from_left
    push = living * (target - sampled)

    left_push = shift(push, "gx", 1)
    right_push = shift(push, "gx", -1)
    row_push = jnp.concatenate([left_push, push, right_push], axis=1)
    lower_push = shift(row_push, "gz", 1)
    upper_push = shift(row_push, "gz", -1)
    forcing = spread_own(layout, facts, own_saved, push)
    forcing = spread_side(layout, facts, side_saved, row_push, forcing)
    velocity, u_first, u_last, w_first, w_last, change = spread_rest(
        layout, facts, (lower_saved, upper_saved), (lower_push, upper_push), forcing, predicted
    )

    ghosts = (
        shift(u_last, "gx", 1),
        shift(u_first, "gx", -1),
        shift(w_last, "gz", 1),
        shift(w_first, "gz", -1),
    )
    pieces = divergence(sizes, counts[1], change, ghosts)
    pieces = exchange(pieces, "gz")
    pieces = transform_z(sizes, counts, table_z(length_z, counts[0]), pieces)
    pieces = exchange(pieces, "gx")
    scale = 1.0 / math.sqrt(length_x * length_z)
    source = transform_x(sizes, counts, table_x(length_x, scale), pieces)
    return velocity, source


def solution(mesh):
    return jax.shard_map(
        on_device,
        mesh=mesh,
        in_specs=(
            P(None, "gx", "gz", None),
            P(("gx", "gz")),
            P(None, ("gx", "gz")),
            P(None, ("gx", "gz"), None),
            P(None, ("gx", "gz"), None),
            P(),
            P(),
        ),
        out_specs=(P(None, "gx", "gz", None), P(None, "gz", "gx", None)),
        check_vma=False,
    )
```

```python
import functools
import math

import jax
import jax.numpy as jnp
import numpy as np
from jax import lax
from jax.experimental import pallas as pl
from jax.experimental.pallas import tpu as pltpu
from jax.sharding import PartitionSpec as P


BOX = 24
HALF = 12
WINDOW = 32
LANES = 128
KERNEL_BYTES = 16 * 1024 * 1024

time_step = 0.1
viscosity = 0.2
drive_force = 1.0


IN_VMEM = pl.BlockSpec(memory_space=pltpu.VMEM)
IN_SMEM = pl.BlockSpec(memory_space=pltpu.SMEM)
TRANSPOSED = (((1,), (1,)), ((), ()))


def float32(*shape):
    return jax.ShapeDtypeStruct(shape, jnp.float32)


def call(kernel, out_shape, scalars, arrays, scratch, flops, moved):
    outputs = len(out_shape) if isinstance(out_shape, (list, tuple)) else 0
    return pl.pallas_call(
        kernel,
        out_shape=out_shape,
        in_specs=[IN_SMEM] * len(scalars) + [IN_VMEM] * len(arrays),
        out_specs=[IN_VMEM] * outputs if outputs else IN_VMEM,
        scratch_shapes=scratch,
        compiler_params=pltpu.CompilerParams(vmem_limit_bytes=KERNEL_BYTES),
        cost_estimate=pl.CostEstimate(flops=flops, bytes_accessed=moved, transcendentals=0),
    )(*scalars, *arrays)


def shift(array, axis, step):
    devices = lax.axis_size(axis)
    return lax.ppermute(array, axis, [(i, (i + step) % devices) for i in range(devices)])


def cosine_coefficients():
    samples = 2.0 + 2.0 * np.cos(np.pi * (np.arange(64) + 0.5) / 64)
    values = np.cos(np.pi / 4 * np.sqrt(samples)) * np.sqrt(0.5)
    fit = np.polynomial.chebyshev.Chebyshev.fit(samples, values, 4, domain=[0, 4])
    return [float(v) for v in fit.convert(kind=np.polynomial.Polynomial).coef]


COSINE = cosine_coefficients()


def weight(offset):
    square = jnp.minimum(offset * offset, 4.0)
    value = COSINE[-1] * square + COSINE[-2]
    for coefficient in COSINE[-3::-1]:
        value = value * square + coefficient
    return value * value


def split(value):
    high = value.astype(jnp.bfloat16)
    low = (value - high.astype(jnp.float32)).astype(jnp.bfloat16)
    return high, low


def row_weights(count, position):
    cells = lax.broadcasted_iota(jnp.int32, (count, position.shape[1]), 0)
    return weight(cells.astype(jnp.float32) - position)


def plane_weights(weight_x, weight_z, half_z, high, low):
    count = 0
    for z in range(0, weight_z.shape[0], half_z):
        part = weight_z[z : z + half_z]
        for x in range(weight_x.shape[0]):
            rows = slice(count * half_z, (count + 1) * half_z)
            high[rows], low[rows] = split(weight_x[x : x + 1] * part)
            count += 1


def window_start(first_y, size_y):
    return pl.multiple_of(jnp.minimum((first_y // 8) * 8, size_y - WINDOW), 8)


def quarters(sizes):
    half_x, half_z = sizes[0] // 2, sizes[1] // 2
    for z in range(2):
        for x in range(2):
            yield slice(x * half_x, (x + 1) * half_x), slice(z * half_z, (z + 1) * half_z)


class Layout:
    def __init__(self, sizes, slots, markers):
        self.sizes, self.slots, self.markers = sizes, slots, markers
        self.tiles = markers // LANES
        self.fact_row = 3 * self.tiles * slots
        self.rows = self.fact_row + slots
        self.ghost_x = 4 * sizes[1]
        self.ghost_z = 4 * sizes[0]
        self.plane = sizes[0] * sizes[1]


def marker_row(layout, marks, base, direction, slot):
    first = base + direction * layout.tiles * layout.slots + slot
    rows = [marks[pl.ds(first + t * layout.slots, 1), :] for t in range(layout.tiles)]
    return jnp.concatenate(rows, axis=1)


def slot_visits(layout, facts, marks, saved, blocks, step_z, high, low, visit, skip):
    size_x, size_z, size_y = layout.sizes
    half_x, half_z = size_x // 2, size_z // 2
    slots = layout.slots

    def body(index, carry):
        block, slot = index // slots, index % slots
        block = blocks[0] + block * (blocks[1] - blocks[0] if len(blocks) > 1 else 0)
        fact = (step_z + 1) * 3 * slots + block * slots + slot
        first_x = facts[0, fact] + (block - 1) * size_x
        first_z = facts[1, fact] + step_z * size_z
        first_y = facts[2, fact]
        meets_x = (first_x > -BOX) & (first_x < size_x)
        meets_z = (first_z > -BOX) & (first_z < size_z)
        active = (facts[3, fact] != 0) & meets_x & meets_z
        whole_x = (first_x > half_x - BOX) & (first_x < half_x)
        whole_z = (first_z > half_z - BOX) & (first_z < half_z)
        upper_x = (first_x >= half_x).astype(jnp.int32)
        upper_z = (first_z >= half_z).astype(jnp.int32)

        def part(all_x, all_z):
            start_x = 0 if all_x else upper_x * half_x
            start_z = 0 if all_z else upper_z * half_z
            lanes = [
                ((0 if all_z else upper_z) + z) * 2 * LANES + (0 if all_x else upper_x) * LANES
                for z in range(2 if all_z else 1)
            ]
            width = (2 if all_x else 1) * LANES
            if all_x and all_z:
                pieces = [(0, 4 * LANES)]
            else:
                pieces = [(pl.multiple_of(lane, LANES), width) for lane in lanes]
            first = window_start(first_y, size_y)
            rows_x = slice(0, size_x if all_x else half_x)
            rows_z = slice(size_x, size_x + (size_z if all_z else half_z))
            rows_y = slice(size_x + size_z, size_x + size_z + WINDOW)
            if marks is not None:
                base = block * layout.rows
                starts = (first_x - start_x, first_z - start_z, first_y - first)
                for direction, rows in enumerate((rows_x, rows_z, rows_y)):
                    position = marker_row(layout, marks, base, direction, slot)
                    position += starts[direction].astype(jnp.float32)
                    saved[index, rows, :] = row_weights(rows.stop - rows.start, position)
            plane_weights(saved[index, rows_x, :], saved[index, rows_z, :], half_z, high, low)
            weight_y = saved[index, rows_y, :]
            visit(index, block * slots + slot, first, weight_y, pieces)

        for all_x in (True, False):
            for all_z in (True, False):
                one = whole_x if all_x else jnp.logical_not(whole_x)
                two = whole_z if all_z else jnp.logical_not(whole_z)
                pl.when(active & one & two)(functools.partial(part, all_x, all_z))

        if skip is not None:

            @pl.when(jnp.logical_not(active))
            def _():
                skip(index)

        return carry

    lax.fori_loop(0, len(blocks) * slots, body, 0)


def rigid_motion(layout, facts, marks, motion, block, slot):
    particle = facts[3, (3 + block) * layout.slots + slot] - 1
    chosen = lax.broadcasted_iota(jnp.int32, motion[0].shape, 1) == particle
    moving, turning = [
        jnp.sum(jnp.where(chosen, part[...], 0.0), axis=1, keepdims=True) for part in motion
    ]
    lever = [
        marker_row(layout, marks, block * layout.rows, direction, slot) - HALF
        for direction in (0, 2, 1)
    ]
    for c in range(3):
        a, b = (c + 1) % 3, (c + 2) % 3
        turned = turning[a : a + 1] * lever[b] - turning[b : b + 1] * lever[a]
        yield moving[c : c + 1] + turned


def sample_slots(
    layout, facts, marks, motion, field_high, field_low, out, saved, blocks, step_z, high, low
):
    def visit(index, row, first, weight_y, pieces):
        rows = pl.ds(first, WINDOW)

        def window(field):
            parts = [
                jnp.concatenate([field[c, rows, pl.ds(lane, width)] for c in range(3)], axis=0)
                for lane, width in pieces
            ]
            return jnp.concatenate(parts, axis=1).astype(jnp.bfloat16)

        window_high, window_low = window(field_high), window(field_low)
        count = window_high.shape[1]
        both = jnp.concatenate([window_high, window_low], axis=0)
        value = jnp.dot(both, high[:count], preferred_element_type=jnp.float32)
        rest = jnp.dot(window_high, low[:count], preferred_element_type=jnp.float32)
        value = value[: 3 * WINDOW] + value[3 * WINDOW :] + rest
        target = None
        if motion:
            target = list(rigid_motion(layout, facts, marks, motion, blocks[0], index))
        for c in range(3):
            part = value[c * WINDOW : (c + 1) * WINDOW] * weight_y
            sampled = jnp.sum(part, axis=0, keepdims=True)
            out[c, pl.ds(index, 1), :] = sampled if target is None else target[c] - sampled

    def skip(index):
        for c in range(3):
            out[c, pl.ds(index, 1), :] = jnp.zeros((1, layout.markers), jnp.float32)

    slot_visits(layout, facts, marks, saved, blocks, step_z, high, low, visit, skip)


def sample_kernel(layout, groups, moved, facts, *refs):
    count = len(groups)
    marks, refs = refs[:count], refs[count:]
    (field_high, field_low), refs = refs[:2], refs[2:]
    motion, refs = refs[:moved], refs[moved:]
    outs, refs = refs[:count], refs[count:]
    saved, (high, low) = refs[:count], refs[count:]
    for i, (blocks, step_z) in enumerate(groups):
        sample_slots(
            layout,
            facts,
            marks[i],
            motion,
            field_high,
            field_low,
            outs[i],
            saved[i],
            blocks,
            step_z,
            high,
            low,
        )


def visit_cost(layout, blocks):
    return len(blocks) * layout.slots * 18 * WINDOW * layout.plane * layout.markers


def weight_scratch(layout):
    return [pltpu.VMEM((layout.plane, layout.markers), jnp.bfloat16)] * 2


def sample(layout, groups, facts, marks, fields, motion):
    markers, weights = layout.markers, layout.sizes[0] + layout.sizes[1] + WINDOW
    counts = [len(blocks) * layout.slots for blocks, _ in groups]
    results = call(
        functools.partial(sample_kernel, layout, groups, len(motion)),
        [float32(3, count, markers) for count in counts]
        + [float32(count, weights, markers) for count in counts],
        [facts],
        [*marks, *fields, *motion],
        weight_scratch(layout),
        sum(visit_cost(layout, blocks) for blocks, _ in groups),
        8 * fields[0].size,
    )
    return results[: len(groups)], results[len(groups) :]


def spread_slots(layout, blocks, step_z, facts, saved, push, own_rows, total, high, low):
    def visit(index, row, first, weight_y, pieces):
        slot = index if own_rows else row
        count = sum(width for _, width in pieces)
        value = jnp.concatenate(
            [weight_y * push[c, pl.ds(slot, 1), :] for c in range(3)], axis=0
        )
        value_high, value_low = split(value)
        both = jnp.concatenate([value_high, value_low], axis=0)
        added = lax.dot_general(
            both, high[:count], TRANSPOSED, preferred_element_type=jnp.float32
        )
        rest = lax.dot_general(
            value_high, low[:count], TRANSPOSED, preferred_element_type=jnp.float32
        )
        added = added[: 3 * WINDOW] + added[3 * WINDOW :] + rest
        column = 0
        for lane, width in pieces:
            for c in range(3):
                part = added[c * WINDOW : (c + 1) * WINDOW, column : column + width]
                total[c, pl.ds(first, WINDOW), pl.ds(lane, width)] += part
            column += width

    slot_visits(layout, facts, None, saved, blocks, step_z, high, low, visit, None)


def spread_own_kernel(layout, facts, saved, push, total, high, low):
    total[...] = jnp.zeros(total.shape, jnp.float32)
    spread_slots(layout, (1,), 0, facts, saved, push, True, total, high, low)


def spread_own(layout, facts, saved, push):
    return call(
        functools.partial(spread_own_kernel, layout),
        float32(3, layout.sizes[2], layout.plane),
        [facts],
        [saved, push],
        weight_scratch(layout),
        visit_cost(layout, (1,)),
        12 * layout.sizes[2] * layout.plane,
    )


def spread_side_kernel(layout, facts, saved, push, before, total, high, low):
    total[...] = before[...]
    spread_slots(layout, (0, 2), 0, facts, saved, push, False, total, high, low)


def spread_side(layout, facts, saved, push, before):
    return call(
        functools.partial(spread_side_kernel, layout),
        float32(*before.shape),
        [facts],
        [saved, push, before],
        weight_scratch(layout),
        visit_cost(layout, (0, 2)),
        8 * before.size,
    )


def spread_rest_kernel(
    layout,
    facts,
    lower_saved,
    upper_saved,
    lower_push,
    upper_push,
    before,
    predicted,
    velocity,
    u_first,
    u_last,
    w_first,
    w_last,
    inner,
    total,
    high,
    low,
):
    size_x, size_z, size_y = layout.sizes
    total[...] = before[...]
    row = (0, 1, 2)
    spread_slots(layout, row, -1, facts, lower_saved, lower_push, False, total, high, low)
    spread_slots(layout, row, 1, facts, upper_saved, upper_push, False, total, high, low)
    for c in range(3):
        for q, (xs, zs) in enumerate(quarters(layout.sizes)):
            part = jnp.transpose(total[c, :, q * LANES : (q + 1) * LANES])
            part = part.reshape(size_x // 2, size_z // 2, size_y)
            velocity[c, xs, zs] = predicted[c, xs, zs] + part
    u_first[...] = velocity[0, 0]
    u_last[...] = velocity[0, size_x - 1]
    for x in range(size_x):
        w_first[x : x + 1] = velocity[2, x, 0:1]
        w_last[x : x + 1] = velocity[2, x, size_z - 1 : size_z]
    row = lax.broadcasted_iota(jnp.int32, (size_z, size_y), 0)
    lane = lax.broadcasted_iota(jnp.int32, (size_z, size_y), 1)
    for x in range(size_x):
        y_minus, y_plus = y_neighbours(velocity[1, x], lane, 0.0, 0.0)
        z_minus, z_plus = z_neighbours(velocity[2, x], row, 0.0, 0.0)
        change = y_plus - y_minus + z_plus - z_minus
        if x > 0:
            change -= velocity[0, x - 1]
        if x < size_x - 1:
            change += velocity[0, x + 1]
        inner[x] = change * 0.5


def spread_rest(layout, facts, saved, pushes, before, predicted):
    size_x, size_z, size_y = layout.sizes
    return call(
        functools.partial(spread_rest_kernel, layout),
        [float32(3, size_x, size_z, size_y)]
        + [float32(size_z, size_y)] * 2
        + [float32(size_x, size_y)] * 2
        + [float32(size_x, size_z, size_y)],
        [facts],
        [*saved, *pushes, before, predicted],
        [pltpu.VMEM(before.shape, jnp.float32)] + weight_scratch(layout),
        2 * visit_cost(layout, (0, 1, 2)),
        12 * before.size,
    )


def pack_kernel(
    layout,
    slot_ids_hbm,
    corners_hbm,
    flow,
    cells_hbm,
    fraction_hbm,
    own,
    x_last,
    x_first,
    z_last,
    z_first,
    slot_ids,
    corners,
    cells,
    fraction,
    edges,
    done,
):
    size_x, size_z, _ = layout.sizes
    slots = layout.slots
    moves = [
        (slot_ids_hbm, slot_ids),
        (corners_hbm, corners),
        (cells_hbm, cells),
        (fraction_hbm, fraction),
    ]
    for c in range(4):
        moves.append((flow.at[c, :, pl.ds(size_z - 8, 8)], edges.at[0, c]))
        moves.append((flow.at[c, :, pl.ds(0, 8)], edges.at[1, c]))
    for c in range(4):
        rows = pl.ds(c * size_z, size_z)
        moves.append((flow.at[c, size_x - 1], x_last.at[rows]))
        moves.append((flow.at[c, 0], x_first.at[rows]))
    copies = [pltpu.make_async_copy(a, b, done.at[i]) for i, (a, b) in enumerate(moves)]
    for copy in copies:
        copy.start()
    for copy in copies[:4]:
        copy.wait()
    length_x = size_x * lax.axis_size("gx")
    length_z = size_z * lax.axis_size("gz")
    offset_x = length_x + HALF - lax.axis_index("gx") * size_x
    offset_z = length_z + HALF - lax.axis_index("gz") * size_z
    targets = ((own, 0), (z_last, layout.ghost_z), (z_first, layout.ghost_z))
    for a, direction in enumerate((0, 2, 1)):
        for t in range(layout.tiles):
            lanes = slice(t * LANES, (t + 1) * LANES)
            place = cells[direction, :, lanes].astype(jnp.float32) + fraction[direction, :, lanes]
            for target, base in targets:
                first = base + (a * layout.tiles + t) * slots
                target[first : first + slots] = place
    lane = lax.broadcasted_iota(jnp.int32, (1, LANES), 1)
    for slot in range(slots):
        first_x = lax.rem(corners[0, slot] + offset_x, length_x) - HALF
        first_z = lax.rem(corners[2, slot] + offset_z, length_z) - HALF
        fact = jnp.where(lane == 0, first_x, slot_ids[slot] + 1)
        fact = jnp.where(lane == 1, first_z, fact)
        fact = jnp.where(lane == 2, corners[1, slot], fact)
        for target, base in targets:
            row = base + layout.fact_row + slot
            target[row : row + 1] = fact.astype(jnp.float32)
    for copy in copies[4:]:
        copy.wait()
    for c in range(4):
        for x in range(size_x):
            row = c * size_x + x
            z_last[row : row + 1] = edges[0, c, x, 7:8]
            z_first[row : row + 1] = edges[1, c, x, 0:1]


def pack(layout, slot_ids, corners, flow, cells, fraction):
    in_hbm = pl.BlockSpec(memory_space=pltpu.HBM)
    size_x, _, size_y = layout.sizes
    return pl.pallas_call(
        functools.partial(pack_kernel, layout),
        out_shape=[float32(layout.rows, LANES)]
        + [float32(layout.ghost_x, LANES)] * 2
        + [float32(layout.ghost_z + layout.rows, LANES)] * 2,
        in_specs=[in_hbm] * 5,
        out_specs=[IN_VMEM] * 5,
        scratch_shapes=[
            pltpu.SMEM(slot_ids.shape, jnp.int32),
            pltpu.SMEM(corners.shape, jnp.int32),
            pltpu.VMEM(cells.shape, jnp.int32),
            pltpu.VMEM(fraction.shape, jnp.float32),
            pltpu.VMEM((2, 4, size_x, 8, size_y), jnp.float32),
            pltpu.SemaphoreType.DMA((20,)),
        ],
        name="pack",
        cost_estimate=pl.CostEstimate(
            flops=flow.size, bytes_accessed=flow.size, transcendentals=0
        ),
    )(slot_ids, corners, flow, cells, fraction)


def join_kernel(left, right, both):
    rows = left.shape[0]
    both[:rows] = left[...]
    both[rows:] = right[...]


def join(left, right):
    return call(
        join_kernel,
        float32(2 * left.shape[0], LANES),
        [],
        [left, right],
        [],
        left.size,
        16 * left.size,
    )


def collect_kernel(layout, own, left, right, below, above, corners_below, corners_above, *refs):
    rows, (facts, table) = refs[:3], refs[3:]
    count = layout.rows
    for row, middle, base, sides in (
        (rows[0], below, layout.ghost_z, corners_below),
        (rows[1], own, 0, None),
        (rows[2], above, layout.ghost_z, corners_above),
    ):
        row[:count] = left[...] if sides is None else sides[:count]
        row[count : 2 * count] = middle[base : base + count]
        row[2 * count :] = right[...] if sides is None else sides[count:]
    for block in range(9):
        first = (block % 3) * count + layout.fact_row
        out = slice(block * layout.slots, (block + 1) * layout.slots)
        table[out] = rows[block // 3][first : first + layout.slots]
    facts[...] = jnp.transpose(table[...])[:8].astype(jnp.int32)


def collect(layout, *tiles):
    return call(
        functools.partial(collect_kernel, layout),
        [float32(3 * layout.rows, LANES)] * 3 + [jax.ShapeDtypeStruct((8, LANES), jnp.int32)],
        [],
        tiles,
        [pltpu.VMEM((LANES, LANES), jnp.float32)],
        layout.rows * LANES,
        72 * layout.rows * LANES,
    )


def y_neighbours(value, lane, below, above):
    size_y = value.shape[-1]
    minus = jnp.where(lane == 0, below, pltpu.roll(value, 1, 1))
    plus = jnp.where(lane == size_y - 1, above, pltpu.roll(value, size_y - 1, 1))
    return minus, plus


def z_neighbours(value, row, below, above):
    size_z = value.shape[0]
    minus = jnp.where(row == 0, below, pltpu.roll(value, 1, 0))
    plus = jnp.where(row == size_z - 1, above, pltpu.roll(value, size_z - 1, 0))
    return minus, plus


def predict_inner_kernel(sizes, flow, inner, u_first, u_last, w_first, w_last):
    size_x, size_z, size_y = sizes
    row = lax.broadcasted_iota(jnp.int32, (size_z, size_y), 0)
    lane = lax.broadcasted_iota(jnp.int32, (size_z, size_y), 1)
    nothing = jnp.zeros((size_z, size_y), jnp.float32)

    def around(c, x):
        value = flow[c, x]
        x_minus = flow[c, x - 1] if x > 0 else nothing
        x_plus = flow[c, x + 1] if x < size_x - 1 else nothing
        z_minus, z_plus = z_neighbours(value, row, 0.0, 0.0)
        edges = (0.0, 0.0) if c < 3 else (value, value)
        y_minus, y_plus = y_neighbours(value, lane, *edges)
        return value, x_minus, x_plus, z_minus, z_plus, y_minus, y_plus

    for x in range(size_x):
        _, x_minus, x_plus, z_minus, z_plus, y_minus, y_plus = around(3, x)
        gradient = (
            (x_plus - x_minus) * 0.5 - drive_force,
            (y_plus - y_minus) * 0.5,
            (z_plus - z_minus) * 0.5,
        )
        carried = (flow[0, x], flow[1, x], flow[2, x])
        for c in range(3):
            value, x_minus, x_plus, z_minus, z_plus, y_minus, y_plus = around(c, x)
            laplace = x_plus + x_minus + z_plus + z_minus + y_plus + y_minus - 6.0 * value
            advect = (
                carried[0] * (x_plus - x_minus)
                + carried[1] * (y_plus - y_minus)
                + carried[2] * (z_plus - z_minus)
            ) * 0.5
            inner[c, x] = value + time_step * (viscosity * laplace - advect - gradient[c])
        w_first[x : x + 1] = flow[2, x, 0:1]
        w_last[x : x + 1] = flow[2, x, size_z - 1 : size_z]
    u_first[...] = flow[0, 0]
    u_last[...] = flow[0, size_x - 1]


def predict_inner(sizes, flow):
    size_x, size_z, size_y = sizes
    return call(
        functools.partial(predict_inner_kernel, sizes),
        [float32(3, *sizes)] + [float32(size_z, size_y)] * 2 + [float32(size_x, size_y)] * 2,
        [],
        [flow],
        [],
        200 * flow.size,
        8 * flow.size,
    )


def predict_outer_kernel(
    layout,
    inner,
    u_first,
    u_last,
    w_first,
    w_last,
    left,
    right,
    lower,
    upper,
    predicted,
    field_high,
    field_low,
):
    size_x, size_z, size_y = layout.sizes
    row = lax.broadcasted_iota(jnp.int32, (8, size_y), 0)
    for x in range(size_x):
        carried_low = w_first[x : x + 1]
        carried_high = w_last[x : x + 1]
        for c in range(3):
            ghost = c * size_x + x
            change_low = (viscosity + 0.5 * carried_low) * lower[ghost : ghost + 1]
            change_high = (viscosity - 0.5 * carried_high) * upper[ghost : ghost + 1]
            if c == 2:
                ghost = 3 * size_x + x
                change_low += 0.5 * lower[ghost : ghost + 1]
                change_high -= 0.5 * upper[ghost : ghost + 1]
            if x in (0, size_x - 1):
                sign, layer, carried = (0.5, left, u_first) if x == 0 else (-0.5, right, u_last)
                ghost = slice(c * size_z, (c + 1) * size_z)
                change = (viscosity + sign * carried[...]) * layer[ghost]
                if c == 0:
                    change += sign * layer[3 * size_z : 4 * size_z]
                predicted[c, x] = inner[c, x] + time_step * change
            else:
                predicted[c, x] = inner[c, x]
            predicted[c, x, 0:8] += jnp.where(row == 0, time_step * change_low, 0.0)
            predicted[c, x, size_z - 8 : size_z] += jnp.where(
                row == 7, time_step * change_high, 0.0
            )
    for c in range(3):
        for q, (xs, zs) in enumerate(quarters(layout.sizes)):
            part = jnp.transpose(predicted[c, xs, zs].reshape(LANES, size_y))
            high = part.astype(jnp.bfloat16).astype(jnp.float32)
            field_high[c, :, q * LANES : (q + 1) * LANES] = high
            field_low[c, :, q * LANES : (q + 1) * LANES] = part - high


def predict_outer(layout, inner, left, right, lower, upper):
    _, _, size_y = layout.sizes
    return call(
        functools.partial(predict_outer_kernel, layout),
        [float32(3, *layout.sizes)] + [float32(3, size_y, layout.plane)] * 2,
        [],
        [*inner, left, right, lower, upper],
        [],
        10 * inner[0].size,
        16 * inner[0].size,
    )


def divergence_kernel(sizes, parts, inner, u_below, u_above, w_below, w_above, *rest):
    outs, whole = rest[:parts], rest[parts]
    size_x, size_z, size_y = sizes
    row = lax.broadcasted_iota(jnp.int32, (size_z, size_y), 0)
    group = LANES // size_z
    for q in range(size_x // group):
        pieces = []
        for x in range(q * group, (q + 1) * group):
            piece = inner[x]
            if x == 0:
                piece -= 0.5 * u_below[...]
            if x == size_x - 1:
                piece += 0.5 * u_above[...]
            piece -= jnp.where(row == 0, 0.5 * w_below[x : x + 1], 0.0)
            piece += jnp.where(row == size_z - 1, 0.5 * w_above[x : x + 1], 0.0)
            pieces.append(piece)
        part = jnp.concatenate(pieces, axis=0)
        whole[:, q * LANES : (q + 1) * LANES] = jnp.transpose(part)
    height = size_y // parts
    for step in range(parts):
        first = pl.multiple_of(lax.rem(lax.axis_index("gz") + step, parts) * height, 8)
        outs[step][...] = whole[pl.ds(first, height), :]


def divergence(sizes, parts, inner, ghosts):
    size_x, size_z, size_y = sizes
    plane = size_x * size_z
    return call(
        functools.partial(divergence_kernel, sizes, parts),
        [float32(size_y // parts, plane)] * parts,
        [],
        [inner, *ghosts],
        [pltpu.VMEM((size_y, plane), jnp.float32)],
        10 * inner.size,
        8 * inner.size,
    )


def swap_groups(values, width):
    count = LANES // width
    lane = lax.broadcasted_iota(jnp.int32, values[0].shape, 1)
    values = list(values)
    step = count // 2
    while step:
        reach = step * width
        keep = lane % (2 * reach) < reach
        for i in range(count):
            if i & step == 0:
                a, b = values[i], values[i + step]
                values[i] = jnp.where(keep, a, pltpu.roll(b, reach, 1))
                values[i + step] = jnp.where(keep, pltpu.roll(a, LANES - reach, 1), b)
        step //= 2
    return values


def transform_z_kernel(sizes, counts, table_high, table_low, *refs):
    size_x, size_z, size_y = sizes
    parts_x, parts_z = counts
    pieces, refs = refs[:parts_z], refs[parts_z:]
    outs, (gathered, turned, whole) = refs[:parts_x], refs[parts_x:]
    height = size_y // parts_z
    group = LANES // size_z
    for step in range(parts_z):
        gathered[lax.rem(lax.axis_index("gz") + parts_z - step, parts_z)] = pieces[step][...]
    for block in range(parts_z // group):
        for q in range(size_x // group):
            lanes = slice(q * LANES, (q + 1) * LANES)
            values = [gathered[block * group + i, :, lanes] for i in range(group)]
            for j, value in enumerate(swap_groups(values, size_z)):
                turned[block, pl.ds(q * group + j, height, stride=size_x), :] = value
    lines = jnp.concatenate([turned[b] for b in range(turned.shape[0])], axis=1)
    high, low = split(lines)
    result = lax.dot_general(
        table_high[...], high, TRANSPOSED, preferred_element_type=jnp.float32
    )
    result += lax.dot_general(
        table_low[...], high, TRANSPOSED, preferred_element_type=jnp.float32
    )
    result += lax.dot_general(
        table_high[...], low, TRANSPOSED, preferred_element_type=jnp.float32
    )
    whole[...] = result
    rows = whole.shape[0] // parts_x
    for step in range(parts_x):
        first = pl.multiple_of(lax.rem(lax.axis_index("gx") + step, parts_x) * rows, 8)
        outs[step][...] = whole[pl.ds(first, rows), :]


def transform_z(sizes, counts, table, pieces):
    size_x, size_z, size_y = sizes
    parts_x, parts_z = counts
    length_z = size_z * parts_z
    height = size_y // parts_z
    columns = height * size_x
    return call(
        functools.partial(transform_z_kernel, sizes, counts),
        [float32(2 * length_z // parts_x, columns)] * parts_x,
        [],
        [*table, *pieces],
        [
            pltpu.VMEM((parts_z, height, size_x * size_z), jnp.float32),
            pltpu.VMEM((length_z // LANES, columns, LANES), jnp.float32),
            pltpu.VMEM((2 * length_z, columns), jnp.float32),
        ],
        12 * length_z * length_z * columns,
        12 * length_z * columns,
    )


def transform_x_kernel(sizes, counts, table_high, table_low, *refs):
    size_x, size_z, size_y = sizes
    parts_x, parts_z = counts
    pieces, (source, gathered, turned) = refs[:parts_x], refs[parts_x:]
    length_x = size_x * parts_x
    modes = size_z * parts_z // parts_x
    height = size_y // parts_z
    group = LANES // size_x
    for step in range(parts_x):
        gathered[lax.rem(lax.axis_index("gx") + parts_x - step, parts_x)] = pieces[step][...]
    for block in range(parts_x // group):
        for q in range(height // group):
            lanes = slice(q * LANES, (q + 1) * LANES)
            values = [gathered[block * group + i, :, lanes] for i in range(group)]
            for j, value in enumerate(swap_groups(values, size_x)):
                first = (q * group + j) * modes
                for c in range(2):
                    column = c * length_x + block * LANES
                    turned[first : first + modes, column : column + LANES] = value[
                        c * modes : (c + 1) * modes
                    ]
    high, low = split(turned[...])
    result = jnp.dot(high, table_high[...], preferred_element_type=jnp.float32)
    result += jnp.dot(low, table_high[...], preferred_element_type=jnp.float32)
    result += jnp.dot(high, table_low[...], preferred_element_type=jnp.float32)
    source[0] = result[:, :length_x].reshape(height, modes, length_x)
    source[1] = result[:, length_x:].reshape(height, modes, length_x)


def transform_x(sizes, counts, table, pieces):
    size_x, size_z, size_y = sizes
    parts_x, parts_z = counts
    length_x = size_x * parts_x
    modes = size_z * parts_z // parts_x
    height = size_y // parts_z
    return call(
        functools.partial(transform_x_kernel, sizes, counts),
        float32(2, height, modes, length_x),
        [],
        [*table, *pieces],
        [
            pltpu.VMEM((parts_x, *pieces[0].shape), jnp.float32),
            pltpu.VMEM((height * modes, 2 * length_x), jnp.float32),
        ],
        24 * length_x * length_x * height * modes,
        24 * length_x * height * modes,
    )


def split_table(table):
    high = table.astype(np.float32).astype(jnp.bfloat16)
    low = (table - high.astype(np.float64)).astype(np.float32).astype(jnp.bfloat16)
    return jnp.asarray(high), jnp.asarray(low)


def angles(length):
    counter = np.arange(length)
    turn = (counter[:, None] * counter[None, :] % length) * (2.0 * np.pi / length)
    return np.cos(turn), np.sin(turn)


def table_z(length, blocks):
    cosine, sine = angles(length)
    modes = length // blocks
    table = np.stack([cosine, -sine]).reshape(2, blocks, modes, length)
    return split_table(table.transpose(1, 0, 2, 3).reshape(2 * length, length))


def table_x(length, scale):
    cosine, sine = angles(length)
    return split_table(np.block([[cosine, -sine], [sine, cosine]]) * scale)


def exchange(pieces, axis):
    return [pieces[0]] + [shift(pieces[d], axis, d) for d in range(1, len(pieces))]


def on_device(
    flow_state, slot_ids, corners, marker_cells, marker_frac, particle_velocity, particle_spin
):
    sizes = flow_state.shape[1:]
    size_x, size_z, _ = sizes
    counts = (lax.axis_size("gx"), lax.axis_size("gz"))
    length_x, length_z = (size_x * counts[0], size_z * counts[1])
    slots, markers = marker_cells.shape[1:]
    layout = Layout(sizes, slots, markers)

    own, x_last, x_first, z_last, z_first = pack(
        layout, slot_ids, corners, flow_state, marker_cells, marker_frac
    )
    left = shift(own, "gx", 1)
    right = shift(own, "gx", -1)
    below, above = shift(z_last, "gz", 1), shift(z_first, "gz", -1)
    x_below, x_above = shift(x_last, "gx", 1), shift(x_first, "gx", -1)
    inner = predict_inner(sizes, flow_state)
    sides = join(left, right)
    corners_below, corners_above = shift(sides, "gz", 1), shift(sides, "gz", -1)
    predicted, *fields = predict_outer(layout, inner, x_below, x_above, below, above)
    lower, row, upper, facts = collect(
        layout, own, left, right, below, above, corners_below, corners_above
    )

    tiles = (0, 1, 2)
    parts, (lower_saved, upper_saved) = sample(
        layout, ((tiles, -1), (tiles, 1)), facts, (lower, upper), fields, ()
    )
    from_upper = shift(parts[0], "gz", -1)
    from_lower = shift(parts[1], "gz", 1)
    (side_part,), (side_saved,) = sample(layout, (((0, 2), 0),), facts, (row,), fields, ())
    from_z = from_upper + from_lower
    from_right = shift(side_part[:, :slots] + from_z[:, :slots], "gx", -1)
    from_left = shift(side_part[:, slots:] + from_z[:, 2 * slots :], "gx", 1)
    motion = (particle_velocity, particle_spin)
    (own_part,), (own_saved,) = sample(layout, (((1,), 0),), facts, (row,), fields, motion)
    push = own_part - (from_z[:, slots : 2 * slots] + from_right + from_left)

    left_push = shift(push, "gx", 1)
    right_push = shift(push, "gx", -1)
    row_push = jnp.concatenate([left_push, push, right_push], axis=1)
    lower_push = shift(row_push, "gz", 1)
    upper_push = shift(row_push, "gz", -1)
    forcing = spread_own(layout, facts, own_saved, push)
    forcing = spread_side(layout, facts, side_saved, row_push, forcing)
    velocity, u_first, u_last, w_first, w_last, change = spread_rest(
        layout, facts, (lower_saved, upper_saved), (lower_push, upper_push), forcing, predicted
    )

    ghosts = (
        shift(u_last, "gx", 1),
        shift(u_first, "gx", -1),
        shift(w_last, "gz", 1),
        shift(w_first, "gz", -1),
    )
    pieces = divergence(sizes, counts[1], change, ghosts)
    pieces = exchange(pieces, "gz")
    pieces = transform_z(sizes, counts, table_z(length_z, counts[0]), pieces)
    pieces = exchange(pieces, "gx")
    scale = 1.0 / math.sqrt(length_x * length_z)
    source = transform_x(sizes, counts, table_x(length_x, scale), pieces)
    return velocity, source


def solution(mesh):
    return jax.shard_map(
        on_device,
        mesh=mesh,
        in_specs=(
            P(None, "gx", "gz", None),
            P(("gx", "gz")),
            P(None, ("gx", "gz")),
            P(None, ("gx", "gz"), None),
            P(None, ("gx", "gz"), None),
            P(),
            P(),
        ),
        out_specs=(P(None, "gx", "gz", None), P(None, "gz", "gx", None)),
        check_vma=False,
    )
```

```python
import functools
import math

import jax
import jax.numpy as jnp
import numpy as np
from jax import lax
from jax.experimental import pallas as pl
from jax.experimental.pallas import tpu as pltpu
from jax.sharding import PartitionSpec as P


BOX = 24
HALF = 12
WINDOW = 32
LANES = 128
KERNEL_BYTES = 16 * 1024 * 1024

time_step = 0.1
viscosity = 0.2
drive_force = 1.0


IN_VMEM = pl.BlockSpec(memory_space=pltpu.VMEM)
IN_SMEM = pl.BlockSpec(memory_space=pltpu.SMEM)
TRANSPOSED = (((1,), (1,)), ((), ()))


def float32(*shape):
    return jax.ShapeDtypeStruct(shape, jnp.float32)


def call(kernel, out_shape, scalars, arrays, scratch, flops, moved):
    outputs = len(out_shape) if isinstance(out_shape, (list, tuple)) else 0
    return pl.pallas_call(
        kernel,
        out_shape=out_shape,
        in_specs=[IN_SMEM] * len(scalars) + [IN_VMEM] * len(arrays),
        out_specs=[IN_VMEM] * outputs if outputs else IN_VMEM,
        scratch_shapes=scratch,
        compiler_params=pltpu.CompilerParams(vmem_limit_bytes=KERNEL_BYTES),
        cost_estimate=pl.CostEstimate(flops=flops, bytes_accessed=moved, transcendentals=0),
    )(*scalars, *arrays)


def swap(array, axis, partner):
    devices = lax.axis_size(axis)
    pairs = [(i, (i + (1 if i % 2 == partner else -1)) % devices) for i in range(devices)]
    return lax.ppermute(array, axis, pairs)


def even(axis):
    return lax.rem(lax.axis_index(axis), 2) == 0


def in_order(axis, shape):
    parity = jnp.full(shape, lax.rem(lax.axis_index(axis), 2), jnp.int32)
    return lambda one, two: (
        jnp.where(parity == 0, two, one),
        jnp.where(parity == 0, one, two),
    )


def cosine_coefficients():
    samples = 2.0 + 2.0 * np.cos(np.pi * (np.arange(64) + 0.5) / 64)
    values = np.cos(np.pi / 4 * np.sqrt(samples)) * np.sqrt(0.5)
    fit = np.polynomial.chebyshev.Chebyshev.fit(samples, values, 4, domain=[0, 4])
    return [float(v) for v in fit.convert(kind=np.polynomial.Polynomial).coef]


COSINE = cosine_coefficients()


def weight(offset):
    square = jnp.minimum(offset * offset, 4.0)
    value = COSINE[-1] * square + COSINE[-2]
    for coefficient in COSINE[-3::-1]:
        value = value * square + coefficient
    return value * value


def split(value):
    high = value.astype(jnp.bfloat16)
    low = (value - high.astype(jnp.float32)).astype(jnp.bfloat16)
    return high, low


def row_weights(count, position):
    cells = lax.broadcasted_iota(jnp.int32, (count, position.shape[1]), 0)
    return weight(cells.astype(jnp.float32) - position)


def plane_weights(weight_x, weight_z, half_z, high, low):
    count = 0
    for z in range(0, weight_z.shape[0], half_z):
        part = weight_z[z : z + half_z]
        for x in range(weight_x.shape[0]):
            rows = slice(count * half_z, (count + 1) * half_z)
            high[rows], low[rows] = split(weight_x[x : x + 1] * part)
            count += 1


def window_start(first_y, size_y):
    return pl.multiple_of(jnp.minimum((first_y // 8) * 8, size_y - WINDOW), 8)


def quarters(sizes):
    half_x, half_z = sizes[0] // 2, sizes[1] // 2
    for z in range(2):
        for x in range(2):
            yield slice(x * half_x, (x + 1) * half_x), slice(z * half_z, (z + 1) * half_z)


class Layout:
    def __init__(self, sizes, slots, markers):
        self.sizes, self.slots, self.markers = sizes, slots, markers
        self.tiles = markers // LANES
        self.fact_row = 3 * self.tiles * slots
        self.rows = self.fact_row + slots
        self.ghost_x = 4 * sizes[1]
        self.ghost_z = 4 * sizes[0]
        self.plane = sizes[0] * sizes[1]


def marker_row(layout, marks, base, direction, slot):
    first = base + direction * layout.tiles * layout.slots + slot
    rows = [marks[pl.ds(first + t * layout.slots, 1), :] for t in range(layout.tiles)]
    return jnp.concatenate(rows, axis=1)


def slot_visits(layout, facts, marks, saved, blocks, step, high, low, visit, skip):
    size_x, size_z, size_y = layout.sizes
    half_x, half_z = size_x // 2, size_z // 2
    slots = layout.slots

    def body(index, carry):
        block, slot = index // slots, index % slots
        block = blocks[0] + block * (blocks[1] - blocks[0] if len(blocks) > 1 else 0)
        fact = (step * 3 + block) * slots + slot
        first_x = facts[0, fact]
        first_z = facts[1, fact]
        first_y = facts[2, fact]
        meets_x = (first_x > -BOX) & (first_x < size_x)
        meets_z = (first_z > -BOX) & (first_z < size_z)
        active = (facts[3, fact] != 0) & meets_x & meets_z
        whole_x = (first_x > half_x - BOX) & (first_x < half_x)
        whole_z = (first_z > half_z - BOX) & (first_z < half_z)
        upper_x = (first_x >= half_x).astype(jnp.int32)
        upper_z = (first_z >= half_z).astype(jnp.int32)

        def part(all_x, all_z):
            start_x = 0 if all_x else upper_x * half_x
            start_z = 0 if all_z else upper_z * half_z
            lanes = [
                ((0 if all_z else upper_z) + z) * 2 * LANES + (0 if all_x else upper_x) * LANES
                for z in range(2 if all_z else 1)
            ]
            width = (2 if all_x else 1) * LANES
            if all_x and all_z:
                pieces = [(0, 4 * LANES)]
            else:
                pieces = [(pl.multiple_of(lane, LANES), width) for lane in lanes]
            first = window_start(first_y, size_y)
            rows_x = slice(0, size_x if all_x else half_x)
            rows_z = slice(size_x, size_x + (size_z if all_z else half_z))
            rows_y = slice(size_x + size_z, size_x + size_z + WINDOW)
            if marks is not None:
                base = block * layout.rows
                starts = (first_x - start_x, first_z - start_z, first_y - first)
                for direction, rows in enumerate((rows_x, rows_z, rows_y)):
                    position = marker_row(layout, marks, base, direction, slot)
                    position += starts[direction].astype(jnp.float32)
                    saved[index, rows, :] = row_weights(rows.stop - rows.start, position)
            plane_weights(saved[index, rows_x, :], saved[index, rows_z, :], half_z, high, low)
            weight_y = saved[index, rows_y, :]
            visit(index, block * slots + slot, first, weight_y, pieces)

        for all_x in (True, False):
            for all_z in (True, False):
                one = whole_x if all_x else jnp.logical_not(whole_x)
                two = whole_z if all_z else jnp.logical_not(whole_z)
                pl.when(active & one & two)(functools.partial(part, all_x, all_z))

        if skip is not None:

            @pl.when(jnp.logical_not(active))
            def _():
                skip(index)

        return carry

    lax.fori_loop(0, len(blocks) * slots, body, 0)


def rigid_motion(layout, facts, marks, motion, block, slot):
    particle = facts[3, (3 + block) * layout.slots + slot] - 1
    chosen = lax.broadcasted_iota(jnp.int32, motion[0].shape, 1) == particle
    moving, turning = [
        jnp.sum(jnp.where(chosen, part[...], 0.0), axis=1, keepdims=True) for part in motion
    ]
    lever = [
        marker_row(layout, marks, block * layout.rows, direction, slot) - HALF
        for direction in (0, 2, 1)
    ]
    for c in range(3):
        a, b = (c + 1) % 3, (c + 2) % 3
        turned = turning[a : a + 1] * lever[b] - turning[b : b + 1] * lever[a]
        yield moving[c : c + 1] + turned


def sample_slots(
    layout, facts, marks, motion, field_high, field_low, out, saved, blocks, step, high, low
):
    def visit(index, row, first, weight_y, pieces):
        rows = pl.ds(first, WINDOW)

        def window(field):
            parts = [
                jnp.concatenate([field[c, rows, pl.ds(lane, width)] for c in range(3)], axis=0)
                for lane, width in pieces
            ]
            return jnp.concatenate(parts, axis=1).astype(jnp.bfloat16)

        window_high, window_low = window(field_high), window(field_low)
        count = window_high.shape[1]
        both = jnp.concatenate([window_high, window_low], axis=0)
        value = jnp.dot(both, high[:count], preferred_element_type=jnp.float32)
        rest = jnp.dot(window_high, low[:count], preferred_element_type=jnp.float32)
        value = value[: 3 * WINDOW] + value[3 * WINDOW :] + rest
        target = None
        if motion:
            target = list(rigid_motion(layout, facts, marks, motion, blocks[0], index))
        for c in range(3):
            part = value[c * WINDOW : (c + 1) * WINDOW] * weight_y
            sampled = jnp.sum(part, axis=0, keepdims=True)
            out[c, pl.ds(index, 1), :] = sampled if target is None else target[c] - sampled

    def skip(index):
        for c in range(3):
            out[c, pl.ds(index, 1), :] = jnp.zeros((1, layout.markers), jnp.float32)

    slot_visits(layout, facts, marks, saved, blocks, step, high, low, visit, skip)


def sample_kernel(layout, groups, moved, facts, *refs):
    count = len(groups)
    marks, refs = refs[:count], refs[count:]
    (field_high, field_low), refs = refs[:2], refs[2:]
    motion, refs = refs[:moved], refs[moved:]
    outs, refs = refs[:count], refs[count:]
    saved, (high, low) = refs[:count], refs[count:]
    for i, (blocks, step) in enumerate(groups):
        sample_slots(
            layout,
            facts,
            marks[i],
            motion,
            field_high,
            field_low,
            outs[i],
            saved[i],
            blocks,
            step,
            high,
            low,
        )


def visit_cost(layout, blocks):
    return len(blocks) * layout.slots * 18 * WINDOW * layout.plane * layout.markers


def weight_scratch(layout):
    return [pltpu.VMEM((layout.plane, layout.markers), jnp.bfloat16)] * 2


def sample(layout, groups, facts, marks, fields, motion):
    markers, weights = layout.markers, layout.sizes[0] + layout.sizes[1] + WINDOW
    counts = [len(blocks) * layout.slots for blocks, _ in groups]
    results = call(
        functools.partial(sample_kernel, layout, groups, len(motion)),
        [float32(3, count, markers) for count in counts]
        + [float32(count, weights, markers) for count in counts],
        [facts],
        [*marks, *fields, *motion],
        weight_scratch(layout),
        sum(visit_cost(layout, blocks) for blocks, _ in groups),
        8 * fields[0].size,
    )
    return results[: len(groups)], results[len(groups) :]


def spread_slots(layout, blocks, step, facts, saved, push, own_rows, total, high, low):
    def visit(index, row, first, weight_y, pieces):
        slot = index if own_rows else row
        count = sum(width for _, width in pieces)
        value = jnp.concatenate(
            [weight_y * push[c, pl.ds(slot, 1), :] for c in range(3)], axis=0
        )
        value_high, value_low = split(value)
        both = jnp.concatenate([value_high, value_low], axis=0)
        added = lax.dot_general(
            both, high[:count], TRANSPOSED, preferred_element_type=jnp.float32
        )
        rest = lax.dot_general(
            value_high, low[:count], TRANSPOSED, preferred_element_type=jnp.float32
        )
        added = added[: 3 * WINDOW] + added[3 * WINDOW :] + rest
        column = 0
        for lane, width in pieces:
            for c in range(3):
                part = added[c * WINDOW : (c + 1) * WINDOW, column : column + width]
                total[c, pl.ds(first, WINDOW), pl.ds(lane, width)] += part
            column += width

    slot_visits(layout, facts, None, saved, blocks, step, high, low, visit, None)


def spread_own_kernel(layout, facts, saved, push, total, high, low):
    total[...] = jnp.zeros(total.shape, jnp.float32)
    spread_slots(layout, (1,), 1, facts, saved, push, True, total, high, low)


def spread_own(layout, facts, saved, push):
    return call(
        functools.partial(spread_own_kernel, layout),
        float32(3, layout.sizes[2], layout.plane),
        [facts],
        [saved, push],
        weight_scratch(layout),
        visit_cost(layout, (1,)),
        12 * layout.sizes[2] * layout.plane,
    )


def spread_side_kernel(layout, facts, saved, push, before, total, high, low):
    total[...] = before[...]
    spread_slots(layout, (0, 2), 1, facts, saved, push, False, total, high, low)


def spread_side(layout, facts, saved, push, before):
    return call(
        functools.partial(spread_side_kernel, layout),
        float32(*before.shape),
        [facts],
        [saved, push, before],
        weight_scratch(layout),
        visit_cost(layout, (0, 2)),
        8 * before.size,
    )


def spread_rest_kernel(
    layout,
    facts,
    saved_0,
    saved_1,
    push_0,
    push_1,
    before,
    predicted,
    velocity,
    u_0,
    u_1,
    w_0,
    w_1,
    inner,
    total,
    high,
    low,
):
    size_x, size_z, size_y = layout.sizes
    total[...] = before[...]
    row = (0, 1, 2)
    spread_slots(layout, row, 0, facts, saved_0, push_0, False, total, high, low)
    spread_slots(layout, row, 2, facts, saved_1, push_1, False, total, high, low)
    for c in range(3):
        for q, (xs, zs) in enumerate(quarters(layout.sizes)):
            part = jnp.transpose(total[c, :, q * LANES : (q + 1) * LANES])
            part = part.reshape(size_x // 2, size_z // 2, size_y)
            velocity[c, xs, zs] = predicted[c, xs, zs] + part
    last = jnp.where(even("gx"), size_x - 1, 0)
    u_0[...] = velocity[0, last]
    u_1[...] = velocity[0, size_x - 1 - last]
    choose = in_order("gz", (1, size_y))
    for x in range(size_x):
        first, last = velocity[2, x, 0:1], velocity[2, x, size_z - 1 : size_z]
        w_0[x : x + 1], w_1[x : x + 1] = choose(first, last)
    row = lax.broadcasted_iota(jnp.int32, (size_z, size_y), 0)
    lane = lax.broadcasted_iota(jnp.int32, (size_z, size_y), 1)
    for x in range(size_x):
        y_minus, y_plus = y_neighbours(velocity[1, x], lane, 0.0, 0.0)
        z_minus, z_plus = z_neighbours(velocity[2, x], row, 0.0, 0.0)
        change = y_plus - y_minus + z_plus - z_minus
        if x > 0:
            change -= velocity[0, x - 1]
        if x < size_x - 1:
            change += velocity[0, x + 1]
        inner[x] = change * 0.5


def spread_rest(layout, facts, saved, pushes, before, predicted):
    size_x, size_z, size_y = layout.sizes
    return call(
        functools.partial(spread_rest_kernel, layout),
        [float32(3, size_x, size_z, size_y)]
        + [float32(size_z, size_y)] * 2
        + [float32(size_x, size_y)] * 2
        + [float32(size_x, size_z, size_y)],
        [facts],
        [*saved, *pushes, before, predicted],
        [pltpu.VMEM(before.shape, jnp.float32)] + weight_scratch(layout),
        2 * visit_cost(layout, (0, 1, 2)),
        12 * before.size,
    )


def pack_kernel(
    layout,
    slot_ids_hbm,
    corners_hbm,
    flow,
    cells_hbm,
    fraction_hbm,
    own,
    x_0,
    x_1,
    z_0,
    z_1,
    slot_ids,
    corners,
    cells,
    fraction,
    edges,
    done,
):
    size_x, size_z, size_y = layout.sizes
    slots = layout.slots
    moves = [
        (slot_ids_hbm, slot_ids),
        (corners_hbm, corners),
        (cells_hbm, cells),
        (fraction_hbm, fraction),
    ]
    for c in range(4):
        moves.append((flow.at[c, :, pl.ds(size_z - 8, 8)], edges.at[0, c]))
        moves.append((flow.at[c, :, pl.ds(0, 8)], edges.at[1, c]))
    last = jnp.where(even("gx"), size_x - 1, 0)
    for c in range(4):
        rows = pl.ds(c * size_z, size_z)
        moves.append((flow.at[c, last], x_0.at[rows]))
        moves.append((flow.at[c, size_x - 1 - last], x_1.at[rows]))
    copies = [pltpu.make_async_copy(a, b, done.at[i]) for i, (a, b) in enumerate(moves)]
    for copy in copies:
        copy.start()
    for copy in copies[:4]:
        copy.wait()
    length_x = size_x * lax.axis_size("gx")
    length_z = size_z * lax.axis_size("gz")
    offset_x = length_x + HALF - lax.axis_index("gx") * size_x
    offset_z = length_z + HALF - lax.axis_index("gz") * size_z
    targets = ((own, 0), (z_0, layout.ghost_z), (z_1, layout.ghost_z))
    for a, direction in enumerate((0, 2, 1)):
        for t in range(layout.tiles):
            lanes = slice(t * LANES, (t + 1) * LANES)
            place = cells[direction, :, lanes].astype(jnp.float32) + fraction[direction, :, lanes]
            for target, base in targets:
                first = base + (a * layout.tiles + t) * slots
                target[first : first + slots] = place
    lane = lax.broadcasted_iota(jnp.int32, (1, LANES), 1)
    for slot in range(slots):
        first_x = lax.rem(corners[0, slot] + offset_x, length_x) - HALF
        first_z = lax.rem(corners[2, slot] + offset_z, length_z) - HALF
        fact = jnp.where(lane == 0, first_x, slot_ids[slot] + 1)
        fact = jnp.where(lane == 1, first_z, fact)
        fact = jnp.where(lane == 2, corners[1, slot], fact)
        for target, base in targets:
            row = base + layout.fact_row + slot
            target[row : row + 1] = fact.astype(jnp.float32)
    for copy in copies[4:]:
        copy.wait()
    choose = in_order("gz", (1, size_y))
    for c in range(4):
        for x in range(size_x):
            row = c * size_x + x
            z_0[row : row + 1], z_1[row : row + 1] = choose(
                edges[1, c, x, 0:1], edges[0, c, x, 7:8]
            )


def pack(layout, slot_ids, corners, flow, cells, fraction):
    in_hbm = pl.BlockSpec(memory_space=pltpu.HBM)
    size_x, _, size_y = layout.sizes
    return pl.pallas_call(
        functools.partial(pack_kernel, layout),
        out_shape=[float32(layout.rows, LANES)]
        + [float32(layout.ghost_x, LANES)] * 2
        + [float32(layout.ghost_z + layout.rows, LANES)] * 2,
        in_specs=[in_hbm] * 5,
        out_specs=[IN_VMEM] * 5,
        scratch_shapes=[
            pltpu.SMEM(slot_ids.shape, jnp.int32),
            pltpu.SMEM(corners.shape, jnp.int32),
            pltpu.VMEM(cells.shape, jnp.int32),
            pltpu.VMEM(fraction.shape, jnp.float32),
            pltpu.VMEM((2, 4, size_x, 8, size_y), jnp.float32),
            pltpu.SemaphoreType.DMA((20,)),
        ],
        name="pack",
        cost_estimate=pl.CostEstimate(
            flops=flow.size, bytes_accessed=flow.size, transcendentals=0
        ),
    )(slot_ids, corners, flow, cells, fraction)


def join_kernel(left, right, both):
    rows = left.shape[0]
    both[:rows] = left[...]
    both[rows:] = right[...]


def join(left, right):
    return call(
        join_kernel,
        float32(2 * left.shape[0], LANES),
        [],
        [left, right],
        [],
        left.size,
        16 * left.size,
    )


def collect_kernel(layout, own, side_0, side_1, one, two, corners_0, corners_1, *refs):
    rows, (facts, table) = refs[:3], refs[3:]
    count, slots = layout.rows, layout.slots
    size_x, size_z, _ = layout.sizes
    for row, middle, base, sides in (
        (rows[0], one, layout.ghost_z, corners_0),
        (rows[1], own, 0, None),
        (rows[2], two, layout.ghost_z, corners_1),
    ):
        row[:count] = side_0[...] if sides is None else sides[:count]
        row[count : 2 * count] = middle[base : base + count]
        row[2 * count :] = side_1[...] if sides is None else sides[count:]
    for block in range(9):
        first = (block % 3) * count + layout.fact_row
        out = slice(block * slots, (block + 1) * slots)
        table[out] = rows[block // 3][first : first + slots]
    kind = lax.broadcasted_iota(jnp.int32, (8, LANES), 0)
    slot = lax.broadcasted_iota(jnp.int32, (8, LANES), 1)
    last = 2 * 3 * slots
    move_x = jnp.where(even("gx"), size_x, -size_x)
    move_z = jnp.where(even("gz"), size_z, -size_z)
    place = slot - jnp.where(slot >= last, last, jnp.where(slot >= 3 * slots, 3 * slots, 0))
    moved_x = jnp.where(place < slots, move_x, jnp.where(place >= 2 * slots, -move_x, 0))
    moved_z = jnp.where(slot < 3 * slots, move_z, jnp.where(slot >= last, -move_z, 0))
    moved = jnp.where(kind == 0, moved_x, jnp.where(kind == 1, moved_z, 0))
    facts[...] = jnp.transpose(table[...])[:8].astype(jnp.int32) + moved


def collect(layout, *tiles):
    return call(
        functools.partial(collect_kernel, layout),
        [float32(3 * layout.rows, LANES)] * 3 + [jax.ShapeDtypeStruct((8, LANES), jnp.int32)],
        [],
        tiles,
        [pltpu.VMEM((LANES, LANES), jnp.float32)],
        layout.rows * LANES,
        72 * layout.rows * LANES,
    )


def y_neighbours(value, lane, below, above):
    size_y = value.shape[-1]
    minus = jnp.where(lane == 0, below, pltpu.roll(value, 1, 1))
    plus = jnp.where(lane == size_y - 1, above, pltpu.roll(value, size_y - 1, 1))
    return minus, plus


def z_neighbours(value, row, below, above):
    size_z = value.shape[0]
    minus = jnp.where(row == 0, below, pltpu.roll(value, 1, 0))
    plus = jnp.where(row == size_z - 1, above, pltpu.roll(value, size_z - 1, 0))
    return minus, plus


def predict_inner_kernel(sizes, flow, inner, u_first, u_last, w_first, w_last):
    size_x, size_z, size_y = sizes
    row = lax.broadcasted_iota(jnp.int32, (size_z, size_y), 0)
    lane = lax.broadcasted_iota(jnp.int32, (size_z, size_y), 1)
    nothing = jnp.zeros((size_z, size_y), jnp.float32)

    def around(c, x):
        value = flow[c, x]
        x_minus = flow[c, x - 1] if x > 0 else nothing
        x_plus = flow[c, x + 1] if x < size_x - 1 else nothing
        z_minus, z_plus = z_neighbours(value, row, 0.0, 0.0)
        edges = (0.0, 0.0) if c < 3 else (value, value)
        y_minus, y_plus = y_neighbours(value, lane, *edges)
        return value, x_minus, x_plus, z_minus, z_plus, y_minus, y_plus

    for x in range(size_x):
        _, x_minus, x_plus, z_minus, z_plus, y_minus, y_plus = around(3, x)
        gradient = (
            (x_plus - x_minus) * 0.5 - drive_force,
            (y_plus - y_minus) * 0.5,
            (z_plus - z_minus) * 0.5,
        )
        carried = (flow[0, x], flow[1, x], flow[2, x])
        for c in range(3):
            value, x_minus, x_plus, z_minus, z_plus, y_minus, y_plus = around(c, x)
            laplace = x_plus + x_minus + z_plus + z_minus + y_plus + y_minus - 6.0 * value
            advect = (
                carried[0] * (x_plus - x_minus)
                + carried[1] * (y_plus - y_minus)
                + carried[2] * (z_plus - z_minus)
            ) * 0.5
            inner[c, x] = value + time_step * (viscosity * laplace - advect - gradient[c])
        w_first[x : x + 1] = flow[2, x, 0:1]
        w_last[x : x + 1] = flow[2, x, size_z - 1 : size_z]
    u_first[...] = flow[0, 0]
    u_last[...] = flow[0, size_x - 1]


def predict_inner(sizes, flow):
    size_x, size_z, size_y = sizes
    return call(
        functools.partial(predict_inner_kernel, sizes),
        [float32(3, *sizes)] + [float32(size_z, size_y)] * 2 + [float32(size_x, size_y)] * 2,
        [],
        [flow],
        [],
        200 * flow.size,
        8 * flow.size,
    )


def predict_outer_kernel(
    layout,
    inner,
    u_first,
    u_last,
    w_first,
    w_last,
    x_0,
    x_1,
    z_0,
    z_1,
    predicted,
    field_high,
    field_low,
):
    size_x, size_z, size_y = layout.sizes
    row = lax.broadcasted_iota(jnp.int32, (8, size_y), 0)
    lower, upper = in_order("gz", z_0[: layout.ghost_z].shape)(
        z_0[: layout.ghost_z], z_1[: layout.ghost_z]
    )
    left, right = in_order("gx", x_0.shape)(x_0[...], x_1[...])
    for x in range(size_x):
        carried_low = w_first[x : x + 1]
        carried_high = w_last[x : x + 1]
        for c in range(3):
            ghost = c * size_x + x
            change_low = (viscosity + 0.5 * carried_low) * lower[ghost : ghost + 1]
            change_high = (viscosity - 0.5 * carried_high) * upper[ghost : ghost + 1]
            if c == 2:
                ghost = 3 * size_x + x
                change_low += 0.5 * lower[ghost : ghost + 1]
                change_high -= 0.5 * upper[ghost : ghost + 1]
            if x in (0, size_x - 1):
                sign, layer, carried = (0.5, left, u_first) if x == 0 else (-0.5, right, u_last)
                ghost = slice(c * size_z, (c + 1) * size_z)
                change = (viscosity + sign * carried[...]) * layer[ghost]
                if c == 0:
                    change += sign * layer[3 * size_z : 4 * size_z]
                predicted[c, x] = inner[c, x] + time_step * change
            else:
                predicted[c, x] = inner[c, x]
            predicted[c, x, 0:8] += jnp.where(row == 0, time_step * change_low, 0.0)
            predicted[c, x, size_z - 8 : size_z] += jnp.where(
                row == 7, time_step * change_high, 0.0
            )
    for c in range(3):
        for q, (xs, zs) in enumerate(quarters(layout.sizes)):
            part = jnp.transpose(predicted[c, xs, zs].reshape(LANES, size_y))
            high = part.astype(jnp.bfloat16).astype(jnp.float32)
            field_high[c, :, q * LANES : (q + 1) * LANES] = high
            field_low[c, :, q * LANES : (q + 1) * LANES] = part - high


def predict_outer(layout, inner, *layers):
    _, _, size_y = layout.sizes
    return call(
        functools.partial(predict_outer_kernel, layout),
        [float32(3, *layout.sizes)] + [float32(3, size_y, layout.plane)] * 2,
        [],
        [*inner, *layers],
        [],
        10 * inner[0].size,
        16 * inner[0].size,
    )


def divergence_kernel(sizes, parts, inner, u_0, u_1, w_0, w_1, *rest):
    outs, whole = rest[:parts], rest[parts]
    size_x, size_z, size_y = sizes
    row = lax.broadcasted_iota(jnp.int32, (size_z, size_y), 0)
    group = LANES // size_z
    u_below, u_above = in_order("gx", u_0.shape)(u_0[...], u_1[...])
    w_below, w_above = in_order("gz", w_0.shape)(w_0[...], w_1[...])
    for q in range(size_x // group):
        pieces = []
        for x in range(q * group, (q + 1) * group):
            piece = inner[x]
            if x == 0:
                piece -= 0.5 * u_below
            if x == size_x - 1:
                piece += 0.5 * u_above
            piece -= jnp.where(row == 0, 0.5 * w_below[x : x + 1], 0.0)
            piece += jnp.where(row == size_z - 1, 0.5 * w_above[x : x + 1], 0.0)
            pieces.append(piece)
        part = jnp.concatenate(pieces, axis=0)
        whole[:, q * LANES : (q + 1) * LANES] = jnp.transpose(part)
    height = size_y // parts
    for step in range(parts):
        first = pl.multiple_of((lax.axis_index("gz") ^ step) * height, 8)
        outs[step][...] = whole[pl.ds(first, height), :]


def divergence(sizes, parts, inner, ghosts):
    size_x, size_z, size_y = sizes
    plane = size_x * size_z
    return call(
        functools.partial(divergence_kernel, sizes, parts),
        [float32(size_y // parts, plane)] * parts,
        [],
        [inner, *ghosts],
        [pltpu.VMEM((size_y, plane), jnp.float32)],
        10 * inner.size,
        8 * inner.size,
    )


def swap_groups(values, width):
    count = LANES // width
    lane = lax.broadcasted_iota(jnp.int32, values[0].shape, 1)
    values = list(values)
    step = count // 2
    while step:
        reach = step * width
        keep = lane % (2 * reach) < reach
        for i in range(count):
            if i & step == 0:
                a, b = values[i], values[i + step]
                values[i] = jnp.where(keep, a, pltpu.roll(b, reach, 1))
                values[i + step] = jnp.where(keep, pltpu.roll(a, LANES - reach, 1), b)
        step //= 2
    return values


def transform_z_kernel(sizes, counts, table_high, table_low, *refs):
    size_x, size_z, size_y = sizes
    parts_x, parts_z = counts
    pieces, refs = refs[:parts_z], refs[parts_z:]
    outs, (gathered, turned, whole) = refs[:parts_x], refs[parts_x:]
    height = size_y // parts_z
    group = LANES // size_z
    for step in range(parts_z):
        gathered[lax.axis_index("gz") ^ step] = pieces[step][...]
    for block in range(parts_z // group):
        for q in range(size_x // group):
            lanes = slice(q * LANES, (q + 1) * LANES)
            values = [gathered[block * group + i, :, lanes] for i in range(group)]
            for j, value in enumerate(swap_groups(values, size_z)):
                turned[block, pl.ds(q * group + j, height, stride=size_x), :] = value
    lines = jnp.concatenate([turned[b] for b in range(turned.shape[0])], axis=1)
    high, low = split(lines)
    result = lax.dot_general(
        table_high[...], high, TRANSPOSED, preferred_element_type=jnp.float32
    )
    result += lax.dot_general(
        table_low[...], high, TRANSPOSED, preferred_element_type=jnp.float32
    )
    result += lax.dot_general(
        table_high[...], low, TRANSPOSED, preferred_element_type=jnp.float32
    )
    whole[...] = result
    rows = whole.shape[0] // parts_x
    for step in range(parts_x):
        first = pl.multiple_of((lax.axis_index("gx") ^ step) * rows, 8)
        outs[step][...] = whole[pl.ds(first, rows), :]


def transform_z(sizes, counts, table, pieces):
    size_x, size_z, size_y = sizes
    parts_x, parts_z = counts
    length_z = size_z * parts_z
    height = size_y // parts_z
    columns = height * size_x
    return call(
        functools.partial(transform_z_kernel, sizes, counts),
        [float32(2 * length_z // parts_x, columns)] * parts_x,
        [],
        [*table, *pieces],
        [
            pltpu.VMEM((parts_z, height, size_x * size_z), jnp.float32),
            pltpu.VMEM((length_z // LANES, columns, LANES), jnp.float32),
            pltpu.VMEM((2 * length_z, columns), jnp.float32),
        ],
        12 * length_z * length_z * columns,
        12 * length_z * columns,
    )


def transform_x_kernel(sizes, counts, table_high, table_low, *refs):
    size_x, size_z, size_y = sizes
    parts_x, parts_z = counts
    pieces, (source, gathered, turned) = refs[:parts_x], refs[parts_x:]
    length_x = size_x * parts_x
    modes = size_z * parts_z // parts_x
    height = size_y // parts_z
    group = LANES // size_x
    for step in range(parts_x):
        gathered[lax.axis_index("gx") ^ step] = pieces[step][...]
    for block in range(parts_x // group):
        for q in range(height // group):
            lanes = slice(q * LANES, (q + 1) * LANES)
            values = [gathered[block * group + i, :, lanes] for i in range(group)]
            for j, value in enumerate(swap_groups(values, size_x)):
                first = (q * group + j) * modes
                for c in range(2):
                    column = c * length_x + block * LANES
                    turned[first : first + modes, column : column + LANES] = value[
                        c * modes : (c + 1) * modes
                    ]
    high, low = split(turned[...])
    result = jnp.dot(high, table_high[...], preferred_element_type=jnp.float32)
    result += jnp.dot(low, table_high[...], preferred_element_type=jnp.float32)
    result += jnp.dot(high, table_low[...], preferred_element_type=jnp.float32)
    source[0] = result[:, :length_x].reshape(height, modes, length_x)
    source[1] = result[:, length_x:].reshape(height, modes, length_x)


def transform_x(sizes, counts, table, pieces):
    size_x, size_z, size_y = sizes
    parts_x, parts_z = counts
    length_x = size_x * parts_x
    modes = size_z * parts_z // parts_x
    height = size_y // parts_z
    return call(
        functools.partial(transform_x_kernel, sizes, counts),
        float32(2, height, modes, length_x),
        [],
        [*table, *pieces],
        [
            pltpu.VMEM((parts_x, *pieces[0].shape), jnp.float32),
            pltpu.VMEM((height * modes, 2 * length_x), jnp.float32),
        ],
        24 * length_x * length_x * height * modes,
        24 * length_x * height * modes,
    )


def split_table(table):
    high = table.astype(np.float32).astype(jnp.bfloat16)
    low = (table - high.astype(np.float64)).astype(np.float32).astype(jnp.bfloat16)
    return jnp.asarray(high), jnp.asarray(low)


def angles(length):
    counter = np.arange(length)
    turn = (counter[:, None] * counter[None, :] % length) * (2.0 * np.pi / length)
    return np.cos(turn), np.sin(turn)


def table_z(length, blocks):
    cosine, sine = angles(length)
    modes = length // blocks
    table = np.stack([cosine, -sine]).reshape(2, blocks, modes, length)
    return split_table(table.transpose(1, 0, 2, 3).reshape(2 * length, length))


def table_x(length, scale):
    cosine, sine = angles(length)
    return split_table(np.block([[cosine, -sine], [sine, cosine]]) * scale)


def exchange(pieces, axis):
    devices = lax.axis_size(axis)
    assert devices & (devices - 1) == 0
    return [pieces[0]] + [
        lax.ppermute(pieces[d], axis, [(i, i ^ d) for i in range(devices)])
        for d in range(1, devices)
    ]


def on_device(
    flow_state, slot_ids, corners, marker_cells, marker_frac, particle_velocity, particle_spin
):
    sizes = flow_state.shape[1:]
    size_x, size_z, _ = sizes
    counts = (lax.axis_size("gx"), lax.axis_size("gz"))
    length_x, length_z = (size_x * counts[0], size_z * counts[1])
    slots, markers = marker_cells.shape[1:]
    layout = Layout(sizes, slots, markers)

    own, x_0, x_1, z_0, z_1 = pack(
        layout, slot_ids, corners, flow_state, marker_cells, marker_frac
    )
    marks_0 = swap(own, "gx", 0)
    marks_1 = swap(own, "gx", 1)
    z_0, z_1 = swap(z_0, "gz", 0), swap(z_1, "gz", 1)
    x_0, x_1 = swap(x_0, "gx", 0), swap(x_1, "gx", 1)
    inner = predict_inner(sizes, flow_state)
    sides = join(marks_0, marks_1)
    corners_0, corners_1 = swap(sides, "gz", 0), swap(sides, "gz", 1)
    predicted, *fields = predict_outer(layout, inner, x_0, x_1, z_0, z_1)
    row_0, row, row_1, facts = collect(
        layout, own, marks_0, marks_1, z_0, z_1, corners_0, corners_1
    )

    tiles = (0, 1, 2)
    parts, rows_saved = sample(layout, ((tiles, 0), (tiles, 2)), facts, (row_0, row_1), fields, ())
    from_z = swap(parts[0], "gz", 0) + swap(parts[1], "gz", 1)
    (side_part,), (side_saved,) = sample(layout, (((0, 2), 1),), facts, (row,), fields, ())
    from_0 = swap(side_part[:, :slots] + from_z[:, :slots], "gx", 0)
    from_1 = swap(side_part[:, slots:] + from_z[:, 2 * slots :], "gx", 1)
    motion = (particle_velocity, particle_spin)
    (own_part,), (own_saved,) = sample(layout, (((1,), 1),), facts, (row,), fields, motion)
    push = own_part - (from_z[:, slots : 2 * slots] + from_0 + from_1)

    row_push = jnp.concatenate([swap(push, "gx", 0), push, swap(push, "gx", 1)], axis=1)
    rows_push = swap(row_push, "gz", 0), swap(row_push, "gz", 1)
    forcing = spread_own(layout, facts, own_saved, push)
    forcing = spread_side(layout, facts, side_saved, row_push, forcing)
    velocity, u_0, u_1, w_0, w_1, change = spread_rest(
        layout, facts, rows_saved, rows_push, forcing, predicted
    )

    ghosts = (swap(u_0, "gx", 0), swap(u_1, "gx", 1), swap(w_0, "gz", 0), swap(w_1, "gz", 1))
    pieces = divergence(sizes, counts[1], change, ghosts)
    pieces = exchange(pieces, "gz")
    pieces = transform_z(sizes, counts, table_z(length_z, counts[0]), pieces)
    pieces = exchange(pieces, "gx")
    scale = 1.0 / math.sqrt(length_x * length_z)
    source = transform_x(sizes, counts, table_x(length_x, scale), pieces)
    return velocity, source


def solution(mesh):
    return jax.shard_map(
        on_device,
        mesh=mesh,
        in_specs=(
            P(None, "gx", "gz", None),
            P(("gx", "gz")),
            P(None, ("gx", "gz")),
            P(None, ("gx", "gz"), None),
            P(None, ("gx", "gz"), None),
            P(),
            P(),
        ),
        out_specs=(P(None, "gx", "gz", None), P(None, "gz", "gx", None)),
        check_vma=False,
    )
```

```python
import functools
import math

import jax
import jax.numpy as jnp
import numpy as np
from jax import lax
from jax.experimental import pallas as pl
from jax.experimental.pallas import tpu as pltpu
from jax.sharding import PartitionSpec as P


BOX = 24
HALF = 12
WINDOW = 32
LANES = 128
KERNEL_BYTES = 16 * 1024 * 1024

time_step = 0.1
viscosity = 0.2
drive_force = 1.0


IN_VMEM = pl.BlockSpec(memory_space=pltpu.VMEM)
IN_SMEM = pl.BlockSpec(memory_space=pltpu.SMEM)
TRANSPOSED = (((1,), (1,)), ((), ()))


def float32(*shape):
    return jax.ShapeDtypeStruct(shape, jnp.float32)


def call(kernel, out_shape, scalars, arrays, scratch, flops, moved):
    outputs = len(out_shape) if isinstance(out_shape, (list, tuple)) else 0
    return pl.pallas_call(
        kernel,
        out_shape=out_shape,
        in_specs=[IN_SMEM] * len(scalars) + [IN_VMEM] * len(arrays),
        out_specs=[IN_VMEM] * outputs if outputs else IN_VMEM,
        scratch_shapes=scratch,
        compiler_params=pltpu.CompilerParams(vmem_limit_bytes=KERNEL_BYTES),
        cost_estimate=pl.CostEstimate(flops=flops, bytes_accessed=moved, transcendentals=0),
    )(*scalars, *arrays)


def swap(array, axis, partner):
    devices = lax.axis_size(axis)
    pairs = [(i, (i + (1 if i % 2 == partner else -1)) % devices) for i in range(devices)]
    return lax.ppermute(array, axis, pairs)


def even(axis):
    return lax.rem(lax.axis_index(axis), 2) == 0


def steps(devices):
    return [0, *range(devices - 1, 0, -1)]


def in_order(axis, shape):
    parity = jnp.full(shape, lax.rem(lax.axis_index(axis), 2), jnp.int32)
    return lambda one, two: (
        jnp.where(parity == 0, two, one),
        jnp.where(parity == 0, one, two),
    )


def cosine_coefficients():
    samples = 2.0 + 2.0 * np.cos(np.pi * (np.arange(64) + 0.5) / 64)
    values = np.cos(np.pi / 4 * np.sqrt(samples)) * np.sqrt(0.5)
    fit = np.polynomial.chebyshev.Chebyshev.fit(samples, values, 4, domain=[0, 4])
    return [float(v) for v in fit.convert(kind=np.polynomial.Polynomial).coef]


COSINE = cosine_coefficients()


def weight(offset):
    square = jnp.minimum(offset * offset, 4.0)
    value = COSINE[-1] * square + COSINE[-2]
    for coefficient in COSINE[-3::-1]:
        value = value * square + coefficient
    return value * value


def split(value):
    high = value.astype(jnp.bfloat16)
    low = (value - high.astype(jnp.float32)).astype(jnp.bfloat16)
    return high, low


def row_weights(count, position):
    cells = lax.broadcasted_iota(jnp.int32, (count, position.shape[1]), 0)
    return weight(cells.astype(jnp.float32) - position)


def plane_weights(weight_x, weight_z, half_z, high, low):
    count = 0
    for z in range(0, weight_z.shape[0], half_z):
        part = weight_z[z : z + half_z]
        for x in range(weight_x.shape[0]):
            rows = slice(count * half_z, (count + 1) * half_z)
            high[rows], low[rows] = split(weight_x[x : x + 1] * part)
            count += 1


def window_start(first_y, size_y):
    return pl.multiple_of(jnp.minimum((first_y // 8) * 8, size_y - WINDOW), 8)


def quarters(sizes):
    half_x, half_z = sizes[0] // 2, sizes[1] // 2
    for z in range(2):
        for x in range(2):
            yield slice(x * half_x, (x + 1) * half_x), slice(z * half_z, (z + 1) * half_z)


class Layout:
    def __init__(self, sizes, slots, markers):
        self.sizes, self.slots, self.markers = sizes, slots, markers
        self.tiles = markers // LANES
        self.fact_row = 3 * self.tiles * slots
        self.rows = self.fact_row + slots
        self.ghost_x = 4 * sizes[1]
        self.ghost_z = 4 * sizes[0]
        self.plane = sizes[0] * sizes[1]


def marker_row(layout, marks, base, direction, slot):
    first = base + direction * layout.tiles * layout.slots + slot
    rows = [marks[pl.ds(first + t * layout.slots, 1), :] for t in range(layout.tiles)]
    return jnp.concatenate(rows, axis=1)


def slot_visits(layout, facts, marks, saved, blocks, step, high, low, visit, skip):
    size_x, size_z, size_y = layout.sizes
    half_x, half_z = size_x // 2, size_z // 2
    slots = layout.slots

    def body(index, carry):
        block, slot = index // slots, index % slots
        block = blocks[0] + block * (blocks[1] - blocks[0] if len(blocks) > 1 else 0)
        fact = (step * 3 + block) * slots + slot
        first_x = facts[0, fact]
        first_z = facts[1, fact]
        first_y = facts[2, fact]
        meets_x = (first_x > -BOX) & (first_x < size_x)
        meets_z = (first_z > -BOX) & (first_z < size_z)
        active = (facts[3, fact] != 0) & meets_x & meets_z
        whole_x = (first_x > half_x - BOX) & (first_x < half_x)
        whole_z = (first_z > half_z - BOX) & (first_z < half_z)
        upper_x = (first_x >= half_x).astype(jnp.int32)
        upper_z = (first_z >= half_z).astype(jnp.int32)

        def part(all_x, all_z):
            start_x = 0 if all_x else upper_x * half_x
            start_z = 0 if all_z else upper_z * half_z
            lanes = [
                ((0 if all_z else upper_z) + z) * 2 * LANES + (0 if all_x else upper_x) * LANES
                for z in range(2 if all_z else 1)
            ]
            width = (2 if all_x else 1) * LANES
            if all_x and all_z:
                pieces = [(0, 4 * LANES)]
            else:
                pieces = [(pl.multiple_of(lane, LANES), width) for lane in lanes]
            first = window_start(first_y, size_y)
            rows_x = slice(0, size_x if all_x else half_x)
            rows_z = slice(size_x, size_x + (size_z if all_z else half_z))
            rows_y = slice(size_x + size_z, size_x + size_z + WINDOW)
            if marks is not None:
                base = block * layout.rows
                starts = (first_x - start_x, first_z - start_z, first_y - first)
                for direction, rows in enumerate((rows_x, rows_z, rows_y)):
                    position = marker_row(layout, marks, base, direction, slot)
                    position += starts[direction].astype(jnp.float32)
                    saved[index, rows, :] = row_weights(rows.stop - rows.start, position)
            plane_weights(saved[index, rows_x, :], saved[index, rows_z, :], half_z, high, low)
            weight_y = saved[index, rows_y, :]
            visit(index, block * slots + slot, first, weight_y, pieces)

        for all_x in (True, False):
            for all_z in (True, False):
                one = whole_x if all_x else jnp.logical_not(whole_x)
                two = whole_z if all_z else jnp.logical_not(whole_z)
                pl.when(active & one & two)(functools.partial(part, all_x, all_z))

        if skip is not None:

            @pl.when(jnp.logical_not(active))
            def _():
                skip(index)

        return carry

    lax.fori_loop(0, len(blocks) * slots, body, 0)


def rigid_motion(layout, facts, marks, motion, block, slot):
    particle = facts[3, (3 + block) * layout.slots + slot] - 1
    chosen = lax.broadcasted_iota(jnp.int32, motion[0].shape, 1) == particle
    moving, turning = [
        jnp.sum(jnp.where(chosen, part[...], 0.0), axis=1, keepdims=True) for part in motion
    ]
    lever = [
        marker_row(layout, marks, block * layout.rows, direction, slot) - HALF
        for direction in (0, 2, 1)
    ]
    for c in range(3):
        a, b = (c + 1) % 3, (c + 2) % 3
        turned = turning[a : a + 1] * lever[b] - turning[b : b + 1] * lever[a]
        yield moving[c : c + 1] + turned


def sample_slots(
    layout, facts, marks, motion, field_high, field_low, out, saved, blocks, step, high, low
):
    def visit(index, row, first, weight_y, pieces):
        rows = pl.ds(first, WINDOW)

        def window(field):
            parts = [
                jnp.concatenate([field[c, rows, pl.ds(lane, width)] for c in range(3)], axis=0)
                for lane, width in pieces
            ]
            return jnp.concatenate(parts, axis=1).astype(jnp.bfloat16)

        window_high, window_low = window(field_high), window(field_low)
        count = window_high.shape[1]
        both = jnp.concatenate([window_high, window_low], axis=0)
        value = jnp.dot(both, high[:count], preferred_element_type=jnp.float32)
        rest = jnp.dot(window_high, low[:count], preferred_element_type=jnp.float32)
        value = value[: 3 * WINDOW] + value[3 * WINDOW :] + rest
        target = None
        if motion:
            target = list(rigid_motion(layout, facts, marks, motion, blocks[0], index))
        for c in range(3):
            part = value[c * WINDOW : (c + 1) * WINDOW] * weight_y
            sampled = jnp.sum(part, axis=0, keepdims=True)
            out[c, pl.ds(index, 1), :] = sampled if target is None else target[c] - sampled

    def skip(index):
        for c in range(3):
            out[c, pl.ds(index, 1), :] = jnp.zeros((1, layout.markers), jnp.float32)

    slot_visits(layout, facts, marks, saved, blocks, step, high, low, visit, skip)


def sample_kernel(layout, groups, moved, facts, *refs):
    count = len(groups)
    marks, refs = refs[:count], refs[count:]
    (field_high, field_low), refs = refs[:2], refs[2:]
    motion, refs = refs[:moved], refs[moved:]
    outs, refs = refs[:count], refs[count:]
    saved, (high, low) = refs[:count], refs[count:]
    for i, (blocks, step) in enumerate(groups):
        sample_slots(
            layout,
            facts,
            marks[i],
            motion,
            field_high,
            field_low,
            outs[i],
            saved[i],
            blocks,
            step,
            high,
            low,
        )


def visit_cost(layout, blocks):
    return len(blocks) * layout.slots * 18 * WINDOW * layout.plane * layout.markers


def weight_scratch(layout):
    return [pltpu.VMEM((layout.plane, layout.markers), jnp.bfloat16)] * 2


def sample(layout, groups, facts, marks, fields, motion):
    markers, weights = layout.markers, layout.sizes[0] + layout.sizes[1] + WINDOW
    counts = [len(blocks) * layout.slots for blocks, _ in groups]
    results = call(
        functools.partial(sample_kernel, layout, groups, len(motion)),
        [float32(3, count, markers) for count in counts]
        + [float32(count, weights, markers) for count in counts],
        [facts],
        [*marks, *fields, *motion],
        weight_scratch(layout),
        sum(visit_cost(layout, blocks) for blocks, _ in groups),
        8 * fields[0].size,
    )
    return results[: len(groups)], results[len(groups) :]


def spread_slots(layout, blocks, step, facts, saved, push, own_rows, total, high, low):
    def visit(index, row, first, weight_y, pieces):
        slot = index if own_rows else row
        count = sum(width for _, width in pieces)
        value = jnp.concatenate(
            [weight_y * push[c, pl.ds(slot, 1), :] for c in range(3)], axis=0
        )
        value_high, value_low = split(value)
        both = jnp.concatenate([value_high, value_low], axis=0)
        added = lax.dot_general(
            both, high[:count], TRANSPOSED, preferred_element_type=jnp.float32
        )
        rest = lax.dot_general(
            value_high, low[:count], TRANSPOSED, preferred_element_type=jnp.float32
        )
        added = added[: 3 * WINDOW] + added[3 * WINDOW :] + rest
        column = 0
        for lane, width in pieces:
            for c in range(3):
                part = added[c * WINDOW : (c + 1) * WINDOW, column : column + width]
                total[c, pl.ds(first, WINDOW), pl.ds(lane, width)] += part
            column += width

    slot_visits(layout, facts, None, saved, blocks, step, high, low, visit, None)


def spread_own_kernel(layout, facts, saved, push, total, high, low):
    total[...] = jnp.zeros(total.shape, jnp.float32)
    spread_slots(layout, (1,), 1, facts, saved, push, True, total, high, low)


def spread_own(layout, facts, saved, push):
    return call(
        functools.partial(spread_own_kernel, layout),
        float32(3, layout.sizes[2], layout.plane),
        [facts],
        [saved, push],
        weight_scratch(layout),
        visit_cost(layout, (1,)),
        12 * layout.sizes[2] * layout.plane,
    )


def spread_side_kernel(layout, facts, saved, push, before, total, high, low):
    total[...] = before[...]
    spread_slots(layout, (0, 2), 1, facts, saved, push, False, total, high, low)


def spread_side(layout, facts, saved, push, before):
    return call(
        functools.partial(spread_side_kernel, layout),
        float32(*before.shape),
        [facts],
        [saved, push, before],
        weight_scratch(layout),
        visit_cost(layout, (0, 2)),
        8 * before.size,
    )


def spread_rest_kernel(
    layout,
    facts,
    saved_0,
    saved_1,
    push_0,
    push_1,
    before,
    predicted,
    velocity,
    u_0,
    u_1,
    w_0,
    w_1,
    inner,
    total,
    high,
    low,
):
    size_x, size_z, size_y = layout.sizes
    total[...] = before[...]
    row = (0, 1, 2)
    spread_slots(layout, row, 0, facts, saved_0, push_0, False, total, high, low)
    spread_slots(layout, row, 2, facts, saved_1, push_1, False, total, high, low)
    for c in range(3):
        for q, (xs, zs) in enumerate(quarters(layout.sizes)):
            part = jnp.transpose(total[c, :, q * LANES : (q + 1) * LANES])
            part = part.reshape(size_x // 2, size_z // 2, size_y)
            velocity[c, xs, zs] = predicted[c, xs, zs] + part
    last = jnp.where(even("gx"), size_x - 1, 0)
    u_0[...] = velocity[0, last]
    u_1[...] = velocity[0, size_x - 1 - last]
    choose = in_order("gz", (1, size_y))
    for x in range(size_x):
        first, last = velocity[2, x, 0:1], velocity[2, x, size_z - 1 : size_z]
        w_0[x : x + 1], w_1[x : x + 1] = choose(first, last)
    row = lax.broadcasted_iota(jnp.int32, (size_z, size_y), 0)
    lane = lax.broadcasted_iota(jnp.int32, (size_z, size_y), 1)
    for x in range(size_x):
        y_minus, y_plus = y_neighbours(velocity[1, x], lane, 0.0, 0.0)
        z_minus, z_plus = z_neighbours(velocity[2, x], row, 0.0, 0.0)
        change = y_plus - y_minus + z_plus - z_minus
        if x > 0:
            change -= velocity[0, x - 1]
        if x < size_x - 1:
            change += velocity[0, x + 1]
        inner[x] = change * 0.5


def spread_rest(layout, facts, saved, pushes, before, predicted):
    size_x, size_z, size_y = layout.sizes
    return call(
        functools.partial(spread_rest_kernel, layout),
        [float32(3, size_x, size_z, size_y)]
        + [float32(size_z, size_y)] * 2
        + [float32(size_x, size_y)] * 2
        + [float32(size_x, size_z, size_y)],
        [facts],
        [*saved, *pushes, before, predicted],
        [pltpu.VMEM(before.shape, jnp.float32)] + weight_scratch(layout),
        2 * visit_cost(layout, (0, 1, 2)),
        12 * before.size,
    )


def pack_kernel(
    layout,
    slot_ids_hbm,
    corners_hbm,
    flow,
    cells_hbm,
    fraction_hbm,
    own,
    x_0,
    x_1,
    z_0,
    z_1,
    slot_ids,
    corners,
    cells,
    fraction,
    edges,
    done,
):
    size_x, size_z, size_y = layout.sizes
    slots = layout.slots
    moves = [
        (slot_ids_hbm, slot_ids),
        (corners_hbm, corners),
        (cells_hbm, cells),
        (fraction_hbm, fraction),
    ]
    for c in range(4):
        moves.append((flow.at[c, :, pl.ds(size_z - 8, 8)], edges.at[0, c]))
        moves.append((flow.at[c, :, pl.ds(0, 8)], edges.at[1, c]))
    last = jnp.where(even("gx"), size_x - 1, 0)
    for c in range(4):
        rows = pl.ds(c * size_z, size_z)
        moves.append((flow.at[c, last], x_0.at[rows]))
        moves.append((flow.at[c, size_x - 1 - last], x_1.at[rows]))
    copies = [pltpu.make_async_copy(a, b, done.at[i]) for i, (a, b) in enumerate(moves)]
    for copy in copies:
        copy.start()
    for copy in copies[:4]:
        copy.wait()
    length_x = size_x * lax.axis_size("gx")
    length_z = size_z * lax.axis_size("gz")
    offset_x = length_x + HALF - lax.axis_index("gx") * size_x
    offset_z = length_z + HALF - lax.axis_index("gz") * size_z
    targets = ((own, 0), (z_0, layout.ghost_z), (z_1, layout.ghost_z))
    for a, direction in enumerate((0, 2, 1)):
        for t in range(layout.tiles):
            lanes = slice(t * LANES, (t + 1) * LANES)
            place = cells[direction, :, lanes].astype(jnp.float32) + fraction[direction, :, lanes]
            for target, base in targets:
                first = base + (a * layout.tiles + t) * slots
                target[first : first + slots] = place
    lane = lax.broadcasted_iota(jnp.int32, (1, LANES), 1)
    for slot in range(slots):
        first_x = lax.rem(corners[0, slot] + offset_x, length_x) - HALF
        first_z = lax.rem(corners[2, slot] + offset_z, length_z) - HALF
        fact = jnp.where(lane == 0, first_x, slot_ids[slot] + 1)
        fact = jnp.where(lane == 1, first_z, fact)
        fact = jnp.where(lane == 2, corners[1, slot], fact)
        for target, base in targets:
            row = base + layout.fact_row + slot
            target[row : row + 1] = fact.astype(jnp.float32)
    for copy in copies[4:]:
        copy.wait()
    choose = in_order("gz", (1, size_y))
    for c in range(4):
        for x in range(size_x):
            row = c * size_x + x
            z_0[row : row + 1], z_1[row : row + 1] = choose(
                edges[1, c, x, 0:1], edges[0, c, x, 7:8]
            )


def pack(layout, slot_ids, corners, flow, cells, fraction):
    in_hbm = pl.BlockSpec(memory_space=pltpu.HBM)
    size_x, _, size_y = layout.sizes
    return pl.pallas_call(
        functools.partial(pack_kernel, layout),
        out_shape=[float32(layout.rows, LANES)]
        + [float32(layout.ghost_x, LANES)] * 2
        + [float32(layout.ghost_z + layout.rows, LANES)] * 2,
        in_specs=[in_hbm] * 5,
        out_specs=[IN_VMEM] * 5,
        scratch_shapes=[
            pltpu.SMEM(slot_ids.shape, jnp.int32),
            pltpu.SMEM(corners.shape, jnp.int32),
            pltpu.VMEM(cells.shape, jnp.int32),
            pltpu.VMEM(fraction.shape, jnp.float32),
            pltpu.VMEM((2, 4, size_x, 8, size_y), jnp.float32),
            pltpu.SemaphoreType.DMA((20,)),
        ],
        name="pack",
        cost_estimate=pl.CostEstimate(
            flops=flow.size, bytes_accessed=flow.size, transcendentals=0
        ),
    )(slot_ids, corners, flow, cells, fraction)


def join_kernel(left, right, both):
    rows = left.shape[0]
    both[:rows] = left[...]
    both[rows:] = right[...]


def join(left, right):
    return call(
        join_kernel,
        float32(2 * left.shape[0], LANES),
        [],
        [left, right],
        [],
        left.size,
        16 * left.size,
    )


def collect_kernel(layout, own, side_0, side_1, one, two, corners_0, corners_1, *refs):
    rows, (facts, table) = refs[:3], refs[3:]
    count, slots = layout.rows, layout.slots
    size_x, size_z, _ = layout.sizes
    for row, middle, base, sides in (
        (rows[0], one, layout.ghost_z, corners_0),
        (rows[1], own, 0, None),
        (rows[2], two, layout.ghost_z, corners_1),
    ):
        row[:count] = side_0[...] if sides is None else sides[:count]
        row[count : 2 * count] = middle[base : base + count]
        row[2 * count :] = side_1[...] if sides is None else sides[count:]
    for block in range(9):
        first = (block % 3) * count + layout.fact_row
        out = slice(block * slots, (block + 1) * slots)
        table[out] = rows[block // 3][first : first + slots]
    kind = lax.broadcasted_iota(jnp.int32, (8, LANES), 0)
    slot = lax.broadcasted_iota(jnp.int32, (8, LANES), 1)
    last = 2 * 3 * slots
    move_x = jnp.where(even("gx"), size_x, -size_x)
    move_z = jnp.where(even("gz"), size_z, -size_z)
    place = slot - jnp.where(slot >= last, last, jnp.where(slot >= 3 * slots, 3 * slots, 0))
    moved_x = jnp.where(place < slots, move_x, jnp.where(place >= 2 * slots, -move_x, 0))
    moved_z = jnp.where(slot < 3 * slots, move_z, jnp.where(slot >= last, -move_z, 0))
    moved = jnp.where(kind == 0, moved_x, jnp.where(kind == 1, moved_z, 0))
    facts[...] = jnp.transpose(table[...])[:8].astype(jnp.int32) + moved


def collect(layout, *tiles):
    return call(
        functools.partial(collect_kernel, layout),
        [float32(3 * layout.rows, LANES)] * 3 + [jax.ShapeDtypeStruct((8, LANES), jnp.int32)],
        [],
        tiles,
        [pltpu.VMEM((LANES, LANES), jnp.float32)],
        layout.rows * LANES,
        72 * layout.rows * LANES,
    )


def y_neighbours(value, lane, below, above):
    size_y = value.shape[-1]
    minus = jnp.where(lane == 0, below, pltpu.roll(value, 1, 1))
    plus = jnp.where(lane == size_y - 1, above, pltpu.roll(value, size_y - 1, 1))
    return minus, plus


def z_neighbours(value, row, below, above):
    size_z = value.shape[0]
    minus = jnp.where(row == 0, below, pltpu.roll(value, 1, 0))
    plus = jnp.where(row == size_z - 1, above, pltpu.roll(value, size_z - 1, 0))
    return minus, plus


def predict_inner_kernel(sizes, flow, own, inner, u_first, u_last, w_first, w_last, kept):
    size_x, size_z, size_y = sizes
    row = lax.broadcasted_iota(jnp.int32, (size_z, size_y), 0)
    lane = lax.broadcasted_iota(jnp.int32, (size_z, size_y), 1)
    nothing = jnp.zeros((size_z, size_y), jnp.float32)

    def around(c, x):
        value = flow[c, x]
        x_minus = flow[c, x - 1] if x > 0 else nothing
        x_plus = flow[c, x + 1] if x < size_x - 1 else nothing
        z_minus, z_plus = z_neighbours(value, row, 0.0, 0.0)
        edges = (0.0, 0.0) if c < 3 else (value, value)
        y_minus, y_plus = y_neighbours(value, lane, *edges)
        return value, x_minus, x_plus, z_minus, z_plus, y_minus, y_plus

    for x in range(size_x):
        _, x_minus, x_plus, z_minus, z_plus, y_minus, y_plus = around(3, x)
        gradient = (
            (x_plus - x_minus) * 0.5 - drive_force,
            (y_plus - y_minus) * 0.5,
            (z_plus - z_minus) * 0.5,
        )
        carried = (flow[0, x], flow[1, x], flow[2, x])
        for c in range(3):
            value, x_minus, x_plus, z_minus, z_plus, y_minus, y_plus = around(c, x)
            laplace = x_plus + x_minus + z_plus + z_minus + y_plus + y_minus - 6.0 * value
            advect = (
                carried[0] * (x_plus - x_minus)
                + carried[1] * (y_plus - y_minus)
                + carried[2] * (z_plus - z_minus)
            ) * 0.5
            inner[c, x] = value + time_step * (viscosity * laplace - advect - gradient[c])
        w_first[x : x + 1] = flow[2, x, 0:1]
        w_last[x : x + 1] = flow[2, x, size_z - 1 : size_z]
    kept[...] = own[...]
    u_first[...] = flow[0, 0]
    u_last[...] = flow[0, size_x - 1]


def predict_inner(sizes, flow, own):
    size_x, size_z, size_y = sizes
    return call(
        functools.partial(predict_inner_kernel, sizes),
        [float32(3, *sizes)]
        + [float32(size_z, size_y)] * 2
        + [float32(size_x, size_y)] * 2
        + [float32(*own.shape)],
        [],
        [flow, own],
        [],
        200 * flow.size,
        8 * flow.size,
    )


def predict_outer_kernel(
    layout,
    inner,
    u_first,
    u_last,
    w_first,
    w_last,
    x_0,
    x_1,
    z_0,
    z_1,
    predicted,
    field_high,
    field_low,
):
    size_x, size_z, size_y = layout.sizes
    row = lax.broadcasted_iota(jnp.int32, (8, size_y), 0)
    lower, upper = in_order("gz", z_0[: layout.ghost_z].shape)(
        z_0[: layout.ghost_z], z_1[: layout.ghost_z]
    )
    left, right = in_order("gx", x_0.shape)(x_0[...], x_1[...])
    for x in range(size_x):
        carried_low = w_first[x : x + 1]
        carried_high = w_last[x : x + 1]
        for c in range(3):
            ghost = c * size_x + x
            change_low = (viscosity + 0.5 * carried_low) * lower[ghost : ghost + 1]
            change_high = (viscosity - 0.5 * carried_high) * upper[ghost : ghost + 1]
            if c == 2:
                ghost = 3 * size_x + x
                change_low += 0.5 * lower[ghost : ghost + 1]
                change_high -= 0.5 * upper[ghost : ghost + 1]
            if x in (0, size_x - 1):
                sign, layer, carried = (0.5, left, u_first) if x == 0 else (-0.5, right, u_last)
                ghost = slice(c * size_z, (c + 1) * size_z)
                change = (viscosity + sign * carried[...]) * layer[ghost]
                if c == 0:
                    change += sign * layer[3 * size_z : 4 * size_z]
                predicted[c, x] = inner[c, x] + time_step * change
            else:
                predicted[c, x] = inner[c, x]
            predicted[c, x, 0:8] += jnp.where(row == 0, time_step * change_low, 0.0)
            predicted[c, x, size_z - 8 : size_z] += jnp.where(
                row == 7, time_step * change_high, 0.0
            )
    for c in range(3):
        for q, (xs, zs) in enumerate(quarters(layout.sizes)):
            part = jnp.transpose(predicted[c, xs, zs].reshape(LANES, size_y))
            high = part.astype(jnp.bfloat16).astype(jnp.float32)
            field_high[c, :, q * LANES : (q + 1) * LANES] = high
            field_low[c, :, q * LANES : (q + 1) * LANES] = part - high


def predict_outer(layout, inner, *layers):
    _, _, size_y = layout.sizes
    return call(
        functools.partial(predict_outer_kernel, layout),
        [float32(3, *layout.sizes)] + [float32(3, size_y, layout.plane)] * 2,
        [],
        [*inner, *layers],
        [],
        10 * inner[0].size,
        16 * inner[0].size,
    )


def divergence_kernel(sizes, parts, inner, u_0, u_1, w_0, w_1, *rest):
    outs, whole = rest[:parts], rest[parts]
    size_x, size_z, size_y = sizes
    row = lax.broadcasted_iota(jnp.int32, (size_z, size_y), 0)
    group = LANES // size_z
    u_below, u_above = in_order("gx", u_0.shape)(u_0[...], u_1[...])
    w_below, w_above = in_order("gz", w_0.shape)(w_0[...], w_1[...])
    for q in range(size_x // group):
        pieces = []
        for x in range(q * group, (q + 1) * group):
            piece = inner[x]
            if x == 0:
                piece -= 0.5 * u_below
            if x == size_x - 1:
                piece += 0.5 * u_above
            piece -= jnp.where(row == 0, 0.5 * w_below[x : x + 1], 0.0)
            piece += jnp.where(row == size_z - 1, 0.5 * w_above[x : x + 1], 0.0)
            pieces.append(piece)
        part = jnp.concatenate(pieces, axis=0)
        whole[:, q * LANES : (q + 1) * LANES] = jnp.transpose(part)
    height = size_y // parts
    for out, step in zip(outs, steps(parts)):
        first = pl.multiple_of((lax.axis_index("gz") ^ step) * height, 8)
        out[...] = whole[pl.ds(first, height), :]


def divergence(sizes, parts, inner, ghosts):
    size_x, size_z, size_y = sizes
    plane = size_x * size_z
    return call(
        functools.partial(divergence_kernel, sizes, parts),
        [float32(size_y // parts, plane)] * parts,
        [],
        [inner, *ghosts],
        [pltpu.VMEM((size_y, plane), jnp.float32)],
        10 * inner.size,
        8 * inner.size,
    )


def swap_groups(values, width):
    count = LANES // width
    lane = lax.broadcasted_iota(jnp.int32, values[0].shape, 1)
    values = list(values)
    step = count // 2
    while step:
        reach = step * width
        keep = lane % (2 * reach) < reach
        for i in range(count):
            if i & step == 0:
                a, b = values[i], values[i + step]
                values[i] = jnp.where(keep, a, pltpu.roll(b, reach, 1))
                values[i + step] = jnp.where(keep, pltpu.roll(a, LANES - reach, 1), b)
        step //= 2
    return values


def transform_z_kernel(sizes, counts, table_high, table_low, *refs):
    size_x, size_z, size_y = sizes
    parts_x, parts_z = counts
    pieces, refs = refs[:parts_z], refs[parts_z:]
    outs, (gathered, turned, whole) = refs[:parts_x], refs[parts_x:]
    height = size_y // parts_z
    group = LANES // size_z
    for piece, step in zip(pieces, steps(parts_z)):
        gathered[lax.axis_index("gz") ^ step] = piece[...]
    for block in range(parts_z // group):
        for q in range(size_x // group):
            lanes = slice(q * LANES, (q + 1) * LANES)
            values = [gathered[block * group + i, :, lanes] for i in range(group)]
            for j, value in enumerate(swap_groups(values, size_z)):
                turned[block, pl.ds(q * group + j, height, stride=size_x), :] = value
    lines = jnp.concatenate([turned[b] for b in range(turned.shape[0])], axis=1)
    high, low = split(lines)
    result = lax.dot_general(
        table_high[...], high, TRANSPOSED, preferred_element_type=jnp.float32
    )
    result += lax.dot_general(
        table_low[...], high, TRANSPOSED, preferred_element_type=jnp.float32
    )
    result += lax.dot_general(
        table_high[...], low, TRANSPOSED, preferred_element_type=jnp.float32
    )
    whole[...] = result
    rows = whole.shape[0] // parts_x
    for out, step in zip(outs, steps(parts_x)):
        first = pl.multiple_of((lax.axis_index("gx") ^ step) * rows, 8)
        out[...] = whole[pl.ds(first, rows), :]


def transform_z(sizes, counts, table, pieces):
    size_x, size_z, size_y = sizes
    parts_x, parts_z = counts
    length_z = size_z * parts_z
    height = size_y // parts_z
    columns = height * size_x
    return call(
        functools.partial(transform_z_kernel, sizes, counts),
        [float32(2 * length_z // parts_x, columns)] * parts_x,
        [],
        [*table, *pieces],
        [
            pltpu.VMEM((parts_z, height, size_x * size_z), jnp.float32),
            pltpu.VMEM((length_z // LANES, columns, LANES), jnp.float32),
            pltpu.VMEM((2 * length_z, columns), jnp.float32),
        ],
        12 * length_z * length_z * columns,
        12 * length_z * columns,
    )


def transform_x_kernel(sizes, counts, table_high, table_low, *refs):
    size_x, size_z, size_y = sizes
    parts_x, parts_z = counts
    pieces, (source, gathered, turned) = refs[:parts_x], refs[parts_x:]
    length_x = size_x * parts_x
    modes = size_z * parts_z // parts_x
    height = size_y // parts_z
    group = LANES // size_x
    for piece, step in zip(pieces, steps(parts_x)):
        gathered[lax.axis_index("gx") ^ step] = piece[...]
    for block in range(parts_x // group):
        for q in range(height // group):
            lanes = slice(q * LANES, (q + 1) * LANES)
            values = [gathered[block * group + i, :, lanes] for i in range(group)]
            for j, value in enumerate(swap_groups(values, size_x)):
                first = (q * group + j) * modes
                for c in range(2):
                    column = c * length_x + block * LANES
                    turned[first : first + modes, column : column + LANES] = value[
                        c * modes : (c + 1) * modes
                    ]
    high, low = split(turned[...])
    result = jnp.dot(high, table_high[...], preferred_element_type=jnp.float32)
    result += jnp.dot(low, table_high[...], preferred_element_type=jnp.float32)
    result += jnp.dot(high, table_low[...], preferred_element_type=jnp.float32)
    source[0] = result[:, :length_x].reshape(height, modes, length_x)
    source[1] = result[:, length_x:].reshape(height, modes, length_x)


def transform_x(sizes, counts, table, pieces):
    size_x, size_z, size_y = sizes
    parts_x, parts_z = counts
    length_x = size_x * parts_x
    modes = size_z * parts_z // parts_x
    height = size_y // parts_z
    return call(
        functools.partial(transform_x_kernel, sizes, counts),
        float32(2, height, modes, length_x),
        [],
        [*table, *pieces],
        [
            pltpu.VMEM((parts_x, *pieces[0].shape), jnp.float32),
            pltpu.VMEM((height * modes, 2 * length_x), jnp.float32),
        ],
        24 * length_x * length_x * height * modes,
        24 * length_x * height * modes,
    )


def split_table(table):
    high = table.astype(np.float32).astype(jnp.bfloat16)
    low = (table - high.astype(np.float64)).astype(np.float32).astype(jnp.bfloat16)
    return jnp.asarray(high), jnp.asarray(low)


def angles(length):
    counter = np.arange(length)
    turn = (counter[:, None] * counter[None, :] % length) * (2.0 * np.pi / length)
    return np.cos(turn), np.sin(turn)


def table_z(length, blocks):
    cosine, sine = angles(length)
    modes = length // blocks
    table = np.stack([cosine, -sine]).reshape(2, blocks, modes, length)
    return split_table(table.transpose(1, 0, 2, 3).reshape(2 * length, length))


def table_x(length, scale):
    cosine, sine = angles(length)
    return split_table(np.block([[cosine, -sine], [sine, cosine]]) * scale)


def exchange(pieces, axis):
    devices = lax.axis_size(axis)
    assert devices & (devices - 1) == 0
    return [pieces[0]] + [
        lax.ppermute(piece, axis, [(i, i ^ step) for i in range(devices)])
        for piece, step in zip(pieces[1:], steps(devices)[1:])
    ]


def on_device(
    flow_state, slot_ids, corners, marker_cells, marker_frac, particle_velocity, particle_spin
):
    sizes = flow_state.shape[1:]
    size_x, size_z, _ = sizes
    counts = (lax.axis_size("gx"), lax.axis_size("gz"))
    length_x, length_z = (size_x * counts[0], size_z * counts[1])
    slots, markers = marker_cells.shape[1:]
    layout = Layout(sizes, slots, markers)

    own, x_0, x_1, z_0, z_1 = pack(
        layout, slot_ids, corners, flow_state, marker_cells, marker_frac
    )
    marks_0 = swap(own, "gx", 0)
    marks_1 = swap(own, "gx", 1)
    z_0, z_1 = swap(z_0, "gz", 0), swap(z_1, "gz", 1)
    x_0, x_1 = swap(x_0, "gx", 0), swap(x_1, "gx", 1)
    *inner, own = predict_inner(sizes, flow_state, own)
    sides = join(marks_0, marks_1)
    corners_0, corners_1 = swap(sides, "gz", 0), swap(sides, "gz", 1)
    predicted, *fields = predict_outer(layout, inner, x_0, x_1, z_0, z_1)
    row_0, row, row_1, facts = collect(
        layout, own, marks_0, marks_1, z_0, z_1, corners_0, corners_1
    )

    tiles = (0, 1, 2)
    parts, rows_saved = sample(layout, ((tiles, 0), (tiles, 2)), facts, (row_0, row_1), fields, ())
    from_z = swap(parts[0], "gz", 0) + swap(parts[1], "gz", 1)
    (side_part,), (side_saved,) = sample(layout, (((0, 2), 1),), facts, (row,), fields, ())
    from_0 = swap(side_part[:, :slots] + from_z[:, :slots], "gx", 0)
    from_1 = swap(side_part[:, slots:] + from_z[:, 2 * slots :], "gx", 1)
    motion = (particle_velocity, particle_spin)
    (own_part,), (own_saved,) = sample(layout, (((1,), 1),), facts, (row,), fields, motion)
    push = own_part - (from_z[:, slots : 2 * slots] + from_0 + from_1)

    row_push = jnp.concatenate([swap(push, "gx", 0), push, swap(push, "gx", 1)], axis=1)
    rows_push = swap(row_push, "gz", 0), swap(row_push, "gz", 1)
    forcing = spread_own(layout, facts, own_saved, push)
    forcing = spread_side(layout, facts, side_saved, row_push, forcing)
    velocity, u_0, u_1, w_0, w_1, change = spread_rest(
        layout, facts, rows_saved, rows_push, forcing, predicted
    )

    ghosts = (swap(u_0, "gx", 0), swap(u_1, "gx", 1), swap(w_0, "gz", 0), swap(w_1, "gz", 1))
    pieces = divergence(sizes, counts[1], change, ghosts)
    pieces = exchange(pieces, "gz")
    pieces = transform_z(sizes, counts, table_z(length_z, counts[0]), pieces)
    pieces = exchange(pieces, "gx")
    scale = 1.0 / math.sqrt(length_x * length_z)
    source = transform_x(sizes, counts, table_x(length_x, scale), pieces)
    return velocity, source


def solution(mesh):
    return jax.shard_map(
        on_device,
        mesh=mesh,
        in_specs=(
            P(None, "gx", "gz", None),
            P(("gx", "gz")),
            P(None, ("gx", "gz")),
            P(None, ("gx", "gz"), None),
            P(None, ("gx", "gz"), None),
            P(),
            P(),
        ),
        out_specs=(P(None, "gx", "gz", None), P(None, "gz", "gx", None)),
        check_vma=False,
    )
```

```python
import functools
import math

import jax
import jax.numpy as jnp
import numpy as np
from jax import lax
from jax.experimental import pallas as pl
from jax.experimental.pallas import tpu as pltpu
from jax.sharding import PartitionSpec as P


BOX = 24
HALF = 12
WINDOW = 32
LANES = 128
KERNEL_BYTES = 16 * 1024 * 1024

time_step = 0.1
viscosity = 0.2
drive_force = 1.0


IN_VMEM = pl.BlockSpec(memory_space=pltpu.VMEM)
IN_SMEM = pl.BlockSpec(memory_space=pltpu.SMEM)
TRANSPOSED = (((1,), (1,)), ((), ()))


def float32(*shape):
    return jax.ShapeDtypeStruct(shape, jnp.float32)


def call(kernel, out_shape, scalars, arrays, scratch, flops, moved):
    outputs = len(out_shape) if isinstance(out_shape, (list, tuple)) else 0
    return pl.pallas_call(
        kernel,
        out_shape=out_shape,
        in_specs=[IN_SMEM] * len(scalars) + [IN_VMEM] * len(arrays),
        out_specs=[IN_VMEM] * outputs if outputs else IN_VMEM,
        scratch_shapes=scratch,
        compiler_params=pltpu.CompilerParams(vmem_limit_bytes=KERNEL_BYTES),
        cost_estimate=pl.CostEstimate(flops=flops, bytes_accessed=moved, transcendentals=0),
    )(*scalars, *arrays)


def swap(array, axis, partner):
    devices = lax.axis_size(axis)
    pairs = [(i, (i + (1 if i % 2 == partner else -1)) % devices) for i in range(devices)]
    return lax.ppermute(array, axis, pairs)


def even(axis):
    return lax.rem(lax.axis_index(axis), 2) == 0


def steps(devices):
    return [0, *range(devices - 1, 0, -1)]


def in_order(axis, shape):
    parity = jnp.full(shape, lax.rem(lax.axis_index(axis), 2), jnp.int32)
    return lambda one, two: (
        jnp.where(parity == 0, two, one),
        jnp.where(parity == 0, one, two),
    )


def cosine_coefficients():
    samples = 2.0 + 2.0 * np.cos(np.pi * (np.arange(64) + 0.5) / 64)
    values = np.cos(np.pi / 4 * np.sqrt(samples)) * np.sqrt(0.5)
    fit = np.polynomial.chebyshev.Chebyshev.fit(samples, values, 4, domain=[0, 4])
    return [float(v) for v in fit.convert(kind=np.polynomial.Polynomial).coef]


COSINE = cosine_coefficients()


def weight(offset):
    square = jnp.minimum(offset * offset, 4.0)
    value = COSINE[-1] * square + COSINE[-2]
    for coefficient in COSINE[-3::-1]:
        value = value * square + coefficient
    return value * value


def split(value):
    high = value.astype(jnp.bfloat16)
    low = (value - high.astype(jnp.float32)).astype(jnp.bfloat16)
    return high, low


def row_weights(count, position):
    cells = lax.broadcasted_iota(jnp.int32, (count, position.shape[1]), 0)
    return weight(cells.astype(jnp.float32) - position)


def plane_weights(weight_x, weight_z, half_z, high, low):
    count = 0
    for z in range(0, weight_z.shape[0], half_z):
        part = weight_z[z : z + half_z]
        for x in range(weight_x.shape[0]):
            rows = slice(count * half_z, (count + 1) * half_z)
            high[rows], low[rows] = split(weight_x[x : x + 1] * part)
            count += 1


def window_start(first_y, size_y):
    return pl.multiple_of(jnp.minimum((first_y // 8) * 8, size_y - WINDOW), 8)


def quarters(sizes):
    half_x, half_z = sizes[0] // 2, sizes[1] // 2
    for z in range(2):
        for x in range(2):
            yield slice(x * half_x, (x + 1) * half_x), slice(z * half_z, (z + 1) * half_z)


class Layout:
    def __init__(self, sizes, slots, markers):
        self.sizes, self.slots, self.markers = sizes, slots, markers
        self.tiles = markers // LANES
        self.fact_row = 3 * self.tiles * slots
        self.rows = self.fact_row + slots
        self.ghost_x = 4 * sizes[1]
        self.ghost_z = 4 * sizes[0]
        self.plane = sizes[0] * sizes[1]


def marker_row(layout, marks, base, direction, slot):
    first = base + direction * layout.tiles * layout.slots + slot
    rows = [marks[pl.ds(first + t * layout.slots, 1), :] for t in range(layout.tiles)]
    return jnp.concatenate(rows, axis=1)


def slot_visits(layout, facts, marks, saved, blocks, step, high, low, visit, skip):
    size_x, size_z, size_y = layout.sizes
    half_x, half_z = size_x // 2, size_z // 2
    slots = layout.slots

    def body(index, carry):
        block, slot = index // slots, index % slots
        block = blocks[0] + block * (blocks[1] - blocks[0] if len(blocks) > 1 else 0)
        fact = (step * 3 + block) * slots + slot
        first_x = facts[0, fact]
        first_z = facts[1, fact]
        first_y = facts[2, fact]
        meets_x = (first_x > -BOX) & (first_x < size_x)
        meets_z = (first_z > -BOX) & (first_z < size_z)
        active = (facts[3, fact] != 0) & meets_x & meets_z
        whole_x = (first_x > half_x - BOX) & (first_x < half_x)
        whole_z = (first_z > half_z - BOX) & (first_z < half_z)
        upper_x = (first_x >= half_x).astype(jnp.int32)
        upper_z = (first_z >= half_z).astype(jnp.int32)

        def part(all_x, all_z):
            start_x = 0 if all_x else upper_x * half_x
            start_z = 0 if all_z else upper_z * half_z
            lanes = [
                ((0 if all_z else upper_z) + z) * 2 * LANES + (0 if all_x else upper_x) * LANES
                for z in range(2 if all_z else 1)
            ]
            width = (2 if all_x else 1) * LANES
            if all_x and all_z:
                pieces = [(0, 4 * LANES)]
            else:
                pieces = [(pl.multiple_of(lane, LANES), width) for lane in lanes]
            first = window_start(first_y, size_y)
            rows_x = slice(0, size_x if all_x else half_x)
            rows_z = slice(size_x, size_x + (size_z if all_z else half_z))
            rows_y = slice(size_x + size_z, size_x + size_z + WINDOW)
            if marks is not None:
                base = block * layout.rows
                starts = (first_x - start_x, first_z - start_z, first_y - first)
                for direction, rows in enumerate((rows_x, rows_z, rows_y)):
                    position = marker_row(layout, marks, base, direction, slot)
                    position += starts[direction].astype(jnp.float32)
                    saved[index, rows, :] = row_weights(rows.stop - rows.start, position)
            plane_weights(saved[index, rows_x, :], saved[index, rows_z, :], half_z, high, low)
            weight_y = saved[index, rows_y, :]
            visit(index, block * slots + slot, first, weight_y, pieces)

        for all_x in (True, False):
            for all_z in (True, False):
                one = whole_x if all_x else jnp.logical_not(whole_x)
                two = whole_z if all_z else jnp.logical_not(whole_z)
                pl.when(active & one & two)(functools.partial(part, all_x, all_z))

        if skip is not None:

            @pl.when(jnp.logical_not(active))
            def _():
                skip(index)

        return carry

    lax.fori_loop(0, len(blocks) * slots, body, 0)


def rigid_motion(layout, facts, marks, motion, block, slot):
    particle = facts[3, (3 + block) * layout.slots + slot] - 1
    chosen = lax.broadcasted_iota(jnp.int32, motion[0].shape, 1) == particle
    moving, turning = [
        jnp.sum(jnp.where(chosen, part[...], 0.0), axis=1, keepdims=True) for part in motion
    ]
    lever = [
        marker_row(layout, marks, block * layout.rows, direction, slot) - HALF
        for direction in (0, 2, 1)
    ]
    for c in range(3):
        a, b = (c + 1) % 3, (c + 2) % 3
        turned = turning[a : a + 1] * lever[b] - turning[b : b + 1] * lever[a]
        yield moving[c : c + 1] + turned


def sample_slots(
    layout, facts, marks, motion, field_high, field_low, out, saved, blocks, step, high, low
):
    def visit(index, row, first, weight_y, pieces):
        rows = pl.ds(first, WINDOW)

        def window(field):
            parts = [
                jnp.concatenate([field[c, rows, pl.ds(lane, width)] for c in range(3)], axis=0)
                for lane, width in pieces
            ]
            return jnp.concatenate(parts, axis=1).astype(jnp.bfloat16)

        window_high, window_low = window(field_high), window(field_low)
        count = window_high.shape[1]
        both = jnp.concatenate([window_high, window_low], axis=0)
        value = jnp.dot(both, high[:count], preferred_element_type=jnp.float32)
        rest = jnp.dot(window_high, low[:count], preferred_element_type=jnp.float32)
        value = value[: 3 * WINDOW] + value[3 * WINDOW :] + rest
        target = None
        if motion:
            target = list(rigid_motion(layout, facts, marks, motion, blocks[0], index))
        for c in range(3):
            part = value[c * WINDOW : (c + 1) * WINDOW] * weight_y
            sampled = jnp.sum(part, axis=0, keepdims=True)
            out[c, pl.ds(index, 1), :] = sampled if target is None else target[c] - sampled

    def skip(index):
        for c in range(3):
            out[c, pl.ds(index, 1), :] = jnp.zeros((1, layout.markers), jnp.float32)

    slot_visits(layout, facts, marks, saved, blocks, step, high, low, visit, skip)


def sample_kernel(layout, groups, moved, facts, *refs):
    count = len(groups)
    marks, refs = refs[:count], refs[count:]
    (field_high, field_low), refs = refs[:2], refs[2:]
    motion, refs = refs[:moved], refs[moved:]
    outs, refs = refs[:count], refs[count:]
    saved, (high, low) = refs[:count], refs[count:]
    for i, (blocks, step) in enumerate(groups):
        sample_slots(
            layout,
            facts,
            marks[i],
            motion,
            field_high,
            field_low,
            outs[i],
            saved[i],
            blocks,
            step,
            high,
            low,
        )


def visit_cost(layout, blocks):
    return len(blocks) * layout.slots * 18 * WINDOW * layout.plane * layout.markers


def weight_scratch(layout):
    return [pltpu.VMEM((layout.plane, layout.markers), jnp.bfloat16)] * 2


def sample(layout, groups, facts, marks, fields, motion):
    markers, weights = layout.markers, layout.sizes[0] + layout.sizes[1] + WINDOW
    counts = [len(blocks) * layout.slots for blocks, _ in groups]
    results = call(
        functools.partial(sample_kernel, layout, groups, len(motion)),
        [float32(3, count, markers) for count in counts]
        + [float32(count, weights, markers) for count in counts],
        [facts],
        [*marks, *fields, *motion],
        weight_scratch(layout),
        sum(visit_cost(layout, blocks) for blocks, _ in groups),
        8 * fields[0].size,
    )
    return results[: len(groups)], results[len(groups) :]


def spread_slots(layout, blocks, step, facts, saved, push, own_rows, total, high, low):
    def visit(index, row, first, weight_y, pieces):
        slot = index if own_rows else row
        count = sum(width for _, width in pieces)
        value = jnp.concatenate(
            [weight_y * push[c, pl.ds(slot, 1), :] for c in range(3)], axis=0
        )
        value_high, value_low = split(value)
        both = jnp.concatenate([value_high, value_low], axis=0)
        added = lax.dot_general(
            both, high[:count], TRANSPOSED, preferred_element_type=jnp.float32
        )
        rest = lax.dot_general(
            value_high, low[:count], TRANSPOSED, preferred_element_type=jnp.float32
        )
        added = added[: 3 * WINDOW] + added[3 * WINDOW :] + rest
        column = 0
        for lane, width in pieces:
            for c in range(3):
                part = added[c * WINDOW : (c + 1) * WINDOW, column : column + width]
                total[c, pl.ds(first, WINDOW), pl.ds(lane, width)] += part
            column += width

    slot_visits(layout, facts, None, saved, blocks, step, high, low, visit, None)


def spread_own_kernel(layout, facts, saved, push, total, high, low):
    total[...] = jnp.zeros(total.shape, jnp.float32)
    spread_slots(layout, (1,), 1, facts, saved, push, True, total, high, low)


def spread_own(layout, facts, saved, push):
    return call(
        functools.partial(spread_own_kernel, layout),
        float32(3, layout.sizes[2], layout.plane),
        [facts],
        [saved, push],
        weight_scratch(layout),
        visit_cost(layout, (1,)),
        12 * layout.sizes[2] * layout.plane,
    )


def spread_side_kernel(layout, facts, saved, push, before, total, high, low):
    total[...] = before[...]
    spread_slots(layout, (0, 2), 1, facts, saved, push, False, total, high, low)


def spread_side(layout, facts, saved, push, before):
    return call(
        functools.partial(spread_side_kernel, layout),
        float32(*before.shape),
        [facts],
        [saved, push, before],
        weight_scratch(layout),
        visit_cost(layout, (0, 2)),
        8 * before.size,
    )


def spread_rest_kernel(
    layout, parts, facts, saved_0, saved_1, push_0, push_1, before, predicted, velocity, *refs
):
    outs, (total, high, low, edges, whole) = refs[:parts], refs[parts:]
    size_x, size_z, size_y = layout.sizes
    total[...] = before[...]
    row = (0, 1, 2)
    spread_slots(layout, row, 0, facts, saved_0, push_0, False, total, high, low)
    spread_slots(layout, row, 2, facts, saved_1, push_1, False, total, high, low)
    for c in range(3):
        for q, (xs, zs) in enumerate(quarters(layout.sizes)):
            part = jnp.transpose(total[c, :, q * LANES : (q + 1) * LANES])
            part = part.reshape(size_x // 2, size_z // 2, size_y)
            velocity[c, xs, zs] = predicted[c, xs, zs] + part
    row = lax.broadcasted_iota(jnp.int32, (size_z, size_y), 0)
    lane = lax.broadcasted_iota(jnp.int32, (size_z, size_y), 1)
    group = LANES // size_z
    for q in range(size_x // group):
        pieces = []
        for x in range(q * group, (q + 1) * group):
            y_minus, y_plus = y_neighbours(velocity[1, x], lane, 0.0, 0.0)
            z_minus, z_plus = z_neighbours(velocity[2, x], row, 0.0, 0.0)
            change = y_plus - y_minus + z_plus - z_minus
            if x > 0:
                change -= velocity[0, x - 1]
            if x < size_x - 1:
                change += velocity[0, x + 1]
            pieces.append(change * 0.5)
        part = jnp.concatenate(pieces, axis=0)
        whole[:, q * LANES : (q + 1) * LANES] = jnp.transpose(part)
    edges[...] = jnp.zeros(edges.shape, jnp.float32)
    edges[:size_z] = velocity[0, 0]
    edges[size_z : 2 * size_z] = velocity[0, size_x - 1]
    for x in range(size_x):
        first = 2 * size_z + 2 * x
        edges[first : first + 1] = velocity[2, x, 0:1]
        edges[first + 1 : first + 2] = velocity[2, x, size_z - 1 : size_z]
    whole[:, layout.plane :] = jnp.transpose(edges[...])
    height = size_y // parts
    for out, step in zip(outs, steps(parts)):
        first = pl.multiple_of((lax.axis_index("gz") ^ step) * height, 8)
        out[...] = whole[pl.ds(first, height), :]


def spread_rest(layout, parts, facts, saved, pushes, before, predicted):
    size_x, size_z, size_y = layout.sizes
    assert 2 * size_z + 2 * size_x <= LANES
    width = layout.plane + LANES
    velocity, *pieces = call(
        functools.partial(spread_rest_kernel, layout, parts),
        [float32(3, size_x, size_z, size_y)] + [float32(size_y // parts, width)] * parts,
        [facts],
        [*saved, *pushes, before, predicted],
        [pltpu.VMEM(before.shape, jnp.float32)]
        + weight_scratch(layout)
        + [pltpu.VMEM((LANES, size_y), jnp.float32), pltpu.VMEM((size_y, width), jnp.float32)],
        2 * visit_cost(layout, (0, 1, 2)),
        12 * before.size,
    )
    return velocity, pieces


def pack_kernel(
    layout,
    slot_ids_hbm,
    corners_hbm,
    flow,
    cells_hbm,
    fraction_hbm,
    own,
    x_0,
    x_1,
    z_0,
    z_1,
    slot_ids,
    corners,
    cells,
    fraction,
    edges,
    done,
):
    size_x, size_z, size_y = layout.sizes
    slots = layout.slots
    moves = [
        (slot_ids_hbm, slot_ids),
        (corners_hbm, corners),
        (cells_hbm, cells),
        (fraction_hbm, fraction),
    ]
    for c in range(4):
        moves.append((flow.at[c, :, pl.ds(size_z - 8, 8)], edges.at[0, c]))
        moves.append((flow.at[c, :, pl.ds(0, 8)], edges.at[1, c]))
    last = jnp.where(even("gx"), size_x - 1, 0)
    for c in range(4):
        rows = pl.ds(c * size_z, size_z)
        moves.append((flow.at[c, last], x_0.at[rows]))
        moves.append((flow.at[c, size_x - 1 - last], x_1.at[rows]))
    copies = [pltpu.make_async_copy(a, b, done.at[i]) for i, (a, b) in enumerate(moves)]
    for copy in copies:
        copy.start()
    for copy in copies[:4]:
        copy.wait()
    length_x = size_x * lax.axis_size("gx")
    length_z = size_z * lax.axis_size("gz")
    offset_x = length_x + HALF - lax.axis_index("gx") * size_x
    offset_z = length_z + HALF - lax.axis_index("gz") * size_z
    targets = ((own, 0), (z_0, layout.ghost_z), (z_1, layout.ghost_z))
    for a, direction in enumerate((0, 2, 1)):
        for t in range(layout.tiles):
            lanes = slice(t * LANES, (t + 1) * LANES)
            place = cells[direction, :, lanes].astype(jnp.float32) + fraction[direction, :, lanes]
            for target, base in targets:
                first = base + (a * layout.tiles + t) * slots
                target[first : first + slots] = place
    lane = lax.broadcasted_iota(jnp.int32, (1, LANES), 1)
    for slot in range(slots):
        first_x = lax.rem(corners[0, slot] + offset_x, length_x) - HALF
        first_z = lax.rem(corners[2, slot] + offset_z, length_z) - HALF
        fact = jnp.where(lane == 0, first_x, slot_ids[slot] + 1)
        fact = jnp.where(lane == 1, first_z, fact)
        fact = jnp.where(lane == 2, corners[1, slot], fact)
        for target, base in targets:
            row = base + layout.fact_row + slot
            target[row : row + 1] = fact.astype(jnp.float32)
    for copy in copies[4:]:
        copy.wait()
    choose = in_order("gz", (1, size_y))
    for c in range(4):
        for x in range(size_x):
            row = c * size_x + x
            z_0[row : row + 1], z_1[row : row + 1] = choose(
                edges[1, c, x, 0:1], edges[0, c, x, 7:8]
            )


def pack(layout, slot_ids, corners, flow, cells, fraction):
    in_hbm = pl.BlockSpec(memory_space=pltpu.HBM)
    size_x, _, size_y = layout.sizes
    return pl.pallas_call(
        functools.partial(pack_kernel, layout),
        out_shape=[float32(layout.rows, LANES)]
        + [float32(layout.ghost_x, LANES)] * 2
        + [float32(layout.ghost_z + layout.rows, LANES)] * 2,
        in_specs=[in_hbm] * 5,
        out_specs=[IN_VMEM] * 5,
        scratch_shapes=[
            pltpu.SMEM(slot_ids.shape, jnp.int32),
            pltpu.SMEM(corners.shape, jnp.int32),
            pltpu.VMEM(cells.shape, jnp.int32),
            pltpu.VMEM(fraction.shape, jnp.float32),
            pltpu.VMEM((2, 4, size_x, 8, size_y), jnp.float32),
            pltpu.SemaphoreType.DMA((20,)),
        ],
        name="pack",
        cost_estimate=pl.CostEstimate(
            flops=flow.size, bytes_accessed=flow.size, transcendentals=0
        ),
    )(slot_ids, corners, flow, cells, fraction)


def join_kernel(left, right, both):
    rows = left.shape[0]
    both[:rows] = left[...]
    both[rows:] = right[...]


def join(left, right):
    return call(
        join_kernel,
        float32(2 * left.shape[0], LANES),
        [],
        [left, right],
        [],
        left.size,
        16 * left.size,
    )


def collect_kernel(layout, own, side_0, side_1, one, two, corners_0, corners_1, *refs):
    rows, (facts, table) = refs[:3], refs[3:]
    count, slots = layout.rows, layout.slots
    size_x, size_z, _ = layout.sizes
    for row, middle, base, sides in (
        (rows[0], one, layout.ghost_z, corners_0),
        (rows[1], own, 0, None),
        (rows[2], two, layout.ghost_z, corners_1),
    ):
        row[:count] = side_0[...] if sides is None else sides[:count]
        row[count : 2 * count] = middle[base : base + count]
        row[2 * count :] = side_1[...] if sides is None else sides[count:]
    for block in range(9):
        first = (block % 3) * count + layout.fact_row
        out = slice(block * slots, (block + 1) * slots)
        table[out] = rows[block // 3][first : first + slots]
    kind = lax.broadcasted_iota(jnp.int32, (8, LANES), 0)
    slot = lax.broadcasted_iota(jnp.int32, (8, LANES), 1)
    last = 2 * 3 * slots
    move_x = jnp.where(even("gx"), size_x, -size_x)
    move_z = jnp.where(even("gz"), size_z, -size_z)
    place = slot - jnp.where(slot >= last, last, jnp.where(slot >= 3 * slots, 3 * slots, 0))
    moved_x = jnp.where(place < slots, move_x, jnp.where(place >= 2 * slots, -move_x, 0))
    moved_z = jnp.where(slot < 3 * slots, move_z, jnp.where(slot >= last, -move_z, 0))
    moved = jnp.where(kind == 0, moved_x, jnp.where(kind == 1, moved_z, 0))
    facts[...] = jnp.transpose(table[...])[:8].astype(jnp.int32) + moved


def collect(layout, *tiles):
    return call(
        functools.partial(collect_kernel, layout),
        [float32(3 * layout.rows, LANES)] * 3 + [jax.ShapeDtypeStruct((8, LANES), jnp.int32)],
        [],
        tiles,
        [pltpu.VMEM((LANES, LANES), jnp.float32)],
        layout.rows * LANES,
        72 * layout.rows * LANES,
    )


def y_neighbours(value, lane, below, above):
    size_y = value.shape[-1]
    minus = jnp.where(lane == 0, below, pltpu.roll(value, 1, 1))
    plus = jnp.where(lane == size_y - 1, above, pltpu.roll(value, size_y - 1, 1))
    return minus, plus


def z_neighbours(value, row, below, above):
    size_z = value.shape[0]
    minus = jnp.where(row == 0, below, pltpu.roll(value, 1, 0))
    plus = jnp.where(row == size_z - 1, above, pltpu.roll(value, size_z - 1, 0))
    return minus, plus


def predict_inner_kernel(sizes, flow, own, inner, u_first, u_last, w_first, w_last, kept):
    size_x, size_z, size_y = sizes
    row = lax.broadcasted_iota(jnp.int32, (size_z, size_y), 0)
    lane = lax.broadcasted_iota(jnp.int32, (size_z, size_y), 1)
    nothing = jnp.zeros((size_z, size_y), jnp.float32)

    def around(c, x):
        value = flow[c, x]
        x_minus = flow[c, x - 1] if x > 0 else nothing
        x_plus = flow[c, x + 1] if x < size_x - 1 else nothing
        z_minus, z_plus = z_neighbours(value, row, 0.0, 0.0)
        edges = (0.0, 0.0) if c < 3 else (value, value)
        y_minus, y_plus = y_neighbours(value, lane, *edges)
        return value, x_minus, x_plus, z_minus, z_plus, y_minus, y_plus

    for x in range(size_x):
        _, x_minus, x_plus, z_minus, z_plus, y_minus, y_plus = around(3, x)
        gradient = (
            (x_plus - x_minus) * 0.5 - drive_force,
            (y_plus - y_minus) * 0.5,
            (z_plus - z_minus) * 0.5,
        )
        carried = (flow[0, x], flow[1, x], flow[2, x])
        for c in range(3):
            value, x_minus, x_plus, z_minus, z_plus, y_minus, y_plus = around(c, x)
            laplace = x_plus + x_minus + z_plus + z_minus + y_plus + y_minus - 6.0 * value
            advect = (
                carried[0] * (x_plus - x_minus)
                + carried[1] * (y_plus - y_minus)
                + carried[2] * (z_plus - z_minus)
            ) * 0.5
            inner[c, x] = value + time_step * (viscosity * laplace - advect - gradient[c])
        w_first[x : x + 1] = flow[2, x, 0:1]
        w_last[x : x + 1] = flow[2, x, size_z - 1 : size_z]
    kept[...] = own[...]
    u_first[...] = flow[0, 0]
    u_last[...] = flow[0, size_x - 1]


def predict_inner(sizes, flow, own):
    size_x, size_z, size_y = sizes
    return call(
        functools.partial(predict_inner_kernel, sizes),
        [float32(3, *sizes)]
        + [float32(size_z, size_y)] * 2
        + [float32(size_x, size_y)] * 2
        + [float32(*own.shape)],
        [],
        [flow, own],
        [],
        200 * flow.size,
        8 * flow.size,
    )


def predict_outer_kernel(
    layout,
    inner,
    u_first,
    u_last,
    w_first,
    w_last,
    x_0,
    x_1,
    z_0,
    z_1,
    predicted,
    field_high,
    field_low,
):
    size_x, size_z, size_y = layout.sizes
    row = lax.broadcasted_iota(jnp.int32, (8, size_y), 0)
    lower, upper = in_order("gz", z_0[: layout.ghost_z].shape)(
        z_0[: layout.ghost_z], z_1[: layout.ghost_z]
    )
    left, right = in_order("gx", x_0.shape)(x_0[...], x_1[...])
    for x in range(size_x):
        carried_low = w_first[x : x + 1]
        carried_high = w_last[x : x + 1]
        for c in range(3):
            ghost = c * size_x + x
            change_low = (viscosity + 0.5 * carried_low) * lower[ghost : ghost + 1]
            change_high = (viscosity - 0.5 * carried_high) * upper[ghost : ghost + 1]
            if c == 2:
                ghost = 3 * size_x + x
                change_low += 0.5 * lower[ghost : ghost + 1]
                change_high -= 0.5 * upper[ghost : ghost + 1]
            if x in (0, size_x - 1):
                sign, layer, carried = (0.5, left, u_first) if x == 0 else (-0.5, right, u_last)
                ghost = slice(c * size_z, (c + 1) * size_z)
                change = (viscosity + sign * carried[...]) * layer[ghost]
                if c == 0:
                    change += sign * layer[3 * size_z : 4 * size_z]
                predicted[c, x] = inner[c, x] + time_step * change
            else:
                predicted[c, x] = inner[c, x]
            predicted[c, x, 0:8] += jnp.where(row == 0, time_step * change_low, 0.0)
            predicted[c, x, size_z - 8 : size_z] += jnp.where(
                row == 7, time_step * change_high, 0.0
            )
    for c in range(3):
        for q, (xs, zs) in enumerate(quarters(layout.sizes)):
            part = jnp.transpose(predicted[c, xs, zs].reshape(LANES, size_y))
            high = part.astype(jnp.bfloat16).astype(jnp.float32)
            field_high[c, :, q * LANES : (q + 1) * LANES] = high
            field_low[c, :, q * LANES : (q + 1) * LANES] = part - high


def predict_outer(layout, inner, *layers):
    _, _, size_y = layout.sizes
    return call(
        functools.partial(predict_outer_kernel, layout),
        [float32(3, *layout.sizes)] + [float32(3, size_y, layout.plane)] * 2,
        [],
        [*inner, *layers],
        [],
        10 * inner[0].size,
        16 * inner[0].size,
    )


def swap_groups(values, width):
    count = len(values)
    lane = lax.broadcasted_iota(jnp.int32, values[0].shape, 1)
    values = list(values)
    step = count // 2
    while step:
        reach = step * width
        keep = lane % (2 * reach) < reach
        for i in range(count):
            if i & step == 0:
                a, b = values[i], values[i + step]
                values[i] = jnp.where(keep, a, pltpu.roll(b, reach, 1))
                values[i + step] = jnp.where(keep, pltpu.roll(a, LANES - reach, 1), b)
        step //= 2
    return values


def transform_z_kernel(sizes, counts, table_high, table_low, *refs):
    size_x, size_z, size_y = sizes
    parts_x, parts_z = counts
    pieces, refs = refs[:parts_z], refs[parts_z:]
    outs, (gathered, turned, whole) = refs[:parts_x], refs[parts_x:]
    height = size_y // parts_z
    columns = height * size_x
    group = LANES // size_z
    for piece, step in zip(pieces, steps(parts_z)):
        gathered[lax.axis_index("gz") ^ step] = piece[...]
    lane = lax.broadcasted_iota(jnp.int32, (height, LANES), 1)
    edges = [gathered[i, :, size_x * size_z :] for i in range(parts_z)]
    blocks = parts_z // group
    for block in range(blocks):
        for q in range(size_x // group):
            lanes = slice(q * LANES, (q + 1) * LANES)
            values = [gathered[block * group + i, :, lanes] for i in range(group)]
            for j, value in enumerate(swap_groups(values, size_z)):
                turned[block, pl.ds(q * group + j, height, stride=size_x), :] = value
        for end in range(2):
            layer = edges[block * group]
            for i in range(group):
                moved = (i - end) * size_z % LANES
                part = edges[block * group + i]
                part = pltpu.roll(part, moved, 1) if moved else part
                layer = part if i == 0 else jnp.where(lane < i * size_z, layer, part)
            turned[block, pl.ds(columns + end, height, stride=2), :] = layer
    for x in range(size_x):
        ends = jnp.zeros((height, LANES), jnp.float32)
        for i in range(parts_z):
            part = pltpu.roll(edges[i], (2 * i - 2 * size_z - 2 * x) % LANES, 1)
            ends = jnp.where((lane >= 2 * i) & (lane < 2 * i + 2), part, ends)
        turned[blocks, pl.ds(x, height, stride=size_x), :] = ends
    turned[blocks, columns:] = jnp.zeros((2 * height, LANES), jnp.float32)
    lines = jnp.concatenate([turned[b] for b in range(blocks + 1)], axis=1)
    high, low = split(lines)
    result = lax.dot_general(
        table_high[...], high, TRANSPOSED, preferred_element_type=jnp.float32
    )
    result += lax.dot_general(
        table_low[...], high, TRANSPOSED, preferred_element_type=jnp.float32
    )
    result += lax.dot_general(
        table_high[...], low, TRANSPOSED, preferred_element_type=jnp.float32
    )
    whole[:, columns:] = jnp.zeros((whole.shape[0], LANES), jnp.float32)
    whole[:, : columns + 2 * height] = result
    rows = whole.shape[0] // parts_x
    modes = rows // 2
    lane = lax.broadcasted_iota(jnp.int32, (modes, LANES), 1)
    for out, step in zip(outs, steps(parts_x)):
        first = pl.multiple_of((lax.axis_index("gx") ^ step) * rows, 8)
        for t in range(columns // LANES):
            out[t * rows : (t + 1) * rows] = whole[
                pl.ds(first, rows), t * LANES : (t + 1) * LANES
            ]
        real = whole[pl.ds(first, modes), columns : columns + LANES]
        imag = whole[pl.ds(first + modes, modes), columns : columns + LANES]
        imag = pltpu.roll(imag, 2 * height, 1)
        out[columns // LANES * rows :] = jnp.where(lane < 2 * height, real, imag)


def transform_z(sizes, counts, table, pieces):
    size_x, size_z, size_y = sizes
    parts_x, parts_z = counts
    length_z = size_z * parts_z
    height = size_y // parts_z
    columns = height * size_x
    assert 2 * parts_z <= LANES and 4 * height <= LANES
    rows = 2 * length_z // parts_x
    return call(
        functools.partial(transform_z_kernel, sizes, counts),
        [float32(columns // LANES * rows + rows // 2, LANES)] * parts_x,
        [],
        [*table, *pieces],
        [
            pltpu.VMEM((parts_z, *pieces[0].shape), jnp.float32),
            pltpu.VMEM((length_z // LANES + 1, columns + 2 * height, LANES), jnp.float32),
            pltpu.VMEM((2 * length_z, columns + LANES), jnp.float32),
        ],
        24 * length_z * length_z * columns,
        12 * length_z * columns,
    )


def transform_x_kernel(sizes, counts, table_high, table_low, *refs):
    size_x, size_z, size_y = sizes
    parts_x, parts_z = counts
    pieces, (source, gathered, turned) = refs[:parts_x], refs[parts_x:]
    length_x = size_x * parts_x
    modes = size_z * parts_z // parts_x
    height = size_y // parts_z
    group = LANES // size_x
    rows = 2 * modes
    main = height // group * rows
    for piece, step in zip(pieces, steps(parts_x)):
        gathered[lax.axis_index("gx") ^ step] = piece[...]
    for block in range(parts_x // group):
        for q in range(height // group):
            values = [
                gathered[block * group + i, q * rows : (q + 1) * rows] for i in range(group)
            ]
            for j, value in enumerate(swap_groups(values, size_x)):
                first = (q * group + j) * modes
                for c in range(2):
                    column = c * length_x + block * LANES
                    turned[first : first + modes, column : column + LANES] = value[
                        c * modes : (c + 1) * modes
                    ]
        ends = [gathered[block * group + i, main:] for i in range(group)]
        column = 2 * length_x + block * LANES
        for j, value in enumerate(swap_groups(ends, 2)):
            for q in range(height // group):
                first = (q * group + j) * modes
                moved = -2 * group * q % LANES
                turned[first : first + modes, column : column + LANES] = (
                    pltpu.roll(value, moved, 1) if moved else value
                )
    high, low = split(turned[...])
    result = jnp.dot(high, table_high[...], preferred_element_type=jnp.float32)
    result += jnp.dot(low, table_high[...], preferred_element_type=jnp.float32)
    result += jnp.dot(high, table_low[...], preferred_element_type=jnp.float32)
    source[0] = result[:, :length_x].reshape(height, modes, length_x)
    source[1] = result[:, length_x:].reshape(height, modes, length_x)


def transform_x(sizes, counts, table, pieces):
    size_x, size_z, size_y = sizes
    parts_x, parts_z = counts
    length_x = size_x * parts_x
    modes = size_z * parts_z // parts_x
    height = size_y // parts_z
    return call(
        functools.partial(transform_x_kernel, sizes, counts),
        float32(2, height, modes, length_x),
        [],
        [*table, *pieces],
        [
            pltpu.VMEM((parts_x, *pieces[0].shape), jnp.float32),
            pltpu.VMEM((height * modes, table[0].shape[0]), jnp.float32),
        ],
        24 * length_x * length_x * height * modes,
        24 * length_x * height * modes,
    )


def split_table(table):
    high = table.astype(np.float32).astype(jnp.bfloat16)
    low = (table - high.astype(np.float64)).astype(np.float32).astype(jnp.bfloat16)
    return jnp.asarray(high), jnp.asarray(low)


def angles(length):
    counter = np.arange(length)
    turn = (counter[:, None] * counter[None, :] % length) * (2.0 * np.pi / length)
    return np.cos(turn), np.sin(turn)


def table_z(length, blocks, parts):
    cosine, sine = angles(length)
    modes, size = length // blocks, length // parts
    table = np.stack([cosine, -sine]).reshape(2, blocks, modes, length)
    table = table.transpose(1, 0, 2, 3).reshape(2 * length, length)
    ends = np.zeros((2 * length, LANES))
    for part in range(parts):
        ends[:, 2 * part] = 0.5 * table[:, (part * size - 1) % length]
        ends[:, 2 * part + 1] = -0.5 * table[:, (part + 1) * size % length]
    return split_table(np.concatenate([table, ends], axis=1))


def table_x(length, parts, height, scale):
    cosine, sine = angles(length)
    size = length // parts
    group = LANES // size
    table = np.block([[cosine, -sine], [sine, cosine]]) * scale
    ends = np.zeros((parts // group * LANES, 2 * length))
    for part in range(parts):
        for c in range(2):
            row = part // group * LANES + c * 2 * height + 2 * (part % group)
            ends[row] = 0.5 * table[c * length + (part * size - 1) % length]
            ends[row + 1] = -0.5 * table[c * length + (part + 1) * size % length]
    return split_table(np.concatenate([table, ends], axis=0))


def exchange(pieces, axis):
    devices = lax.axis_size(axis)
    assert devices & (devices - 1) == 0
    return [pieces[0]] + [
        lax.ppermute(piece, axis, [(i, i ^ step) for i in range(devices)])
        for piece, step in zip(pieces[1:], steps(devices)[1:])
    ]


def on_device(
    flow_state, slot_ids, corners, marker_cells, marker_frac, particle_velocity, particle_spin
):
    sizes = flow_state.shape[1:]
    size_x, size_z, size_y = sizes
    counts = (lax.axis_size("gx"), lax.axis_size("gz"))
    length_x, length_z = (size_x * counts[0], size_z * counts[1])
    slots, markers = marker_cells.shape[1:]
    layout = Layout(sizes, slots, markers)

    own, x_0, x_1, z_0, z_1 = pack(
        layout, slot_ids, corners, flow_state, marker_cells, marker_frac
    )
    marks_0 = swap(own, "gx", 0)
    marks_1 = swap(own, "gx", 1)
    z_0, z_1 = swap(z_0, "gz", 0), swap(z_1, "gz", 1)
    x_0, x_1 = swap(x_0, "gx", 0), swap(x_1, "gx", 1)
    *inner, own = predict_inner(sizes, flow_state, own)
    sides = join(marks_0, marks_1)
    corners_0, corners_1 = swap(sides, "gz", 0), swap(sides, "gz", 1)
    predicted, *fields = predict_outer(layout, inner, x_0, x_1, z_0, z_1)
    row_0, row, row_1, facts = collect(
        layout, own, marks_0, marks_1, z_0, z_1, corners_0, corners_1
    )

    tiles = (0, 1, 2)
    parts, rows_saved = sample(layout, ((tiles, 0), (tiles, 2)), facts, (row_0, row_1), fields, ())
    from_z = swap(parts[0], "gz", 0) + swap(parts[1], "gz", 1)
    (side_part,), (side_saved,) = sample(layout, (((0, 2), 1),), facts, (row,), fields, ())
    from_0 = swap(side_part[:, :slots] + from_z[:, :slots], "gx", 0)
    from_1 = swap(side_part[:, slots:] + from_z[:, 2 * slots :], "gx", 1)
    motion = (particle_velocity, particle_spin)
    (own_part,), (own_saved,) = sample(layout, (((1,), 1),), facts, (row,), fields, motion)
    push = own_part - (from_z[:, slots : 2 * slots] + from_0 + from_1)

    row_push = jnp.concatenate([swap(push, "gx", 0), push, swap(push, "gx", 1)], axis=1)
    rows_push = swap(row_push, "gz", 0), swap(row_push, "gz", 1)
    forcing = spread_own(layout, facts, own_saved, push)
    forcing = spread_side(layout, facts, side_saved, row_push, forcing)
    velocity, pieces = spread_rest(
        layout, counts[1], facts, rows_saved, rows_push, forcing, predicted
    )

    pieces = exchange(pieces, "gz")
    pieces = transform_z(sizes, counts, table_z(length_z, *counts), pieces)
    pieces = exchange(pieces, "gx")
    scale = 1.0 / math.sqrt(length_x * length_z)
    table = table_x(length_x, counts[0], size_y // counts[1], scale)
    source = transform_x(sizes, counts, table, pieces)
    return velocity, source


def solution(mesh):
    return jax.shard_map(
        on_device,
        mesh=mesh,
        in_specs=(
            P(None, "gx", "gz", None),
            P(("gx", "gz")),
            P(None, ("gx", "gz")),
            P(None, ("gx", "gz"), None),
            P(None, ("gx", "gz"), None),
            P(),
            P(),
        ),
        out_specs=(P(None, "gx", "gz", None), P(None, "gz", "gx", None)),
        check_vma=False,
    )
```

```python
import functools
import math

import jax
import jax.numpy as jnp
import numpy as np
from jax import lax
from jax.experimental import pallas as pl
from jax.experimental.pallas import tpu as pltpu
from jax.sharding import PartitionSpec as P


BOX = 24
HALF = 12
WINDOW = 32
LANES = 128
KERNEL_BYTES = 16 * 1024 * 1024

time_step = 0.1
viscosity = 0.2
drive_force = 1.0


IN_VMEM = pl.BlockSpec(memory_space=pltpu.VMEM)
IN_SMEM = pl.BlockSpec(memory_space=pltpu.SMEM)
TRANSPOSED = (((1,), (1,)), ((), ()))


def float32(*shape):
    return jax.ShapeDtypeStruct(shape, jnp.float32)


def call(kernel, out_shape, scalars, arrays, scratch, flops, moved):
    outputs = len(out_shape) if isinstance(out_shape, (list, tuple)) else 0
    return pl.pallas_call(
        kernel,
        out_shape=out_shape,
        in_specs=[IN_SMEM] * len(scalars) + [IN_VMEM] * len(arrays),
        out_specs=[IN_VMEM] * outputs if outputs else IN_VMEM,
        scratch_shapes=scratch,
        compiler_params=pltpu.CompilerParams(vmem_limit_bytes=KERNEL_BYTES),
        cost_estimate=pl.CostEstimate(flops=flops, bytes_accessed=moved, transcendentals=0),
    )(*scalars, *arrays)


def swap(array, axis, partner):
    devices = lax.axis_size(axis)
    pairs = [(i, (i + (1 if i % 2 == partner else -1)) % devices) for i in range(devices)]
    return lax.ppermute(array, axis, pairs)


def even(axis):
    return lax.rem(lax.axis_index(axis), 2) == 0


def steps(devices):
    return [0, *range(devices - 1, 0, -1)]


def in_order(axis, shape):
    parity = jnp.full(shape, lax.rem(lax.axis_index(axis), 2), jnp.int32)
    return lambda one, two: (
        jnp.where(parity == 0, two, one),
        jnp.where(parity == 0, one, two),
    )


def cosine_coefficients():
    samples = 2.0 + 2.0 * np.cos(np.pi * (np.arange(64) + 0.5) / 64)
    values = np.cos(np.pi / 4 * np.sqrt(samples)) * np.sqrt(0.5)
    fit = np.polynomial.chebyshev.Chebyshev.fit(samples, values, 4, domain=[0, 4])
    return [float(v) for v in fit.convert(kind=np.polynomial.Polynomial).coef]


COSINE = cosine_coefficients()


def weight(offset):
    square = jnp.minimum(offset * offset, 4.0)
    value = COSINE[-1] * square + COSINE[-2]
    for coefficient in COSINE[-3::-1]:
        value = value * square + coefficient
    return value * value


def split(value):
    high = value.astype(jnp.bfloat16)
    low = (value - high.astype(jnp.float32)).astype(jnp.bfloat16)
    return high, low


def row_weights(count, position):
    cells = lax.broadcasted_iota(jnp.int32, (count, position.shape[1]), 0)
    return weight(cells.astype(jnp.float32) - position)


def plane_weights(weight_x, weight_z, half_z, high, low):
    count = 0
    for z in range(0, weight_z.shape[0], half_z):
        part = weight_z[z : z + half_z]
        for x in range(weight_x.shape[0]):
            rows = slice(count * half_z, (count + 1) * half_z)
            high[rows], low[rows] = split(weight_x[x : x + 1] * part)
            count += 1


BODIES = ((True, True), (True, False), (False, True), (False, False))


def quarters(sizes):
    half_x, half_z = sizes[0] // 2, sizes[1] // 2
    for z in range(2):
        for x in range(2):
            yield slice(x * half_x, (x + 1) * half_x), slice(z * half_z, (z + 1) * half_z)


class Layout:
    def __init__(self, sizes, slots, markers):
        self.sizes, self.slots, self.markers = sizes, slots, markers
        self.tiles = markers // LANES
        self.fact_row = 3 * self.tiles * slots
        self.rows = self.fact_row + slots
        self.ghost_x = 4 * sizes[1]
        self.ghost_z = 4 * sizes[0]
        self.plane = sizes[0] * sizes[1]


def marker_row(layout, marks, base, direction, slot):
    first = base + direction * layout.tiles * layout.slots + slot
    rows = [marks[pl.ds(first + t * layout.slots, 1), :] for t in range(layout.tiles)]
    return jnp.concatenate(rows, axis=1)


def slot_visits(layout, facts, marks, saved, blocks, step, high, low, visit):
    size_x, size_z, _ = layout.sizes
    half_x, half_z = size_x // 2, size_z // 2
    slots = layout.slots

    def body(index, carry):
        block, slot = index // slots, index % slots
        block = blocks[0] + block * (blocks[1] - blocks[0] if len(blocks) > 1 else 0)
        fact = (step * 3 + block) * slots + slot
        kind = facts[4, fact]

        def part(all_x, all_z):
            first_x, first_z, first_y = facts[0, fact], facts[1, fact], facts[2, fact]
            first = pl.multiple_of(facts[5, fact], 8)
            upper_x = 0 if all_x else facts[6, fact]
            upper_z = 0 if all_z else facts[7, fact]
            start_x, start_z = upper_x * half_x, upper_z * half_z
            lanes = [(upper_z + z) * 2 * LANES + upper_x * LANES for z in range(1 + all_z)]
            width = (1 + all_x) * LANES
            if all_x and all_z:
                pieces = [(0, 4 * LANES)]
            else:
                pieces = [(pl.multiple_of(lane, LANES), width) for lane in lanes]
            rows_x = slice(0, size_x if all_x else half_x)
            rows_z = slice(size_x, size_x + (size_z if all_z else half_z))
            rows_y = slice(size_x + size_z, size_x + size_z + WINDOW)
            if marks is not None:
                base = block * layout.rows
                starts = (first_x - start_x, first_z - start_z, first_y - first)
                for direction, rows in enumerate((rows_x, rows_z, rows_y)):
                    position = marker_row(layout, marks, base, direction, slot)
                    position += starts[direction].astype(jnp.float32)
                    saved[index, rows, :] = row_weights(rows.stop - rows.start, position)
            plane_weights(saved[index, rows_x, :], saved[index, rows_z, :], half_z, high, low)
            weight_y = saved[index, rows_y, :]
            visit(index, block * slots + slot, first, weight_y, pieces)

        @pl.when(kind != 0)
        def _():
            for number, (all_x, all_z) in enumerate(BODIES):
                pl.when(kind == number + 1)(functools.partial(part, all_x, all_z))

        return carry

    lax.fori_loop(0, len(blocks) * slots, body, 0)


def rigid_motion(layout, facts, marks, motion, block, slot):
    particle = facts[3, (3 + block) * layout.slots + slot] - 1
    chosen = lax.broadcasted_iota(jnp.int32, motion[0].shape, 1) == particle
    moving, turning = [
        jnp.sum(jnp.where(chosen, part[...], 0.0), axis=1, keepdims=True) for part in motion
    ]
    lever = [
        marker_row(layout, marks, block * layout.rows, direction, slot) - HALF
        for direction in (0, 2, 1)
    ]
    for c in range(3):
        a, b = (c + 1) % 3, (c + 2) % 3
        turned = turning[a : a + 1] * lever[b] - turning[b : b + 1] * lever[a]
        yield moving[c : c + 1] + turned


def sample_slots(
    layout, facts, marks, motion, field_high, field_low, out, saved, blocks, step, high, low
):
    def visit(index, row, first, weight_y, pieces):
        rows = pl.ds(first, WINDOW)

        def window(field):
            parts = [
                jnp.concatenate([field[c, rows, pl.ds(lane, width)] for c in range(3)], axis=0)
                for lane, width in pieces
            ]
            return jnp.concatenate(parts, axis=1).astype(jnp.bfloat16)

        window_high, window_low = window(field_high), window(field_low)
        count = window_high.shape[1]
        both = jnp.concatenate([window_high, window_low], axis=0)
        value = jnp.dot(both, high[:count], preferred_element_type=jnp.float32)
        rest = jnp.dot(window_high, low[:count], preferred_element_type=jnp.float32)
        value = value[: 3 * WINDOW] + value[3 * WINDOW :] + rest
        target = None
        if motion:
            target = list(rigid_motion(layout, facts, marks, motion, blocks[0], index))
        for c in range(3):
            part = value[c * WINDOW : (c + 1) * WINDOW] * weight_y
            sampled = jnp.sum(part, axis=0, keepdims=True)
            out[c, pl.ds(index, 1), :] = sampled if target is None else target[c] - sampled

    out[...] = jnp.zeros(out.shape, jnp.float32)
    slot_visits(layout, facts, marks, saved, blocks, step, high, low, visit)


def sample_kernel(layout, groups, moved, facts, *refs):
    count = len(groups)
    marks, refs = refs[:count], refs[count:]
    (field_high, field_low), refs = refs[:2], refs[2:]
    motion, refs = refs[:moved], refs[moved:]
    outs, refs = refs[:count], refs[count:]
    saved, (high, low) = refs[:count], refs[count:]
    for i, (blocks, step) in enumerate(groups):
        sample_slots(
            layout,
            facts,
            marks[i],
            motion,
            field_high,
            field_low,
            outs[i],
            saved[i],
            blocks,
            step,
            high,
            low,
        )


def visit_cost(layout, blocks):
    return len(blocks) * layout.slots * 18 * WINDOW * layout.plane * layout.markers


def weight_scratch(layout):
    return [pltpu.VMEM((layout.plane, layout.markers), jnp.bfloat16)] * 2


def sample(layout, groups, facts, marks, fields, motion):
    markers, weights = layout.markers, layout.sizes[0] + layout.sizes[1] + WINDOW
    counts = [len(blocks) * layout.slots for blocks, _ in groups]
    results = call(
        functools.partial(sample_kernel, layout, groups, len(motion)),
        [float32(3, count, markers) for count in counts]
        + [float32(count, weights, markers) for count in counts],
        [facts],
        [*marks, *fields, *motion],
        weight_scratch(layout),
        sum(visit_cost(layout, blocks) for blocks, _ in groups),
        8 * fields[0].size,
    )
    return results[: len(groups)], results[len(groups) :]


def spread_slots(layout, blocks, step, facts, saved, push, own_rows, total, high, low):
    def visit(index, row, first, weight_y, pieces):
        slot = index if own_rows else row
        count = sum(width for _, width in pieces)
        value = jnp.concatenate(
            [weight_y * push[c, pl.ds(slot, 1), :] for c in range(3)], axis=0
        )
        value_high, value_low = split(value)
        both = jnp.concatenate([value_high, value_low], axis=0)
        added = lax.dot_general(
            both, high[:count], TRANSPOSED, preferred_element_type=jnp.float32
        )
        rest = lax.dot_general(
            value_high, low[:count], TRANSPOSED, preferred_element_type=jnp.float32
        )
        added = added[: 3 * WINDOW] + added[3 * WINDOW :] + rest
        column = 0
        for lane, width in pieces:
            for c in range(3):
                part = added[c * WINDOW : (c + 1) * WINDOW, column : column + width]
                total[c, pl.ds(first, WINDOW), pl.ds(lane, width)] += part
            column += width

    slot_visits(layout, facts, None, saved, blocks, step, high, low, visit)


def spread_own_kernel(layout, facts, saved, push, total, high, low):
    total[...] = jnp.zeros(total.shape, jnp.float32)
    spread_slots(layout, (1,), 1, facts, saved, push, True, total, high, low)


def spread_own(layout, facts, saved, push):
    return call(
        functools.partial(spread_own_kernel, layout),
        float32(3, layout.sizes[2], layout.plane),
        [facts],
        [saved, push],
        weight_scratch(layout),
        visit_cost(layout, (1,)),
        12 * layout.sizes[2] * layout.plane,
    )


def spread_side_kernel(layout, facts, saved, push, before, total, high, low):
    total[...] = before[...]
    spread_slots(layout, (0, 2), 1, facts, saved, push, False, total, high, low)


def spread_side(layout, facts, saved, push, before):
    return call(
        functools.partial(spread_side_kernel, layout),
        float32(*before.shape),
        [facts],
        [saved, push, before],
        weight_scratch(layout),
        visit_cost(layout, (0, 2)),
        8 * before.size,
    )


def spread_rest_kernel(
    layout, parts, facts, saved_0, saved_1, push_0, push_1, before, predicted, velocity, *refs
):
    outs, (total, high, low, edges, whole) = refs[:parts], refs[parts:]
    size_x, size_z, size_y = layout.sizes
    total[...] = before[...]
    row = (0, 1, 2)
    spread_slots(layout, row, 0, facts, saved_0, push_0, False, total, high, low)
    spread_slots(layout, row, 2, facts, saved_1, push_1, False, total, high, low)
    for c in range(3):
        for q, (xs, zs) in enumerate(quarters(layout.sizes)):
            part = jnp.transpose(total[c, :, q * LANES : (q + 1) * LANES])
            part = part.reshape(size_x // 2, size_z // 2, size_y)
            velocity[c, xs, zs] = predicted[c, xs, zs] + part
    row = lax.broadcasted_iota(jnp.int32, (size_z, size_y), 0)
    lane = lax.broadcasted_iota(jnp.int32, (size_z, size_y), 1)
    group = LANES // size_z
    for q in range(size_x // group):
        pieces = []
        for x in range(q * group, (q + 1) * group):
            y_minus, y_plus = y_neighbours(velocity[1, x], lane, 0.0, 0.0)
            z_minus, z_plus = z_neighbours(velocity[2, x], row, 0.0, 0.0)
            change = y_plus - y_minus + z_plus - z_minus
            if x > 0:
                change -= velocity[0, x - 1]
            if x < size_x - 1:
                change += velocity[0, x + 1]
            pieces.append(change * 0.5)
        part = jnp.concatenate(pieces, axis=0)
        whole[:, q * LANES : (q + 1) * LANES] = jnp.transpose(part)
    edges[...] = jnp.zeros(edges.shape, jnp.float32)
    edges[:size_z] = velocity[0, 0]
    edges[size_z : 2 * size_z] = velocity[0, size_x - 1]
    for x in range(size_x):
        first = 2 * size_z + 2 * x
        edges[first : first + 1] = velocity[2, x, 0:1]
        edges[first + 1 : first + 2] = velocity[2, x, size_z - 1 : size_z]
    whole[:, layout.plane :] = jnp.transpose(edges[...])
    height = size_y // parts
    for out, step in zip(outs, steps(parts)):
        first = pl.multiple_of((lax.axis_index("gz") ^ step) * height, 8)
        out[...] = whole[pl.ds(first, height), :]


def spread_rest(layout, parts, facts, saved, pushes, before, predicted):
    size_x, size_z, size_y = layout.sizes
    assert 2 * size_z + 2 * size_x <= LANES
    width = layout.plane + LANES
    velocity, *pieces = call(
        functools.partial(spread_rest_kernel, layout, parts),
        [float32(3, size_x, size_z, size_y)] + [float32(size_y // parts, width)] * parts,
        [facts],
        [*saved, *pushes, before, predicted],
        [pltpu.VMEM(before.shape, jnp.float32)]
        + weight_scratch(layout)
        + [pltpu.VMEM((LANES, size_y), jnp.float32), pltpu.VMEM((size_y, width), jnp.float32)],
        2 * visit_cost(layout, (0, 1, 2)),
        12 * before.size,
    )
    return velocity, pieces


def pack_kernel(
    layout,
    slot_ids_hbm,
    corners_hbm,
    flow,
    cells_hbm,
    fraction_hbm,
    own,
    x_0,
    x_1,
    z_0,
    z_1,
    slot_ids,
    corners,
    cells,
    fraction,
    edges,
    done,
):
    size_x, size_z, size_y = layout.sizes
    slots = layout.slots
    moves = [
        (slot_ids_hbm, slot_ids),
        (corners_hbm, corners),
        (cells_hbm, cells),
        (fraction_hbm, fraction),
    ]
    for c in range(4):
        moves.append((flow.at[c, :, pl.ds(size_z - 8, 8)], edges.at[0, c]))
        moves.append((flow.at[c, :, pl.ds(0, 8)], edges.at[1, c]))
    last = jnp.where(even("gx"), size_x - 1, 0)
    for c in range(4):
        rows = pl.ds(c * size_z, size_z)
        moves.append((flow.at[c, last], x_0.at[rows]))
        moves.append((flow.at[c, size_x - 1 - last], x_1.at[rows]))
    copies = [pltpu.make_async_copy(a, b, done.at[i]) for i, (a, b) in enumerate(moves)]
    for copy in copies:
        copy.start()
    for copy in copies[:4]:
        copy.wait()
    length_x = size_x * lax.axis_size("gx")
    length_z = size_z * lax.axis_size("gz")
    offset_x = length_x + HALF - lax.axis_index("gx") * size_x
    offset_z = length_z + HALF - lax.axis_index("gz") * size_z
    targets = ((own, 0), (z_0, layout.ghost_z), (z_1, layout.ghost_z))
    for a, direction in enumerate((0, 2, 1)):
        for t in range(layout.tiles):
            lanes = slice(t * LANES, (t + 1) * LANES)
            place = cells[direction, :, lanes].astype(jnp.float32) + fraction[direction, :, lanes]
            for target, base in targets:
                first = base + (a * layout.tiles + t) * slots
                target[first : first + slots] = place
    lane = lax.broadcasted_iota(jnp.int32, (1, LANES), 1)
    for slot in range(slots):
        first_x = lax.rem(corners[0, slot] + offset_x, length_x) - HALF
        first_z = lax.rem(corners[2, slot] + offset_z, length_z) - HALF
        fact = jnp.where(lane == 0, first_x, slot_ids[slot] + 1)
        fact = jnp.where(lane == 1, first_z, fact)
        fact = jnp.where(lane == 2, corners[1, slot], fact)
        for target, base in targets:
            row = base + layout.fact_row + slot
            target[row : row + 1] = fact.astype(jnp.float32)
    for copy in copies[4:]:
        copy.wait()
    choose = in_order("gz", (1, size_y))
    for c in range(4):
        for x in range(size_x):
            row = c * size_x + x
            z_0[row : row + 1], z_1[row : row + 1] = choose(
                edges[1, c, x, 0:1], edges[0, c, x, 7:8]
            )


def pack(layout, slot_ids, corners, flow, cells, fraction):
    in_hbm = pl.BlockSpec(memory_space=pltpu.HBM)
    size_x, _, size_y = layout.sizes
    return pl.pallas_call(
        functools.partial(pack_kernel, layout),
        out_shape=[float32(layout.rows, LANES)]
        + [float32(layout.ghost_x, LANES)] * 2
        + [float32(layout.ghost_z + layout.rows, LANES)] * 2,
        in_specs=[in_hbm] * 5,
        out_specs=[IN_VMEM] * 5,
        scratch_shapes=[
            pltpu.SMEM(slot_ids.shape, jnp.int32),
            pltpu.SMEM(corners.shape, jnp.int32),
            pltpu.VMEM(cells.shape, jnp.int32),
            pltpu.VMEM(fraction.shape, jnp.float32),
            pltpu.VMEM((2, 4, size_x, 8, size_y), jnp.float32),
            pltpu.SemaphoreType.DMA((20,)),
        ],
        name="pack",
        cost_estimate=pl.CostEstimate(
            flops=flow.size, bytes_accessed=flow.size, transcendentals=0
        ),
    )(slot_ids, corners, flow, cells, fraction)


def join_kernel(left, right, both):
    rows = left.shape[0]
    both[:rows] = left[...]
    both[rows:] = right[...]


def join(left, right):
    return call(
        join_kernel,
        float32(2 * left.shape[0], LANES),
        [],
        [left, right],
        [],
        left.size,
        16 * left.size,
    )


def collect_kernel(layout, own, side_0, side_1, one, two, corners_0, corners_1, *refs):
    rows, (facts, table) = refs[:3], refs[3:]
    count, slots = layout.rows, layout.slots
    size_x, size_z, size_y = layout.sizes
    for row, middle, base, sides in (
        (rows[0], one, layout.ghost_z, corners_0),
        (rows[1], own, 0, None),
        (rows[2], two, layout.ghost_z, corners_1),
    ):
        row[:count] = side_0[...] if sides is None else sides[:count]
        row[count : 2 * count] = middle[base : base + count]
        row[2 * count :] = side_1[...] if sides is None else sides[count:]
    for block in range(9):
        first = (block % 3) * count + layout.fact_row
        out = slice(block * slots, (block + 1) * slots)
        table[out] = rows[block // 3][first : first + slots]
    kind = lax.broadcasted_iota(jnp.int32, (8, LANES), 0)
    slot = lax.broadcasted_iota(jnp.int32, (8, LANES), 1)
    last = 2 * 3 * slots
    move_x = jnp.where(even("gx"), size_x, -size_x)
    move_z = jnp.where(even("gz"), size_z, -size_z)
    place = slot - jnp.where(slot >= last, last, jnp.where(slot >= 3 * slots, 3 * slots, 0))
    moved_x = jnp.where(place < slots, move_x, jnp.where(place >= 2 * slots, -move_x, 0))
    moved_z = jnp.where(slot < 3 * slots, move_z, jnp.where(slot >= last, -move_z, 0))
    moved = jnp.where(kind == 0, moved_x, jnp.where(kind == 1, moved_z, 0))
    known = jnp.transpose(table[...])[:8].astype(jnp.int32) + moved
    first_x, first_z, first_y, particle = [known[i : i + 1] for i in range(4)]
    half_x, half_z = size_x // 2, size_z // 2

    def between(value, low, high):
        return (value > low) & (value < high)

    meets = between(first_x, -BOX, size_x) & between(first_z, -BOX, size_z) & (particle > 0)
    part_x = jnp.where(between(first_x, half_x - BOX, half_x), 0, 2)
    part_z = jnp.where(between(first_z, half_z - BOX, half_z), 0, 1)
    facts[...] = known
    facts[4:5] = jnp.where(meets, 1 + part_x + part_z, 0)
    facts[5:6] = jnp.minimum(jnp.bitwise_and(first_y, -8), size_y - WINDOW)
    facts[6:7] = jnp.where(first_x >= half_x, 1, 0)
    facts[7:8] = jnp.where(first_z >= half_z, 1, 0)


def collect(layout, *tiles):
    return call(
        functools.partial(collect_kernel, layout),
        [float32(3 * layout.rows, LANES)] * 3 + [jax.ShapeDtypeStruct((8, LANES), jnp.int32)],
        [],
        tiles,
        [pltpu.VMEM((LANES, LANES), jnp.float32)],
        layout.rows * LANES,
        72 * layout.rows * LANES,
    )


def y_neighbours(value, lane, below, above):
    size_y = value.shape[-1]
    minus = jnp.where(lane == 0, below, pltpu.roll(value, 1, 1))
    plus = jnp.where(lane == size_y - 1, above, pltpu.roll(value, size_y - 1, 1))
    return minus, plus


def z_neighbours(value, row, below, above):
    size_z = value.shape[0]
    minus = jnp.where(row == 0, below, pltpu.roll(value, 1, 0))
    plus = jnp.where(row == size_z - 1, above, pltpu.roll(value, size_z - 1, 0))
    return minus, plus


def predict_inner_kernel(sizes, flow, own, inner, u_first, u_last, w_first, w_last, kept):
    size_x, size_z, size_y = sizes
    row = lax.broadcasted_iota(jnp.int32, (size_z, size_y), 0)
    lane = lax.broadcasted_iota(jnp.int32, (size_z, size_y), 1)
    nothing = jnp.zeros((size_z, size_y), jnp.float32)

    def around(c, x):
        value = flow[c, x]
        x_minus = flow[c, x - 1] if x > 0 else nothing
        x_plus = flow[c, x + 1] if x < size_x - 1 else nothing
        z_minus, z_plus = z_neighbours(value, row, 0.0, 0.0)
        edges = (0.0, 0.0) if c < 3 else (value, value)
        y_minus, y_plus = y_neighbours(value, lane, *edges)
        return value, x_minus, x_plus, z_minus, z_plus, y_minus, y_plus

    for x in range(size_x):
        _, x_minus, x_plus, z_minus, z_plus, y_minus, y_plus = around(3, x)
        gradient = (
            (x_plus - x_minus) * 0.5 - drive_force,
            (y_plus - y_minus) * 0.5,
            (z_plus - z_minus) * 0.5,
        )
        carried = (flow[0, x], flow[1, x], flow[2, x])
        for c in range(3):
            value, x_minus, x_plus, z_minus, z_plus, y_minus, y_plus = around(c, x)
            laplace = x_plus + x_minus + z_plus + z_minus + y_plus + y_minus - 6.0 * value
            advect = (
                carried[0] * (x_plus - x_minus)
                + carried[1] * (y_plus - y_minus)
                + carried[2] * (z_plus - z_minus)
            ) * 0.5
            inner[c, x] = value + time_step * (viscosity * laplace - advect - gradient[c])
        w_first[x : x + 1] = flow[2, x, 0:1]
        w_last[x : x + 1] = flow[2, x, size_z - 1 : size_z]
    kept[...] = own[...]
    u_first[...] = flow[0, 0]
    u_last[...] = flow[0, size_x - 1]


def predict_inner(sizes, flow, own):
    size_x, size_z, size_y = sizes
    return call(
        functools.partial(predict_inner_kernel, sizes),
        [float32(3, *sizes)]
        + [float32(size_z, size_y)] * 2
        + [float32(size_x, size_y)] * 2
        + [float32(*own.shape)],
        [],
        [flow, own],
        [],
        200 * flow.size,
        8 * flow.size,
    )


def predict_outer_kernel(
    layout,
    inner,
    u_first,
    u_last,
    w_first,
    w_last,
    x_0,
    x_1,
    z_0,
    z_1,
    predicted,
    field_high,
    field_low,
):
    size_x, size_z, size_y = layout.sizes
    row = lax.broadcasted_iota(jnp.int32, (8, size_y), 0)
    lower, upper = in_order("gz", z_0[: layout.ghost_z].shape)(
        z_0[: layout.ghost_z], z_1[: layout.ghost_z]
    )
    left, right = in_order("gx", x_0.shape)(x_0[...], x_1[...])
    for x in range(size_x):
        carried_low = w_first[x : x + 1]
        carried_high = w_last[x : x + 1]
        for c in range(3):
            ghost = c * size_x + x
            change_low = (viscosity + 0.5 * carried_low) * lower[ghost : ghost + 1]
            change_high = (viscosity - 0.5 * carried_high) * upper[ghost : ghost + 1]
            if c == 2:
                ghost = 3 * size_x + x
                change_low += 0.5 * lower[ghost : ghost + 1]
                change_high -= 0.5 * upper[ghost : ghost + 1]
            if x in (0, size_x - 1):
                sign, layer, carried = (0.5, left, u_first) if x == 0 else (-0.5, right, u_last)
                ghost = slice(c * size_z, (c + 1) * size_z)
                change = (viscosity + sign * carried[...]) * layer[ghost]
                if c == 0:
                    change += sign * layer[3 * size_z : 4 * size_z]
                predicted[c, x] = inner[c, x] + time_step * change
            else:
                predicted[c, x] = inner[c, x]
            predicted[c, x, 0:8] += jnp.where(row == 0, time_step * change_low, 0.0)
            predicted[c, x, size_z - 8 : size_z] += jnp.where(
                row == 7, time_step * change_high, 0.0
            )
    for c in range(3):
        for q, (xs, zs) in enumerate(quarters(layout.sizes)):
            part = jnp.transpose(predicted[c, xs, zs].reshape(LANES, size_y))
            high = part.astype(jnp.bfloat16).astype(jnp.float32)
            field_high[c, :, q * LANES : (q + 1) * LANES] = high
            field_low[c, :, q * LANES : (q + 1) * LANES] = part - high


def predict_outer(layout, inner, *layers):
    _, _, size_y = layout.sizes
    return call(
        functools.partial(predict_outer_kernel, layout),
        [float32(3, *layout.sizes)] + [float32(3, size_y, layout.plane)] * 2,
        [],
        [*inner, *layers],
        [],
        10 * inner[0].size,
        16 * inner[0].size,
    )


def swap_groups(values, width):
    count = len(values)
    lane = lax.broadcasted_iota(jnp.int32, values[0].shape, 1)
    values = list(values)
    step = count // 2
    while step:
        reach = step * width
        keep = lane % (2 * reach) < reach
        for i in range(count):
            if i & step == 0:
                a, b = values[i], values[i + step]
                values[i] = jnp.where(keep, a, pltpu.roll(b, reach, 1))
                values[i + step] = jnp.where(keep, pltpu.roll(a, LANES - reach, 1), b)
        step //= 2
    return values


def transform_z_kernel(sizes, counts, table_high, table_low, *refs):
    size_x, size_z, size_y = sizes
    parts_x, parts_z = counts
    pieces, refs = refs[:parts_z], refs[parts_z:]
    outs, (gathered, turned, whole) = refs[:parts_x], refs[parts_x:]
    height = size_y // parts_z
    columns = height * size_x
    group = LANES // size_z
    for piece, step in zip(pieces, steps(parts_z)):
        gathered[lax.axis_index("gz") ^ step] = piece[...]
    lane = lax.broadcasted_iota(jnp.int32, (height, LANES), 1)
    edges = [gathered[i, :, size_x * size_z :] for i in range(parts_z)]
    blocks = parts_z // group
    for block in range(blocks):
        for q in range(size_x // group):
            lanes = slice(q * LANES, (q + 1) * LANES)
            values = [gathered[block * group + i, :, lanes] for i in range(group)]
            for j, value in enumerate(swap_groups(values, size_z)):
                turned[block, pl.ds(q * group + j, height, stride=size_x), :] = value
        for end in range(2):
            layer = edges[block * group]
            for i in range(group):
                moved = (i - end) * size_z % LANES
                part = edges[block * group + i]
                part = pltpu.roll(part, moved, 1) if moved else part
                layer = part if i == 0 else jnp.where(lane < i * size_z, layer, part)
            turned[block, pl.ds(columns + end, height, stride=2), :] = layer
    for x in range(size_x):
        ends = jnp.zeros((height, LANES), jnp.float32)
        for i in range(parts_z):
            part = pltpu.roll(edges[i], (2 * i - 2 * size_z - 2 * x) % LANES, 1)
            ends = jnp.where((lane >= 2 * i) & (lane < 2 * i + 2), part, ends)
        turned[blocks, pl.ds(x, height, stride=size_x), :] = ends
    turned[blocks, columns:] = jnp.zeros((2 * height, LANES), jnp.float32)
    lines = jnp.concatenate([turned[b] for b in range(blocks + 1)], axis=1)
    high, low = split(lines)
    result = lax.dot_general(
        table_high[...], high, TRANSPOSED, preferred_element_type=jnp.float32
    )
    result += lax.dot_general(
        table_low[...], high, TRANSPOSED, preferred_element_type=jnp.float32
    )
    result += lax.dot_general(
        table_high[...], low, TRANSPOSED, preferred_element_type=jnp.float32
    )
    whole[:, columns:] = jnp.zeros((whole.shape[0], LANES), jnp.float32)
    whole[:, : columns + 2 * height] = result
    rows = whole.shape[0] // parts_x
    modes = rows // 2
    lane = lax.broadcasted_iota(jnp.int32, (modes, LANES), 1)
    for out, step in zip(outs, steps(parts_x)):
        first = pl.multiple_of((lax.axis_index("gx") ^ step) * rows, 8)
        for t in range(columns // LANES):
            out[t * rows : (t + 1) * rows] = whole[
                pl.ds(first, rows), t * LANES : (t + 1) * LANES
            ]
        real = whole[pl.ds(first, modes), columns : columns + LANES]
        imag = whole[pl.ds(first + modes, modes), columns : columns + LANES]
        imag = pltpu.roll(imag, 2 * height, 1)
        out[columns // LANES * rows :] = jnp.where(lane < 2 * height, real, imag)


def transform_z(sizes, counts, table, pieces):
    size_x, size_z, size_y = sizes
    parts_x, parts_z = counts
    length_z = size_z * parts_z
    height = size_y // parts_z
    columns = height * size_x
    assert 2 * parts_z <= LANES and 4 * height <= LANES
    rows = 2 * length_z // parts_x
    return call(
        functools.partial(transform_z_kernel, sizes, counts),
        [float32(columns // LANES * rows + rows // 2, LANES)] * parts_x,
        [],
        [*table, *pieces],
        [
            pltpu.VMEM((parts_z, *pieces[0].shape), jnp.float32),
            pltpu.VMEM((length_z // LANES + 1, columns + 2 * height, LANES), jnp.float32),
            pltpu.VMEM((2 * length_z, columns + LANES), jnp.float32),
        ],
        24 * length_z * length_z * columns,
        12 * length_z * columns,
    )


def transform_x_kernel(sizes, counts, table_high, table_low, *refs):
    size_x, size_z, size_y = sizes
    parts_x, parts_z = counts
    pieces, (source, gathered, turned) = refs[:parts_x], refs[parts_x:]
    length_x = size_x * parts_x
    modes = size_z * parts_z // parts_x
    height = size_y // parts_z
    group = LANES // size_x
    rows = 2 * modes
    main = height // group * rows
    for piece, step in zip(pieces, steps(parts_x)):
        gathered[lax.axis_index("gx") ^ step] = piece[...]
    for block in range(parts_x // group):
        for q in range(height // group):
            values = [
                gathered[block * group + i, q * rows : (q + 1) * rows] for i in range(group)
            ]
            for j, value in enumerate(swap_groups(values, size_x)):
                first = (q * group + j) * modes
                for c in range(2):
                    column = c * length_x + block * LANES
                    turned[first : first + modes, column : column + LANES] = value[
                        c * modes : (c + 1) * modes
                    ]
        ends = [gathered[block * group + i, main:] for i in range(group)]
        column = 2 * length_x + block * LANES
        for j, value in enumerate(swap_groups(ends, 2)):
            for q in range(height // group):
                first = (q * group + j) * modes
                moved = -2 * group * q % LANES
                turned[first : first + modes, column : column + LANES] = (
                    pltpu.roll(value, moved, 1) if moved else value
                )
    high, low = split(turned[...])
    result = jnp.dot(high, table_high[...], preferred_element_type=jnp.float32)
    result += jnp.dot(low, table_high[...], preferred_element_type=jnp.float32)
    result += jnp.dot(high, table_low[...], preferred_element_type=jnp.float32)
    source[0] = result[:, :length_x].reshape(height, modes, length_x)
    source[1] = result[:, length_x:].reshape(height, modes, length_x)


def transform_x(sizes, counts, table, pieces):
    size_x, size_z, size_y = sizes
    parts_x, parts_z = counts
    length_x = size_x * parts_x
    modes = size_z * parts_z // parts_x
    height = size_y // parts_z
    return call(
        functools.partial(transform_x_kernel, sizes, counts),
        float32(2, height, modes, length_x),
        [],
        [*table, *pieces],
        [
            pltpu.VMEM((parts_x, *pieces[0].shape), jnp.float32),
            pltpu.VMEM((height * modes, table[0].shape[0]), jnp.float32),
        ],
        24 * length_x * length_x * height * modes,
        24 * length_x * height * modes,
    )


def split_table(table):
    high = table.astype(np.float32).astype(jnp.bfloat16)
    low = (table - high.astype(np.float64)).astype(np.float32).astype(jnp.bfloat16)
    return jnp.asarray(high), jnp.asarray(low)


def angles(length):
    counter = np.arange(length)
    turn = (counter[:, None] * counter[None, :] % length) * (2.0 * np.pi / length)
    return np.cos(turn), np.sin(turn)


def table_z(length, blocks, parts):
    cosine, sine = angles(length)
    modes, size = length // blocks, length // parts
    table = np.stack([cosine, -sine]).reshape(2, blocks, modes, length)
    table = table.transpose(1, 0, 2, 3).reshape(2 * length, length)
    ends = np.zeros((2 * length, LANES))
    for part in range(parts):
        ends[:, 2 * part] = 0.5 * table[:, (part * size - 1) % length]
        ends[:, 2 * part + 1] = -0.5 * table[:, (part + 1) * size % length]
    return split_table(np.concatenate([table, ends], axis=1))


def table_x(length, parts, height, scale):
    cosine, sine = angles(length)
    size = length // parts
    group = LANES // size
    table = np.block([[cosine, -sine], [sine, cosine]]) * scale
    ends = np.zeros((parts // group * LANES, 2 * length))
    for part in range(parts):
        for c in range(2):
            row = part // group * LANES + c * 2 * height + 2 * (part % group)
            ends[row] = 0.5 * table[c * length + (part * size - 1) % length]
            ends[row + 1] = -0.5 * table[c * length + (part + 1) * size % length]
    return split_table(np.concatenate([table, ends], axis=0))


def exchange(pieces, axis):
    devices = lax.axis_size(axis)
    assert devices & (devices - 1) == 0
    return [pieces[0]] + [
        lax.ppermute(piece, axis, [(i, i ^ step) for i in range(devices)])
        for piece, step in zip(pieces[1:], steps(devices)[1:])
    ]


def on_device(
    flow_state, slot_ids, corners, marker_cells, marker_frac, particle_velocity, particle_spin
):
    sizes = flow_state.shape[1:]
    size_x, size_z, size_y = sizes
    counts = (lax.axis_size("gx"), lax.axis_size("gz"))
    length_x, length_z = (size_x * counts[0], size_z * counts[1])
    slots, markers = marker_cells.shape[1:]
    layout = Layout(sizes, slots, markers)

    own, x_0, x_1, z_0, z_1 = pack(
        layout, slot_ids, corners, flow_state, marker_cells, marker_frac
    )
    marks_0 = swap(own, "gx", 0)
    marks_1 = swap(own, "gx", 1)
    z_0, z_1 = swap(z_0, "gz", 0), swap(z_1, "gz", 1)
    x_0, x_1 = swap(x_0, "gx", 0), swap(x_1, "gx", 1)
    *inner, own = predict_inner(sizes, flow_state, own)
    sides = join(marks_0, marks_1)
    corners_0, corners_1 = swap(sides, "gz", 0), swap(sides, "gz", 1)
    predicted, *fields = predict_outer(layout, inner, x_0, x_1, z_0, z_1)
    row_0, row, row_1, facts = collect(
        layout, own, marks_0, marks_1, z_0, z_1, corners_0, corners_1
    )

    tiles = (0, 1, 2)
    parts, rows_saved = sample(layout, ((tiles, 0), (tiles, 2)), facts, (row_0, row_1), fields, ())
    from_z = swap(parts[0], "gz", 0) + swap(parts[1], "gz", 1)
    (side_part,), (side_saved,) = sample(layout, (((0, 2), 1),), facts, (row,), fields, ())
    from_0 = swap(side_part[:, :slots] + from_z[:, :slots], "gx", 0)
    from_1 = swap(side_part[:, slots:] + from_z[:, 2 * slots :], "gx", 1)
    motion = (particle_velocity, particle_spin)
    (own_part,), (own_saved,) = sample(layout, (((1,), 1),), facts, (row,), fields, motion)
    push = own_part - (from_z[:, slots : 2 * slots] + from_0 + from_1)

    row_push = jnp.concatenate([swap(push, "gx", 0), push, swap(push, "gx", 1)], axis=1)
    rows_push = swap(row_push, "gz", 0), swap(row_push, "gz", 1)
    forcing = spread_own(layout, facts, own_saved, push)
    forcing = spread_side(layout, facts, side_saved, row_push, forcing)
    velocity, pieces = spread_rest(
        layout, counts[1], facts, rows_saved, rows_push, forcing, predicted
    )

    pieces = exchange(pieces, "gz")
    pieces = transform_z(sizes, counts, table_z(length_z, *counts), pieces)
    pieces = exchange(pieces, "gx")
    scale = 1.0 / math.sqrt(length_x * length_z)
    table = table_x(length_x, counts[0], size_y // counts[1], scale)
    source = transform_x(sizes, counts, table, pieces)
    return velocity, source


def solution(mesh):
    return jax.shard_map(
        on_device,
        mesh=mesh,
        in_specs=(
            P(None, "gx", "gz", None),
            P(("gx", "gz")),
            P(None, ("gx", "gz")),
            P(None, ("gx", "gz"), None),
            P(None, ("gx", "gz"), None),
            P(),
            P(),
        ),
        out_specs=(P(None, "gx", "gz", None), P(None, "gz", "gx", None)),
        check_vma=False,
    )
```

```python
import functools
import math

import jax
import jax.numpy as jnp
import numpy as np
from jax import lax
from jax.experimental import pallas as pl
from jax.experimental.pallas import tpu as pltpu
from jax.sharding import PartitionSpec as P


BOX = 24
HALF = 12
WINDOW = 32
LANES = 128
KERNEL_BYTES = 16 * 1024 * 1024

time_step = 0.1
viscosity = 0.2
drive_force = 1.0


IN_VMEM = pl.BlockSpec(memory_space=pltpu.VMEM)
IN_SMEM = pl.BlockSpec(memory_space=pltpu.SMEM)
TRANSPOSED = (((1,), (1,)), ((), ()))


def float32(*shape):
    return jax.ShapeDtypeStruct(shape, jnp.float32)


def call(kernel, out_shape, scalars, arrays, scratch, flops, moved):
    outputs = len(out_shape) if isinstance(out_shape, (list, tuple)) else 0
    return pl.pallas_call(
        kernel,
        out_shape=out_shape,
        in_specs=[IN_SMEM] * len(scalars) + [IN_VMEM] * len(arrays),
        out_specs=[IN_VMEM] * outputs if outputs else IN_VMEM,
        scratch_shapes=scratch,
        compiler_params=pltpu.CompilerParams(vmem_limit_bytes=KERNEL_BYTES),
        cost_estimate=pl.CostEstimate(flops=flops, bytes_accessed=moved, transcendentals=0),
    )(*scalars, *arrays)


def swap(array, axis, partner):
    devices = lax.axis_size(axis)
    pairs = [(i, (i + (1 if i % 2 == partner else -1)) % devices) for i in range(devices)]
    return lax.ppermute(array, axis, pairs)


def even(axis):
    return lax.rem(lax.axis_index(axis), 2) == 0


def steps(devices):
    return [0, *range(devices - 1, 0, -1)]


def in_order(axis, shape):
    parity = jnp.full(shape, lax.rem(lax.axis_index(axis), 2), jnp.int32)
    return lambda one, two: (
        jnp.where(parity == 0, two, one),
        jnp.where(parity == 0, one, two),
    )


def cosine_coefficients():
    samples = 2.0 + 2.0 * np.cos(np.pi * (np.arange(64) + 0.5) / 64)
    values = np.cos(np.pi / 4 * np.sqrt(samples)) * np.sqrt(0.5)
    fit = np.polynomial.chebyshev.Chebyshev.fit(samples, values, 4, domain=[0, 4])
    return [float(v) for v in fit.convert(kind=np.polynomial.Polynomial).coef]


COSINE = cosine_coefficients()


def weight(offset):
    square = jnp.minimum(offset * offset, 4.0)
    value = COSINE[-1] * square + COSINE[-2]
    for coefficient in COSINE[-3::-1]:
        value = value * square + coefficient
    return value * value


def split(value):
    high = value.astype(jnp.bfloat16)
    low = (value - high.astype(jnp.float32)).astype(jnp.bfloat16)
    return high, low


def row_weights(count, position):
    cells = lax.broadcasted_iota(jnp.int32, (count, position.shape[1]), 0)
    return weight(cells.astype(jnp.float32) - position)


def plane_weights(weight_x, weight_z, half_z, high, low):
    count = 0
    for z in range(0, weight_z.shape[0], half_z):
        part = weight_z[z : z + half_z]
        for x in range(weight_x.shape[0]):
            rows = slice(count * half_z, (count + 1) * half_z)
            high[rows], low[rows] = split(weight_x[x : x + 1] * part)
            count += 1


BODIES = ((True, True), (True, False), (False, True), (False, False))


def quarters(sizes):
    half_x, half_z = sizes[0] // 2, sizes[1] // 2
    for z in range(2):
        for x in range(2):
            yield slice(x * half_x, (x + 1) * half_x), slice(z * half_z, (z + 1) * half_z)


class Layout:
    def __init__(self, sizes, slots, markers):
        self.sizes, self.slots, self.markers = sizes, slots, markers
        self.tiles = markers // LANES
        self.fact_row = 3 * self.tiles * slots
        self.rows = self.fact_row + slots
        self.ghost_x = 4 * sizes[1]
        self.ghost_z = 4 * sizes[0]
        self.plane = sizes[0] * sizes[1]


def marker_row(layout, marks, base, direction, slot):
    first = base + direction * layout.tiles * layout.slots + slot
    rows = [marks[pl.ds(first + t * layout.slots, 1), :] for t in range(layout.tiles)]
    return jnp.concatenate(rows, axis=1)


def slot_visits(layout, facts, marks, saved, blocks, step, high, low, visit):
    size_x, size_z, _ = layout.sizes
    half_x, half_z = size_x // 2, size_z // 2
    slots = layout.slots

    def body(index, carry):
        block, slot = index // slots, index % slots
        block = blocks[0] + block * (blocks[1] - blocks[0] if len(blocks) > 1 else 0)
        fact = (step * 3 + block) * slots + slot
        kind = facts[4, fact]

        def part(all_x, all_z):
            first_x, first_z, first_y = facts[0, fact], facts[1, fact], facts[2, fact]
            first = pl.multiple_of(facts[5, fact], 8)
            upper_x = 0 if all_x else facts[6, fact]
            upper_z = 0 if all_z else facts[7, fact]
            start_x, start_z = upper_x * half_x, upper_z * half_z
            lanes = [(upper_z + z) * 2 * LANES + upper_x * LANES for z in range(1 + all_z)]
            width = (1 + all_x) * LANES
            if all_x and all_z:
                pieces = [(0, 4 * LANES)]
            else:
                pieces = [(pl.multiple_of(lane, LANES), width) for lane in lanes]
            rows_x = slice(0, size_x if all_x else half_x)
            rows_z = slice(size_x, size_x + (size_z if all_z else half_z))
            rows_y = slice(size_x + size_z, size_x + size_z + WINDOW)
            if marks is not None:
                base = block * layout.rows
                starts = (first_x - start_x, first_z - start_z, first_y - first)
                for direction, rows in enumerate((rows_x, rows_z, rows_y)):
                    position = marker_row(layout, marks, base, direction, slot)
                    position += starts[direction].astype(jnp.float32)
                    saved[index, rows, :] = row_weights(rows.stop - rows.start, position)
            plane_weights(saved[index, rows_x, :], saved[index, rows_z, :], half_z, high, low)
            weight_y = saved[index, rows_y, :]
            visit(index, block * slots + slot, first, weight_y, pieces)

        @pl.when(kind != 0)
        def _():
            for number, (all_x, all_z) in enumerate(BODIES):
                pl.when(kind == number + 1)(functools.partial(part, all_x, all_z))

        return carry

    lax.fori_loop(0, len(blocks) * slots, body, 0)


def rigid_motion(layout, facts, marks, motion, block, slot):
    particle = facts[3, (3 + block) * layout.slots + slot] - 1
    chosen = lax.broadcasted_iota(jnp.int32, motion[0].shape, 1) == particle
    moving, turning = [
        jnp.sum(jnp.where(chosen, part[...], 0.0), axis=1, keepdims=True) for part in motion
    ]
    lever = [
        marker_row(layout, marks, block * layout.rows, direction, slot) - HALF
        for direction in (0, 2, 1)
    ]
    for c in range(3):
        a, b = (c + 1) % 3, (c + 2) % 3
        turned = turning[a : a + 1] * lever[b] - turning[b : b + 1] * lever[a]
        yield moving[c : c + 1] + turned


def sample_slots(
    layout, facts, marks, motion, field_high, field_low, out, saved, blocks, step, high, low
):
    def visit(index, row, first, weight_y, pieces):
        rows = pl.ds(first, WINDOW)

        def window(field):
            parts = [
                jnp.concatenate([field[c, rows, pl.ds(lane, width)] for c in range(3)], axis=0)
                for lane, width in pieces
            ]
            return jnp.concatenate(parts, axis=1).astype(jnp.bfloat16)

        window_high, window_low = window(field_high), window(field_low)
        count = window_high.shape[1]
        both = jnp.concatenate([window_high, window_low], axis=0)
        value = jnp.dot(both, high[:count], preferred_element_type=jnp.float32)
        rest = jnp.dot(window_high, low[:count], preferred_element_type=jnp.float32)
        value = value[: 3 * WINDOW] + value[3 * WINDOW :] + rest
        target = None
        if motion:
            target = list(rigid_motion(layout, facts, marks, motion, blocks[0], index))
        for c in range(3):
            part = value[c * WINDOW : (c + 1) * WINDOW] * weight_y
            sampled = jnp.sum(part, axis=0, keepdims=True)
            out[c, pl.ds(index, 1), :] = sampled if target is None else target[c] - sampled

    out[...] = jnp.zeros(out.shape, jnp.float32)
    slot_visits(layout, facts, marks, saved, blocks, step, high, low, visit)


def sample_kernel(layout, groups, moved, facts, *refs):
    count = len(groups)
    marks, refs = refs[:count], refs[count:]
    (field_high, field_low), refs = refs[:2], refs[2:]
    motion, refs = refs[:moved], refs[moved:]
    outs, refs = refs[:count], refs[count:]
    saved, (high, low) = refs[:count], refs[count:]
    for i, (blocks, step) in enumerate(groups):
        sample_slots(
            layout,
            facts,
            marks[i],
            motion,
            field_high,
            field_low,
            outs[i],
            saved[i],
            blocks,
            step,
            high,
            low,
        )


def visit_cost(layout, blocks):
    return len(blocks) * layout.slots * 18 * WINDOW * layout.plane * layout.markers


def weight_scratch(layout):
    return [pltpu.VMEM((layout.plane, layout.markers), jnp.bfloat16)] * 2


def sample(layout, groups, facts, marks, fields, motion):
    markers, weights = layout.markers, layout.sizes[0] + layout.sizes[1] + WINDOW
    counts = [len(blocks) * layout.slots for blocks, _ in groups]
    results = call(
        functools.partial(sample_kernel, layout, groups, len(motion)),
        [float32(3, count, markers) for count in counts]
        + [float32(count, weights, markers) for count in counts],
        [facts],
        [*marks, *fields, *motion],
        weight_scratch(layout),
        sum(visit_cost(layout, blocks) for blocks, _ in groups),
        8 * fields[0].size,
    )
    return results[: len(groups)], results[len(groups) :]


def spread_slots(layout, blocks, step, facts, saved, push, own_rows, total, high, low):
    def visit(index, row, first, weight_y, pieces):
        slot = index if own_rows else row
        count = sum(width for _, width in pieces)
        value = jnp.concatenate(
            [weight_y * push[c, pl.ds(slot, 1), :] for c in range(3)], axis=0
        )
        value_high, value_low = split(value)
        both = jnp.concatenate([value_high, value_low], axis=0)
        added = lax.dot_general(
            both, high[:count], TRANSPOSED, preferred_element_type=jnp.float32
        )
        rest = lax.dot_general(
            value_high, low[:count], TRANSPOSED, preferred_element_type=jnp.float32
        )
        added = added[: 3 * WINDOW] + added[3 * WINDOW :] + rest
        column = 0
        for lane, width in pieces:
            for c in range(3):
                part = added[c * WINDOW : (c + 1) * WINDOW, column : column + width]
                total[c, pl.ds(first, WINDOW), pl.ds(lane, width)] += part
            column += width

    slot_visits(layout, facts, None, saved, blocks, step, high, low, visit)


def spread_own_kernel(layout, facts, saved, push, total, high, low):
    total[...] = jnp.zeros(total.shape, jnp.float32)
    spread_slots(layout, (1,), 1, facts, saved, push, True, total, high, low)


def spread_own(layout, facts, saved, push):
    return call(
        functools.partial(spread_own_kernel, layout),
        float32(3, layout.sizes[2], layout.plane),
        [facts],
        [saved, push],
        weight_scratch(layout),
        visit_cost(layout, (1,)),
        12 * layout.sizes[2] * layout.plane,
    )


def spread_side_kernel(layout, facts, saved, push, before, total, high, low):
    total[...] = before[...]
    spread_slots(layout, (0, 2), 1, facts, saved, push, False, total, high, low)


def spread_side(layout, facts, saved, push, before):
    return call(
        functools.partial(spread_side_kernel, layout),
        float32(*before.shape),
        [facts],
        [saved, push, before],
        weight_scratch(layout),
        visit_cost(layout, (0, 2)),
        8 * before.size,
    )


def spread_rest_kernel(
    layout, parts, facts, saved_0, saved_1, push_0, push_1, before, predicted, velocity, *refs
):
    outs, (total, high, low, edges, whole) = refs[:parts], refs[parts:]
    size_x, size_z, size_y = layout.sizes
    total[...] = before[...]
    row = (0, 1, 2)
    spread_slots(layout, row, 0, facts, saved_0, push_0, False, total, high, low)
    spread_slots(layout, row, 2, facts, saved_1, push_1, False, total, high, low)
    for c in range(3):
        for q, (xs, zs) in enumerate(quarters(layout.sizes)):
            part = jnp.transpose(total[c, :, q * LANES : (q + 1) * LANES])
            part = part.reshape(size_x // 2, size_z // 2, size_y)
            velocity[c, xs, zs] = predicted[c, xs, zs] + part
    row = lax.broadcasted_iota(jnp.int32, (size_z, size_y), 0)
    lane = lax.broadcasted_iota(jnp.int32, (size_z, size_y), 1)
    group = LANES // size_z
    for q in range(size_x // group):
        pieces = []
        for x in range(q * group, (q + 1) * group):
            y_minus, y_plus = y_neighbours(velocity[1, x], lane, 0.0, 0.0)
            z_minus, z_plus = z_neighbours(velocity[2, x], row, 0.0, 0.0)
            change = y_plus - y_minus + z_plus - z_minus
            if x > 0:
                change -= velocity[0, x - 1]
            if x < size_x - 1:
                change += velocity[0, x + 1]
            pieces.append(change * 0.5)
        part = jnp.concatenate(pieces, axis=0)
        whole[:, q * LANES : (q + 1) * LANES] = jnp.transpose(part)
    edges[...] = jnp.zeros(edges.shape, jnp.float32)
    edges[:size_z] = velocity[0, 0]
    edges[size_z : 2 * size_z] = velocity[0, size_x - 1]
    for x in range(size_x):
        first = 2 * size_z + 2 * x
        edges[first : first + 1] = velocity[2, x, 0:1]
        edges[first + 1 : first + 2] = velocity[2, x, size_z - 1 : size_z]
    whole[:, layout.plane :] = jnp.transpose(edges[...])
    height = size_y // parts
    for out, step in zip(outs, steps(parts)):
        first = pl.multiple_of((lax.axis_index("gz") ^ step) * height, 8)
        out[...] = whole[pl.ds(first, height), :]


def spread_rest(layout, parts, facts, saved, pushes, before, predicted):
    size_x, size_z, size_y = layout.sizes
    assert 2 * size_z + 2 * size_x <= LANES
    width = layout.plane + LANES
    velocity, *pieces = call(
        functools.partial(spread_rest_kernel, layout, parts),
        [float32(3, size_x, size_z, size_y)] + [float32(size_y // parts, width)] * parts,
        [facts],
        [*saved, *pushes, before, predicted],
        [pltpu.VMEM(before.shape, jnp.float32)]
        + weight_scratch(layout)
        + [pltpu.VMEM((LANES, size_y), jnp.float32), pltpu.VMEM((size_y, width), jnp.float32)],
        2 * visit_cost(layout, (0, 1, 2)),
        12 * before.size,
    )
    return velocity, pieces


def pack_kernel(
    layout,
    slot_ids_hbm,
    corners_hbm,
    flow,
    cells_hbm,
    fraction_hbm,
    own,
    x_0,
    x_1,
    z_0,
    z_1,
    slot_ids,
    corners,
    cells,
    fraction,
    edges,
    done,
):
    size_x, size_z, size_y = layout.sizes
    slots = layout.slots
    moves = [
        (slot_ids_hbm, slot_ids),
        (corners_hbm, corners),
        (cells_hbm, cells),
        (fraction_hbm, fraction),
    ]
    for c in range(4):
        moves.append((flow.at[c, :, pl.ds(size_z - 8, 8)], edges.at[0, c]))
        moves.append((flow.at[c, :, pl.ds(0, 8)], edges.at[1, c]))
    last = jnp.where(even("gx"), size_x - 1, 0)
    for c in range(4):
        rows = pl.ds(c * size_z, size_z)
        moves.append((flow.at[c, last], x_0.at[rows]))
        moves.append((flow.at[c, size_x - 1 - last], x_1.at[rows]))
    copies = [pltpu.make_async_copy(a, b, done.at[i]) for i, (a, b) in enumerate(moves)]
    for copy in copies:
        copy.start()
    for copy in copies[:4]:
        copy.wait()
    length_x = size_x * lax.axis_size("gx")
    length_z = size_z * lax.axis_size("gz")
    offset_x = length_x + HALF - lax.axis_index("gx") * size_x
    offset_z = length_z + HALF - lax.axis_index("gz") * size_z
    targets = ((own, 0), (z_0, layout.ghost_z), (z_1, layout.ghost_z))
    for a, direction in enumerate((0, 2, 1)):
        for t in range(layout.tiles):
            lanes = slice(t * LANES, (t + 1) * LANES)
            place = cells[direction, :, lanes].astype(jnp.float32) + fraction[direction, :, lanes]
            for target, base in targets:
                first = base + (a * layout.tiles + t) * slots
                target[first : first + slots] = place
    lane = lax.broadcasted_iota(jnp.int32, (1, LANES), 1)
    for slot in range(slots):
        first_x = lax.rem(corners[0, slot] + offset_x, length_x) - HALF
        first_z = lax.rem(corners[2, slot] + offset_z, length_z) - HALF
        fact = jnp.where(lane == 0, first_x, slot_ids[slot] + 1)
        fact = jnp.where(lane == 1, first_z, fact)
        fact = jnp.where(lane == 2, corners[1, slot], fact)
        for target, base in targets:
            row = base + layout.fact_row + slot
            target[row : row + 1] = fact.astype(jnp.float32)
    for copy in copies[4:]:
        copy.wait()
    choose = in_order("gz", (1, size_y))
    for c in range(4):
        for x in range(size_x):
            row = c * size_x + x
            z_0[row : row + 1], z_1[row : row + 1] = choose(
                edges[1, c, x, 0:1], edges[0, c, x, 7:8]
            )


def pack(layout, slot_ids, corners, flow, cells, fraction):
    in_hbm = pl.BlockSpec(memory_space=pltpu.HBM)
    size_x, _, size_y = layout.sizes
    return pl.pallas_call(
        functools.partial(pack_kernel, layout),
        out_shape=[float32(layout.rows, LANES)]
        + [float32(layout.ghost_x, LANES)] * 2
        + [float32(layout.ghost_z + layout.rows, LANES)] * 2,
        in_specs=[in_hbm] * 5,
        out_specs=[IN_VMEM] * 5,
        scratch_shapes=[
            pltpu.SMEM(slot_ids.shape, jnp.int32),
            pltpu.SMEM(corners.shape, jnp.int32),
            pltpu.VMEM(cells.shape, jnp.int32),
            pltpu.VMEM(fraction.shape, jnp.float32),
            pltpu.VMEM((2, 4, size_x, 8, size_y), jnp.float32),
            pltpu.SemaphoreType.DMA((20,)),
        ],
        name="pack",
        cost_estimate=pl.CostEstimate(
            flops=flow.size, bytes_accessed=flow.size, transcendentals=0
        ),
    )(slot_ids, corners, flow, cells, fraction)


def join_kernel(left, right, both):
    rows = left.shape[0]
    both[:rows] = left[...]
    both[rows:] = right[...]


def join(left, right):
    return call(
        join_kernel,
        float32(2 * left.shape[0], LANES),
        [],
        [left, right],
        [],
        left.size,
        16 * left.size,
    )


def collect_kernel(layout, own, side_0, side_1, one, two, corners_0, corners_1, *refs):
    rows, (facts, table) = refs[:3], refs[3:]
    count, slots = layout.rows, layout.slots
    size_x, size_z, size_y = layout.sizes
    for row, middle, base, sides in (
        (rows[0], one, layout.ghost_z, corners_0),
        (rows[1], own, 0, None),
        (rows[2], two, layout.ghost_z, corners_1),
    ):
        row[:count] = side_0[...] if sides is None else sides[:count]
        row[count : 2 * count] = middle[base : base + count]
        row[2 * count :] = side_1[...] if sides is None else sides[count:]
    for block in range(9):
        first = (block % 3) * count + layout.fact_row
        out = slice(block * slots, (block + 1) * slots)
        table[out] = rows[block // 3][first : first + slots]
    kind = lax.broadcasted_iota(jnp.int32, (8, LANES), 0)
    slot = lax.broadcasted_iota(jnp.int32, (8, LANES), 1)
    last = 2 * 3 * slots
    move_x = jnp.where(even("gx"), size_x, -size_x)
    move_z = jnp.where(even("gz"), size_z, -size_z)
    place = slot - jnp.where(slot >= last, last, jnp.where(slot >= 3 * slots, 3 * slots, 0))
    moved_x = jnp.where(place < slots, move_x, jnp.where(place >= 2 * slots, -move_x, 0))
    moved_z = jnp.where(slot < 3 * slots, move_z, jnp.where(slot >= last, -move_z, 0))
    moved = jnp.where(kind == 0, moved_x, jnp.where(kind == 1, moved_z, 0))
    known = jnp.transpose(table[...])[:8].astype(jnp.int32) + moved
    first_x, first_z, first_y, particle = [known[i : i + 1] for i in range(4)]
    half_x, half_z = size_x // 2, size_z // 2

    def between(value, low, high):
        return (value > low) & (value < high)

    meets = between(first_x, -BOX, size_x) & between(first_z, -BOX, size_z) & (particle > 0)
    part_x = jnp.where(between(first_x, half_x - BOX, half_x), 0, 2)
    part_z = jnp.where(between(first_z, half_z - BOX, half_z), 0, 1)
    facts[...] = known
    facts[4:5] = jnp.where(meets, 1 + part_x + part_z, 0)
    facts[5:6] = jnp.minimum(jnp.bitwise_and(first_y, -8), size_y - WINDOW)
    facts[6:7] = jnp.where(first_x >= half_x, 1, 0)
    facts[7:8] = jnp.where(first_z >= half_z, 1, 0)


def collect(layout, *tiles):
    return call(
        functools.partial(collect_kernel, layout),
        [float32(3 * layout.rows, LANES)] * 3 + [jax.ShapeDtypeStruct((8, LANES), jnp.int32)],
        [],
        tiles,
        [pltpu.VMEM((LANES, LANES), jnp.float32)],
        layout.rows * LANES,
        72 * layout.rows * LANES,
    )


def y_neighbours(value, lane, below, above):
    size_y = value.shape[-1]
    minus = jnp.where(lane == 0, below, pltpu.roll(value, 1, 1))
    plus = jnp.where(lane == size_y - 1, above, pltpu.roll(value, size_y - 1, 1))
    return minus, plus


def z_neighbours(value, row, below, above):
    size_z = value.shape[0]
    minus = jnp.where(row == 0, below, pltpu.roll(value, 1, 0))
    plus = jnp.where(row == size_z - 1, above, pltpu.roll(value, size_z - 1, 0))
    return minus, plus


def predict_inner_kernel(sizes, flow, own, inner, u_first, u_last, w_first, w_last, kept):
    size_x, size_z, size_y = sizes
    row = lax.broadcasted_iota(jnp.int32, (size_z, size_y), 0)
    lane = lax.broadcasted_iota(jnp.int32, (size_z, size_y), 1)
    nothing = jnp.zeros((size_z, size_y), jnp.float32)

    def around(c, x):
        value = flow[c, x]
        x_minus = flow[c, x - 1] if x > 0 else nothing
        x_plus = flow[c, x + 1] if x < size_x - 1 else nothing
        z_minus, z_plus = z_neighbours(value, row, 0.0, 0.0)
        edges = (0.0, 0.0) if c < 3 else (value, value)
        y_minus, y_plus = y_neighbours(value, lane, *edges)
        return value, x_minus, x_plus, z_minus, z_plus, y_minus, y_plus

    for x in range(size_x):
        _, x_minus, x_plus, z_minus, z_plus, y_minus, y_plus = around(3, x)
        gradient = (
            (x_plus - x_minus) * 0.5 - drive_force,
            (y_plus - y_minus) * 0.5,
            (z_plus - z_minus) * 0.5,
        )
        carried = (flow[0, x], flow[1, x], flow[2, x])
        for c in range(3):
            value, x_minus, x_plus, z_minus, z_plus, y_minus, y_plus = around(c, x)
            laplace = x_plus + x_minus + z_plus + z_minus + y_plus + y_minus - 6.0 * value
            advect = (
                carried[0] * (x_plus - x_minus)
                + carried[1] * (y_plus - y_minus)
                + carried[2] * (z_plus - z_minus)
            ) * 0.5
            inner[c, x] = value + time_step * (viscosity * laplace - advect - gradient[c])
        w_first[x : x + 1] = flow[2, x, 0:1]
        w_last[x : x + 1] = flow[2, x, size_z - 1 : size_z]
    kept[...] = own[...]
    u_first[...] = flow[0, 0]
    u_last[...] = flow[0, size_x - 1]


def predict_inner(sizes, flow, own):
    size_x, size_z, size_y = sizes
    return call(
        functools.partial(predict_inner_kernel, sizes),
        [float32(3, *sizes)]
        + [float32(size_z, size_y)] * 2
        + [float32(size_x, size_y)] * 2
        + [float32(*own.shape)],
        [],
        [flow, own],
        [],
        200 * flow.size,
        8 * flow.size,
    )


def predict_outer_kernel(
    layout,
    inner,
    u_first,
    u_last,
    w_first,
    w_last,
    x_0,
    x_1,
    z_0,
    z_1,
    predicted,
    field_high,
    field_low,
):
    size_x, size_z, size_y = layout.sizes
    row = lax.broadcasted_iota(jnp.int32, (8, size_y), 0)
    lower, upper = in_order("gz", z_0[: layout.ghost_z].shape)(
        z_0[: layout.ghost_z], z_1[: layout.ghost_z]
    )
    left, right = in_order("gx", x_0.shape)(x_0[...], x_1[...])
    for x in range(size_x):
        carried_low = w_first[x : x + 1]
        carried_high = w_last[x : x + 1]
        for c in range(3):
            ghost = c * size_x + x
            change_low = (viscosity + 0.5 * carried_low) * lower[ghost : ghost + 1]
            change_high = (viscosity - 0.5 * carried_high) * upper[ghost : ghost + 1]
            if c == 2:
                ghost = 3 * size_x + x
                change_low += 0.5 * lower[ghost : ghost + 1]
                change_high -= 0.5 * upper[ghost : ghost + 1]
            if x in (0, size_x - 1):
                sign, layer, carried = (0.5, left, u_first) if x == 0 else (-0.5, right, u_last)
                ghost = slice(c * size_z, (c + 1) * size_z)
                change = (viscosity + sign * carried[...]) * layer[ghost]
                if c == 0:
                    change += sign * layer[3 * size_z : 4 * size_z]
                predicted[c, x] = inner[c, x] + time_step * change
            else:
                predicted[c, x] = inner[c, x]
            predicted[c, x, 0:8] += jnp.where(row == 0, time_step * change_low, 0.0)
            predicted[c, x, size_z - 8 : size_z] += jnp.where(
                row == 7, time_step * change_high, 0.0
            )
    for c in range(3):
        for q, (xs, zs) in enumerate(quarters(layout.sizes)):
            part = jnp.transpose(predicted[c, xs, zs].reshape(LANES, size_y))
            high = part.astype(jnp.bfloat16).astype(jnp.float32)
            field_high[c, :, q * LANES : (q + 1) * LANES] = high
            field_low[c, :, q * LANES : (q + 1) * LANES] = part - high


def predict_outer(layout, inner, *layers):
    _, _, size_y = layout.sizes
    return call(
        functools.partial(predict_outer_kernel, layout),
        [float32(3, *layout.sizes)] + [float32(3, size_y, layout.plane)] * 2,
        [],
        [*inner, *layers],
        [],
        10 * inner[0].size,
        16 * inner[0].size,
    )


def swap_groups(values, width):
    count = len(values)
    lane = lax.broadcasted_iota(jnp.int32, values[0].shape, 1)
    values = list(values)
    step = count // 2
    while step:
        reach = step * width
        keep = lane % (2 * reach) < reach
        for i in range(count):
            if i & step == 0:
                a, b = values[i], values[i + step]
                if 2 * reach == LANES:
                    crossed = pltpu.roll(jnp.where(keep, b, a), reach, 1)
                    values[i] = jnp.where(keep, a, crossed)
                    values[i + step] = jnp.where(keep, crossed, b)
                    continue
                values[i] = jnp.where(keep, a, pltpu.roll(b, reach, 1))
                values[i + step] = jnp.where(keep, pltpu.roll(a, LANES - reach, 1), b)
        step //= 2
    return values


def copy_kernel(source, target):
    target[...] = source[...]


def copied(array):
    return call(copy_kernel, float32(*array.shape), [], [array], [], 1, 8 * array.size)


def transform_z_kernel(sizes, counts, table_high, table_low, *refs):
    size_x, size_z, size_y = sizes
    parts_x, parts_z = counts
    pieces, refs = refs[:parts_z], refs[parts_z:]
    outs, (gathered, turned, whole) = refs[:parts_x], refs[parts_x:]
    height = size_y // parts_z
    columns = height * size_x
    group = LANES // size_z
    for piece, step in zip(pieces, steps(parts_z)):
        gathered[lax.axis_index("gz") ^ step] = piece[...]
    lane = lax.broadcasted_iota(jnp.int32, (height, LANES), 1)
    edges = [gathered[i, :, size_x * size_z :] for i in range(parts_z)]
    blocks = parts_z // group
    for block in range(blocks):
        for q in range(size_x // group):
            lanes = slice(q * LANES, (q + 1) * LANES)
            values = [gathered[block * group + i, :, lanes] for i in range(group)]
            for j, value in enumerate(swap_groups(values, size_z)):
                turned[block, pl.ds(q * group + j, height, stride=size_x), :] = value
        for end in range(2):
            layer = edges[block * group]
            for i in range(group):
                moved = (i - end) * size_z % LANES
                part = edges[block * group + i]
                part = pltpu.roll(part, moved, 1) if moved else part
                layer = part if i == 0 else jnp.where(lane < i * size_z, layer, part)
            turned[block, pl.ds(columns + end, height, stride=2), :] = layer
        for i in range(group):
            moved = (i - 2) * size_z % LANES
            part = edges[block * group + i]
            part = pltpu.roll(part, moved, 1) if moved else part
            ends = part if i == 0 else jnp.where(lane < i * size_z, ends, part)
        for x in range(size_x):
            moved = -2 * x % LANES
            turned[blocks + block, pl.ds(x, height, stride=size_x), :] = (
                pltpu.roll(ends, moved, 1) if moved else ends
            )
        turned[blocks + block, columns:] = jnp.zeros((2 * height, LANES), jnp.float32)
    lines = jnp.concatenate([turned[b] for b in range(2 * blocks)], axis=1)
    high, low = split(lines)
    result = lax.dot_general(
        table_high[...], high, TRANSPOSED, preferred_element_type=jnp.float32
    )
    result += lax.dot_general(
        table_low[...], high, TRANSPOSED, preferred_element_type=jnp.float32
    )
    result += lax.dot_general(
        table_high[...], low, TRANSPOSED, preferred_element_type=jnp.float32
    )
    whole[:, columns:] = jnp.zeros((whole.shape[0], LANES), jnp.float32)
    whole[:, : columns + 2 * height] = result
    rows = whole.shape[0] // parts_x
    modes = rows // 2
    lane = lax.broadcasted_iota(jnp.int32, (modes, LANES), 1)
    for out, step in zip(outs, steps(parts_x)):
        first = pl.multiple_of((lax.axis_index("gx") ^ step) * rows, 8)
        for t in range(columns // LANES):
            out[t * rows : (t + 1) * rows] = whole[
                pl.ds(first, rows), t * LANES : (t + 1) * LANES
            ]
        real = whole[pl.ds(first, modes), columns : columns + LANES]
        imag = whole[pl.ds(first + modes, modes), columns : columns + LANES]
        imag = pltpu.roll(imag, 2 * height, 1)
        out[columns // LANES * rows :] = jnp.where(lane < 2 * height, real, imag)


def transform_z(sizes, counts, table, pieces):
    size_x, size_z, size_y = sizes
    parts_x, parts_z = counts
    length_z = size_z * parts_z
    height = size_y // parts_z
    columns = height * size_x
    assert 4 * height <= LANES
    rows = 2 * length_z // parts_x
    return call(
        functools.partial(transform_z_kernel, sizes, counts),
        [float32(columns // LANES * rows + rows // 2, LANES)] * parts_x,
        [],
        [*table, *pieces],
        [
            pltpu.VMEM((parts_z, *pieces[0].shape), jnp.float32),
            pltpu.VMEM((2 * length_z // LANES, columns + 2 * height, LANES), jnp.float32),
            pltpu.VMEM((2 * length_z, columns + LANES), jnp.float32),
        ],
        24 * length_z * length_z * columns,
        12 * length_z * columns,
    )


def transform_x_kernel(sizes, counts, table_high, table_low, *refs):
    size_x, size_z, size_y = sizes
    parts_x, parts_z = counts
    pieces, (source, gathered, turned) = refs[:parts_x], refs[parts_x:]
    length_x = size_x * parts_x
    modes = size_z * parts_z // parts_x
    height = size_y // parts_z
    group = LANES // size_x
    rows = 2 * modes
    main = height // group * rows
    for piece, step in zip(pieces, steps(parts_x)):
        gathered[lax.axis_index("gx") ^ step] = piece[...]
    for block in range(parts_x // group):
        for q in range(height // group):
            values = [
                gathered[block * group + i, q * rows : (q + 1) * rows] for i in range(group)
            ]
            for j, value in enumerate(swap_groups(values, size_x)):
                first = (q * group + j) * modes
                for c in range(2):
                    column = c * length_x + block * LANES
                    turned[first : first + modes, column : column + LANES] = value[
                        c * modes : (c + 1) * modes
                    ]
        ends = [gathered[block * group + i, main:] for i in range(group)]
        column = 2 * length_x + block * LANES
        for j, value in enumerate(swap_groups(ends, 2)):
            for q in range(height // group):
                first = (q * group + j) * modes
                moved = -2 * group * q % LANES
                turned[first : first + modes, column : column + LANES] = (
                    pltpu.roll(value, moved, 1) if moved else value
                )
    high, low = split(turned[...])
    result = jnp.dot(high, table_high[...], preferred_element_type=jnp.float32)
    result += jnp.dot(low, table_high[...], preferred_element_type=jnp.float32)
    result += jnp.dot(high, table_low[...], preferred_element_type=jnp.float32)
    source[0] = result[:, :length_x].reshape(height, modes, length_x)
    source[1] = result[:, length_x:].reshape(height, modes, length_x)


def transform_x(sizes, counts, table, pieces):
    size_x, size_z, size_y = sizes
    parts_x, parts_z = counts
    length_x = size_x * parts_x
    modes = size_z * parts_z // parts_x
    height = size_y // parts_z
    return call(
        functools.partial(transform_x_kernel, sizes, counts),
        float32(2, height, modes, length_x),
        [],
        [*table, *pieces],
        [
            pltpu.VMEM((parts_x, *pieces[0].shape), jnp.float32),
            pltpu.VMEM((height * modes, table[0].shape[0]), jnp.float32),
        ],
        24 * length_x * length_x * height * modes,
        24 * length_x * height * modes,
    )


def split_table(table):
    high = table.astype(np.float32).astype(jnp.bfloat16)
    low = (table - high.astype(np.float64)).astype(np.float32).astype(jnp.bfloat16)
    return jnp.asarray(high), jnp.asarray(low)


def angles(length):
    counter = np.arange(length)
    turn = (counter[:, None] * counter[None, :] % length) * (2.0 * np.pi / length)
    return np.cos(turn), np.sin(turn)


def table_z(length, blocks, parts):
    cosine, sine = angles(length)
    modes, size = length // blocks, length // parts
    table = np.stack([cosine, -sine]).reshape(2, blocks, modes, length)
    table = table.transpose(1, 0, 2, 3).reshape(2 * length, length)
    ends = np.zeros((2 * length, length))
    for part in range(parts):
        ends[:, part * size] = 0.5 * table[:, (part * size - 1) % length]
        ends[:, part * size + 1] = -0.5 * table[:, (part + 1) * size % length]
    return split_table(np.concatenate([table, ends], axis=1))


def table_x(length, parts, height, scale):
    cosine, sine = angles(length)
    size = length // parts
    group = LANES // size
    table = np.block([[cosine, -sine], [sine, cosine]]) * scale
    ends = np.zeros((parts // group * LANES, 2 * length))
    for part in range(parts):
        for c in range(2):
            row = part // group * LANES + c * 2 * height + 2 * (part % group)
            ends[row] = 0.5 * table[c * length + (part * size - 1) % length]
            ends[row + 1] = -0.5 * table[c * length + (part + 1) * size % length]
    return split_table(np.concatenate([table, ends], axis=0))


def exchange(pieces, axis):
    devices = lax.axis_size(axis)
    assert devices & (devices - 1) == 0
    received = [pieces[0]]
    for piece, step in zip(pieces[1:], steps(devices)[1:]):
        received.append(lax.ppermute(piece, axis, [(i, i ^ step) for i in range(devices)]))
    return received


def on_device(
    flow_state, slot_ids, corners, marker_cells, marker_frac, particle_velocity, particle_spin
):
    sizes = flow_state.shape[1:]
    size_x, size_z, size_y = sizes
    counts = (lax.axis_size("gx"), lax.axis_size("gz"))
    length_x, length_z = (size_x * counts[0], size_z * counts[1])
    slots, markers = marker_cells.shape[1:]
    layout = Layout(sizes, slots, markers)

    own, x_0, x_1, z_0, z_1 = pack(
        layout, slot_ids, corners, flow_state, marker_cells, marker_frac
    )
    marks_0 = swap(own, "gx", 0)
    marks_1 = swap(own, "gx", 1)
    z_0, z_1 = swap(z_0, "gz", 0), swap(z_1, "gz", 1)
    x_0, x_1 = swap(x_0, "gx", 0), swap(x_1, "gx", 1)
    *inner, own = predict_inner(sizes, flow_state, own)
    sides = join(marks_0, marks_1)
    corners_0, corners_1 = swap(sides, "gz", 0), swap(sides, "gz", 1)
    predicted, *fields = predict_outer(layout, inner, x_0, x_1, z_0, z_1)
    row_0, row, row_1, facts = collect(
        layout, own, marks_0, marks_1, z_0, z_1, corners_0, corners_1
    )

    tiles = (0, 1, 2)
    parts, rows_saved = sample(layout, ((tiles, 0), (tiles, 2)), facts, (row_0, row_1), fields, ())
    from_z = swap(parts[0], "gz", 0) + swap(parts[1], "gz", 1)
    (side_part,), (side_saved,) = sample(layout, (((0, 2), 1),), facts, (row,), fields, ())
    from_0 = swap(side_part[:, :slots] + from_z[:, :slots], "gx", 0)
    from_1 = swap(side_part[:, slots:] + from_z[:, 2 * slots :], "gx", 1)
    motion = (particle_velocity, particle_spin)
    (own_part,), (own_saved,) = sample(layout, (((1,), 1),), facts, (row,), fields, motion)
    push = own_part - (from_z[:, slots : 2 * slots] + from_0 + from_1)

    row_push = jnp.concatenate([swap(push, "gx", 0), push, swap(push, "gx", 1)], axis=1)
    rows_push = swap(row_push, "gz", 0), swap(row_push, "gz", 1)
    forcing = spread_own(layout, facts, own_saved, push)
    forcing = spread_side(layout, facts, side_saved, row_push, forcing)
    velocity, pieces = spread_rest(
        layout, counts[1], facts, rows_saved, rows_push, forcing, predicted
    )

    pieces = exchange(pieces, "gz")
    pieces = transform_z(sizes, counts, table_z(length_z, *counts), pieces)
    pieces = exchange(pieces, "gx")
    velocity = copied(velocity)
    scale = 1.0 / math.sqrt(length_x * length_z)
    table = table_x(length_x, counts[0], size_y // counts[1], scale)
    source = transform_x(sizes, counts, table, pieces)
    return velocity, source


def solution(mesh):
    return jax.shard_map(
        on_device,
        mesh=mesh,
        in_specs=(
            P(None, "gx", "gz", None),
            P(("gx", "gz")),
            P(None, ("gx", "gz")),
            P(None, ("gx", "gz"), None),
            P(None, ("gx", "gz"), None),
            P(),
            P(),
        ),
        out_specs=(P(None, "gx", "gz", None), P(None, "gz", "gx", None)),
        check_vma=False,
    )
```

```python
import functools
import math

import jax
import jax.numpy as jnp
import numpy as np
from jax import lax
from jax.experimental import pallas as pl
from jax.experimental.pallas import tpu as pltpu
from jax.sharding import PartitionSpec as P


BOX = 24
HALF = 12
WINDOW = 32
LANES = 128
KERNEL_BYTES = 16 * 1024 * 1024

time_step = 0.1
viscosity = 0.2
drive_force = 1.0


IN_VMEM = pl.BlockSpec(memory_space=pltpu.VMEM)
IN_SMEM = pl.BlockSpec(memory_space=pltpu.SMEM)
TRANSPOSED = (((1,), (1,)), ((), ()))


def float32(*shape):
    return jax.ShapeDtypeStruct(shape, jnp.float32)


def call(kernel, out_shape, scalars, arrays, scratch, flops, moved):
    outputs = len(out_shape) if isinstance(out_shape, (list, tuple)) else 0
    return pl.pallas_call(
        kernel,
        out_shape=out_shape,
        in_specs=[IN_SMEM] * len(scalars) + [IN_VMEM] * len(arrays),
        out_specs=[IN_VMEM] * outputs if outputs else IN_VMEM,
        scratch_shapes=scratch,
        compiler_params=pltpu.CompilerParams(vmem_limit_bytes=KERNEL_BYTES),
        cost_estimate=pl.CostEstimate(flops=flops, bytes_accessed=moved, transcendentals=0),
    )(*scalars, *arrays)


def swap(array, axis, partner):
    devices = lax.axis_size(axis)
    pairs = [(i, (i + (1 if i % 2 == partner else -1)) % devices) for i in range(devices)]
    return lax.ppermute(array, axis, pairs)


def even(axis):
    return lax.rem(lax.axis_index(axis), 2) == 0


def steps(devices):
    halves = [1 << bit for bit in reversed(range(devices.bit_length() - 1))]
    return [0] + [step for half in halves for step in range(half, 2 * half)]


def in_order(axis, shape):
    parity = jnp.full(shape, lax.rem(lax.axis_index(axis), 2), jnp.int32)
    return lambda one, two: (
        jnp.where(parity == 0, two, one),
        jnp.where(parity == 0, one, two),
    )


def cosine_coefficients():
    samples = 2.0 + 2.0 * np.cos(np.pi * (np.arange(64) + 0.5) / 64)
    values = np.cos(np.pi / 4 * np.sqrt(samples)) * np.sqrt(0.5)
    fit = np.polynomial.chebyshev.Chebyshev.fit(samples, values, 4, domain=[0, 4])
    return [float(v) for v in fit.convert(kind=np.polynomial.Polynomial).coef]


COSINE = cosine_coefficients()


def weight(offset):
    square = jnp.minimum(offset * offset, 4.0)
    value = COSINE[-1] * square + COSINE[-2]
    for coefficient in COSINE[-3::-1]:
        value = value * square + coefficient
    return value * value


def split(value):
    high = value.astype(jnp.bfloat16)
    low = (value - high.astype(jnp.float32)).astype(jnp.bfloat16)
    return high, low


def row_weights(count, position):
    cells = lax.broadcasted_iota(jnp.int32, (count, position.shape[1]), 0)
    return weight(cells.astype(jnp.float32) - position)


def plane_weights(weight_x, weight_z, half_z, high, low):
    count = 0
    for z in range(0, weight_z.shape[0], half_z):
        part = weight_z[z : z + half_z]
        for x in range(weight_x.shape[0]):
            rows = slice(count * half_z, (count + 1) * half_z)
            high[rows], low[rows] = split(weight_x[x : x + 1] * part)
            count += 1


BODIES = ((True, True), (True, False), (False, True), (False, False))


def quarters(sizes):
    half_x, half_z = sizes[0] // 2, sizes[1] // 2
    for z in range(2):
        for x in range(2):
            yield slice(x * half_x, (x + 1) * half_x), slice(z * half_z, (z + 1) * half_z)


class Layout:
    def __init__(self, sizes, slots, markers):
        self.sizes, self.slots, self.markers = sizes, slots, markers
        self.tiles = markers // LANES
        self.fact_row = 3 * self.tiles * slots
        self.rows = self.fact_row + slots
        self.ghost_x = 4 * sizes[1]
        self.ghost_z = 4 * sizes[0]
        self.plane = sizes[0] * sizes[1]


def marker_row(layout, marks, base, direction, slot):
    first = base + direction * layout.tiles * layout.slots + slot
    rows = [marks[pl.ds(first + t * layout.slots, 1), :] for t in range(layout.tiles)]
    return jnp.concatenate(rows, axis=1)


def slot_visits(layout, facts, marks, saved, blocks, step, high, low, visit):
    size_x, size_z, _ = layout.sizes
    half_x, half_z = size_x // 2, size_z // 2
    slots = layout.slots

    def body(index, carry):
        block, slot = index // slots, index % slots
        block = blocks[0] + block * (blocks[1] - blocks[0] if len(blocks) > 1 else 0)
        fact = (step * 3 + block) * slots + slot
        kind = facts[4, fact]

        def part(all_x, all_z):
            first_x, first_z, first_y = facts[0, fact], facts[1, fact], facts[2, fact]
            first = pl.multiple_of(facts[5, fact], 8)
            upper_x = 0 if all_x else facts[6, fact]
            upper_z = 0 if all_z else facts[7, fact]
            start_x, start_z = upper_x * half_x, upper_z * half_z
            lanes = [(upper_z + z) * 2 * LANES + upper_x * LANES for z in range(1 + all_z)]
            width = (1 + all_x) * LANES
            if all_x and all_z:
                pieces = [(0, 4 * LANES)]
            else:
                pieces = [(pl.multiple_of(lane, LANES), width) for lane in lanes]
            rows_x = slice(0, size_x if all_x else half_x)
            rows_z = slice(size_x, size_x + (size_z if all_z else half_z))
            rows_y = slice(size_x + size_z, size_x + size_z + WINDOW)
            if marks is not None:
                base = block * layout.rows
                starts = (first_x - start_x, first_z - start_z, first_y - first)
                for direction, rows in enumerate((rows_x, rows_z, rows_y)):
                    position = marker_row(layout, marks, base, direction, slot)
                    position += starts[direction].astype(jnp.float32)
                    saved[index, rows, :] = row_weights(rows.stop - rows.start, position)
            plane_weights(saved[index, rows_x, :], saved[index, rows_z, :], half_z, high, low)
            weight_y = saved[index, rows_y, :]
            visit(index, block * slots + slot, first, weight_y, pieces)

        @pl.when(kind != 0)
        def _():
            for number, (all_x, all_z) in enumerate(BODIES):
                pl.when(kind == number + 1)(functools.partial(part, all_x, all_z))

        return carry

    lax.fori_loop(0, len(blocks) * slots, body, 0)


def rigid_motion(layout, facts, marks, motion, block, slot):
    particle = facts[3, (3 + block) * layout.slots + slot] - 1
    chosen = lax.broadcasted_iota(jnp.int32, motion[0].shape, 1) == particle
    moving, turning = [
        jnp.sum(jnp.where(chosen, part[...], 0.0), axis=1, keepdims=True) for part in motion
    ]
    lever = [
        marker_row(layout, marks, block * layout.rows, direction, slot) - HALF
        for direction in (0, 2, 1)
    ]
    for c in range(3):
        a, b = (c + 1) % 3, (c + 2) % 3
        turned = turning[a : a + 1] * lever[b] - turning[b : b + 1] * lever[a]
        yield moving[c : c + 1] + turned


def sample_slots(
    layout, facts, marks, motion, field_high, field_low, out, saved, blocks, step, high, low
):
    def visit(index, row, first, weight_y, pieces):
        rows = pl.ds(first, WINDOW)

        def window(field):
            parts = [
                jnp.concatenate([field[c, rows, pl.ds(lane, width)] for c in range(3)], axis=0)
                for lane, width in pieces
            ]
            return jnp.concatenate(parts, axis=1).astype(jnp.bfloat16)

        window_high, window_low = window(field_high), window(field_low)
        count = window_high.shape[1]
        both = jnp.concatenate([window_high, window_low], axis=0)
        value = jnp.dot(both, high[:count], preferred_element_type=jnp.float32)
        rest = jnp.dot(window_high, low[:count], preferred_element_type=jnp.float32)
        value = value[: 3 * WINDOW] + value[3 * WINDOW :] + rest
        target = None
        if motion:
            target = list(rigid_motion(layout, facts, marks, motion, blocks[0], index))
        for c in range(3):
            part = value[c * WINDOW : (c + 1) * WINDOW] * weight_y
            sampled = jnp.sum(part, axis=0, keepdims=True)
            out[c, pl.ds(index, 1), :] = sampled if target is None else target[c] - sampled

    out[...] = jnp.zeros(out.shape, jnp.float32)
    slot_visits(layout, facts, marks, saved, blocks, step, high, low, visit)


def sample_kernel(layout, groups, moved, facts, *refs):
    count = len(groups)
    marks, refs = refs[:count], refs[count:]
    (field_high, field_low), refs = refs[:2], refs[2:]
    motion, refs = refs[:moved], refs[moved:]
    outs, refs = refs[:count], refs[count:]
    saved, (high, low) = refs[:count], refs[count:]
    for i, (blocks, step) in enumerate(groups):
        sample_slots(
            layout,
            facts,
            marks[i],
            motion,
            field_high,
            field_low,
            outs[i],
            saved[i],
            blocks,
            step,
            high,
            low,
        )


def visit_cost(layout, blocks):
    return len(blocks) * layout.slots * 18 * WINDOW * layout.plane * layout.markers


def weight_scratch(layout):
    return [pltpu.VMEM((layout.plane, layout.markers), jnp.bfloat16)] * 2


def sample(layout, groups, facts, marks, fields, motion):
    markers, weights = layout.markers, layout.sizes[0] + layout.sizes[1] + WINDOW
    counts = [len(blocks) * layout.slots for blocks, _ in groups]
    results = call(
        functools.partial(sample_kernel, layout, groups, len(motion)),
        [float32(3, count, markers) for count in counts]
        + [float32(count, weights, markers) for count in counts],
        [facts],
        [*marks, *fields, *motion],
        weight_scratch(layout),
        sum(visit_cost(layout, blocks) for blocks, _ in groups),
        8 * fields[0].size,
    )
    return results[: len(groups)], results[len(groups) :]


def spread_slots(layout, blocks, step, facts, saved, push, own_rows, total, high, low):
    def visit(index, row, first, weight_y, pieces):
        slot = index if own_rows else row
        count = sum(width for _, width in pieces)
        value = jnp.concatenate(
            [weight_y * push[c, pl.ds(slot, 1), :] for c in range(3)], axis=0
        )
        value_high, value_low = split(value)
        both = jnp.concatenate([value_high, value_low], axis=0)
        added = lax.dot_general(
            both, high[:count], TRANSPOSED, preferred_element_type=jnp.float32
        )
        rest = lax.dot_general(
            value_high, low[:count], TRANSPOSED, preferred_element_type=jnp.float32
        )
        added = added[: 3 * WINDOW] + added[3 * WINDOW :] + rest
        column = 0
        for lane, width in pieces:
            for c in range(3):
                part = added[c * WINDOW : (c + 1) * WINDOW, column : column + width]
                total[c, pl.ds(first, WINDOW), pl.ds(lane, width)] += part
            column += width

    slot_visits(layout, facts, None, saved, blocks, step, high, low, visit)


def spread_own_kernel(layout, facts, saved, push, total, high, low):
    total[...] = jnp.zeros(total.shape, jnp.float32)
    spread_slots(layout, (1,), 1, facts, saved, push, True, total, high, low)


def spread_own(layout, facts, saved, push):
    return call(
        functools.partial(spread_own_kernel, layout),
        float32(3, layout.sizes[2], layout.plane),
        [facts],
        [saved, push],
        weight_scratch(layout),
        visit_cost(layout, (1,)),
        12 * layout.sizes[2] * layout.plane,
    )


def spread_side_kernel(layout, facts, saved, push, before, total, high, low):
    total[...] = before[...]
    spread_slots(layout, (0, 2), 1, facts, saved, push, False, total, high, low)


def spread_side(layout, facts, saved, push, before):
    return call(
        functools.partial(spread_side_kernel, layout),
        float32(*before.shape),
        [facts],
        [saved, push, before],
        weight_scratch(layout),
        visit_cost(layout, (0, 2)),
        8 * before.size,
    )


def spread_rest_kernel(
    layout, parts, facts, saved_0, saved_1, push_0, push_1, before, predicted, velocity, *refs
):
    outs, (total, high, low, edges, whole) = refs[:parts], refs[parts:]
    size_x, size_z, size_y = layout.sizes
    total[...] = before[...]
    row = (0, 1, 2)
    spread_slots(layout, row, 0, facts, saved_0, push_0, False, total, high, low)
    spread_slots(layout, row, 2, facts, saved_1, push_1, False, total, high, low)
    for c in range(3):
        for q, (xs, zs) in enumerate(quarters(layout.sizes)):
            part = jnp.transpose(total[c, :, q * LANES : (q + 1) * LANES])
            part = part.reshape(size_x // 2, size_z // 2, size_y)
            velocity[c, xs, zs] = predicted[c, xs, zs] + part
    row = lax.broadcasted_iota(jnp.int32, (size_z, size_y), 0)
    lane = lax.broadcasted_iota(jnp.int32, (size_z, size_y), 1)
    group = LANES // size_z
    for q in range(size_x // group):
        pieces = []
        for x in range(q * group, (q + 1) * group):
            y_minus, y_plus = y_neighbours(velocity[1, x], lane, 0.0, 0.0)
            z_minus, z_plus = z_neighbours(velocity[2, x], row, 0.0, 0.0)
            change = y_plus - y_minus + z_plus - z_minus
            if x > 0:
                change -= velocity[0, x - 1]
            if x < size_x - 1:
                change += velocity[0, x + 1]
            pieces.append(change * 0.5)
        part = jnp.concatenate(pieces, axis=0)
        whole[:, q * LANES : (q + 1) * LANES] = jnp.transpose(part)
    edges[...] = jnp.zeros(edges.shape, jnp.float32)
    edges[:size_z] = velocity[0, 0]
    edges[size_z : 2 * size_z] = velocity[0, size_x - 1]
    for x in range(size_x):
        first = 2 * size_z + 2 * x
        edges[first : first + 1] = velocity[2, x, 0:1]
        edges[first + 1 : first + 2] = velocity[2, x, size_z - 1 : size_z]
    whole[:, layout.plane :] = jnp.transpose(edges[...])
    height = size_y // parts
    for out, step in zip(outs, steps(parts)):
        first = pl.multiple_of((lax.axis_index("gz") ^ step) * height, 8)
        out[...] = whole[pl.ds(first, height), :]


def spread_rest(layout, parts, facts, saved, pushes, before, predicted):
    size_x, size_z, size_y = layout.sizes
    assert 2 * size_z + 2 * size_x <= LANES
    width = layout.plane + LANES
    velocity, *pieces = call(
        functools.partial(spread_rest_kernel, layout, parts),
        [float32(3, size_x, size_z, size_y)] + [float32(size_y // parts, width)] * parts,
        [facts],
        [*saved, *pushes, before, predicted],
        [pltpu.VMEM(before.shape, jnp.float32)]
        + weight_scratch(layout)
        + [pltpu.VMEM((LANES, size_y), jnp.float32), pltpu.VMEM((size_y, width), jnp.float32)],
        2 * visit_cost(layout, (0, 1, 2)),
        12 * before.size,
    )
    return velocity, pieces


def pack_kernel(
    layout,
    slot_ids_hbm,
    corners_hbm,
    flow,
    cells_hbm,
    fraction_hbm,
    own,
    x_0,
    x_1,
    z_0,
    z_1,
    slot_ids,
    corners,
    cells,
    fraction,
    edges,
    done,
):
    size_x, size_z, size_y = layout.sizes
    slots = layout.slots
    moves = [
        (slot_ids_hbm, slot_ids),
        (corners_hbm, corners),
        (cells_hbm, cells),
        (fraction_hbm, fraction),
    ]
    for c in range(4):
        moves.append((flow.at[c, :, pl.ds(size_z - 8, 8)], edges.at[0, c]))
        moves.append((flow.at[c, :, pl.ds(0, 8)], edges.at[1, c]))
    last = jnp.where(even("gx"), size_x - 1, 0)
    for c in range(4):
        rows = pl.ds(c * size_z, size_z)
        moves.append((flow.at[c, last], x_0.at[rows]))
        moves.append((flow.at[c, size_x - 1 - last], x_1.at[rows]))
    copies = [pltpu.make_async_copy(a, b, done.at[i]) for i, (a, b) in enumerate(moves)]
    for copy in copies:
        copy.start()
    for copy in copies[:4]:
        copy.wait()
    length_x = size_x * lax.axis_size("gx")
    length_z = size_z * lax.axis_size("gz")
    offset_x = length_x + HALF - lax.axis_index("gx") * size_x
    offset_z = length_z + HALF - lax.axis_index("gz") * size_z
    targets = ((own, 0), (z_0, layout.ghost_z), (z_1, layout.ghost_z))
    for a, direction in enumerate((0, 2, 1)):
        for t in range(layout.tiles):
            lanes = slice(t * LANES, (t + 1) * LANES)
            place = cells[direction, :, lanes].astype(jnp.float32) + fraction[direction, :, lanes]
            for target, base in targets:
                first = base + (a * layout.tiles + t) * slots
                target[first : first + slots] = place
    lane = lax.broadcasted_iota(jnp.int32, (1, LANES), 1)
    for slot in range(slots):
        first_x = lax.rem(corners[0, slot] + offset_x, length_x) - HALF
        first_z = lax.rem(corners[2, slot] + offset_z, length_z) - HALF
        fact = jnp.where(lane == 0, first_x, slot_ids[slot] + 1)
        fact = jnp.where(lane == 1, first_z, fact)
        fact = jnp.where(lane == 2, corners[1, slot], fact)
        for target, base in targets:
            row = base + layout.fact_row + slot
            target[row : row + 1] = fact.astype(jnp.float32)
    for copy in copies[4:]:
        copy.wait()
    choose = in_order("gz", (1, size_y))
    for c in range(4):
        for x in range(size_x):
            row = c * size_x + x
            z_0[row : row + 1], z_1[row : row + 1] = choose(
                edges[1, c, x, 0:1], edges[0, c, x, 7:8]
            )


def pack(layout, slot_ids, corners, flow, cells, fraction):
    in_hbm = pl.BlockSpec(memory_space=pltpu.HBM)
    size_x, _, size_y = layout.sizes
    return pl.pallas_call(
        functools.partial(pack_kernel, layout),
        out_shape=[float32(layout.rows, LANES)]
        + [float32(layout.ghost_x, LANES)] * 2
        + [float32(layout.ghost_z + layout.rows, LANES)] * 2,
        in_specs=[in_hbm] * 5,
        out_specs=[IN_VMEM] * 5,
        scratch_shapes=[
            pltpu.SMEM(slot_ids.shape, jnp.int32),
            pltpu.SMEM(corners.shape, jnp.int32),
            pltpu.VMEM(cells.shape, jnp.int32),
            pltpu.VMEM(fraction.shape, jnp.float32),
            pltpu.VMEM((2, 4, size_x, 8, size_y), jnp.float32),
            pltpu.SemaphoreType.DMA((20,)),
        ],
        name="pack",
        cost_estimate=pl.CostEstimate(
            flops=flow.size, bytes_accessed=flow.size, transcendentals=0
        ),
    )(slot_ids, corners, flow, cells, fraction)


def join_kernel(left, right, both):
    rows = left.shape[0]
    both[:rows] = left[...]
    both[rows:] = right[...]


def join(left, right):
    return call(
        join_kernel,
        float32(2 * left.shape[0], LANES),
        [],
        [left, right],
        [],
        left.size,
        16 * left.size,
    )


def collect_kernel(layout, own, side_0, side_1, one, two, corners_0, corners_1, *refs):
    rows, (facts, table) = refs[:3], refs[3:]
    count, slots = layout.rows, layout.slots
    size_x, size_z, size_y = layout.sizes
    for row, middle, base, sides in (
        (rows[0], one, layout.ghost_z, corners_0),
        (rows[1], own, 0, None),
        (rows[2], two, layout.ghost_z, corners_1),
    ):
        row[:count] = side_0[...] if sides is None else sides[:count]
        row[count : 2 * count] = middle[base : base + count]
        row[2 * count :] = side_1[...] if sides is None else sides[count:]
    for block in range(9):
        first = (block % 3) * count + layout.fact_row
        out = slice(block * slots, (block + 1) * slots)
        table[out] = rows[block // 3][first : first + slots]
    kind = lax.broadcasted_iota(jnp.int32, (8, LANES), 0)
    slot = lax.broadcasted_iota(jnp.int32, (8, LANES), 1)
    last = 2 * 3 * slots
    move_x = jnp.where(even("gx"), size_x, -size_x)
    move_z = jnp.where(even("gz"), size_z, -size_z)
    place = slot - jnp.where(slot >= last, last, jnp.where(slot >= 3 * slots, 3 * slots, 0))
    moved_x = jnp.where(place < slots, move_x, jnp.where(place >= 2 * slots, -move_x, 0))
    moved_z = jnp.where(slot < 3 * slots, move_z, jnp.where(slot >= last, -move_z, 0))
    moved = jnp.where(kind == 0, moved_x, jnp.where(kind == 1, moved_z, 0))
    known = jnp.transpose(table[...])[:8].astype(jnp.int32) + moved
    first_x, first_z, first_y, particle = [known[i : i + 1] for i in range(4)]
    half_x, half_z = size_x // 2, size_z // 2

    def between(value, low, high):
        return (value > low) & (value < high)

    meets = between(first_x, -BOX, size_x) & between(first_z, -BOX, size_z) & (particle > 0)
    part_x = jnp.where(between(first_x, half_x - BOX, half_x), 0, 2)
    part_z = jnp.where(between(first_z, half_z - BOX, half_z), 0, 1)
    facts[...] = known
    facts[4:5] = jnp.where(meets, 1 + part_x + part_z, 0)
    facts[5:6] = jnp.minimum(jnp.bitwise_and(first_y, -8), size_y - WINDOW)
    facts[6:7] = jnp.where(first_x >= half_x, 1, 0)
    facts[7:8] = jnp.where(first_z >= half_z, 1, 0)


def collect(layout, *tiles):
    return call(
        functools.partial(collect_kernel, layout),
        [float32(3 * layout.rows, LANES)] * 3 + [jax.ShapeDtypeStruct((8, LANES), jnp.int32)],
        [],
        tiles,
        [pltpu.VMEM((LANES, LANES), jnp.float32)],
        layout.rows * LANES,
        72 * layout.rows * LANES,
    )


def y_neighbours(value, lane, below, above):
    size_y = value.shape[-1]
    minus = jnp.where(lane == 0, below, pltpu.roll(value, 1, 1))
    plus = jnp.where(lane == size_y - 1, above, pltpu.roll(value, size_y - 1, 1))
    return minus, plus


def z_neighbours(value, row, below, above):
    size_z = value.shape[0]
    minus = jnp.where(row == 0, below, pltpu.roll(value, 1, 0))
    plus = jnp.where(row == size_z - 1, above, pltpu.roll(value, size_z - 1, 0))
    return minus, plus


def predict_inner_kernel(sizes, flow, own, inner, u_first, u_last, w_first, w_last, kept):
    size_x, size_z, size_y = sizes
    row = lax.broadcasted_iota(jnp.int32, (size_z, size_y), 0)
    lane = lax.broadcasted_iota(jnp.int32, (size_z, size_y), 1)
    nothing = jnp.zeros((size_z, size_y), jnp.float32)

    def around(c, x):
        value = flow[c, x]
        x_minus = flow[c, x - 1] if x > 0 else nothing
        x_plus = flow[c, x + 1] if x < size_x - 1 else nothing
        z_minus, z_plus = z_neighbours(value, row, 0.0, 0.0)
        edges = (0.0, 0.0) if c < 3 else (value, value)
        y_minus, y_plus = y_neighbours(value, lane, *edges)
        return value, x_minus, x_plus, z_minus, z_plus, y_minus, y_plus

    for x in range(size_x):
        _, x_minus, x_plus, z_minus, z_plus, y_minus, y_plus = around(3, x)
        gradient = (
            (x_plus - x_minus) * 0.5 - drive_force,
            (y_plus - y_minus) * 0.5,
            (z_plus - z_minus) * 0.5,
        )
        carried = (flow[0, x], flow[1, x], flow[2, x])
        for c in range(3):
            value, x_minus, x_plus, z_minus, z_plus, y_minus, y_plus = around(c, x)
            laplace = x_plus + x_minus + z_plus + z_minus + y_plus + y_minus - 6.0 * value
            advect = (
                carried[0] * (x_plus - x_minus)
                + carried[1] * (y_plus - y_minus)
                + carried[2] * (z_plus - z_minus)
            ) * 0.5
            inner[c, x] = value + time_step * (viscosity * laplace - advect - gradient[c])
        w_first[x : x + 1] = flow[2, x, 0:1]
        w_last[x : x + 1] = flow[2, x, size_z - 1 : size_z]
    kept[...] = own[...]
    u_first[...] = flow[0, 0]
    u_last[...] = flow[0, size_x - 1]


def predict_inner(sizes, flow, own):
    size_x, size_z, size_y = sizes
    return call(
        functools.partial(predict_inner_kernel, sizes),
        [float32(3, *sizes)]
        + [float32(size_z, size_y)] * 2
        + [float32(size_x, size_y)] * 2
        + [float32(*own.shape)],
        [],
        [flow, own],
        [],
        200 * flow.size,
        8 * flow.size,
    )


def predict_outer_kernel(
    layout,
    inner,
    u_first,
    u_last,
    w_first,
    w_last,
    x_0,
    x_1,
    z_0,
    z_1,
    predicted,
    field_high,
    field_low,
):
    size_x, size_z, size_y = layout.sizes
    row = lax.broadcasted_iota(jnp.int32, (8, size_y), 0)
    lower, upper = in_order("gz", z_0[: layout.ghost_z].shape)(
        z_0[: layout.ghost_z], z_1[: layout.ghost_z]
    )
    left, right = in_order("gx", x_0.shape)(x_0[...], x_1[...])
    for x in range(size_x):
        carried_low = w_first[x : x + 1]
        carried_high = w_last[x : x + 1]
        for c in range(3):
            ghost = c * size_x + x
            change_low = (viscosity + 0.5 * carried_low) * lower[ghost : ghost + 1]
            change_high = (viscosity - 0.5 * carried_high) * upper[ghost : ghost + 1]
            if c == 2:
                ghost = 3 * size_x + x
                change_low += 0.5 * lower[ghost : ghost + 1]
                change_high -= 0.5 * upper[ghost : ghost + 1]
            if x in (0, size_x - 1):
                sign, layer, carried = (0.5, left, u_first) if x == 0 else (-0.5, right, u_last)
                ghost = slice(c * size_z, (c + 1) * size_z)
                change = (viscosity + sign * carried[...]) * layer[ghost]
                if c == 0:
                    change += sign * layer[3 * size_z : 4 * size_z]
                predicted[c, x] = inner[c, x] + time_step * change
            else:
                predicted[c, x] = inner[c, x]
            predicted[c, x, 0:8] += jnp.where(row == 0, time_step * change_low, 0.0)
            predicted[c, x, size_z - 8 : size_z] += jnp.where(
                row == 7, time_step * change_high, 0.0
            )
    for c in range(3):
        for q, (xs, zs) in enumerate(quarters(layout.sizes)):
            part = jnp.transpose(predicted[c, xs, zs].reshape(LANES, size_y))
            high = part.astype(jnp.bfloat16).astype(jnp.float32)
            field_high[c, :, q * LANES : (q + 1) * LANES] = high
            field_low[c, :, q * LANES : (q + 1) * LANES] = part - high


def predict_outer(layout, inner, *layers):
    _, _, size_y = layout.sizes
    return call(
        functools.partial(predict_outer_kernel, layout),
        [float32(3, *layout.sizes)] + [float32(3, size_y, layout.plane)] * 2,
        [],
        [*inner, *layers],
        [],
        10 * inner[0].size,
        16 * inner[0].size,
    )


def swap_groups(values, width):
    count = len(values)
    lane = lax.broadcasted_iota(jnp.int32, values[0].shape, 1)
    values = list(values)
    step = count // 2
    while step:
        reach = step * width
        keep = lane % (2 * reach) < reach
        for i in range(count):
            if i & step == 0:
                a, b = values[i], values[i + step]
                if 2 * reach == LANES:
                    crossed = pltpu.roll(jnp.where(keep, b, a), reach, 1)
                    values[i] = jnp.where(keep, a, crossed)
                    values[i + step] = jnp.where(keep, crossed, b)
                    continue
                values[i] = jnp.where(keep, a, pltpu.roll(b, reach, 1))
                values[i + step] = jnp.where(keep, pltpu.roll(a, LANES - reach, 1), b)
        step //= 2
    return values


def copy_kernel(source, target):
    target[...] = source[...]


def copied(array):
    return call(copy_kernel, float32(*array.shape), [], [array], [], 1, 8 * array.size)


def transform_z_kernel(sizes, counts, table_high, table_low, *refs):
    size_x, size_z, size_y = sizes
    parts_x, parts_z = counts
    pieces, refs = refs[:parts_z], refs[parts_z:]
    outs, (gathered, turned, whole) = refs[:parts_x], refs[parts_x:]
    height = size_y // parts_z
    columns = height * size_x
    group = LANES // size_z
    for piece, step in zip(pieces, steps(parts_z)):
        gathered[lax.axis_index("gz") ^ step] = piece[...]
    lane = lax.broadcasted_iota(jnp.int32, (height, LANES), 1)
    edges = [gathered[i, :, size_x * size_z :] for i in range(parts_z)]
    blocks = parts_z // group
    for block in range(blocks):
        for q in range(size_x // group):
            lanes = slice(q * LANES, (q + 1) * LANES)
            values = [gathered[block * group + i, :, lanes] for i in range(group)]
            for j, value in enumerate(swap_groups(values, size_z)):
                turned[block, pl.ds(q * group + j, height, stride=size_x), :] = value
        for end in range(2):
            layer = edges[block * group]
            for i in range(group):
                moved = (i - end) * size_z % LANES
                part = edges[block * group + i]
                part = pltpu.roll(part, moved, 1) if moved else part
                layer = part if i == 0 else jnp.where(lane < i * size_z, layer, part)
            turned[block, pl.ds(columns + end, height, stride=2), :] = layer
        for i in range(group):
            moved = (i - 2) * size_z % LANES
            part = edges[block * group + i]
            part = pltpu.roll(part, moved, 1) if moved else part
            ends = part if i == 0 else jnp.where(lane < i * size_z, ends, part)
        for x in range(size_x):
            moved = -2 * x % LANES
            turned[blocks + block, pl.ds(x, height, stride=size_x), :] = (
                pltpu.roll(ends, moved, 1) if moved else ends
            )
        turned[blocks + block, columns:] = jnp.zeros((2 * height, LANES), jnp.float32)
    lines = jnp.concatenate([turned[b] for b in range(2 * blocks)], axis=1)
    high, low = split(lines)
    result = lax.dot_general(
        table_high[...], high, TRANSPOSED, preferred_element_type=jnp.float32
    )
    result += lax.dot_general(
        table_low[...], high, TRANSPOSED, preferred_element_type=jnp.float32
    )
    result += lax.dot_general(
        table_high[...], low, TRANSPOSED, preferred_element_type=jnp.float32
    )
    whole[:, columns:] = jnp.zeros((whole.shape[0], LANES), jnp.float32)
    whole[:, : columns + 2 * height] = result
    rows = whole.shape[0] // parts_x
    modes = rows // 2
    lane = lax.broadcasted_iota(jnp.int32, (modes, LANES), 1)
    for out, step in zip(outs, steps(parts_x)):
        first = pl.multiple_of((lax.axis_index("gx") ^ step) * rows, 8)
        for t in range(columns // LANES):
            out[t * rows : (t + 1) * rows] = whole[
                pl.ds(first, rows), t * LANES : (t + 1) * LANES
            ]
        real = whole[pl.ds(first, modes), columns : columns + LANES]
        imag = whole[pl.ds(first + modes, modes), columns : columns + LANES]
        imag = pltpu.roll(imag, 2 * height, 1)
        out[columns // LANES * rows :] = jnp.where(lane < 2 * height, real, imag)


def transform_z(sizes, counts, table, pieces):
    size_x, size_z, size_y = sizes
    parts_x, parts_z = counts
    length_z = size_z * parts_z
    height = size_y // parts_z
    columns = height * size_x
    assert 4 * height <= LANES
    rows = 2 * length_z // parts_x
    return call(
        functools.partial(transform_z_kernel, sizes, counts),
        [float32(columns // LANES * rows + rows // 2, LANES)] * parts_x,
        [],
        [*table, *pieces],
        [
            pltpu.VMEM((parts_z, *pieces[0].shape), jnp.float32),
            pltpu.VMEM((2 * length_z // LANES, columns + 2 * height, LANES), jnp.float32),
            pltpu.VMEM((2 * length_z, columns + LANES), jnp.float32),
        ],
        24 * length_z * length_z * columns,
        12 * length_z * columns,
    )


def transform_x_kernel(sizes, counts, table_high, table_low, *refs):
    size_x, size_z, size_y = sizes
    parts_x, parts_z = counts
    pieces, (source, gathered, turned) = refs[:parts_x], refs[parts_x:]
    length_x = size_x * parts_x
    modes = size_z * parts_z // parts_x
    height = size_y // parts_z
    group = LANES // size_x
    rows = 2 * modes
    main = height // group * rows
    for piece, step in zip(pieces, steps(parts_x)):
        gathered[lax.axis_index("gx") ^ step] = piece[...]
    for block in range(parts_x // group):
        for q in range(height // group):
            values = [
                gathered[block * group + i, q * rows : (q + 1) * rows] for i in range(group)
            ]
            for j, value in enumerate(swap_groups(values, size_x)):
                first = (q * group + j) * modes
                for c in range(2):
                    column = c * length_x + block * LANES
                    turned[first : first + modes, column : column + LANES] = value[
                        c * modes : (c + 1) * modes
                    ]
        ends = [gathered[block * group + i, main:] for i in range(group)]
        column = 2 * length_x + block * LANES
        for j, value in enumerate(swap_groups(ends, 2)):
            for q in range(height // group):
                first = (q * group + j) * modes
                moved = -2 * group * q % LANES
                turned[first : first + modes, column : column + LANES] = (
                    pltpu.roll(value, moved, 1) if moved else value
                )
    high, low = split(turned[...])
    result = jnp.dot(high, table_high[...], preferred_element_type=jnp.float32)
    result += jnp.dot(low, table_high[...], preferred_element_type=jnp.float32)
    result += jnp.dot(high, table_low[...], preferred_element_type=jnp.float32)
    source[0] = result[:, :length_x].reshape(height, modes, length_x)
    source[1] = result[:, length_x:].reshape(height, modes, length_x)


def transform_x(sizes, counts, table, pieces):
    size_x, size_z, size_y = sizes
    parts_x, parts_z = counts
    length_x = size_x * parts_x
    modes = size_z * parts_z // parts_x
    height = size_y // parts_z
    return call(
        functools.partial(transform_x_kernel, sizes, counts),
        float32(2, height, modes, length_x),
        [],
        [*table, *pieces],
        [
            pltpu.VMEM((parts_x, *pieces[0].shape), jnp.float32),
            pltpu.VMEM((height * modes, table[0].shape[0]), jnp.float32),
        ],
        24 * length_x * length_x * height * modes,
        24 * length_x * height * modes,
    )


def split_table(table):
    high = table.astype(np.float32).astype(jnp.bfloat16)
    low = (table - high.astype(np.float64)).astype(np.float32).astype(jnp.bfloat16)
    return jnp.asarray(high), jnp.asarray(low)


def angles(length):
    counter = np.arange(length)
    turn = (counter[:, None] * counter[None, :] % length) * (2.0 * np.pi / length)
    return np.cos(turn), np.sin(turn)


def table_z(length, blocks, parts):
    cosine, sine = angles(length)
    modes, size = length // blocks, length // parts
    table = np.stack([cosine, -sine]).reshape(2, blocks, modes, length)
    table = table.transpose(1, 0, 2, 3).reshape(2 * length, length)
    ends = np.zeros((2 * length, length))
    for part in range(parts):
        ends[:, part * size] = 0.5 * table[:, (part * size - 1) % length]
        ends[:, part * size + 1] = -0.5 * table[:, (part + 1) * size % length]
    return split_table(np.concatenate([table, ends], axis=1))


def table_x(length, parts, height, scale):
    cosine, sine = angles(length)
    size = length // parts
    group = LANES // size
    table = np.block([[cosine, -sine], [sine, cosine]]) * scale
    ends = np.zeros((parts // group * LANES, 2 * length))
    for part in range(parts):
        for c in range(2):
            row = part // group * LANES + c * 2 * height + 2 * (part % group)
            ends[row] = 0.5 * table[c * length + (part * size - 1) % length]
            ends[row + 1] = -0.5 * table[c * length + (part + 1) * size % length]
    return split_table(np.concatenate([table, ends], axis=0))


def exchange(pieces, axis):
    devices = lax.axis_size(axis)
    assert devices & (devices - 1) == 0
    received = [pieces[0]]
    for piece, step in zip(pieces[1:], steps(devices)[1:]):
        received.append(lax.ppermute(piece, axis, [(i, i ^ step) for i in range(devices)]))
    return received


def on_device(
    flow_state, slot_ids, corners, marker_cells, marker_frac, particle_velocity, particle_spin
):
    sizes = flow_state.shape[1:]
    size_x, size_z, size_y = sizes
    counts = (lax.axis_size("gx"), lax.axis_size("gz"))
    length_x, length_z = (size_x * counts[0], size_z * counts[1])
    slots, markers = marker_cells.shape[1:]
    layout = Layout(sizes, slots, markers)

    own, x_0, x_1, z_0, z_1 = pack(
        layout, slot_ids, corners, flow_state, marker_cells, marker_frac
    )
    marks_0 = swap(own, "gx", 0)
    marks_1 = swap(own, "gx", 1)
    z_0, z_1 = swap(z_0, "gz", 0), swap(z_1, "gz", 1)
    x_0, x_1 = swap(x_0, "gx", 0), swap(x_1, "gx", 1)
    *inner, own = predict_inner(sizes, flow_state, own)
    sides = join(marks_0, marks_1)
    corners_0, corners_1 = swap(sides, "gz", 0), swap(sides, "gz", 1)
    predicted, *fields = predict_outer(layout, inner, x_0, x_1, z_0, z_1)
    row_0, row, row_1, facts = collect(
        layout, own, marks_0, marks_1, z_0, z_1, corners_0, corners_1
    )

    tiles = (0, 1, 2)
    parts, rows_saved = sample(layout, ((tiles, 0), (tiles, 2)), facts, (row_0, row_1), fields, ())
    from_z = swap(parts[0], "gz", 0) + swap(parts[1], "gz", 1)
    (side_part,), (side_saved,) = sample(layout, (((0, 2), 1),), facts, (row,), fields, ())
    from_0 = swap(side_part[:, :slots] + from_z[:, :slots], "gx", 0)
    from_1 = swap(side_part[:, slots:] + from_z[:, 2 * slots :], "gx", 1)
    motion = (particle_velocity, particle_spin)
    (own_part,), (own_saved,) = sample(layout, (((1,), 1),), facts, (row,), fields, motion)
    push = own_part - (from_z[:, slots : 2 * slots] + from_0 + from_1)

    push_0 = swap(push, "gx", 0)
    push_1 = swap(push, "gx", 1)
    row_push = jnp.concatenate([push_0, push, push_1], axis=1)
    rows_push = swap(row_push, "gz", 0), swap(row_push, "gz", 1)
    forcing = spread_own(layout, facts, own_saved, push)
    forcing = spread_side(layout, facts, side_saved, row_push, forcing)
    velocity, pieces = spread_rest(
        layout, counts[1], facts, rows_saved, rows_push, forcing, predicted
    )

    pieces = exchange(pieces, "gz")
    pieces = transform_z(sizes, counts, table_z(length_z, *counts), pieces)
    pieces = exchange(pieces, "gx")
    velocity = copied(velocity)
    scale = 1.0 / math.sqrt(length_x * length_z)
    table = table_x(length_x, counts[0], size_y // counts[1], scale)
    source = transform_x(sizes, counts, table, pieces)
    return velocity, source


def solution(mesh):
    return jax.shard_map(
        on_device,
        mesh=mesh,
        in_specs=(
            P(None, "gx", "gz", None),
            P(("gx", "gz")),
            P(None, ("gx", "gz")),
            P(None, ("gx", "gz"), None),
            P(None, ("gx", "gz"), None),
            P(),
            P(),
        ),
        out_specs=(P(None, "gx", "gz", None), P(None, "gz", "gx", None)),
        check_vma=False,
    )
```
